32 devices in a mesh: rep: 2 (over y), grp: 16 (over z, x, core).
Axes of the slice: x: 2, y: 2, z: 4, core: 2. Of those that a mesh axis runs over, the one named last changes fastest.
Arguments:
- block_input: bfloat16 [32768, 768], P(('rep', 'grp')), may hold values from -6 to 6
- prev_logits: float32 [32768, 8], P(('rep', 'grp')), may hold values from -6 to 6
- routes: int32 [32768, 2], P(('rep', 'grp')), may hold values from 0 to 7, all different within a row; in each aligned block of 512 rows (0 to 511, 512 to 1023, ...) at most 256 rows name the same one
- segments: int32 [64, 512], P(('rep', 'grp')), may hold values from 0 to 3, never falling along the last dimension, each value on 1 to 256 neighbouring positions
- grad_out: bfloat16 [32768, 768], P(('rep', 'grp')), may hold values from -6 to 6
- gain_attn: float32 [768], P('grp'), may hold values from 0.5 to 1.5
- w_query: float32 [768, 768], P('grp'), may hold values from -0.21875 to 0.21875
- w_key: float32 [768, 768], P('grp'), may hold values from -0.21875 to 0.21875
- w_value: float32 [768, 768], P('grp'), may hold values from -0.21875 to 0.21875
- w_output: float32 [768, 768], P('grp'), may hold values from -0.875 to 0.875
- gain_mix: float32 [768], P('grp'), may hold values from 0.5 to 1.5
- router: float32 [768, 8], P('grp'), may hold values from -0.21650635 to 0.21650635
- route_map: float32 [8, 8], replicated, may hold values from -1.2 to 1.2
- const_proj: float32 [768, 4], P('grp'), may hold values from -0.21875 to 0.21875
- const_vec: float32 [768, 2], P('grp'), may hold values from -6 to 6
- w_gate: float32 [768, 4, 2048], P('grp'), may hold values from -0.21875 to 0.21875
- w_up: float32 [768, 4, 2048], P('grp'), may hold values from -0.21875 to 0.21875
- w_down: float32 [2048, 4, 768], P('grp'), may hold values from -0.25 to 0.25
Outputs:
- block_output: float32 [32768, 768], P(('rep', 'grp'))
- grad_input: float32 [32768, 768], P(('rep', 'grp'))
- grad_gain_attn: float32 [768], P('grp')
- grad_w_query: float32 [768, 768], P('grp')
- grad_w_key: float32 [768, 768], P('grp')
- grad_w_value: float32 [768, 768], P('grp')
- grad_w_output: float32 [768, 768], P('grp')
- grad_gain_mix: float32 [768], P('grp')
- grad_router: float32 [768, 8], P('grp')
- grad_route_map: float32 [8, 8], replicated
- grad_const_proj: float32 [768, 4], P('grp')
- grad_const_vec: float32 [768, 2], P('grp')
- grad_w_gate: float32 [768, 4, 2048], P('grp')
- grad_w_up: float32 [768, 4, 2048], P('grp')
- grad_w_down: float32 [2048, 4, 768], P('grp')
The draws below stay inside these ranges and needn't reach their ends.
Inputs may be any that keep to these rules, and one draw needn't show every extreme that they name: `routes`: each row names two different experts; within one sequence no expert is named by more than 256 tokens. `segments`: document numbers never fall along a sequence; a document has at most 256 tokens.
All inputs are finite; a program needn't handle non-finite values.
Results may differ from the reference program's by a relative error of at most 0.017.
Values may be sent and summed in bfloat16 or wider, within the bound.
A program may use at most 448 MiB of HBM per device.

```python
import math
import jax
import jax.numpy as jnp
import numpy as np
from jax import lax

D = 768
HEAD_DIM = 64
FF = 2048
FFN_EXP = 4
BLOCK = 256
SEQ = 512
EXPERTS = 8
CAP = 256
NSEQ = 64
TOKENS = 32768


def steps_of(stream_key, extent, split, least, largest):
    def one(dim, parts):
        heights = jax.random.uniform(jax.random.fold_in(jax.random.fold_in(stream_key, 6), dim), (parts,), jnp.float32, least / len(split), largest / len(split))
        return jnp.repeat(jnp.exp(heights), extent[dim] // parts).reshape((-1,) + (1,) * (len(extent) - dim - 1))

    gain = one(*split[0])
    for cut in split[1:]:
        gain = gain * one(*cut)
    return gain


def length_profile(amount, total, limit, slope):
    loads = [(1 << 20) // math.isqrt(rank ** slope) + 1 for rank in range(2, amount + 1)]
    spare, given = total - limit - (amount - 1), [1] * (amount - 1)
    while spare > 0:
        free = [i for i in range(amount - 1) if given[i] < limit]
        pool, budget = sum([loads[i] for i in free]), spare
        for i in free:
            addition = min(limit - given[i], max(1, budget * loads[i] // pool), spare)
            given[i] = given[i] + addition
            spare = spare - addition
    return np.array([limit] + given)


def ragged(own_key, amount, total, most, skew):
    if amount == 2:
        one = jax.random.randint(own_key, (), max(1, total - most), min(most, total - 1) + 1)
        return jnp.stack([one, total - one])
    sizes = jnp.asarray(length_profile(amount, total, most, skew), jnp.int32)
    twos = (amount - 1) // 2
    source_of, receiver = sizes[1:1 + 2 * twos:2], sizes[2:2 + 2 * twos:2]
    slack = jnp.minimum(source_of - 1, most - receiver)
    moved = jax.random.randint(jax.random.fold_in(own_key, 1), (twos,), 0, 1 << 20) % (slack + 1)
    sizes = sizes.at[1:1 + 2 * twos:2].set(source_of - moved).at[2:2 + 2 * twos:2].set(receiver + moved)
    return sizes[jax.random.permutation(jax.random.fold_in(own_key, 2), amount)]


def deal_out(own_key, own, number, rows, count, top, most, lean):
    sequence = jax.random.permutation(own_key, count)
    heavy_load, usual = load_shares(count, rows * top, most, lean, True), load_shares(count, rows * top, most, lean, False)
    places = jnp.arange(count)

    def named(sizes, offset_by):
        used = int((sizes > 0).sum())
        fixed = max(1, used // 4)
        moved = fixed + (places - fixed + offset_by * (used - fixed)) % max(1, count - fixed)
        return jnp.zeros((count,), jnp.int32).at[sequence[jnp.where(places < fixed, places, moved)]].set(jnp.asarray(sizes, jnp.int32))

    sizes = jnp.where(number % 4 == 0, named(heavy_load, number // 4), named(usual, number - number // 4 - 1))
    mixed = jax.random.permutation(jax.random.fold_in(own, 3), count)
    giver, taker = mixed[0:count // 2 * 2:2], mixed[1:count // 2 * 2:2]
    room = jnp.minimum(sizes[giver] - 1, most - sizes[taker]) // 2
    room = jnp.where((giver == sequence[0]) | (taker == sequence[0]) | (sizes[taker] == 0), 0, jnp.maximum(room, 0))
    moved = jax.random.randint(jax.random.fold_in(own, 4), (count // 2,), 0, 1 << 20) % (room + 1)
    sizes = sizes.at[giver].add(-moved).at[taker].add(moved)
    members = jnp.searchsorted(jnp.cumsum(sizes), jnp.arange(rows * top), side="right").astype(jnp.int32)
    table = members.reshape(top, rows).T
    table = table[jax.random.permutation(jax.random.fold_in(own, 1), rows)]
    offset_by = jax.random.randint(jax.random.fold_in(own, 2), (rows, 1), 0, top)
    return jnp.take_along_axis(table, (jnp.arange(top)[None, :] + offset_by) % top, axis=1)


def load_shares(amount, total, bound, lean, full):
    weights = [(1 << 20) // math.isqrt(grade ** lean) + 1 for grade in range(1, amount + 1)]
    largest = bound if full else min(bound, max(-(-total // amount), total * weights[0] // sum(weights)))
    least = 1 if total - largest >= amount - 1 else 0
    holding, rest = [largest] + [least] * (amount - 1), total - largest - least * (amount - 1)
    while rest > 0:
        candidates = [i for i in range(1, amount) if holding[i] < largest] or [i for i in range(1, amount) if holding[i] < bound]
        mass, budget = sum([weights[i] for i in candidates]), rest
        for i in candidates:
            extra = min(bound - holding[i], max(1, budget * weights[i] // mass), rest)
            holding[i] = holding[i] + extra
            rest = rest - extra
    return np.array(holding)


def scatter_about(stream_key, extent, width, most, pieces=(), dtype=jnp.bfloat16):
    values = width * jax.random.normal(stream_key, extent, jnp.float32)
    if pieces:
        values = values * steps_of(stream_key, extent, pieces, -0.22, 0.18)
    return jnp.clip(values, -most, most).astype(dtype)


def setup_inputs(seed: int = 0) -> dict:
    seeds = jax.random.split(jax.random.key(seed), 19)
    block_input = scatter_about(seeds[0], (TOKENS, D), 1.0, 6.0, ((0, 32),))
    prev_logits = scatter_about(seeds[1], (TOKENS, EXPERTS), 1.0, 6.0, ((0, 32),), jnp.float32)
    routes_keys = jax.random.split(jax.random.fold_in(seeds[2], 1), TOKENS // SEQ)
    routes_turns = jax.random.permutation(jax.random.fold_in(seeds[2], 3), TOKENS // SEQ)
    routes = jax.vmap(lambda own, number: deal_out(jax.random.fold_in(seeds[2], 2), own, number, SEQ, EXPERTS, 2, CAP, 0))(routes_keys, routes_turns).reshape((TOKENS, 2))
    segments = jax.vmap(lambda own: jnp.searchsorted(jnp.cumsum(ragged(own, 4, SEQ, SEQ // 2, 0)), jnp.arange(SEQ), side="right"))(jax.random.split(seeds[3], NSEQ)).reshape((NSEQ, SEQ)).astype(jnp.int32)
    grad_out = scatter_about(seeds[4], (TOKENS, D), 1.0, 6.0, ((0, 32),))
    gain_attn = jnp.clip(1.0 + 0.1 * jax.random.normal(seeds[5], (D,), jnp.float32), 0.5, 1.5)
    w_query = scatter_about(seeds[6], (D, D), D ** -0.5, 0.21875, ((0, 16),), jnp.float32)
    w_key = scatter_about(seeds[7], (D, D), D ** -0.5, 0.21875, ((0, 16),), jnp.float32)
    w_value = scatter_about(seeds[8], (D, D), D ** -0.5, 0.21875, ((0, 16),), jnp.float32)
    w_output = scatter_about(seeds[9], (D, D), (D // 16) ** -0.5, 0.875, ((0, 16),), jnp.float32)
    gain_mix = jnp.clip(1.0 + 0.1 * jax.random.normal(seeds[10], (D,), jnp.float32), 0.5, 1.5)
    router = scatter_about(seeds[11], (D, EXPERTS), (0.6 * D ** -0.5), 0.21650635, ((0, 16),), jnp.float32)
    route_map = scatter_about(seeds[12], (EXPERTS, EXPERTS), 0.2, 1.2, (), jnp.float32)
    const_proj = scatter_about(seeds[13], (D, 4), D ** -0.5, 0.21875, ((0, 16),), jnp.float32)
    const_vec = scatter_about(seeds[14], (D, 2), 1.0, 6.0, ((0, 16),), jnp.float32)
    w_gate = scatter_about(seeds[15], (D, FFN_EXP, FF), D ** -0.5, 0.21875, ((0, 16),), jnp.float32)
    w_up = scatter_about(seeds[16], (D, FFN_EXP, FF), D ** -0.5, 0.21875, ((0, 16),), jnp.float32)
    w_down = scatter_about(seeds[17], (FF, FFN_EXP, D), (FF // 4) ** -0.5, 0.25, ((0, 16),), jnp.float32)
    return dict(block_input=block_input, prev_logits=prev_logits, routes=routes, segments=segments, grad_out=grad_out, gain_attn=gain_attn, w_query=w_query, w_key=w_key, w_value=w_value, w_output=w_output, gain_mix=gain_mix, router=router, route_map=route_map, const_proj=const_proj, const_vec=const_vec, w_gate=w_gate, w_up=w_up, w_down=w_down)


@jax.custom_vjp
def low(v):
    return lax.optimization_barrier(v.astype(jnp.bfloat16)).astype(jnp.float32)

@jax.custom_vjp
def low_back(v):
    return v

def low_keep(v):
    return (low(v), None)

def low_pass(kept, grad):
    return (grad,)

def back_keep(v):
    return (v, None)

def back_low(kept, grad):
    return (low(grad),)
low.defvjp(low_keep, low_pass)
low_back.defvjp(back_keep, back_low)
epsilon = 1e-05
highest = lax.Precision.HIGHEST

def matmul(left, right):
    return jnp.dot(left, right, precision=highest)

def rotary(length, head_width):
    halfway = head_width // 2
    frequency = 10000.0 ** (-jnp.arange(halfway).astype(jnp.float32) / halfway)
    angles = jnp.arange(length).astype(jnp.float32)[:, None] * frequency[None, :]
    return (jnp.cos(angles), jnp.sin(angles))

def rotate(values, cosine_table, sine_table):
    halfway = values.shape[-1] // 2
    lower_half = values[..., :halfway]
    upper_half = values[..., halfway:]
    cosine_part = cosine_table[:, None, :]
    sine_part = sine_table[:, None, :]
    return jnp.concatenate([lower_half * cosine_part - upper_half * sine_part, lower_half * sine_part + upper_half * cosine_part], axis=-1)

def rms_scale(values):
    return lax.rsqrt(lax.optimization_barrier(jnp.mean(values * values, axis=-1, keepdims=True)) + epsilon)

def sequence_pass(weights, tokens, previous, chosen, labels):
    gain_attn, w_query, w_key, w_value, w_output, gain_mix, router, route_map, const_proj, const_vec, w_gate, w_up, w_down = weights
    length = tokens.shape[0]
    model_width = tokens.shape[1]
    head_count = model_width // HEAD_DIM
    cosine_table, sine_table = rotary(length, HEAD_DIM)
    normed = tokens * rms_scale(tokens) * gain_attn
    normed_low = low(normed)
    queries = low(rotate(low_back(matmul(normed_low, w_query)).reshape(length, head_count, HEAD_DIM), cosine_table, sine_table))
    keys_rot = low(rotate(low_back(matmul(normed_low, w_key)).reshape(length, head_count, HEAD_DIM), cosine_table, sine_table))
    values_low = low(low_back(matmul(normed_low, w_value))).reshape(length, head_count, HEAD_DIM)
    scores = low_back(jnp.einsum('qhd,khd->hqk', queries, keys_rot, precision=highest) * 0.125)
    places = jnp.arange(length) // BLOCK
    allowed = (labels[:, None] == labels[None, :]) & (places[None, :] <= places[:, None])
    scores = jnp.where(allowed[None], scores, -1000000000.0)
    attention = jax.nn.softmax(scores, axis=-1)
    mixture = jnp.einsum('hqk,khd->qhd', low(attention), values_low, precision=highest).reshape(length, model_width)
    mixture_low = low(low_back(mixture))
    hidden = tokens + low_back(matmul(mixture_low, w_output))
    normed_mix = hidden * rms_scale(hidden) * gain_mix
    mix_low = low(normed_mix)
    logits = matmul(mix_low, router) + matmul(previous, route_map)
    expert_kinds = router.shape[1]
    ffn_count = w_gate.shape[1]
    kinds_range = jnp.arange(expert_kinds)
    first_hot = (chosen[:, 0:1] == kinds_range[None, :]).astype(jnp.float32)
    second_hot = (chosen[:, 1:2] == kinds_range[None, :]).astype(jnp.float32)
    picked = jnp.stack([lax.optimization_barrier(jnp.sum(logits * first_hot, axis=-1)), lax.optimization_barrier(jnp.sum(logits * second_hot, axis=-1))], axis=-1)
    gate_pair = jax.nn.softmax(picked, axis=-1)
    weight_of = gate_pair[:, 0:1] * first_hot + gate_pair[:, 1:2] * second_hot
    result = hidden + weight_of[:, ffn_count + 1:ffn_count + 2] * normed_mix
    for expert in range(ffn_count):
        gate_pre = low_back(matmul(mix_low, w_gate[:, expert, :]))
        up_pre = low_back(matmul(mix_low, w_up[:, expert, :]))
        activated = low(jax.nn.silu(gate_pre) * up_pre)
        output = low_back(matmul(activated, w_down[:, expert, :]))
        result = result + weight_of[:, expert:expert + 1] * output
    for constant in range(2):
        mixing = jax.nn.softmax(matmul(normed_mix, const_proj[:, 2 * constant:2 * constant + 2]), axis=-1)
        constant_value = mixing[:, 0:1] * normed_mix + mixing[:, 1:2] * const_vec[None, :, constant]
        column = ffn_count + 2 + constant
        result = result + weight_of[:, column:column + 1] * constant_value
    return result

def forward(params, tokens, previous, routes, segments):
    lowered = tuple((params[number] if number == 7 else low(params[number]) for number in range(len(params))))
    length = segments.shape[1]
    model_width = tokens.shape[1]
    stepper = jax.checkpoint(sequence_pass)
    token_seqs = tokens.reshape(-1, length, model_width)
    prev_seqs = previous.reshape(-1, length, previous.shape[1])
    route_seqs = routes.reshape(-1, length, 2)

    def one_sequence(bundle):
        return stepper(lowered, bundle[0], bundle[1], bundle[2], bundle[3])
    outputs = lax.map(one_sequence, (token_seqs, prev_seqs, route_seqs, segments))
    return outputs.reshape(-1, model_width)

def reference(block_input, prev_logits, routes, segments, grad_out, gain_attn, w_query, w_key, w_value, w_output, gain_mix, router, route_map, const_proj, const_vec, w_gate, w_up, w_down):
    params = (gain_attn, w_query, w_key, w_value, w_output, gain_mix, router, route_map, const_proj, const_vec, w_gate, w_up, w_down)

    def whole_pass(inputs, weights):
        return forward(weights, inputs, prev_logits, routes, segments)
    result, pullback = jax.vjp(whole_pass, block_input.astype(jnp.float32), params)
    grad_input, grads = pullback(grad_out.astype(jnp.float32))
    return (result, grad_input, grads[0], grads[1], grads[2], grads[3], grads[4], grads[5], grads[6], grads[7], grads[8], grads[9], grads[10], grads[11], grads[12])
```

```python
import functools

import jax
import jax.numpy as jnp
from jax import lax
from jax.experimental import pallas as pl
from jax.experimental.pallas import tpu as pltpu
from jax.sharding import PartitionSpec as P

HEAD_DIM = 64
BLOCK = 256
EPS = 1e-05
NEG = -1000000000.0
F32 = jnp.float32
BF16 = jnp.bfloat16
LANES = 128


def nn(a, b):
    return lax.dot_general(a, b, (((1,), (0,)), ((), ())), preferred_element_type=F32)


def nt(a, b):
    return lax.dot_general(a, b, (((1,), (1,)), ((), ())), preferred_element_type=F32)


def tn(a, b):
    return lax.dot_general(a, b, (((0,), (0,)), ((), ())), preferred_element_type=F32)


def iota(shape, dim):
    return lax.broadcasted_iota(jnp.int32, shape, dim)


def split2(values):
    high = values.astype(BF16)
    low = (values - high.astype(F32)).astype(BF16)
    return high, low


def whole(shape, buffers=None):
    zeros = (0,) * len(shape)
    if buffers:
        return pl.BlockSpec(shape, lambda *_: zeros, pipeline_mode=pl.Buffered(buffers))
    return pl.BlockSpec(shape, lambda *_: zeros)


def per_seq(shape):
    tail = (0,) * len(shape)
    return pl.BlockSpec((1,) + shape, lambda b, *_: (b,) + tail)


def rms_scale(values):
    return lax.rsqrt(jnp.mean(values * values, axis=-1, keepdims=True) + EPS)


def slot_mask(position_row, capacity):
    places = iota((capacity, position_row.shape[1]), 0).astype(F32)
    return jnp.where(places == position_row, 1.0, 0.0).astype(BF16)


def grad_rows_kernel(own_ref, routes_ref, grad_ref, r0, r1, r2, r3, pos_ref):
    own = own_ref[0]
    kinds, length = pos_ref.shape[1:]
    capacity = r0.shape[1]
    ids = iota((kinds, length), 0)
    first = routes_ref[0, 0:1, :] == ids
    second = routes_ref[0, 1:2, :] == ids
    hits = jnp.where(first | second, 1.0, 0.0)
    before = jnp.where(iota((length, length), 0) < iota((length, length), 1), 1.0, 0.0)
    slots = nn(hits.astype(BF16), before.astype(BF16))
    pos_ref[0] = jnp.where(hits > 0.0, slots, -1.0)
    for number, rows in enumerate((r0, r1, r2, r3)):
        line = pos_ref[0, pl.ds(own ^ number, 1), :]
        rows[0] = nn(slot_mask(line, capacity), grad_ref[0]).astype(BF16)


def swap_halves(values, low_half):
    return jnp.where(low_half, pltpu.roll(values, 96, 1), pltpu.roll(values, 32, 1))


def forward_kernel(
    own_ref,
    x_ref,
    seg_row_ref,
    seg_col_ref,
    routes_ref,
    prev_ref,
    map_ref,
    small_ref,
    wq_ref,
    wk_ref,
    wv_ref,
    wo_ref,
    cos_ref,
    sin_ref,
    pos_ref,
    q_ref,
    k_ref,
    v_ref,
    o_ref,
    h_ref,
    lse_ref,
    aux_ref,
    r0,
    r1,
    r2,
    r3,
    bias_ref,
    proj_ref,
):
    own = own_ref[0]
    length, width = x_ref.shape[1:]
    kinds = pos_ref.shape[1]
    capacity = length // 2
    tokens = x_ref[0].astype(F32)
    gain_one = small_ref[kinds + 6 : kinds + 7, :]
    gain_two = small_ref[kinds + 7 : kinds + 8, :]
    a1 = (tokens * rms_scale(tokens) * gain_one).astype(BF16)
    lane = iota((1, LANES), 1)
    low_half = (lane % HEAD_DIM) < (HEAD_DIM // 2)
    first_head = lane < HEAD_DIM
    mask_a = jnp.where(first_head, 1.0, 0.0).astype(BF16)
    mask_b = jnp.where(first_head, 0.0, 1.0).astype(BF16)
    pairs = width // LANES

    for weights, target, scale in ((wq_ref, q_ref, 0.125), (wk_ref, k_ref, 1.0)):
        proj_ref[...] = nn(a1, weights[...])

        def turn(h, carry):
            cols = pl.ds(pl.multiple_of(h * LANES, LANES), LANES)
            part = proj_ref[:, cols]
            turned = part * cos_ref[...] + swap_halves(part, low_half) * sin_ref[...]
            target[0, :, cols] = turned.astype(BF16) * jnp.asarray(scale, BF16)
            return carry

        lax.fori_loop(0, pairs, turn, 0)
    v_ref[0] = nn(a1, wv_ref[...]).astype(BF16)

    allowed = (seg_col_ref[0] == seg_row_ref[0]) & (
        iota((length, length), 1) // BLOCK <= iota((length, length), 0) // BLOCK
    )
    bias_ref[...] = jnp.where(allowed, 0.0, NEG)
    lse_ref[...] = jnp.zeros_like(lse_ref)

    def pair(h, carry):
        cols = pl.ds(pl.multiple_of(h * LANES, LANES), LANES)
        for begin in range(0, length, BLOCK):
            end = begin + BLOCK
            queries = q_ref[0, begin:end, cols]
            keys = k_ref[0, 0:end, cols]
            values = v_ref[0, 0:end, cols]
            bias = bias_ref[begin:end, 0:end]
            sums = lse_ref[0, begin:end, :]
            outs = []
            for half, mask in enumerate((mask_a, mask_b)):
                scores = nt(queries * mask, keys) + bias
                top = jnp.max(scores, axis=-1, keepdims=True)
                grown = jnp.exp(scores - top)
                total = jnp.sum(grown, axis=-1, keepdims=True)
                chances = (grown * (1.0 / total)).astype(BF16)
                outs.append(nn(chances, values))
                sums = jnp.where(lane == 2 * h + half, top + jnp.log(total), sums)
            lse_ref[0, begin:end, :] = sums
            o_ref[0, begin:end, cols] = jnp.where(first_head, outs[0], outs[1]).astype(BF16)
        return carry

    lax.fori_loop(0, pairs, pair, 0)

    hidden = tokens + nn(o_ref[0], wo_ref[...])
    h_ref[0] = hidden
    a2 = (hidden * rms_scale(hidden) * gain_two).astype(BF16)
    logits = nt(small_ref[...].astype(BF16), a2)[0:kinds, :]
    for j in range(kinds):
        logits = logits + map_ref[:, j : j + 1] * prev_ref[0, j : j + 1, :]
    ids = iota((kinds, length), 0)
    first = jnp.where(routes_ref[0, 0:1, :] == ids, 1.0, 0.0)
    second = jnp.where(routes_ref[0, 1:2, :] == ids, 1.0, 0.0)
    one = jnp.sum(logits * first, axis=0, keepdims=True)
    two = jnp.sum(logits * second, axis=0, keepdims=True)
    top = jnp.maximum(one, two)
    grown_one, grown_two = jnp.exp(one - top), jnp.exp(two - top)
    gate_one = grown_one / (grown_one + grown_two)
    gate_two = grown_two / (grown_one + grown_two)
    aux_ref[0, 0:kinds, :] = gate_one * first + gate_two * second
    aux_ref[0, kinds : kinds + 1, :] = gate_one
    aux_ref[0, kinds + 1 : kinds + 2, :] = gate_two
    aux_ref[0, kinds + 2 :, :] = jnp.zeros((aux_ref.shape[1] - kinds - 2, length), F32)

    place = iota((16, length), 0)
    for number, rows in enumerate((r0, r1, r2, r3)):
        mask = slot_mask(pos_ref[0, pl.ds(own ^ number, 1), :], capacity)
        rows[0, 0:capacity, :] = nn(mask, a2).astype(BF16)
        line = aux_ref[0, pl.ds(own ^ number, 1), :]
        high = line.astype(BF16).astype(F32)
        mid = (line - high).astype(BF16).astype(F32)
        low = line - high - mid
        parts = jnp.where(place == 0, high, jnp.where(place == 1, mid, jnp.where(place == 2, low, 0.0)))
        spread = nt(parts.astype(BF16), mask)
        rows[0, capacity:, 0:capacity] = spread.astype(BF16)
        rows[0, capacity:, capacity:] = jnp.zeros((16, width - capacity), BF16)


def expert_kernel(
    a0,
    a1,
    a2,
    a3,
    g0,
    g1,
    g2,
    g3,
    gate_ref,
    up_ref,
    down_ref,
    v0,
    v1,
    v2,
    v3,
    d0,
    d1,
    d2,
    d3,
    grad_gate_ref,
    grad_up_ref,
    grad_down_ref,
    rows_ref,
    grads_ref,
    gates_ref,
    rows_t_ref,
    grads_t_ref,
    column_ref,
    acc_value_ref,
    acc_input_ref,
    acc_gate_ref,
    acc_up_ref,
    acc_down_ref,
    sems,
):
    step = pl.program_id(0)
    last = pl.num_programs(0) - 1
    batches, capacity, width = g0.shape
    blocks = 4 * batches

    @pl.when(step == 0)
    def _():
        copies = []
        for number, (rows, grads) in enumerate(zip((a0, a1, a2, a3), (g0, g1, g2, g3))):
            for member in range(batches):
                block = number * batches + member
                span = pl.ds(block * capacity, capacity)
                copies.append(
                    pltpu.make_async_copy(
                        rows.at[member, pl.ds(capacity, 16), pl.ds(0, capacity)],
                        gates_ref.at[block],
                        sems.at[3 * block],
                    )
                )
                copies.append(
                    pltpu.make_async_copy(
                        rows.at[member, pl.ds(0, capacity), :], rows_ref.at[span, :], sems.at[3 * block + 1]
                    )
                )
                copies.append(
                    pltpu.make_async_copy(grads.at[member], grads_ref.at[span, :], sems.at[3 * block + 2])
                )
        for copy in copies:
            copy.start()
        for copy in copies:
            copy.wait()
        same = iota((capacity, capacity), 0) == iota((capacity, capacity), 1)

        def prepare(block, carry):
            span = pl.ds(pl.multiple_of(block * capacity, capacity), capacity)
            parts = gates_ref[block].astype(F32)
            line = jnp.sum(parts, axis=0, keepdims=True)
            column = jnp.sum(jnp.where(same, line, 0.0), axis=1, keepdims=True)
            column_ref[span, :] = jnp.broadcast_to(column, (capacity, LANES))
            scaled = (grads_ref[span, :].astype(F32) * column).astype(BF16)
            grads_ref[span, :] = scaled
            grads_t_ref[:, span] = jnp.transpose(scaled)
            rows_t_ref[:, span] = jnp.transpose(rows_ref[span, :])
            return carry

        lax.fori_loop(0, blocks, prepare, 0)

    acc_gate_ref[...] = jnp.zeros_like(acc_gate_ref)
    acc_up_ref[...] = jnp.zeros_like(acc_up_ref)
    acc_down_ref[...] = jnp.zeros_like(acc_down_ref)

    def work(block, carry):
        span = pl.ds(pl.multiple_of(block * capacity, capacity), capacity)
        rows = rows_ref[span, :]
        grads = grads_ref[span, :]
        gate = nn(rows, gate_ref[...])
        up = nn(rows, up_ref[...])
        back = nt(grads, down_ref[...])
        sig = 1.0 / (1.0 + jnp.exp(-gate))
        silu = gate * sig
        act = (silu * up).astype(BF16)
        grad_gate = (back * up * (sig * (1.0 + gate * (1.0 - sig)))).astype(BF16)
        grad_up = (back * silu).astype(BF16)
        value = nn(act, down_ref[...])
        grad_rows = nt(grad_gate, gate_ref[...]) + nt(grad_up, up_ref[...])
        rows_t = rows_t_ref[:, span]
        acc_gate_ref[...] += nn(rows_t, grad_gate)
        acc_up_ref[...] += nn(rows_t, grad_up)
        acc_down_ref[...] += nn(grads_t_ref[:, span], act)

        @pl.when(step == 0)
        def _():
            acc_value_ref[span, :] = value
            acc_input_ref[span, :] = grad_rows

        @pl.when((step > 0) & (step < last))
        def _():
            acc_value_ref[span, :] += value
            acc_input_ref[span, :] += grad_rows

        @pl.when(step == last)
        def _():
            rows_ref[span, :] = (acc_value_ref[span, :] + value).astype(BF16)
            grads_ref[span, :] = (acc_input_ref[span, :] + grad_rows).astype(BF16)

        return carry

    lax.fori_loop(0, blocks, work, 0)
    grad_gate_ref[...] = acc_gate_ref[...].astype(BF16)
    grad_up_ref[...] = acc_up_ref[...].astype(BF16)
    grad_down_ref[...] = jnp.transpose(acc_down_ref[...].astype(BF16))

    @pl.when(step == last)
    def _():
        copies = []
        for number, (values, grads) in enumerate(zip((v0, v1, v2, v3), (d0, d1, d2, d3))):
            for member in range(batches):
                block = number * batches + member
                span = pl.ds(block * capacity, capacity)
                copies.append(pltpu.make_async_copy(rows_ref.at[span, :], values.at[member], sems.at[3 * block]))
                copies.append(pltpu.make_async_copy(grads_ref.at[span, :], grads.at[member], sems.at[3 * block + 1]))
        for copy in copies:
            copy.start()
        for copy in copies:
            copy.wait()


def combine_kernel(
    own_ref,
    v0,
    v1,
    v2,
    v3,
    d0,
    d1,
    d2,
    d3,
    pos_ref,
    aux_ref,
    routes_ref,
    prev_ref,
    h_ref,
    g_ref,
    o_ref,
    small_ref,
    wo_ref,
    out_ref,
    dh_ref,
    dob_ref,
    grad_wo_ref,
    sgrad_ref,
    grad_map_ref,
    acc_ref,
    cols_ref,
):
    own = own_ref[0]
    step = pl.program_id(0)
    length, width = h_ref.shape[1:]
    kinds = pos_ref.shape[1]
    ffn = kinds - 4
    capacity = v0.shape[1]
    hidden = h_ref[0]
    inverse = rms_scale(hidden)
    gain = small_ref[kinds + 7 : kinds + 8, :]
    n2 = hidden * inverse * gain
    n2_high, n2_low = split2(n2)
    grad_low = g_ref[0]
    grad = grad_low.astype(F32)
    small = small_ref[...].astype(BF16)
    cols_ref[0:kinds, :] = pos_ref[0]
    cols_ref[kinds : kinds + 16, :] = aux_ref[0]
    cols_ref[kinds + 16 :, :] = jnp.zeros((LANES - kinds - 16, length), F32)
    cols = jnp.transpose(cols_ref[...])
    lane = iota((1, LANES), 1)

    def column(source, index):
        return jnp.sum(jnp.where(lane == index, source, 0.0), axis=1, keepdims=True)

    gate_one = column(cols, 2 * kinds)
    gate_two = column(cols, 2 * kinds + 1)
    hot_one = jnp.where(routes_ref[0, :, 0:1] == lane, 1.0, 0.0)
    hot_two = jnp.where(routes_ref[0, :, 1:2] == lane, 1.0, 0.0)

    result = hidden
    grad_n2 = jnp.zeros((length, width), F32)
    dws = jnp.zeros((length, LANES), F32)
    slot_lane = iota((1, capacity), 1).astype(F32)
    for number, (values, grads) in enumerate(zip((v0, v1, v2, v3), (d0, d1, d2, d3))):
        expert = own ^ number
        mask = jnp.where(column(cols, expert) == slot_lane, 1.0, 0.0).astype(BF16)
        taken = nn(mask, values[0])
        result = result + column(cols, kinds + expert) * taken
        dws = jnp.where(lane == expert, jnp.sum(grad * taken, axis=1, keepdims=True), dws)
        grad_n2 = grad_n2 + nn(mask, grads[0])

    mixes = nt(n2_high, small) + nt(n2_low, small)
    inner = nt(grad_low, small)
    with_n2 = jnp.sum(grad * n2, axis=1, keepdims=True)
    weight_copy = column(cols, kinds + ffn + 1)
    dws = jnp.where(lane == ffn + 1, with_n2, dws)
    share = weight_copy
    coefs = jnp.zeros((length, LANES), F32)
    for constant in range(2):
        weight = column(cols, kinds + ffn + 2 + constant)
        za = mixes[:, kinds + 2 * constant : kinds + 2 * constant + 1]
        zb = mixes[:, kinds + 2 * constant + 1 : kinds + 2 * constant + 2]
        top = jnp.maximum(za, zb)
        ea, eb = jnp.exp(za - top), jnp.exp(zb - top)
        alpha_a = ea / (ea + eb)
        alpha_b = eb / (ea + eb)
        with_vec = inner[:, kinds + 4 + constant : kinds + 5 + constant]
        vec = small_ref[kinds + 4 + constant : kinds + 5 + constant, :]
        result = result + (weight * alpha_b) * vec
        share = share + weight * alpha_a
        dws = jnp.where(lane == ffn + 2 + constant, alpha_a * with_n2 + alpha_b * with_vec, dws)
        da = weight * with_n2
        db = weight * with_vec
        mean = alpha_a * da + alpha_b * db
        coefs = jnp.where(lane == kinds + 2 * constant, alpha_a * (da - mean), coefs)
        coefs = jnp.where(lane == kinds + 2 * constant + 1, alpha_b * (db - mean), coefs)
        coefs = jnp.where(lane == kinds + 4 + constant, weight * alpha_b, coefs)
    out_ref[0] = result + share * n2

    dg_one = jnp.sum(dws * hot_one, axis=1, keepdims=True)
    dg_two = jnp.sum(dws * hot_two, axis=1, keepdims=True)
    mean = gate_one * dg_one + gate_two * dg_two
    dlogits = gate_one * (dg_one - mean) * hot_one + gate_two * (dg_two - mean) * hot_two
    coefs = jnp.where(lane < kinds, dlogits, coefs)
    back = jnp.where(lane < kinds + 4, coefs, 0.0)[:, 0:16]
    back_high, back_low = split2(back)
    grad_n2 = grad_n2 + nn(back_high, small) + nn(back_low, small) + share * grad

    coefs_t = jnp.transpose(coefs)[0:16, :]
    high, low = split2(coefs_t)
    by_n2 = nn(high, n2_high) + nn(low, n2_high)
    by_low = nn(high, n2_low)
    by_grad = nn(high, grad_low) + nn(low, grad_low)
    row = iota((16, 1), 0)
    parts = jnp.where(row < kinds, by_n2, jnp.where(row < kinds + 4, by_n2 + by_low, by_grad))
    gain_part = jnp.sum(grad_n2 * hidden * inverse, axis=0, keepdims=True)
    parts = jnp.where(row == kinds + 7, gain_part, jnp.where(row == kinds + 6, 0.0, parts))
    dlog_t = coefs_t[0:kinds, :]
    map_lane = iota((kinds, LANES), 1)
    map_part = jnp.zeros((kinds, LANES), F32)
    for j in range(kinds):
        map_part = jnp.where(
            map_lane == j, jnp.sum(dlog_t * prev_ref[0, j : j + 1, :], axis=1, keepdims=True), map_part
        )

    scaled = gain * grad_n2
    inner_mean = jnp.mean(scaled * hidden, axis=-1, keepdims=True)
    dh = grad + inverse * scaled - hidden * (inverse * inverse * inverse) * inner_mean
    dh_ref[0] = dh
    db = dh.astype(BF16)
    dob_ref[0] = nt(db, wo_ref[...]).astype(BF16)
    wo_part = nn(jnp.transpose(o_ref[0]), db)

    @pl.when(step == 0)
    def _():
        acc_ref[...] = wo_part
        sgrad_ref[...] = parts
        grad_map_ref[...] = map_part

    @pl.when(step > 0)
    def _():
        acc_ref[...] += wo_part
        sgrad_ref[...] += parts
        grad_map_ref[...] += map_part

    @pl.when(step == pl.num_programs(0) - 1)
    def _():
        grad_wo_ref[...] = acc_ref[...].astype(BF16)


def backward_kernel(
    x_ref,
    seg_row_ref,
    seg_col_ref,
    q_ref,
    k_ref,
    v_ref,
    dob_ref,
    lse_ref,
    dh_ref,
    small_ref,
    wq_ref,
    wk_ref,
    wv_ref,
    cos_ref,
    sin_ref,
    gin_ref,
    grad_w_ref,
    gain_ref,
    bias_ref,
    lse_t_ref,
    dqkv_ref,
    acc_ref,
):
    step = pl.program_id(0)
    length, width = x_ref.shape[1:]
    kinds = small_ref.shape[0] - 8
    pairs = width // LANES
    lane = iota((1, LANES), 1)
    low_half = (lane % HEAD_DIM) < (HEAD_DIM // 2)
    first_head = lane < HEAD_DIM
    mask_a = jnp.where(first_head, 1.0, 0.0).astype(BF16)
    mask_b = jnp.where(first_head, 0.0, 1.0).astype(BF16)
    allowed = (seg_col_ref[0] == seg_row_ref[0]) & (
        iota((length, length), 0) // BLOCK <= iota((length, length), 1) // BLOCK
    )
    bias_ref[...] = jnp.where(allowed, 0.0, NEG)
    lse_t_ref[...] = jnp.transpose(lse_ref[0])

    def pair(h, carry):
        cols = pl.ds(pl.multiple_of(h * LANES, LANES), LANES)
        keys_t = jnp.transpose(k_ref[0, :, cols])
        grad_keys = None
        grad_values = None
        grad_queries = []
        for begin in range(0, length, BLOCK):
            end = begin + BLOCK
            queries = q_ref[0, begin:end, cols]
            outs = dob_ref[0, begin:end, cols]
            keys = k_ref[0, 0:end, cols]
            values = v_ref[0, 0:end, cols]
            queries = jnp.concatenate([queries * mask_a, queries * mask_b], axis=0)
            outs = jnp.concatenate([outs * mask_a, outs * mask_b], axis=0)
            bias = bias_ref[0:end, begin:end]
            bias = jnp.concatenate([bias, bias], axis=1)
            line = jnp.concatenate(
                [lse_t_ref[pl.ds(2 * h, 1), begin:end], lse_t_ref[pl.ds(2 * h + 1, 1), begin:end]], axis=1
            )
            chances = jnp.exp(nt(keys, queries) + bias - line)
            grad_chances = nt(values, outs)
            delta = jnp.sum(chances * grad_chances, axis=0, keepdims=True)
            grad_scores = (chances * (grad_chances - delta)).astype(BF16)
            dv = nn(chances.astype(BF16), outs)
            dk = nn(grad_scores, queries)
            dq = jnp.transpose(nn(keys_t[:, 0:end], grad_scores))
            grad_queries.append(jnp.where(first_head, dq[0:BLOCK], dq[BLOCK:]))
            if grad_keys is None:
                grad_keys, grad_values = dk, dv
            else:
                grad_keys = jnp.concatenate([grad_keys + dk[0:begin], dk[begin:]], axis=0)
                grad_values = jnp.concatenate([grad_values + dv[0:begin], dv[begin:]], axis=0)
        dq = jnp.concatenate(grad_queries, axis=0) * 0.125
        dq = dq * cos_ref[...] - swap_halves(dq, low_half) * sin_ref[...]
        dk = grad_keys * cos_ref[...] - swap_halves(grad_keys, low_half) * sin_ref[...]
        dqkv_ref[:, cols] = dq.astype(BF16)
        dqkv_ref[:, pl.ds(pl.multiple_of(width + h * LANES, LANES), LANES)] = dk.astype(BF16)
        dqkv_ref[:, pl.ds(pl.multiple_of(2 * width + h * LANES, LANES), LANES)] = grad_values.astype(BF16)
        return carry

    lax.fori_loop(0, pairs, pair, 0)

    tokens = x_ref[0].astype(F32)
    inverse = rms_scale(tokens)
    gain = small_ref[kinds + 6 : kinds + 7, :]
    a1_t = jnp.transpose((tokens * inverse * gain).astype(BF16))
    dn1 = (
        nt(dqkv_ref[:, 0:width], wq_ref[...])
        + nt(dqkv_ref[:, width : 2 * width], wk_ref[...])
        + nt(dqkv_ref[:, 2 * width :], wv_ref[...])
    )
    scaled = gain * dn1
    inner_mean = jnp.mean(scaled * tokens, axis=-1, keepdims=True)
    gin_ref[0] = dh_ref[0] + inverse * scaled - tokens * (inverse * inverse * inverse) * inner_mean
    gain_part = jnp.broadcast_to(jnp.sum(dn1 * tokens * inverse, axis=0, keepdims=True), gain_ref.shape)

    @pl.when(step == 0)
    def _():
        acc_ref[...] = jnp.zeros_like(acc_ref)
        gain_ref[...] = gain_part

    @pl.when(step > 0)
    def _():
        gain_ref[...] += gain_part

    for part in range(3):
        span = slice(part * width, (part + 1) * width)
        acc_ref[:, span] += nn(a1_t, dqkv_ref[:, span])

    @pl.when(step == pl.num_programs(0) - 1)
    def _():
        grad_w_ref[...] = acc_ref[...].astype(BF16)


def params(limit_mib):
    return pltpu.CompilerParams(vmem_limit_bytes=limit_mib * 1024 * 1024, dimension_semantics=("arbitrary",))


def rotary(length):
    halfway = HEAD_DIM // 2
    frequency = 10000.0 ** (-jnp.arange(halfway).astype(F32) / halfway)
    angles = jnp.arange(length).astype(F32)[:, None] * frequency[None, :]
    cosine, sine = jnp.cos(angles), jnp.sin(angles)
    return (
        jnp.concatenate([cosine] * 4, axis=1),
        jnp.concatenate([-sine, sine, -sine, sine], axis=1),
    )


def local(
    reps,
    group,
    block_input,
    prev_logits,
    routes,
    segments,
    grad_out,
    gain_attn,
    w_query,
    w_key,
    w_value,
    w_output,
    gain_mix,
    router,
    route_map,
    const_proj,
    const_vec,
    w_gate,
    w_up,
    w_down,
):
    batches, length = segments.shape
    width = block_input.shape[1]
    kinds = router.shape[1]
    ffn = w_gate.shape[1]
    hidden = w_gate.shape[2]
    rows_d = w_gate.shape[0]
    rows_f = w_down.shape[0]
    capacity = length // 2
    planes = group // 4
    assert reps == 2 and ffn == 4 and group % 4 == 0
    g = lax.axis_index("grp")
    y = lax.axis_index("rep")
    core = g % 2
    x = (g // 2) % 2
    z = g // 4
    own = (2 * y + x).astype(jnp.int32)
    own_arr = own.reshape(1)

    x_flip = [(i, i ^ 2) for i in range(group)]
    core_flip = [(i, i ^ 1) for i in range(group)]
    y_flip = [(0, 1), (1, 0)]
    xy_flip = [(r * group + i, (1 - r) * group + (i ^ 2)) for r in range(2) for i in range(group)]

    def z_shift(k):
        return [(i, (i + 4 * k) % group) for i in range(group)]

    def to_plane(parts):
        return [
            parts[0],
            lax.ppermute(parts[1], "grp", x_flip),
            lax.ppermute(parts[2], "rep", y_flip),
            lax.ppermute(parts[3], ("rep", "grp"), xy_flip),
        ]

    small_shard = jnp.concatenate(
        [router, const_proj, const_vec, gain_attn[:, None], gain_mix[:, None]], axis=1
    ).astype(BF16)
    small_shard = jnp.pad(small_shard, ((0, 0), (0, LANES - small_shard.shape[1])))
    shard = jnp.concatenate([w.astype(BF16) for w in (w_query, w_key, w_value, w_output)] + [small_shard], axis=1)
    attn = lax.all_gather(shard, "grp", axis=0, tiled=True)
    small = attn[:, 4 * width : 4 * width + kinds + 8].astype(F32).T

    def pick(array, expert):
        return lax.dynamic_index_in_dim(array, expert, axis=1, keepdims=False)

    def gather_expert(mine, other):
        crossed = lax.ppermute(other, "grp", x_flip)
        both = jnp.where(x == 0, jnp.stack([mine, crossed]), jnp.stack([crossed, mine]))
        pieces = [both] + [lax.ppermute(both, "grp", z_shift(k)) for k in range(1, planes)]
        stacked = jnp.stack(pieces)
        half = jnp.take(stacked, (z - jnp.arange(planes)) % planes, axis=0)
        swapped = lax.ppermute(half, "grp", core_flip)
        return jnp.where(core == 0, jnp.stack([half, swapped], axis=2), jnp.stack([swapped, half], axis=2))

    gate_up = gather_expert(
        jnp.stack([pick(w_gate, own), pick(w_up, own)]).astype(BF16),
        jnp.stack([pick(w_gate, own ^ 1), pick(w_up, own ^ 1)]).astype(BF16),
    )
    down = gather_expert(pick(w_down, own).astype(BF16), pick(w_down, own ^ 1).astype(BF16))
    gate_full = gate_up[:, :, :, 0].reshape(width, hidden)
    up_full = gate_up[:, :, :, 1].reshape(width, hidden)
    down_full = down.reshape(hidden, width)

    tokens = block_input.reshape(batches, length, width)
    grads = grad_out.reshape(batches, length, width)
    route_cols = routes.reshape(batches, length, 2)
    route_rows = route_cols.transpose(0, 2, 1)
    prev_rows = prev_logits.reshape(batches, length, kinds).transpose(0, 2, 1)
    seg_row = segments[:, None, :]
    seg_col = segments[:, :, None]
    cos, sin = rotary(length)

    def spec_w(j):
        return pl.BlockSpec((width, width), lambda b, *_: (0, j), pipeline_mode=pl.Buffered(1))

    row_shape = jax.ShapeDtypeStruct((batches, capacity, width), BF16)
    *grad_rows, pos = pl.pallas_call(
        grad_rows_kernel,
        grid_spec=pltpu.PrefetchScalarGridSpec(
            num_scalar_prefetch=1,
            grid=(batches,),
            in_specs=[per_seq((2, length)), per_seq((length, width))],
            out_specs=[per_seq((capacity, width))] * 4 + [per_seq((kinds, length))],
        ),
        out_shape=[row_shape] * 4 + [jax.ShapeDtypeStruct((batches, kinds, length), F32)],
        compiler_params=params(32),
        cost_estimate=pl.CostEstimate(flops=4 * 10**9, bytes_accessed=8 * 10**6, transcendentals=0),
        name="grad_rows",
    )(own_arr, route_rows, grads)
    grad_rows = to_plane(grad_rows)

    seq_bf16 = jax.ShapeDtypeStruct((batches, length, width), BF16)
    seq_f32 = jax.ShapeDtypeStruct((batches, length, width), F32)
    q, k, v, o, h1, lse, aux, *a_rows = pl.pallas_call(
        forward_kernel,
        grid_spec=pltpu.PrefetchScalarGridSpec(
            num_scalar_prefetch=1,
            grid=(batches,),
            in_specs=[
                per_seq((length, width)),
                per_seq((1, length)),
                per_seq((length, 1)),
                per_seq((2, length)),
                per_seq((kinds, length)),
                whole((kinds, kinds)),
                whole((kinds + 8, width)),
                spec_w(0),
                spec_w(1),
                spec_w(2),
                spec_w(3),
                whole((length, LANES)),
                whole((length, LANES)),
                per_seq((kinds, length)),
            ],
            out_specs=[per_seq((length, width))] * 5
            + [per_seq((length, LANES)), per_seq((16, length))]
            + [per_seq((capacity + 16, width))] * 4,
            scratch_shapes=[pltpu.VMEM((length, length), F32), pltpu.VMEM((length, width), F32)],
        ),
        out_shape=[seq_bf16] * 4
        + [
            seq_f32,
            jax.ShapeDtypeStruct((batches, length, LANES), F32),
            jax.ShapeDtypeStruct((batches, 16, length), F32),
        ]
        + [jax.ShapeDtypeStruct((batches, capacity + 16, width), BF16)] * 4,
        compiler_params=params(56),
        cost_estimate=pl.CostEstimate(flops=20 * 10**9, bytes_accessed=20 * 10**6, transcendentals=10**7),
        name="forward",
    )(own_arr, tokens, seg_row, seg_col, route_rows, prev_rows, route_map.T, small, attn, attn, attn, attn, cos, sin, pos)
    a_rows = to_plane(a_rows)

    tile = hidden // 4
    total = 4 * batches * capacity
    any_spec = pl.BlockSpec(memory_space=pl.ANY)
    outs = pl.pallas_call(
        expert_kernel,
        grid=(hidden // tile,),
        in_specs=[any_spec] * 8
        + [
            pl.BlockSpec((width, tile), lambda f: (0, f)),
            pl.BlockSpec((width, tile), lambda f: (0, f)),
            pl.BlockSpec((tile, width), lambda f: (f, 0)),
        ],
        out_specs=[any_spec] * 8
        + [
            pl.BlockSpec((width, tile), lambda f: (0, f)),
            pl.BlockSpec((width, tile), lambda f: (0, f)),
            pl.BlockSpec((tile, width), lambda f: (f, 0)),
        ],
        scratch_shapes=[
            pltpu.VMEM((total, width), BF16),
            pltpu.VMEM((total, width), BF16),
            pltpu.VMEM((4 * batches, 16, capacity), BF16),
            pltpu.VMEM((width, total), BF16),
            pltpu.VMEM((width, total), BF16),
            pltpu.VMEM((total, LANES), F32),
            pltpu.VMEM((total, width), F32),
            pltpu.VMEM((total, width), F32),
            pltpu.VMEM((width, tile), F32),
            pltpu.VMEM((width, tile), F32),
            pltpu.VMEM((width, tile), F32),
            pltpu.SemaphoreType.DMA((12 * batches,)),
        ],
        out_shape=[row_shape] * 8
        + [
            jax.ShapeDtypeStruct((width, hidden), BF16),
            jax.ShapeDtypeStruct((width, hidden), BF16),
            jax.ShapeDtypeStruct((hidden, width), BF16),
        ],
        compiler_params=params(60),
        cost_estimate=pl.CostEstimate(flops=58 * 10**9, bytes_accessed=40 * 10**6, transcendentals=10**7),
        name="expert",
    )(*a_rows, *grad_rows, gate_full, up_full, down_full)
    value_rows = to_plane(outs[0:4])
    input_rows = to_plane(outs[4:8])
    grad_gate_full, grad_up_full, grad_down_full = outs[8:]

    def scatter_expert(full):
        keep = lax.dynamic_index_in_dim(full, core, axis=2, keepdims=False)
        send = lax.dynamic_index_in_dim(full, 1 - core, axis=2, keepdims=False)
        half = (keep.astype(F32) + lax.ppermute(send, "grp", core_flip).astype(F32)).astype(BF16)
        summed = lax.dynamic_index_in_dim(half, z, axis=0, keepdims=False).astype(F32)
        for k in range(1, planes):
            part = lax.dynamic_index_in_dim(half, (z + k) % planes, axis=0, keepdims=False)
            summed = summed + lax.ppermute(part, "grp", z_shift(k)).astype(F32)
        summed = summed.astype(BF16)
        mine = lax.dynamic_index_in_dim(summed, x, axis=0, keepdims=False)
        other = lax.dynamic_index_in_dim(summed, 1 - x, axis=0, keepdims=False)
        arrived = to_plane([mine, other, mine, other])

        def order(first):
            return lambda: tuple(arrived[first ^ e] for e in range(4))

        return lax.switch(own, [order(i) for i in range(4)])

    grad_gate_up = scatter_expert(
        jnp.stack(
            [
                grad_gate_full.reshape(planes, 2, 2, rows_d, hidden),
                grad_up_full.reshape(planes, 2, 2, rows_d, hidden),
            ],
            axis=3,
        )
    )
    grad_down = scatter_expert(grad_down_full.reshape(planes, 2, 2, rows_f, width))
    grad_gate = jnp.stack([part[0] for part in grad_gate_up], axis=1).astype(F32)
    grad_up = jnp.stack([part[1] for part in grad_gate_up], axis=1).astype(F32)
    grad_down = jnp.stack(grad_down, axis=1).astype(F32)

    result, dh1, dob, grad_wo, sgrad, grad_map = pl.pallas_call(
        combine_kernel,
        grid_spec=pltpu.PrefetchScalarGridSpec(
            num_scalar_prefetch=1,
            grid=(batches,),
            in_specs=[per_seq((capacity, width))] * 8
            + [
                per_seq((kinds, length)),
                per_seq((16, length)),
                per_seq((length, 2)),
                per_seq((kinds, length)),
                per_seq((length, width)),
                per_seq((length, width)),
                per_seq((length, width)),
                whole((kinds + 8, width)),
                spec_w(3),
            ],
            out_specs=[per_seq((length, width))] * 3
            + [whole((width, width)), whole((16, width)), whole((kinds, LANES))],
            scratch_shapes=[pltpu.VMEM((width, width), F32), pltpu.VMEM((LANES, length), F32)],
        ),
        out_shape=[
            seq_f32,
            seq_f32,
            seq_bf16,
            jax.ShapeDtypeStruct((width, width), BF16),
            jax.ShapeDtypeStruct((16, width), F32),
            jax.ShapeDtypeStruct((kinds, LANES), F32),
        ],
        compiler_params=params(56),
        cost_estimate=pl.CostEstimate(flops=12 * 10**9, bytes_accessed=20 * 10**6, transcendentals=10**5),
        name="combine",
    )(own_arr, *value_rows, *input_rows, pos, aux, route_cols, prev_rows, h1, grads, o, small, attn)

    gin, grad_qkv, gain_one = pl.pallas_call(
        backward_kernel,
        grid=(batches,),
        in_specs=[
            per_seq((length, width)),
            per_seq((1, length)),
            per_seq((length, 1)),
            per_seq((length, width)),
            per_seq((length, width)),
            per_seq((length, width)),
            per_seq((length, width)),
            per_seq((length, LANES)),
            per_seq((length, width)),
            whole((kinds + 8, width)),
            spec_w(0),
            spec_w(1),
            spec_w(2),
            whole((length, LANES)),
            whole((length, LANES)),
        ],
        out_specs=[per_seq((length, width)), whole((width, 3 * width)), whole((8, width))],
        scratch_shapes=[
            pltpu.VMEM((length, length), F32),
            pltpu.VMEM((LANES, length), F32),
            pltpu.VMEM((length, 3 * width), BF16),
            pltpu.VMEM((width, 3 * width), F32),
        ],
        out_shape=[
            seq_f32,
            jax.ShapeDtypeStruct((width, 3 * width), BF16),
            jax.ShapeDtypeStruct((8, width), F32),
        ],
        compiler_params=params(56),
        cost_estimate=pl.CostEstimate(flops=30 * 10**9, bytes_accessed=20 * 10**6, transcendentals=10**7),
        name="backward",
    )(tokens, seg_row, seg_col, q, k, v, dob, lse, dh1, small, attn, attn, attn, cos, sin)

    def to_owner(full):
        part = lax.psum_scatter(full, "grp", scatter_dimension=0, tiled=True)
        return lax.psum(part, "rep").astype(F32)

    wo_total = to_owner(grad_wo)
    qkv_total = to_owner(grad_qkv)
    sgrad = jnp.where(iota((16, 1), 0) == kinds + 6, gain_one[0:1], sgrad)
    packed = jnp.concatenate([sgrad, jnp.pad(grad_map, ((0, 0), (0, width - LANES)))], axis=0)
    packed = lax.psum(packed, ("rep", "grp"))
    sums = lax.dynamic_slice_in_dim(packed[0:16], g * rows_d, rows_d, axis=1).T
    map_total = packed[16:, 0:kinds].T
    return (
        result.reshape(batches * length, width),
        gin.reshape(batches * length, width),
        sums[:, kinds + 6],
        qkv_total[:, 0:width],
        qkv_total[:, width : 2 * width],
        qkv_total[:, 2 * width :],
        wo_total,
        sums[:, kinds + 7],
        sums[:, 0:kinds],
        map_total,
        sums[:, kinds : kinds + 4],
        sums[:, kinds + 4 : kinds + 6],
        grad_gate,
        grad_up,
        grad_down,
    )


def solution(mesh):
    rows = P(("rep", "grp"), None)
    in_specs = (
        (rows,) * 5
        + (P("grp"),)
        + (P("grp", None),) * 4
        + (P("grp"), P("grp", None), P(), P("grp", None), P("grp", None))
        + (P("grp", None, None),) * 3
    )
    out_specs = (
        (rows,) * 2
        + (P("grp"),)
        + (P("grp", None),) * 4
        + (P("grp"), P("grp", None), P(), P("grp", None), P("grp", None))
        + (P("grp", None, None),) * 3
    )
    body = functools.partial(local, mesh.shape["rep"], mesh.shape["grp"])
    return jax.shard_map(body, mesh=mesh, in_specs=in_specs, out_specs=out_specs, check_vma=False)
```

```python
import functools

import jax
import jax.numpy as jnp
from jax import lax
from jax.experimental import pallas as pl
from jax.experimental.pallas import tpu as pltpu
from jax.sharding import PartitionSpec as P

HEAD_DIM = 64
BLOCK = 256
EPS = 1e-05
NEG = -1000000000.0
F32 = jnp.float32
BF16 = jnp.bfloat16
LANES = 128


def nn(a, b):
    return lax.dot_general(a, b, (((1,), (0,)), ((), ())), preferred_element_type=F32)


def nt(a, b):
    return lax.dot_general(a, b, (((1,), (1,)), ((), ())), preferred_element_type=F32)


def tn(a, b):
    return lax.dot_general(a, b, (((0,), (0,)), ((), ())), preferred_element_type=F32)


def iota(shape, dim):
    return lax.broadcasted_iota(jnp.int32, shape, dim)


def split2(values):
    high = values.astype(BF16)
    low = (values - high.astype(F32)).astype(BF16)
    return high, low


def whole(shape, buffers=None):
    zeros = (0,) * len(shape)
    if buffers:
        return pl.BlockSpec(shape, lambda *_: zeros, pipeline_mode=pl.Buffered(buffers))
    return pl.BlockSpec(shape, lambda *_: zeros)


def per_seq(shape):
    tail = (0,) * len(shape)
    return pl.BlockSpec((1,) + shape, lambda b, *_: (b,) + tail)


def rms_scale(values):
    return lax.rsqrt(jnp.mean(values * values, axis=-1, keepdims=True) + EPS)


def slot_mask(position_row, capacity):
    places = iota((capacity, position_row.shape[1]), 0).astype(F32)
    return jnp.where(places == position_row, 1.0, 0.0).astype(BF16)


def grad_rows_kernel(own_ref, routes_ref, grad_ref, r0, r1, r2, r3, pos_ref):
    own = own_ref[0]
    kinds, length = pos_ref.shape[1:]
    capacity = r0.shape[1]
    ids = iota((kinds, length), 0)
    first = routes_ref[0, 0:1, :] == ids
    second = routes_ref[0, 1:2, :] == ids
    hits = jnp.where(first | second, 1.0, 0.0)
    before = jnp.where(iota((length, length), 0) < iota((length, length), 1), 1.0, 0.0)
    slots = nn(hits.astype(BF16), before.astype(BF16))
    pos_ref[0] = jnp.where(hits > 0.0, slots, -1.0)
    for number, rows in enumerate((r0, r1, r2, r3)):
        line = pos_ref[0, pl.ds(own ^ number, 1), :]
        rows[0] = nn(slot_mask(line, capacity), grad_ref[0]).astype(BF16)


def swap_halves(values, low_half):
    return jnp.where(low_half, pltpu.roll(values, 96, 1), pltpu.roll(values, 32, 1))


def sequence_forward(
    x_ref,
    seg_row_ref,
    seg_col_ref,
    routes_ref,
    prev_ref,
    map_ref,
    small_ref,
    wq_ref,
    wk_ref,
    wv_ref,
    wo_ref,
    cos_ref,
    sin_ref,
    pos_ref,
    q_ref,
    k_ref,
    v_ref,
    o_ref,
    h_ref,
    lse_ref,
    aux_ref,
    rows_refs,
    bias_ref,
    proj_ref,
    expert_of,
):
    length, width = x_ref.shape[1:]
    kinds = pos_ref.shape[1]
    capacity = length // 2
    tokens = x_ref[0].astype(F32)
    gain_one = small_ref[kinds + 6 : kinds + 7, :]
    gain_two = small_ref[kinds + 7 : kinds + 8, :]
    a1 = (tokens * rms_scale(tokens) * gain_one).astype(BF16)
    lane = iota((1, LANES), 1)
    low_half = (lane % HEAD_DIM) < (HEAD_DIM // 2)
    first_head = lane < HEAD_DIM
    mask_a = jnp.where(first_head, 1.0, 0.0).astype(BF16)
    mask_b = jnp.where(first_head, 0.0, 1.0).astype(BF16)
    pairs = width // LANES

    for weights, target, scale in ((wq_ref, q_ref, 0.125), (wk_ref, k_ref, 1.0)):
        proj_ref[...] = nn(a1, weights[...])

        def turn(h, carry):
            cols = pl.ds(pl.multiple_of(h * LANES, LANES), LANES)
            part = proj_ref[:, cols]
            turned = part * cos_ref[...] + swap_halves(part, low_half) * sin_ref[...]
            target[0, :, cols] = turned.astype(BF16) * jnp.asarray(scale, BF16)
            return carry

        lax.fori_loop(0, pairs, turn, 0)
    v_ref[0] = nn(a1, wv_ref[...]).astype(BF16)

    allowed = (seg_col_ref[0] == seg_row_ref[0]) & (
        iota((length, length), 1) // BLOCK <= iota((length, length), 0) // BLOCK
    )
    bias_ref[...] = jnp.where(allowed, 0.0, NEG)
    lse_ref[...] = jnp.zeros_like(lse_ref)

    def pair(h, carry):
        cols = pl.ds(pl.multiple_of(h * LANES, LANES), LANES)
        for begin in range(0, length, BLOCK):
            end = begin + BLOCK
            queries = q_ref[0, begin:end, cols]
            keys = k_ref[0, 0:end, cols]
            values = v_ref[0, 0:end, cols]
            bias = bias_ref[begin:end, 0:end]
            sums = lse_ref[0, begin:end, :]
            outs = []
            for half, mask in enumerate((mask_a, mask_b)):
                scores = nt(queries * mask, keys) + bias
                top = jnp.max(scores, axis=-1, keepdims=True)
                grown = jnp.exp(scores - top)
                total = jnp.sum(grown, axis=-1, keepdims=True)
                chances = (grown * (1.0 / total)).astype(BF16)
                outs.append(nn(chances, values))
                sums = jnp.where(lane == 2 * h + half, top + jnp.log(total), sums)
            lse_ref[0, begin:end, :] = sums
            o_ref[0, begin:end, cols] = jnp.where(first_head, outs[0], outs[1]).astype(BF16)
        return carry

    lax.fori_loop(0, pairs, pair, 0)

    hidden = tokens + nn(o_ref[0], wo_ref[...])
    h_ref[0] = hidden
    a2 = (hidden * rms_scale(hidden) * gain_two).astype(BF16)
    logits = nt(small_ref[...].astype(BF16), a2)[0:kinds, :]
    for j in range(kinds):
        logits = logits + map_ref[:, j : j + 1] * prev_ref[0, j : j + 1, :]
    ids = iota((kinds, length), 0)
    first = jnp.where(routes_ref[0, 0:1, :] == ids, 1.0, 0.0)
    second = jnp.where(routes_ref[0, 1:2, :] == ids, 1.0, 0.0)
    one = jnp.sum(logits * first, axis=0, keepdims=True)
    two = jnp.sum(logits * second, axis=0, keepdims=True)
    top = jnp.maximum(one, two)
    grown_one, grown_two = jnp.exp(one - top), jnp.exp(two - top)
    gate_one = grown_one / (grown_one + grown_two)
    gate_two = grown_two / (grown_one + grown_two)
    aux_ref[0, 0:kinds, :] = gate_one * first + gate_two * second
    aux_ref[0, kinds : kinds + 1, :] = gate_one
    aux_ref[0, kinds + 1 : kinds + 2, :] = gate_two
    aux_ref[0, kinds + 2 :, :] = jnp.zeros((aux_ref.shape[1] - kinds - 2, length), F32)

    place = iota((16, length), 0)
    for number, rows in enumerate(rows_refs):
        mask = slot_mask(pos_ref[0, pl.ds(expert_of(number), 1), :], capacity)
        rows[0, 0:capacity, :] = nn(mask, a2).astype(BF16)
        line = aux_ref[0, pl.ds(expert_of(number), 1), :]
        high = line.astype(BF16).astype(F32)
        mid = (line - high).astype(BF16).astype(F32)
        low = line - high - mid
        parts = jnp.where(place == 0, high, jnp.where(place == 1, mid, jnp.where(place == 2, low, 0.0)))
        spread = nt(parts.astype(BF16), mask)
        rows[0, capacity:, 0:capacity] = spread.astype(BF16)
        rows[0, capacity:, capacity:] = jnp.zeros((16, width - capacity), BF16)


def forward_kernel(
    own_ref,
    x_ref,
    seg_row_ref,
    seg_col_ref,
    routes_ref,
    prev_ref,
    map_ref,
    small_ref,
    wq_ref,
    wk_ref,
    wv_ref,
    wo_ref,
    cos_ref,
    sin_ref,
    pos_ref,
    q_ref,
    k_ref,
    v_ref,
    o_ref,
    h_ref,
    lse_ref,
    aux_ref,
    r0,
    r1,
    r2,
    r3,
    bias_ref,
    proj_ref,
):
    own = own_ref[0]
    sequence_forward(
        x_ref,
        seg_row_ref,
        seg_col_ref,
        routes_ref,
        prev_ref,
        map_ref,
        small_ref,
        wq_ref,
        wk_ref,
        wv_ref,
        wo_ref,
        cos_ref,
        sin_ref,
        pos_ref,
        q_ref,
        k_ref,
        v_ref,
        o_ref,
        h_ref,
        lse_ref,
        aux_ref,
        (r0, r1, r2, r3),
        bias_ref,
        proj_ref,
        lambda number: own ^ number,
    )


MESH = pl.DeviceIdType.MESH


class Place:
    def __init__(self, group):
        self.group = group
        self.planes = group // 4
        self.g = lax.axis_index("grp")
        self.y = lax.axis_index("rep")
        self.core = self.g % 2
        self.x = (self.g // 2) % 2
        self.z = self.g // 4
        self.core_peer = (self.y, self.g + 1 - 2 * self.core)
        self.x_peer = (self.y, self.g + 2 - 4 * self.x)
        self.y_peer = (1 - self.y, self.g)
        self.xy_peer = (1 - self.y, self.g + 2 - 4 * self.x)
        self.plane_peers = (None, self.x_peer, self.y_peer, self.xy_peer)

    def z_peer(self, k):
        return (self.y, (self.g + 4 * k) % self.group)

    def block(self, z, x, core):
        return (z * 2 + x) * 2 + core

    def expert(self, number):
        y = self.y if number < 2 else 1 - self.y
        x = self.x if number % 2 == 0 else 1 - self.x
        return 2 * y + x

    def barrier(self, peers):
        semaphore = pltpu.get_barrier_semaphore()
        for peer in peers:
            pl.semaphore_signal(semaphore, inc=1, device_id=peer, device_id_type=MESH)
        pl.semaphore_wait(semaphore, len(peers))


def remote(src, dst, send, recv, peer):
    return pltpu.make_async_remote_copy(
        src_ref=src, dst_ref=dst, send_sem=send, recv_sem=recv, device_id=peer, device_id_type=MESH
    )


def fused_forward_kernel(
    group,
    x_ref,
    seg_row_ref,
    seg_col_ref,
    routes_ref,
    prev_ref,
    map_ref,
    grad_ref,
    cos_ref,
    sin_ref,
    shard_ref,
    shard_o_ref,
    gate4_ref,
    up4_ref,
    down4_ref,
    q_ref,
    k_ref,
    v_ref,
    o_ref,
    h_ref,
    lse_ref,
    aux_ref,
    pos_ref,
    small_ref,
    attn_out_ref,
    attn_o_out_ref,
    rows_in_ref,
    grads_in_ref,
    gate_full_ref,
    up_full_ref,
    down_full_ref,
    attn_ref,
    attn_o_ref,
    bias_ref,
    proj_ref,
    rows_ref,
    grows_ref,
    local_sem,
    attn_send,
    attn_recv,
    ffn_local,
    ffn_send,
    ffn_x,
    ffn_z,
    ffn_core,
    out_sem,
    row_local,
    row_send,
    row_recv,
):
    step = pl.program_id(0)
    last = pl.num_programs(0) - 1
    here = Place(group)
    planes = here.planes
    batches, kinds, length = pos_ref.shape
    width = x_ref.shape[2]
    capacity = length // 2
    shards = ((shard_ref, attn_ref), (shard_o_ref, attn_o_ref))
    experts = ((gate4_ref, gate_full_ref), (up4_ref, up_full_ref), (down4_ref, down_full_ref))
    depth = shard_ref.shape[0]
    mine = here.block(here.z, here.x, here.core)

    def rows_of(block):
        return pl.ds(pl.multiple_of(block * depth, 16), depth)

    def attn_copy(t, hop, index, block, peer):
        full = shards[t][1]
        return remote(
            full.at[rows_of(block), :],
            full.at[rows_of(block), :],
            attn_send.at[t, hop, index],
            attn_recv.at[t, block],
            peer,
        )

    def to_z(t, k):
        return attn_copy(t, 0, k, mine, here.z_peer(k))

    def to_x(t, z):
        return attn_copy(t, 1, z, here.block(z, here.x, here.core), here.x_peer)

    def to_core(t, z, x):
        return attn_copy(t, 2, 2 * z + x, here.block(z, x, here.core), here.core_peer)

    def ffn_to_x(j):
        source, full = experts[j]
        return remote(
            source.at[here.expert(1)],
            full.at[here.z, here.x, here.core],
            ffn_send.at[j, 0],
            ffn_x.at[j],
            here.x_peer,
        )

    def ffn_mine(j):
        source, full = experts[j]
        return pltpu.make_async_copy(source.at[here.expert(0)], full.at[here.z, here.x, here.core], ffn_local.at[j])

    def ffn_to_z(j, k):
        full = experts[j][1]
        part = full.at[here.z, :, here.core]
        return remote(part, part, ffn_send.at[j, k], ffn_z.at[j, here.z], here.z_peer(k))

    def ffn_from_z(j, k):
        full = experts[j][1]
        z = (here.z + planes - k) % planes
        part = full.at[z, :, here.core]
        return remote(part, part, ffn_send.at[j, k], ffn_z.at[j, z], here.z_peer(k))

    def ffn_to_core(j, z):
        full = experts[j][1]
        part = full.at[z, :, here.core]
        return remote(part, part, ffn_send.at[j, planes + z], ffn_core.at[j, z], here.core_peer)

    def ffn_from_core(j, z):
        full = experts[j][1]
        part = full.at[z, :, 1 - here.core]
        return remote(part, part, ffn_send.at[j, planes + z], ffn_core.at[j, z], here.core_peer)

    def row_copy(kind, member, number):
        source, target = ((grows_ref, grads_in_ref), (rows_ref, rows_in_ref))[kind]
        src, dst = source.at[member, number], target.at[number, member]
        if number == 0:
            return pltpu.make_async_copy(src, dst, row_local.at[kind, member])
        return remote(
            src,
            dst,
            row_send.at[kind, member, number],
            row_recv.at[kind, member, number],
            here.plane_peers[number],
        )

    def outs(t):
        full, target = ((attn_ref, attn_out_ref), (attn_o_ref, attn_o_out_ref))[t]
        return pltpu.make_async_copy(full, target, out_sem.at[t])

    @pl.when(step == 0)
    def _():
        z_peers = [here.z_peer(k) for k in range(1, planes)]
        own_copies = [
            pltpu.make_async_copy(source, full.at[rows_of(mine), :], local_sem.at[t])
            for t, (source, full) in enumerate(shards)
        ]
        for copy in own_copies:
            copy.start()
        for j in range(3):
            ffn_mine(j).start()
        here.barrier([here.core_peer, here.x_peer, here.y_peer, here.xy_peer] + z_peers)
        for copy in own_copies:
            copy.wait()
        for t in range(2):
            for k in range(1, planes):
                to_z(t, k).start()
            to_x(t, here.z).start()
            to_core(t, here.z, here.x).start()
        for j in range(3):
            ffn_to_x(j).start()

        ids = iota((kinds, length), 0)
        before = jnp.where(iota((length, length), 0) < iota((length, length), 1), 1.0, 0.0).astype(BF16)
        for member in range(batches):
            first = routes_ref[member, 0:1, :] == ids
            second = routes_ref[member, 1:2, :] == ids
            hits = jnp.where(first | second, 1.0, 0.0)
            pos_ref[member] = jnp.where(hits > 0.0, nn(hits.astype(BF16), before), -1.0)
            for number in range(4):
                line = pos_ref[member, pl.ds(here.expert(number), 1), :]
                grows_ref[member, number] = nn(slot_mask(line, capacity), grad_ref[member]).astype(BF16)
            row_copy(0, member, 0).start()
            row_copy(0, member, 2).start()

        for t in range(2):
            for k in range(1, planes):
                z = (here.z + planes - k) % planes
                attn_copy(t, 0, k, here.block(z, here.x, here.core), here.x_peer).wait_recv()
                to_x(t, z).start()
                to_core(t, z, here.x).start()
            if t == 0:
                for j in range(3):
                    ffn_mine(j).wait()
                    ffn_from_x = remote(
                        experts[j][0].at[here.expert(1)],
                        experts[j][1].at[here.z, 1 - here.x, here.core],
                        ffn_send.at[j, 0],
                        ffn_x.at[j],
                        here.x_peer,
                    )
                    ffn_from_x.wait_recv()
            for k in range(planes):
                z = (here.z + planes - k) % planes
                attn_copy(t, 1, z, here.block(z, 1 - here.x, here.core), here.x_peer).wait_recv()
                to_core(t, z, 1 - here.x).start()
            for z in range(planes):
                for x in range(2):
                    attn_copy(t, 2, 2 * z + x, here.block(z, x, 1 - here.core), here.core_peer).wait_recv()
            if t == 0:
                for j in range(3):
                    for k in range(1, planes):
                        ffn_to_z(j, k).start()
                    ffn_to_core(j, here.z).start()
        for t in range(2):
            outs(t).start()
        for member in range(batches):
            row_copy(0, member, 1).start()
            row_copy(0, member, 3).start()
        small_ref[...] = jnp.transpose(attn_ref[:, 3 * width :].astype(F32))[0 : kinds + 8, :]

    sequence_forward(
        x_ref,
        seg_row_ref,
        seg_col_ref,
        routes_ref.at[pl.ds(step, 1)],
        prev_ref,
        map_ref,
        small_ref,
        attn_ref.at[:, 0:width],
        attn_ref.at[:, width : 2 * width],
        attn_ref.at[:, 2 * width : 3 * width],
        attn_o_ref,
        cos_ref,
        sin_ref,
        pos_ref.at[pl.ds(step, 1)],
        q_ref,
        k_ref,
        v_ref,
        o_ref,
        h_ref,
        lse_ref,
        aux_ref,
        [rows_ref.at[pl.ds(step, 1), number] for number in range(4)],
        bias_ref,
        proj_ref,
        here.expert,
    )
    for member in range(batches):

        @pl.when(step == member)
        def _():
            for number in range(4):
                row_copy(1, member, number).start()

    @pl.when(step == 0)
    def _():
        for k in range(1, planes):
            for j in range(3):
                ffn_from_z(j, k).wait_recv()
                ffn_to_core(j, (here.z + planes - k) % planes).start()

    @pl.when(step == last)
    def _():
        for t in range(2):
            outs(t).wait()
            for k in range(1, planes):
                to_z(t, k).wait_send()
            for z in range(planes):
                to_x(t, z).wait_send()
                for x in range(2):
                    to_core(t, z, x).wait_send()
        for j in range(3):
            ffn_to_x(j).wait_send()
            for k in range(1, planes):
                ffn_to_z(j, k).wait_send()
            for z in range(planes):
                ffn_to_core(j, z).wait_send()
                ffn_from_core(j, z).wait_recv()
        for kind in range(2):
            for member in range(batches):
                for number in range(4):
                    copy = row_copy(kind, member, number)
                    copy.wait()


def expert_kernel(
    a_ref,
    g_ref,
    gate_ref,
    up_ref,
    down_ref,
    v0,
    v1,
    v2,
    v3,
    d0,
    d1,
    d2,
    d3,
    grad_gate_ref,
    grad_up_ref,
    grad_down_ref,
    rows_ref,
    grads_ref,
    gates_ref,
    rows_t_ref,
    grads_t_ref,
    column_ref,
    acc_value_ref,
    acc_input_ref,
    acc_gate_ref,
    acc_up_ref,
    acc_down_ref,
    sems,
):
    step = pl.program_id(0)
    last = pl.num_programs(0) - 1
    batches, capacity, width = g_ref.shape[1:]
    blocks = 4 * batches

    @pl.when(step == 0)
    def _():
        copies = []
        for number in range(4):
            rows, grads = a_ref.at[number], g_ref.at[number]
            for member in range(batches):
                block = number * batches + member
                span = pl.ds(block * capacity, capacity)
                copies.append(
                    pltpu.make_async_copy(
                        rows.at[member, pl.ds(capacity, 16), pl.ds(0, capacity)],
                        gates_ref.at[block],
                        sems.at[3 * block],
                    )
                )
                copies.append(
                    pltpu.make_async_copy(
                        rows.at[member, pl.ds(0, capacity), :], rows_ref.at[span, :], sems.at[3 * block + 1]
                    )
                )
                copies.append(
                    pltpu.make_async_copy(grads.at[member], grads_ref.at[span, :], sems.at[3 * block + 2])
                )
        for copy in copies:
            copy.start()
        for copy in copies:
            copy.wait()
        same = iota((capacity, capacity), 0) == iota((capacity, capacity), 1)

        def prepare(block, carry):
            span = pl.ds(pl.multiple_of(block * capacity, capacity), capacity)
            parts = gates_ref[block].astype(F32)
            line = jnp.sum(parts, axis=0, keepdims=True)
            column = jnp.sum(jnp.where(same, line, 0.0), axis=1, keepdims=True)
            column_ref[span, :] = jnp.broadcast_to(column, (capacity, LANES))
            scaled = (grads_ref[span, :].astype(F32) * column).astype(BF16)
            grads_ref[span, :] = scaled
            grads_t_ref[:, span] = jnp.transpose(scaled)
            rows_t_ref[:, span] = jnp.transpose(rows_ref[span, :])
            return carry

        lax.fori_loop(0, blocks, prepare, 0)

    acc_gate_ref[...] = jnp.zeros_like(acc_gate_ref)
    acc_up_ref[...] = jnp.zeros_like(acc_up_ref)
    acc_down_ref[...] = jnp.zeros_like(acc_down_ref)

    def work(block, carry):
        span = pl.ds(pl.multiple_of(block * capacity, capacity), capacity)
        rows = rows_ref[span, :]
        grads = grads_ref[span, :]
        gate = nn(rows, gate_ref[...])
        up = nn(rows, up_ref[...])
        back = nt(grads, down_ref[...])
        sig = 1.0 / (1.0 + jnp.exp(-gate))
        silu = gate * sig
        act = (silu * up).astype(BF16)
        grad_gate = (back * up * (sig * (1.0 + gate * (1.0 - sig)))).astype(BF16)
        grad_up = (back * silu).astype(BF16)
        value = nn(act, down_ref[...])
        grad_rows = nt(grad_gate, gate_ref[...]) + nt(grad_up, up_ref[...])
        rows_t = rows_t_ref[:, span]
        acc_gate_ref[...] += nn(rows_t, grad_gate)
        acc_up_ref[...] += nn(rows_t, grad_up)
        acc_down_ref[...] += nn(grads_t_ref[:, span], act)

        @pl.when(step == 0)
        def _():
            acc_value_ref[span, :] = value
            acc_input_ref[span, :] = grad_rows

        @pl.when((step > 0) & (step < last))
        def _():
            acc_value_ref[span, :] += value
            acc_input_ref[span, :] += grad_rows

        @pl.when(step == last)
        def _():
            rows_ref[span, :] = (acc_value_ref[span, :] + value).astype(BF16)
            grads_ref[span, :] = (acc_input_ref[span, :] + grad_rows).astype(BF16)

        return carry

    lax.fori_loop(0, blocks, work, 0)
    grad_gate_ref[...] = acc_gate_ref[...].astype(BF16)
    grad_up_ref[...] = acc_up_ref[...].astype(BF16)
    grad_down_ref[...] = jnp.transpose(acc_down_ref[...].astype(BF16))

    @pl.when(step == last)
    def _():
        copies = []
        for number, (values, grads) in enumerate(zip((v0, v1, v2, v3), (d0, d1, d2, d3))):
            for member in range(batches):
                block = number * batches + member
                span = pl.ds(block * capacity, capacity)
                copies.append(pltpu.make_async_copy(rows_ref.at[span, :], values.at[member], sems.at[3 * block]))
                copies.append(pltpu.make_async_copy(grads_ref.at[span, :], grads.at[member], sems.at[3 * block + 1]))
        for copy in copies:
            copy.start()
        for copy in copies:
            copy.wait()


def combine_kernel(
    own_ref,
    v0,
    v1,
    v2,
    v3,
    d0,
    d1,
    d2,
    d3,
    pos_ref,
    aux_ref,
    routes_ref,
    prev_ref,
    h_ref,
    g_ref,
    o_ref,
    small_ref,
    wo_ref,
    out_ref,
    dh_ref,
    dob_ref,
    grad_wo_ref,
    sgrad_ref,
    grad_map_ref,
    acc_ref,
    cols_ref,
):
    own = own_ref[0]
    step = pl.program_id(0)
    length, width = h_ref.shape[1:]
    kinds = pos_ref.shape[1]
    ffn = kinds - 4
    capacity = v0.shape[1]
    hidden = h_ref[0]
    inverse = rms_scale(hidden)
    gain = small_ref[kinds + 7 : kinds + 8, :]
    n2 = hidden * inverse * gain
    n2_high, n2_low = split2(n2)
    grad_low = g_ref[0]
    grad = grad_low.astype(F32)
    small = small_ref[...].astype(BF16)
    cols_ref[0:kinds, :] = pos_ref[0]
    cols_ref[kinds : kinds + 16, :] = aux_ref[0]
    cols_ref[kinds + 16 :, :] = jnp.zeros((LANES - kinds - 16, length), F32)
    cols = jnp.transpose(cols_ref[...])
    lane = iota((1, LANES), 1)

    def column(source, index):
        return jnp.sum(jnp.where(lane == index, source, 0.0), axis=1, keepdims=True)

    gate_one = column(cols, 2 * kinds)
    gate_two = column(cols, 2 * kinds + 1)
    hot_one = jnp.where(routes_ref[0, :, 0:1] == lane, 1.0, 0.0)
    hot_two = jnp.where(routes_ref[0, :, 1:2] == lane, 1.0, 0.0)

    result = hidden
    grad_n2 = jnp.zeros((length, width), F32)
    dws = jnp.zeros((length, LANES), F32)
    slot_lane = iota((1, capacity), 1).astype(F32)
    for number, (values, grads) in enumerate(zip((v0, v1, v2, v3), (d0, d1, d2, d3))):
        expert = own ^ number
        mask = jnp.where(column(cols, expert) == slot_lane, 1.0, 0.0).astype(BF16)
        taken = nn(mask, values[0])
        result = result + column(cols, kinds + expert) * taken
        dws = jnp.where(lane == expert, jnp.sum(grad * taken, axis=1, keepdims=True), dws)
        grad_n2 = grad_n2 + nn(mask, grads[0])

    mixes = nt(n2_high, small) + nt(n2_low, small)
    inner = nt(grad_low, small)
    with_n2 = jnp.sum(grad * n2, axis=1, keepdims=True)
    weight_copy = column(cols, kinds + ffn + 1)
    dws = jnp.where(lane == ffn + 1, with_n2, dws)
    share = weight_copy
    coefs = jnp.zeros((length, LANES), F32)
    for constant in range(2):
        weight = column(cols, kinds + ffn + 2 + constant)
        za = mixes[:, kinds + 2 * constant : kinds + 2 * constant + 1]
        zb = mixes[:, kinds + 2 * constant + 1 : kinds + 2 * constant + 2]
        top = jnp.maximum(za, zb)
        ea, eb = jnp.exp(za - top), jnp.exp(zb - top)
        alpha_a = ea / (ea + eb)
        alpha_b = eb / (ea + eb)
        with_vec = inner[:, kinds + 4 + constant : kinds + 5 + constant]
        vec = small_ref[kinds + 4 + constant : kinds + 5 + constant, :]
        result = result + (weight * alpha_b) * vec
        share = share + weight * alpha_a
        dws = jnp.where(lane == ffn + 2 + constant, alpha_a * with_n2 + alpha_b * with_vec, dws)
        da = weight * with_n2
        db = weight * with_vec
        mean = alpha_a * da + alpha_b * db
        coefs = jnp.where(lane == kinds + 2 * constant, alpha_a * (da - mean), coefs)
        coefs = jnp.where(lane == kinds + 2 * constant + 1, alpha_b * (db - mean), coefs)
        coefs = jnp.where(lane == kinds + 4 + constant, weight * alpha_b, coefs)
    out_ref[0] = result + share * n2

    dg_one = jnp.sum(dws * hot_one, axis=1, keepdims=True)
    dg_two = jnp.sum(dws * hot_two, axis=1, keepdims=True)
    mean = gate_one * dg_one + gate_two * dg_two
    dlogits = gate_one * (dg_one - mean) * hot_one + gate_two * (dg_two - mean) * hot_two
    coefs = jnp.where(lane < kinds, dlogits, coefs)
    back = jnp.where(lane < kinds + 4, coefs, 0.0)[:, 0:16]
    back_high, back_low = split2(back)
    grad_n2 = grad_n2 + nn(back_high, small) + nn(back_low, small) + share * grad

    coefs_t = jnp.transpose(coefs)[0:16, :]
    high, low = split2(coefs_t)
    by_n2 = nn(high, n2_high) + nn(low, n2_high)
    by_low = nn(high, n2_low)
    by_grad = nn(high, grad_low) + nn(low, grad_low)
    row = iota((16, 1), 0)
    parts = jnp.where(row < kinds, by_n2, jnp.where(row < kinds + 4, by_n2 + by_low, by_grad))
    gain_part = jnp.sum(grad_n2 * hidden * inverse, axis=0, keepdims=True)
    parts = jnp.where(row == kinds + 7, gain_part, jnp.where(row == kinds + 6, 0.0, parts))
    dlog_t = coefs_t[0:kinds, :]
    map_lane = iota((kinds, LANES), 1)
    map_part = jnp.zeros((kinds, LANES), F32)
    for j in range(kinds):
        map_part = jnp.where(
            map_lane == j, jnp.sum(dlog_t * prev_ref[0, j : j + 1, :], axis=1, keepdims=True), map_part
        )

    scaled = gain * grad_n2
    inner_mean = jnp.mean(scaled * hidden, axis=-1, keepdims=True)
    dh = grad + inverse * scaled - hidden * (inverse * inverse * inverse) * inner_mean
    dh_ref[0] = dh
    db = dh.astype(BF16)
    dob_ref[0] = nt(db, wo_ref[...]).astype(BF16)
    wo_part = nn(jnp.transpose(o_ref[0]), db)

    @pl.when(step == 0)
    def _():
        acc_ref[...] = wo_part
        sgrad_ref[...] = parts
        grad_map_ref[...] = map_part

    @pl.when(step > 0)
    def _():
        acc_ref[...] += wo_part
        sgrad_ref[...] += parts
        grad_map_ref[...] += map_part

    @pl.when(step == pl.num_programs(0) - 1)
    def _():
        grad_wo_ref[...] = acc_ref[...].astype(BF16)


def backward_kernel(
    depth,
    x_ref,
    seg_row_ref,
    seg_col_ref,
    q_ref,
    k_ref,
    v_ref,
    dob_ref,
    lse_ref,
    dh_ref,
    small_ref,
    wq_ref,
    wk_ref,
    wv_ref,
    cos_ref,
    sin_ref,
    grad_wo_ref,
    sgrad_ref,
    grad_map_ref,
    gin_ref,
    grad_w_ref,
    gain_ref,
    bias_ref,
    lse_t_ref,
    dqkv_ref,
    acc_ref,
):
    step = pl.program_id(0)
    length, width = x_ref.shape[1:]
    kinds = small_ref.shape[0] - 8
    pairs = width // LANES
    lane = iota((1, LANES), 1)
    low_half = (lane % HEAD_DIM) < (HEAD_DIM // 2)
    first_head = lane < HEAD_DIM
    mask_a = jnp.where(first_head, 1.0, 0.0).astype(BF16)
    mask_b = jnp.where(first_head, 0.0, 1.0).astype(BF16)
    allowed = (seg_col_ref[0] == seg_row_ref[0]) & (
        iota((length, length), 0) // BLOCK <= iota((length, length), 1) // BLOCK
    )
    bias_ref[...] = jnp.where(allowed, 0.0, NEG)
    lse_t_ref[...] = jnp.transpose(lse_ref[0])

    def pair(h, carry):
        cols = pl.ds(pl.multiple_of(h * LANES, LANES), LANES)
        keys_t = jnp.transpose(k_ref[0, :, cols])
        grad_keys = None
        grad_values = None
        grad_queries = []
        for begin in range(0, length, BLOCK):
            end = begin + BLOCK
            queries = q_ref[0, begin:end, cols]
            outs = dob_ref[0, begin:end, cols]
            keys = k_ref[0, 0:end, cols]
            values = v_ref[0, 0:end, cols]
            queries = jnp.concatenate([queries * mask_a, queries * mask_b], axis=0)
            outs = jnp.concatenate([outs * mask_a, outs * mask_b], axis=0)
            bias = bias_ref[0:end, begin:end]
            bias = jnp.concatenate([bias, bias], axis=1)
            line = jnp.concatenate(
                [lse_t_ref[pl.ds(2 * h, 1), begin:end], lse_t_ref[pl.ds(2 * h + 1, 1), begin:end]], axis=1
            )
            chances = jnp.exp(nt(keys, queries) + bias - line)
            grad_chances = nt(values, outs)
            delta = jnp.sum(chances * grad_chances, axis=0, keepdims=True)
            grad_scores = (chances * (grad_chances - delta)).astype(BF16)
            dv = nn(chances.astype(BF16), outs)
            dk = nn(grad_scores, queries)
            dq = jnp.transpose(nn(keys_t[:, 0:end], grad_scores))
            grad_queries.append(jnp.where(first_head, dq[0:BLOCK], dq[BLOCK:]))
            if grad_keys is None:
                grad_keys, grad_values = dk, dv
            else:
                grad_keys = jnp.concatenate([grad_keys + dk[0:begin], dk[begin:]], axis=0)
                grad_values = jnp.concatenate([grad_values + dv[0:begin], dv[begin:]], axis=0)
        dq = jnp.concatenate(grad_queries, axis=0) * 0.125
        dq = dq * cos_ref[...] - swap_halves(dq, low_half) * sin_ref[...]
        dk = grad_keys * cos_ref[...] - swap_halves(grad_keys, low_half) * sin_ref[...]
        dqkv_ref[:, cols] = dq.astype(BF16)
        dqkv_ref[:, pl.ds(pl.multiple_of(width + h * LANES, LANES), LANES)] = dk.astype(BF16)
        dqkv_ref[:, pl.ds(pl.multiple_of(2 * width + h * LANES, LANES), LANES)] = grad_values.astype(BF16)
        return carry

    lax.fori_loop(0, pairs, pair, 0)

    tokens = x_ref[0].astype(F32)
    inverse = rms_scale(tokens)
    gain = small_ref[kinds + 6 : kinds + 7, :]
    a1_t = jnp.transpose((tokens * inverse * gain).astype(BF16))
    dn1 = (
        nt(dqkv_ref[:, 0:width], wq_ref[...])
        + nt(dqkv_ref[:, width : 2 * width], wk_ref[...])
        + nt(dqkv_ref[:, 2 * width :], wv_ref[...])
    )
    scaled = gain * dn1
    inner_mean = jnp.mean(scaled * tokens, axis=-1, keepdims=True)
    gin_ref[0] = dh_ref[0] + inverse * scaled - tokens * (inverse * inverse * inverse) * inner_mean
    gain_part = jnp.broadcast_to(jnp.sum(dn1 * tokens * inverse, axis=0, keepdims=True), gain_ref.shape)

    @pl.when(step == 0)
    def _():
        acc_ref[...] = jnp.zeros_like(acc_ref)
        gain_ref[...] = gain_part

    @pl.when(step > 0)
    def _():
        gain_ref[...] += gain_part

    for part in range(3):
        span = slice(part * width, (part + 1) * width)
        acc_ref[:, span] += nn(a1_t, dqkv_ref[:, span])

    @pl.when(step == pl.num_programs(0) - 1)
    def _():
        grad_w_ref[:, 0 : 3 * width] = acc_ref[...].astype(BF16)
        grad_w_ref[:, 3 * width : 4 * width] = grad_wo_ref[...]
        row = iota((16, 1), 0)
        table = jnp.where(row == kinds + 6, gain_ref[0:1, :], sgrad_ref[...])
        chosen = jnp.where(iota((LANES, width), 1) % depth == iota((LANES, width), 0), 1.0, 0.0).astype(BF16)
        maps = nn(grad_map_ref[...].astype(BF16), chosen)
        table = jnp.concatenate([table, maps, jnp.zeros((LANES - 16 - kinds, width), F32)], axis=0)
        grad_w_ref[:, 4 * width : 4 * width + LANES] = jnp.transpose(table).astype(BF16)
        grad_w_ref[:, 4 * width + LANES :] = jnp.zeros((width, LANES), BF16)


def reduce_kernel(
    group,
    full_ref,
    out_ref,
    acc_ref,
    core_ref,
    y_first_ref,
    x_second_ref,
    x_first_ref,
    y_second_ref,
    z_ref,
    done_ref,
    other_ref,
    local_sem,
    send,
    recv,
    z_send,
    z_recv,
):
    here = Place(group)
    planes = here.planes
    near = planes // 2
    depth, columns = acc_ref.shape[2:]
    half = columns // 2
    x, y = here.x, here.y
    mine = pl.ds(pl.multiple_of(y * half, LANES), half)
    theirs = pl.ds(pl.multiple_of((1 - y) * half, LANES), half)
    here.barrier(
        [here.core_peer, here.x_peer, here.y_peer] + [here.z_peer(k) for k in range(1, planes)]
    )
    own = pltpu.make_async_copy(full_ref.at[:, :, here.core], acc_ref, local_sem)
    own.start()
    swap = remote(full_ref.at[:, :, 1 - here.core], core_ref, send.at[0], recv.at[0], here.core_peer)
    swap.start()
    own.wait()
    swap.wait_recv()

    def add(target, source):
        target[...] = (target[...].astype(F32) + source[...].astype(F32)).astype(BF16)

    def add_core(z, carry):
        for column in range(2):
            add(acc_ref.at[z, column], core_ref.at[z, column])
        return carry

    lax.fori_loop(0, planes, add_core, 0)
    y_first = remote(acc_ref.at[0:near, :, :, theirs], y_first_ref, send.at[1], recv.at[1], here.y_peer)
    x_first = remote(acc_ref.at[near:planes, 1 - x], x_first_ref, send.at[2], recv.at[2], here.x_peer)
    y_first.start()
    x_first.start()
    y_first.wait_recv()
    for z in range(near):
        for column in range(2):
            add(acc_ref.at[z, column, :, mine], y_first_ref.at[z, column])
    x_second = remote(acc_ref.at[0:near, 1 - x, :, mine], x_second_ref, send.at[3], recv.at[3], here.x_peer)
    x_second.start()
    x_first.wait_recv()
    for z in range(near, planes):
        add(acc_ref.at[z, x], x_first_ref.at[z - near])
    y_second = remote(acc_ref.at[near:planes, x, :, theirs], y_second_ref, send.at[4], recv.at[4], here.y_peer)
    y_second.start()
    x_second.wait_recv()
    for z in range(near):
        add(acc_ref.at[z, x, :, mine], x_second_ref.at[z])
    y_second.wait_recv()
    for z in range(near, planes):
        add(acc_ref.at[z, x, :, mine], y_second_ref.at[z - near])
    along = []
    for k in range(1, planes):
        to = (here.z + k) % planes
        along.append(
            remote(acc_ref.at[to, x, :, mine], z_ref.at[k - 1], z_send.at[k - 1], z_recv.at[k - 1], here.z_peer(k))
        )
        along[-1].start()
    total = acc_ref[here.z, x, :, mine].astype(F32)
    for k in range(1, planes):
        along[k - 1].wait_recv()
        total = total + z_ref[k - 1].astype(F32)
    done_ref[...] = total.astype(BF16)
    back = remote(done_ref, other_ref, send.at[5], recv.at[5], here.y_peer)
    back.start()
    out_ref[:, mine] = done_ref[...].astype(F32)
    back.wait_recv()
    out_ref[:, theirs] = other_ref[...].astype(F32)
    for copy in [swap, y_first, x_first, x_second, y_second, back] + along:
        copy.wait_send()


def params(limit_mib):
    return pltpu.CompilerParams(vmem_limit_bytes=limit_mib * 1024 * 1024, dimension_semantics=("arbitrary",))


def rotary(length):
    halfway = HEAD_DIM // 2
    frequency = 10000.0 ** (-jnp.arange(halfway).astype(F32) / halfway)
    angles = jnp.arange(length).astype(F32)[:, None] * frequency[None, :]
    cosine, sine = jnp.cos(angles), jnp.sin(angles)
    return (
        jnp.concatenate([cosine] * 4, axis=1),
        jnp.concatenate([-sine, sine, -sine, sine], axis=1),
    )


def local(
    reps,
    group,
    block_input,
    prev_logits,
    routes,
    segments,
    grad_out,
    gain_attn,
    w_query,
    w_key,
    w_value,
    w_output,
    gain_mix,
    router,
    route_map,
    const_proj,
    const_vec,
    w_gate,
    w_up,
    w_down,
):
    batches, length = segments.shape
    width = block_input.shape[1]
    kinds = router.shape[1]
    ffn = w_gate.shape[1]
    hidden = w_gate.shape[2]
    rows_d = w_gate.shape[0]
    rows_f = w_down.shape[0]
    capacity = length // 2
    planes = group // 4
    assert reps == 2 and ffn == 4 and group % 4 == 0
    g = lax.axis_index("grp")
    y = lax.axis_index("rep")
    core = g % 2
    x = (g // 2) % 2
    z = g // 4
    own = (2 * y + x).astype(jnp.int32)
    own_arr = own.reshape(1)

    x_flip = [(i, i ^ 2) for i in range(group)]
    core_flip = [(i, i ^ 1) for i in range(group)]
    y_flip = [(0, 1), (1, 0)]
    xy_flip = [(r * group + i, (1 - r) * group + (i ^ 2)) for r in range(2) for i in range(group)]

    def z_shift(k):
        return [(i, (i + 4 * k) % group) for i in range(group)]

    def to_plane(parts):
        return [
            parts[0],
            lax.ppermute(parts[1], "grp", x_flip),
            lax.ppermute(parts[2], "rep", y_flip),
            lax.ppermute(parts[3], ("rep", "grp"), xy_flip),
        ]

    tokens = block_input.reshape(batches, length, width)
    grads = grad_out.reshape(batches, length, width)
    route_cols = routes.reshape(batches, length, 2)
    route_rows = route_cols.transpose(0, 2, 1)
    prev_rows = prev_logits.reshape(batches, length, kinds).transpose(0, 2, 1)
    seg_row = segments[:, None, :]
    seg_col = segments[:, :, None]
    cos, sin = rotary(length)

    def spec_w(j):
        return pl.BlockSpec((width, width), lambda b, *_: (0, j), pipeline_mode=pl.Buffered(1))

    row_shape = jax.ShapeDtypeStruct((batches, capacity, width), BF16)
    seq_bf16 = jax.ShapeDtypeStruct((batches, length, width), BF16)
    seq_f32 = jax.ShapeDtypeStruct((batches, length, width), F32)
    small_shard = jnp.concatenate(
        [router, const_proj, const_vec, gain_attn[:, None], gain_mix[:, None]], axis=1
    ).astype(BF16)
    small_shard = jnp.pad(small_shard, ((0, 0), (0, LANES - small_shard.shape[1])))
    shard = jnp.concatenate([w.astype(BF16) for w in (w_query, w_key, w_value)] + [small_shard], axis=1)
    shard_o = w_output.astype(BF16)
    if rows_d % 16 == 0 and rows_f % 16 == 0:
        any_space = pl.BlockSpec(memory_space=pl.ANY)
        out_struct = jax.ShapeDtypeStruct
        (
            q, k, v, o, h1, lse, aux, pos, small, attn, attn_o, a_rows, grad_rows, gate_full, up_full, down_full,
        ) = pl.pallas_call(
            functools.partial(fused_forward_kernel, group),
            grid=(batches,),
            in_specs=[
                per_seq((length, width)),
                per_seq((1, length)),
                per_seq((length, 1)),
                whole((batches, 2, length)),
                per_seq((kinds, length)),
                whole((kinds, kinds)),
                whole((batches, length, width)),
                whole((length, LANES)),
                whole((length, LANES)),
            ]
            + [any_space] * 5,
            out_specs=[per_seq((length, width))] * 5
            + [
                per_seq((length, LANES)),
                per_seq((16, length)),
                whole((batches, kinds, length)),
                whole((kinds + 8, width)),
            ]
            + [any_space] * 7,
            scratch_shapes=[
                pltpu.VMEM((width, 3 * width + LANES), BF16),
                pltpu.VMEM((width, width), BF16),
                pltpu.VMEM((length, length), F32),
                pltpu.VMEM((length, width), F32),
                pltpu.VMEM((batches, 4, capacity + 16, width), BF16),
                pltpu.VMEM((batches, 4, capacity, width), BF16),
                pltpu.SemaphoreType.DMA((2,)),
                pltpu.SemaphoreType.DMA((2, 3, 2 * planes)),
                pltpu.SemaphoreType.DMA((2, group)),
                pltpu.SemaphoreType.DMA((3,)),
                pltpu.SemaphoreType.DMA((3, 2 * planes)),
                pltpu.SemaphoreType.DMA((3,)),
                pltpu.SemaphoreType.DMA((3, planes)),
                pltpu.SemaphoreType.DMA((3, planes)),
                pltpu.SemaphoreType.DMA((2,)),
                pltpu.SemaphoreType.DMA((2, batches)),
                pltpu.SemaphoreType.DMA((2, batches, 4)),
                pltpu.SemaphoreType.DMA((2, batches, 4)),
            ],
            out_shape=[seq_bf16] * 4
            + [
                seq_f32,
                out_struct((batches, length, LANES), F32),
                out_struct((batches, 16, length), F32),
                out_struct((batches, kinds, length), F32),
                out_struct((kinds + 8, width), F32),
                out_struct((width, 3 * width + LANES), BF16),
                out_struct((width, width), BF16),
                out_struct((4, batches, capacity + 16, width), BF16),
                out_struct((4, batches, capacity, width), BF16),
                out_struct((planes, 2, 2, rows_d, hidden), BF16),
                out_struct((planes, 2, 2, rows_d, hidden), BF16),
                out_struct((planes, 2, 2, rows_f, width), BF16),
            ],
            compiler_params=pltpu.CompilerParams(
                vmem_limit_bytes=58 * 1024 * 1024,
                dimension_semantics=("arbitrary",),
                collective_id=1,
                has_side_effects=True,
            ),
            cost_estimate=pl.CostEstimate(flops=40 * 10**9, bytes_accessed=60 * 10**6, transcendentals=10**7),
            name="fused_forward",
        )(
            tokens, seg_row, seg_col, route_rows, prev_rows, route_map.T, grads, cos, sin,
            shard, shard_o,
            w_gate.astype(BF16).transpose(1, 0, 2),
            w_up.astype(BF16).transpose(1, 0, 2),
            w_down.astype(BF16).transpose(1, 0, 2),
        )
        gate_full = gate_full.reshape(width, hidden)
        up_full = up_full.reshape(width, hidden)
        down_full = down_full.reshape(hidden, width)
    else:
        attn = lax.all_gather(shard, "grp", axis=0, tiled=True)
        attn_o = lax.all_gather(shard_o, "grp", axis=0, tiled=True)
        small = attn[:, 3 * width : 3 * width + kinds + 8].astype(F32).T

        def pick(array, expert):
            return lax.dynamic_index_in_dim(array, expert, axis=1, keepdims=False)

        def gather_expert(mine, other):
            crossed = lax.ppermute(other, "grp", x_flip)
            both = jnp.where(x == 0, jnp.stack([mine, crossed]), jnp.stack([crossed, mine]))
            pieces = [both] + [lax.ppermute(both, "grp", z_shift(k)) for k in range(1, planes)]
            stacked = jnp.stack(pieces)
            half = jnp.take(stacked, (z - jnp.arange(planes)) % planes, axis=0)
            swapped = lax.ppermute(half, "grp", core_flip)
            return jnp.where(core == 0, jnp.stack([half, swapped], axis=2), jnp.stack([swapped, half], axis=2))

        gate_up = gather_expert(
            jnp.stack([pick(w_gate, own), pick(w_up, own)]).astype(BF16),
            jnp.stack([pick(w_gate, own ^ 1), pick(w_up, own ^ 1)]).astype(BF16),
        )
        down = gather_expert(pick(w_down, own).astype(BF16), pick(w_down, own ^ 1).astype(BF16))
        gate_full = gate_up[:, :, :, 0].reshape(width, hidden)
        up_full = gate_up[:, :, :, 1].reshape(width, hidden)
        down_full = down.reshape(hidden, width)

        *grad_rows, pos = pl.pallas_call(
            grad_rows_kernel,
            grid_spec=pltpu.PrefetchScalarGridSpec(
                num_scalar_prefetch=1,
                grid=(batches,),
                in_specs=[per_seq((2, length)), per_seq((length, width))],
                out_specs=[per_seq((capacity, width))] * 4 + [per_seq((kinds, length))],
            ),
            out_shape=[row_shape] * 4 + [jax.ShapeDtypeStruct((batches, kinds, length), F32)],
            compiler_params=params(32),
            cost_estimate=pl.CostEstimate(flops=4 * 10**9, bytes_accessed=8 * 10**6, transcendentals=0),
            name="grad_rows",
        )(own_arr, route_rows, grads)
        grad_rows = to_plane(grad_rows)

        q, k, v, o, h1, lse, aux, *a_rows = pl.pallas_call(
            forward_kernel,
            grid_spec=pltpu.PrefetchScalarGridSpec(
                num_scalar_prefetch=1,
                grid=(batches,),
                in_specs=[
                    per_seq((length, width)),
                    per_seq((1, length)),
                    per_seq((length, 1)),
                    per_seq((2, length)),
                    per_seq((kinds, length)),
                    whole((kinds, kinds)),
                    whole((kinds + 8, width)),
                    spec_w(0),
                    spec_w(1),
                    spec_w(2),
                    spec_w(0),
                    whole((length, LANES)),
                    whole((length, LANES)),
                    per_seq((kinds, length)),
                ],
                out_specs=[per_seq((length, width))] * 5
                + [per_seq((length, LANES)), per_seq((16, length))]
                + [per_seq((capacity + 16, width))] * 4,
                scratch_shapes=[pltpu.VMEM((length, length), F32), pltpu.VMEM((length, width), F32)],
            ),
            out_shape=[seq_bf16] * 4
            + [
                seq_f32,
                jax.ShapeDtypeStruct((batches, length, LANES), F32),
                jax.ShapeDtypeStruct((batches, 16, length), F32),
            ]
            + [jax.ShapeDtypeStruct((batches, capacity + 16, width), BF16)] * 4,
            compiler_params=params(56),
            cost_estimate=pl.CostEstimate(flops=20 * 10**9, bytes_accessed=20 * 10**6, transcendentals=10**7),
            name="forward",
        )(own_arr, tokens, seg_row, seg_col, route_rows, prev_rows, route_map.T, small, attn, attn, attn, attn_o, cos, sin, pos)
        a_rows = to_plane(a_rows)

        a_rows = jnp.stack(a_rows)
        grad_rows = jnp.stack(grad_rows)

    tile = hidden // 4
    total = 4 * batches * capacity
    any_spec = pl.BlockSpec(memory_space=pl.ANY)
    outs = pl.pallas_call(
        expert_kernel,
        grid=(hidden // tile,),
        in_specs=[any_spec] * 2
        + [
            pl.BlockSpec((width, tile), lambda f: (0, f)),
            pl.BlockSpec((width, tile), lambda f: (0, f)),
            pl.BlockSpec((tile, width), lambda f: (f, 0)),
        ],
        out_specs=[any_spec] * 8
        + [
            pl.BlockSpec((width, tile), lambda f: (0, f)),
            pl.BlockSpec((width, tile), lambda f: (0, f)),
            pl.BlockSpec((tile, width), lambda f: (f, 0)),
        ],
        scratch_shapes=[
            pltpu.VMEM((total, width), BF16),
            pltpu.VMEM((total, width), BF16),
            pltpu.VMEM((4 * batches, 16, capacity), BF16),
            pltpu.VMEM((width, total), BF16),
            pltpu.VMEM((width, total), BF16),
            pltpu.VMEM((total, LANES), F32),
            pltpu.VMEM((total, width), F32),
            pltpu.VMEM((total, width), F32),
            pltpu.VMEM((width, tile), F32),
            pltpu.VMEM((width, tile), F32),
            pltpu.VMEM((width, tile), F32),
            pltpu.SemaphoreType.DMA((12 * batches,)),
        ],
        out_shape=[row_shape] * 8
        + [
            jax.ShapeDtypeStruct((width, hidden), BF16),
            jax.ShapeDtypeStruct((width, hidden), BF16),
            jax.ShapeDtypeStruct((hidden, width), BF16),
        ],
        compiler_params=params(60),
        cost_estimate=pl.CostEstimate(flops=58 * 10**9, bytes_accessed=40 * 10**6, transcendentals=10**7),
        name="expert",
    )(a_rows, grad_rows, gate_full, up_full, down_full)
    value_rows = to_plane(outs[0:4])
    input_rows = to_plane(outs[4:8])
    grad_gate_full, grad_up_full, grad_down_full = outs[8:]

    def scatter_expert(full):
        keep = lax.dynamic_index_in_dim(full, core, axis=2, keepdims=False)
        send = lax.dynamic_index_in_dim(full, 1 - core, axis=2, keepdims=False)
        half = (keep.astype(F32) + lax.ppermute(send, "grp", core_flip).astype(F32)).astype(BF16)
        summed = lax.dynamic_index_in_dim(half, z, axis=0, keepdims=False).astype(F32)
        for k in range(1, planes):
            part = lax.dynamic_index_in_dim(half, (z + k) % planes, axis=0, keepdims=False)
            summed = summed + lax.ppermute(part, "grp", z_shift(k)).astype(F32)
        summed = summed.astype(BF16)
        mine = lax.dynamic_index_in_dim(summed, x, axis=0, keepdims=False)
        other = lax.dynamic_index_in_dim(summed, 1 - x, axis=0, keepdims=False)
        arrived = to_plane([mine, other, mine, other])

        def order(first):
            return lambda: tuple(arrived[first ^ e] for e in range(4))

        return lax.switch(own, [order(i) for i in range(4)])

    grad_gate_up = scatter_expert(
        jnp.stack(
            [
                grad_gate_full.reshape(planes, 2, 2, rows_d, hidden),
                grad_up_full.reshape(planes, 2, 2, rows_d, hidden),
            ],
            axis=3,
        )
    )
    grad_down = scatter_expert(grad_down_full.reshape(planes, 2, 2, rows_f, width))
    grad_gate = jnp.stack([part[0] for part in grad_gate_up], axis=1).astype(F32)
    grad_up = jnp.stack([part[1] for part in grad_gate_up], axis=1).astype(F32)
    grad_down = jnp.stack(grad_down, axis=1).astype(F32)

    result, dh1, dob, grad_wo, sgrad, grad_map = pl.pallas_call(
        combine_kernel,
        grid_spec=pltpu.PrefetchScalarGridSpec(
            num_scalar_prefetch=1,
            grid=(batches,),
            in_specs=[per_seq((capacity, width))] * 8
            + [
                per_seq((kinds, length)),
                per_seq((16, length)),
                per_seq((length, 2)),
                per_seq((kinds, length)),
                per_seq((length, width)),
                per_seq((length, width)),
                per_seq((length, width)),
                whole((kinds + 8, width)),
                spec_w(0),
            ],
            out_specs=[per_seq((length, width))] * 3
            + [whole((width, width)), whole((16, width)), whole((kinds, LANES))],
            scratch_shapes=[pltpu.VMEM((width, width), F32), pltpu.VMEM((LANES, length), F32)],
        ),
        out_shape=[
            seq_f32,
            seq_f32,
            seq_bf16,
            jax.ShapeDtypeStruct((width, width), BF16),
            jax.ShapeDtypeStruct((16, width), F32),
            jax.ShapeDtypeStruct((kinds, LANES), F32),
        ],
        compiler_params=params(56),
        cost_estimate=pl.CostEstimate(flops=12 * 10**9, bytes_accessed=20 * 10**6, transcendentals=10**5),
        name="combine",
    )(own_arr, *value_rows, *input_rows, pos, aux, route_cols, prev_rows, h1, grads, o, small, attn_o)

    gin, grad_attn, gain_one = pl.pallas_call(
        functools.partial(backward_kernel, rows_d),
        grid=(batches,),
        in_specs=[
            per_seq((length, width)),
            per_seq((1, length)),
            per_seq((length, 1)),
            per_seq((length, width)),
            per_seq((length, width)),
            per_seq((length, width)),
            per_seq((length, width)),
            per_seq((length, LANES)),
            per_seq((length, width)),
            whole((kinds + 8, width)),
            spec_w(0),
            spec_w(1),
            spec_w(2),
            whole((length, LANES)),
            whole((length, LANES)),
            whole((width, width)),
            whole((16, width)),
            whole((kinds, LANES)),
        ],
        out_specs=[per_seq((length, width)), whole((width, 4 * width + 2 * LANES), 1), whole((8, width))],
        scratch_shapes=[
            pltpu.VMEM((length, length), F32),
            pltpu.VMEM((LANES, length), F32),
            pltpu.VMEM((length, 3 * width), BF16),
            pltpu.VMEM((width, 3 * width), F32),
        ],
        out_shape=[
            seq_f32,
            jax.ShapeDtypeStruct((width, 4 * width + 2 * LANES), BF16),
            jax.ShapeDtypeStruct((8, width), F32),
        ],
        compiler_params=params(56),
        cost_estimate=pl.CostEstimate(flops=30 * 10**9, bytes_accessed=20 * 10**6, transcendentals=10**7),
        name="backward",
    )(tokens, seg_row, seg_col, q, k, v, dob, lse, dh1, small, attn, attn, attn, cos, sin, grad_wo, sgrad, grad_map)

    if rows_d % 16 == 0 and planes % 2 == 0:
        columns = 4 * width + 2 * LANES
        near = planes // 2
        sums = pl.pallas_call(
            functools.partial(reduce_kernel, group),
            in_specs=[pl.BlockSpec(memory_space=pl.ANY)],
            out_specs=pl.BlockSpec(memory_space=pltpu.VMEM),
            out_shape=jax.ShapeDtypeStruct((rows_d, columns), F32),
            scratch_shapes=[
                pltpu.VMEM((planes, 2, rows_d, columns), BF16),
                pltpu.VMEM((planes, 2, rows_d, columns), BF16),
                pltpu.VMEM((near, 2, rows_d, columns // 2), BF16),
                pltpu.VMEM((near, rows_d, columns // 2), BF16),
                pltpu.VMEM((near, rows_d, columns), BF16),
                pltpu.VMEM((near, rows_d, columns // 2), BF16),
                pltpu.VMEM((planes - 1, rows_d, columns // 2), BF16),
                pltpu.VMEM((rows_d, columns // 2), BF16),
                pltpu.VMEM((rows_d, columns // 2), BF16),
                pltpu.SemaphoreType.DMA,
                pltpu.SemaphoreType.DMA((6,)),
                pltpu.SemaphoreType.DMA((6,)),
                pltpu.SemaphoreType.DMA((planes - 1,)),
                pltpu.SemaphoreType.DMA((planes - 1,)),
            ],
            compiler_params=pltpu.CompilerParams(
                vmem_limit_bytes=32 * 1024 * 1024, collective_id=2, has_side_effects=True
            ),
            name="reduce",
        )(grad_attn.reshape(planes, 2, 2, rows_d, columns))
        attn_total = sums[:, 0 : 4 * width]
        sums = sums[:, 4 * width :]
        map_total = sums[0:kinds, 16 : 16 + kinds]
    else:
        part = lax.psum_scatter(grad_attn[:, 0 : 4 * width], "grp", scatter_dimension=0, tiled=True)
        attn_total = lax.psum(part, "rep").astype(F32)
        sgrad = jnp.where(iota((16, 1), 0) == kinds + 6, gain_one[0:1], sgrad)
        packed = jnp.concatenate([sgrad, jnp.pad(grad_map, ((0, 0), (0, width - LANES)))], axis=0)
        packed = lax.psum(packed, ("rep", "grp"))
        sums = lax.dynamic_slice_in_dim(packed[0:16], g * rows_d, rows_d, axis=1).T
        map_total = packed[16:, 0:kinds].T
    return (
        result.reshape(batches * length, width),
        gin.reshape(batches * length, width),
        sums[:, kinds + 6],
        attn_total[:, 0:width],
        attn_total[:, width : 2 * width],
        attn_total[:, 2 * width : 3 * width],
        attn_total[:, 3 * width :],
        sums[:, kinds + 7],
        sums[:, 0:kinds],
        map_total,
        sums[:, kinds : kinds + 4],
        sums[:, kinds + 4 : kinds + 6],
        grad_gate,
        grad_up,
        grad_down,
    )


def solution(mesh):
    rows = P(("rep", "grp"), None)
    in_specs = (
        (rows,) * 5
        + (P("grp"),)
        + (P("grp", None),) * 4
        + (P("grp"), P("grp", None), P(), P("grp", None), P("grp", None))
        + (P("grp", None, None),) * 3
    )
    out_specs = (
        (rows,) * 2
        + (P("grp"),)
        + (P("grp", None),) * 4
        + (P("grp"), P("grp", None), P(), P("grp", None), P("grp", None))
        + (P("grp", None, None),) * 3
    )
    body = functools.partial(local, mesh.shape["rep"], mesh.shape["grp"])
    return jax.shard_map(body, mesh=mesh, in_specs=in_specs, out_specs=out_specs, check_vma=False)
```

```python
import functools

import jax
import jax.numpy as jnp
from jax import lax
from jax.experimental import pallas as pl
from jax.experimental.pallas import tpu as pltpu
from jax.sharding import PartitionSpec as P

HEAD_DIM = 64
BLOCK = 256
EPS = 1e-05
NEG = -1000000000.0
F32 = jnp.float32
BF16 = jnp.bfloat16
LANES = 128


def nn(a, b):
    return lax.dot_general(a, b, (((1,), (0,)), ((), ())), preferred_element_type=F32)


def nt(a, b):
    return lax.dot_general(a, b, (((1,), (1,)), ((), ())), preferred_element_type=F32)


def tn(a, b):
    return lax.dot_general(a, b, (((0,), (0,)), ((), ())), preferred_element_type=F32)


def iota(shape, dim):
    return lax.broadcasted_iota(jnp.int32, shape, dim)


def split2(values):
    high = values.astype(BF16)
    low = (values - high.astype(F32)).astype(BF16)
    return high, low


def whole(shape, buffers=None):
    zeros = (0,) * len(shape)
    if buffers:
        return pl.BlockSpec(shape, lambda *_: zeros, pipeline_mode=pl.Buffered(buffers))
    return pl.BlockSpec(shape, lambda *_: zeros)


def per_seq(shape):
    tail = (0,) * len(shape)
    return pl.BlockSpec((1,) + shape, lambda b, *_: (b,) + tail)


def rms_scale(values):
    return lax.rsqrt(jnp.mean(values * values, axis=-1, keepdims=True) + EPS)


def slot_mask(position_row, capacity):
    places = iota((capacity, position_row.shape[1]), 0).astype(F32)
    return jnp.where(places == position_row, 1.0, 0.0).astype(BF16)


def grad_rows_kernel(own_ref, routes_ref, grad_ref, r0, r1, r2, r3, pos_ref):
    own = own_ref[0]
    kinds, length = pos_ref.shape[1:]
    capacity = r0.shape[1]
    ids = iota((kinds, length), 0)
    first = routes_ref[0, 0:1, :] == ids
    second = routes_ref[0, 1:2, :] == ids
    hits = jnp.where(first | second, 1.0, 0.0)
    before = jnp.where(iota((length, length), 0) < iota((length, length), 1), 1.0, 0.0)
    slots = nn(hits.astype(BF16), before.astype(BF16))
    pos_ref[0] = jnp.where(hits > 0.0, slots, -1.0)
    for number, rows in enumerate((r0, r1, r2, r3)):
        line = pos_ref[0, pl.ds(own ^ number, 1), :]
        rows[0] = nn(slot_mask(line, capacity), grad_ref[0]).astype(BF16)


def swap_halves(values, low_half):
    return jnp.where(low_half, pltpu.roll(values, 96, 1), pltpu.roll(values, 32, 1))


def sequence_forward(
    x_ref,
    seg_row_ref,
    seg_col_ref,
    routes_ref,
    prev_ref,
    map_ref,
    small_ref,
    wq_ref,
    wk_ref,
    wv_ref,
    wo_ref,
    cos_ref,
    sin_ref,
    pos_ref,
    q_ref,
    k_ref,
    v_ref,
    o_ref,
    h_ref,
    lse_ref,
    aux_ref,
    rows_refs,
    bias_ref,
    proj_ref,
    expert_of,
    between=None,
):
    length, width = x_ref.shape[1:]
    kinds = pos_ref.shape[1]
    capacity = length // 2
    tokens = x_ref[0].astype(F32)
    gain_one = small_ref[kinds + 6 : kinds + 7, :]
    gain_two = small_ref[kinds + 7 : kinds + 8, :]
    a1 = (tokens * rms_scale(tokens) * gain_one).astype(BF16)
    lane = iota((1, LANES), 1)
    low_half = (lane % HEAD_DIM) < (HEAD_DIM // 2)
    first_head = lane < HEAD_DIM
    mask_a = jnp.where(first_head, 1.0, 0.0).astype(BF16)
    mask_b = jnp.where(first_head, 0.0, 1.0).astype(BF16)
    pairs = width // LANES

    for weights, target, scale in ((wq_ref, q_ref, 0.125), (wk_ref, k_ref, 1.0)):
        proj_ref[...] = nn(a1, weights[...])

        def turn(h, carry):
            cols = pl.ds(pl.multiple_of(h * LANES, LANES), LANES)
            part = proj_ref[:, cols]
            turned = part * cos_ref[...] + swap_halves(part, low_half) * sin_ref[...]
            target[0, :, cols] = turned.astype(BF16) * jnp.asarray(scale, BF16)
            return carry

        lax.fori_loop(0, pairs, turn, 0)
    v_ref[0] = nn(a1, wv_ref[...]).astype(BF16)

    allowed = (seg_col_ref[0] == seg_row_ref[0]) & (
        iota((length, length), 1) // BLOCK <= iota((length, length), 0) // BLOCK
    )
    bias_ref[...] = jnp.where(allowed, 0.0, NEG)
    lse_ref[...] = jnp.zeros_like(lse_ref)
    if between is not None:
        between()

    def pair(h, carry):
        cols = pl.ds(pl.multiple_of(h * LANES, LANES), LANES)
        for begin in range(0, length, BLOCK):
            end = begin + BLOCK
            queries = q_ref[0, begin:end, cols]
            keys = k_ref[0, 0:end, cols]
            values = v_ref[0, 0:end, cols]
            bias = bias_ref[begin:end, 0:end]
            sums = lse_ref[0, begin:end, :]
            outs = []
            for half, mask in enumerate((mask_a, mask_b)):
                scores = nt(queries * mask, keys) + bias
                top = jnp.max(scores, axis=-1, keepdims=True)
                grown = jnp.exp(scores - top)
                total = jnp.sum(grown, axis=-1, keepdims=True)
                chances = (grown * (1.0 / total)).astype(BF16)
                outs.append(nn(chances, values))
                sums = jnp.where(lane == 2 * h + half, top + jnp.log(total), sums)
            lse_ref[0, begin:end, :] = sums
            o_ref[0, begin:end, cols] = jnp.where(first_head, outs[0], outs[1]).astype(BF16)
        return carry

    lax.fori_loop(0, pairs, pair, 0)

    hidden = tokens + nn(o_ref[0], wo_ref[...])
    h_ref[0] = hidden
    a2 = (hidden * rms_scale(hidden) * gain_two).astype(BF16)
    logits = nt(small_ref[...].astype(BF16), a2)[0:kinds, :]
    for j in range(kinds):
        logits = logits + map_ref[:, j : j + 1] * prev_ref[0, j : j + 1, :]
    ids = iota((kinds, length), 0)
    first = jnp.where(routes_ref[0, 0:1, :] == ids, 1.0, 0.0)
    second = jnp.where(routes_ref[0, 1:2, :] == ids, 1.0, 0.0)
    one = jnp.sum(logits * first, axis=0, keepdims=True)
    two = jnp.sum(logits * second, axis=0, keepdims=True)
    top = jnp.maximum(one, two)
    grown_one, grown_two = jnp.exp(one - top), jnp.exp(two - top)
    gate_one = grown_one / (grown_one + grown_two)
    gate_two = grown_two / (grown_one + grown_two)
    aux_ref[0, 0:kinds, :] = gate_one * first + gate_two * second
    aux_ref[0, kinds : kinds + 1, :] = gate_one
    aux_ref[0, kinds + 1 : kinds + 2, :] = gate_two
    aux_ref[0, kinds + 2 :, :] = jnp.zeros((aux_ref.shape[1] - kinds - 2, length), F32)

    place = iota((16, length), 0)
    for number, rows in enumerate(rows_refs):
        mask = slot_mask(pos_ref[0, pl.ds(expert_of(number), 1), :], capacity)
        rows[0, 0:capacity, :] = nn(mask, a2).astype(BF16)
        line = aux_ref[0, pl.ds(expert_of(number), 1), :]
        high = line.astype(BF16).astype(F32)
        mid = (line - high).astype(BF16).astype(F32)
        low = line - high - mid
        parts = jnp.where(place == 0, high, jnp.where(place == 1, mid, jnp.where(place == 2, low, 0.0)))
        spread = nt(parts.astype(BF16), mask)
        filled = jnp.max(pos_ref[0, pl.ds(expert_of(number), 1), :], axis=1, keepdims=True) + 1.0
        spread = jnp.where(iota((16, 1), 0) == 3, filled, spread)
        rows[0, capacity:, 0:capacity] = spread.astype(BF16)
        rows[0, capacity:, capacity:] = jnp.zeros((16, width - capacity), BF16)


def forward_kernel(
    own_ref,
    x_ref,
    seg_row_ref,
    seg_col_ref,
    routes_ref,
    prev_ref,
    map_ref,
    small_ref,
    wq_ref,
    wk_ref,
    wv_ref,
    wo_ref,
    cos_ref,
    sin_ref,
    pos_ref,
    q_ref,
    k_ref,
    v_ref,
    o_ref,
    h_ref,
    lse_ref,
    aux_ref,
    r0,
    r1,
    r2,
    r3,
    bias_ref,
    proj_ref,
):
    own = own_ref[0]
    sequence_forward(
        x_ref,
        seg_row_ref,
        seg_col_ref,
        routes_ref,
        prev_ref,
        map_ref,
        small_ref,
        wq_ref,
        wk_ref,
        wv_ref,
        wo_ref,
        cos_ref,
        sin_ref,
        pos_ref,
        q_ref,
        k_ref,
        v_ref,
        o_ref,
        h_ref,
        lse_ref,
        aux_ref,
        (r0, r1, r2, r3),
        bias_ref,
        proj_ref,
        lambda number: own ^ number,
    )


MESH = pl.DeviceIdType.MESH


class Place:
    def __init__(self, group):
        self.group = group
        self.planes = group // 4
        self.g = lax.axis_index("grp")
        self.y = lax.axis_index("rep")
        self.core = self.g % 2
        self.x = (self.g // 2) % 2
        self.z = self.g // 4
        self.core_peer = (self.y, self.g + 1 - 2 * self.core)
        self.x_peer = (self.y, self.g + 2 - 4 * self.x)
        self.y_peer = (1 - self.y, self.g)
        self.xy_peer = (1 - self.y, self.g + 2 - 4 * self.x)
        self.plane_peers = (None, self.x_peer, self.y_peer, self.xy_peer)

    def z_peer(self, k):
        return (self.y, (self.g + 4 * k) % self.group)

    def block(self, z, x, core):
        return (z * 2 + x) * 2 + core

    def expert(self, number):
        y = self.y if number < 2 else 1 - self.y
        x = self.x if number % 2 == 0 else 1 - self.x
        return 2 * y + x

    def barrier(self, peers):
        semaphore = pltpu.get_barrier_semaphore()
        for peer in peers:
            pl.semaphore_signal(semaphore, inc=1, device_id=peer, device_id_type=MESH)
        pl.semaphore_wait(semaphore, len(peers))


def remote(src, dst, send, recv, peer):
    return pltpu.make_async_remote_copy(
        src_ref=src, dst_ref=dst, send_sem=send, recv_sem=recv, device_id=peer, device_id_type=MESH
    )


def fused_forward_kernel(
    group,
    x_ref,
    seg_row_ref,
    seg_col_ref,
    routes_ref,
    prev_ref,
    map_ref,
    grad_ref,
    cos_ref,
    sin_ref,
    shard_ref,
    shard_o_ref,
    gate4_ref,
    up4_ref,
    down4_ref,
    q_ref,
    k_ref,
    v_ref,
    o_ref,
    h_ref,
    lse_ref,
    aux_ref,
    pos_ref,
    small_ref,
    attn_out_ref,
    attn_o_out_ref,
    rows_in_ref,
    grads_in_ref,
    gate_full_ref,
    up_full_ref,
    down_full_ref,
    attn_ref,
    attn_o_ref,
    bias_ref,
    proj_ref,
    rows_ref,
    grows_ref,
    local_sem,
    attn_send,
    attn_recv,
    ffn_local,
    ffn_send,
    ffn_recv,
    out_sem,
    row_local,
    row_send,
    row_recv,
):
    step = pl.program_id(0)
    last = pl.num_programs(0) - 1
    here = Place(group)
    planes = here.planes
    batches, kinds, length = pos_ref.shape
    width = x_ref.shape[2]
    capacity = length // 2
    shards = ((shard_ref, attn_ref), (shard_o_ref, attn_o_ref))
    experts = ((gate4_ref, gate_full_ref), (up4_ref, up_full_ref), (down4_ref, down_full_ref))
    depth = shard_ref.shape[0]
    mine = here.block(here.z, here.x, here.core)

    def rows_of(block):
        return pl.ds(pl.multiple_of(block * depth, 16), depth)

    def attn_part(t, block, part):
        full = shards[t][1]
        half = full.shape[1] // 2
        if part is None:
            return full.at[rows_of(block), :]
        return full.at[rows_of(block), pl.ds(pl.multiple_of(part * half, LANES), half)]

    def attn_copy(t, slot, z, x, part, peer):
        ref = attn_part(t, here.block(z, x, here.core), part)
        return remote(ref, ref, attn_send.at[t, slot], attn_recv.at[t, slot], peer)

    def to_z(t, k):
        return attn_copy(t, k, here.z, here.x, None, here.z_peer(1 if k == 0 else planes - 1))

    def from_z(t, k):
        return attn_copy(t, k, z_at(planes - 1 if k == 0 else 1), here.x, None, here.x_peer)

    def pass_z(t, k):
        z = z_at(planes - 1 if k == 0 else 1)
        return attn_copy(t, 2 + k, z, here.x, k, here.z_peer(1 if k == 0 else planes - 1))

    def passed_z(t, k):
        return attn_copy(t, 2 + k, z_at(2), here.x, k, here.x_peer)

    def to_x(t, step_z):
        return attn_copy(t, 4 + step_z, z_at(step_z), here.x, here.y, here.x_peer)

    def from_x(t, step_z):
        return attn_copy(t, 4 + step_z, z_at(step_z), 1 - here.x, here.y, here.x_peer)

    def to_y(t, step_z):
        return attn_copy(t, 4 + planes + step_z, z_at(step_z), 1 - here.x, here.y, here.y_peer)

    def from_y(t, step_z):
        return attn_copy(t, 4 + planes + step_z, z_at(step_z), 1 - here.x, 1 - here.y, here.y_peer)

    def to_core(t, step_z, x):
        return attn_copy(t, 4 + 2 * planes + 2 * step_z + x, z_at(step_z), here.x if x == 0 else 1 - here.x, None, here.core_peer)

    def from_core(t, step_z, x):
        ref = attn_part(t, here.block(z_at(step_z), here.x if x == 0 else 1 - here.x, 1 - here.core), None)
        slot = 4 + 2 * planes + 2 * step_z + x
        return remote(ref, ref, attn_send.at[t, slot], attn_recv.at[t, slot], here.core_peer)

    def z_at(k):
        return (here.z + k) % planes

    def ffn_to_x(j):
        source, full = experts[j]
        return remote(
            source.at[here.expert(1)],
            full.at[here.z, here.x, here.core],
            ffn_send.at[j, 0],
            ffn_recv.at[j, 0],
            here.x_peer,
        )

    def ffn_from_x(j):
        source, full = experts[j]
        return remote(
            source.at[here.expert(1)],
            full.at[here.z, 1 - here.x, here.core],
            ffn_send.at[j, 0],
            ffn_recv.at[j, 0],
            here.x_peer,
        )

    def ffn_mine(j):
        source, full = experts[j]
        return pltpu.make_async_copy(source.at[here.expert(0)], full.at[here.z, here.x, here.core], ffn_local.at[j])

    def ffn_copy(j, slot, z, x, core, peer):
        full = experts[j][1]
        part = full.at[z, :, core] if x is None else full.at[z, x, core]
        return remote(part, part, ffn_send.at[j, slot], ffn_recv.at[j, slot], peer)

    def ffn_to_z(j, k):
        return ffn_copy(j, 1 + k, here.z, None, here.core, here.z_peer(1 if k == 0 else planes - 1))

    def ffn_from_z(j, k):
        return ffn_copy(j, 1 + k, z_at(planes - 1 if k == 0 else 1), None, here.core, here.x_peer)

    def ffn_pass_z(j, k):
        z = z_at(planes - 1 if k == 0 else 1)
        return ffn_copy(j, 3 + k, z, k, here.core, here.z_peer(1 if k == 0 else planes - 1))

    def ffn_passed_z(j, k):
        return ffn_copy(j, 3 + k, z_at(2), k, here.core, here.x_peer)

    def ffn_to_core(j, step_z):
        return ffn_copy(j, 5 + step_z, z_at(step_z), None, here.core, here.core_peer)

    def ffn_from_core(j, step_z):
        return ffn_copy(j, 5 + step_z, z_at(step_z), None, 1 - here.core, here.core_peer)

    def row_copy(kind, member, number):
        source, target = ((grows_ref, grads_in_ref), (rows_ref, rows_in_ref))[kind]
        src, dst = source.at[member, number], target.at[number, member]
        if number == 0:
            return pltpu.make_async_copy(src, dst, row_local.at[kind, member])
        return remote(
            src,
            dst,
            row_send.at[kind, member, number],
            row_recv.at[kind, member, number],
            here.plane_peers[number],
        )

    def outs(t):
        full, target = ((attn_ref, attn_out_ref), (attn_o_ref, attn_o_out_ref))[t]
        return pltpu.make_async_copy(full, target, out_sem.at[t])

    @pl.when(step == 0)
    def _():
        own_copies = [
            pltpu.make_async_copy(source, full.at[rows_of(mine), :], local_sem.at[t])
            for t, (source, full) in enumerate(shards)
        ]
        for copy in own_copies:
            copy.start()
        for j in range(3):
            ffn_mine(j).start()
        here.barrier(
            [here.core_peer, here.x_peer, here.y_peer, here.xy_peer, here.z_peer(1), here.z_peer(planes - 1)]
        )
        for copy in own_copies:
            copy.wait()
        for t in range(2):
            to_z(t, 0).start()
            to_z(t, 1).start()
            to_x(t, 0).start()
            to_core(t, 0, 0).start()
        for j in range(3):
            ffn_to_x(j).start()

        ids = iota((kinds, length), 0)
        before = jnp.where(iota((length, length), 0) < iota((length, length), 1), 1.0, 0.0).astype(BF16)
        for member in range(batches):
            first = routes_ref[member, 0:1, :] == ids
            second = routes_ref[member, 1:2, :] == ids
            hits = jnp.where(first | second, 1.0, 0.0)
            pos_ref[member] = jnp.where(hits > 0.0, nn(hits.astype(BF16), before), -1.0)
            for number in range(4):
                line = pos_ref[member, pl.ds(here.expert(number), 1), :]
                grows_ref[member, number] = nn(slot_mask(line, capacity), grad_ref[member]).astype(BF16)
            row_copy(0, member, 0).start()

        for t in range(2):
            for k, step_z in enumerate((planes - 1, 1)):
                from_z(t, k).wait_recv()
                pass_z(t, k).start()
                to_x(t, step_z).start()
                to_core(t, step_z, 0).start()
        for t in range(2):
            from_x(t, 0).wait_recv()
            to_y(t, 0).start()
        for j in range(3):
            ffn_mine(j).wait()
            ffn_from_x(j).wait_recv()
            ffn_to_z(j, 0).start()
            ffn_to_z(j, 1).start()
            ffn_to_core(j, 0).start()
        for t in range(2):
            passed_z(t, 0).wait_recv()
            passed_z(t, 1).wait_recv()
            to_x(t, 2).start()
            to_core(t, 2, 0).start()
        for member in range(batches):
            row_copy(0, member, 2).start()
        for t in range(2):
            for step_z in (planes - 1, 1, 2):
                from_x(t, step_z).wait_recv()
                to_y(t, step_z).start()
        for t in range(2):
            for step_z in (0, planes - 1, 1, 2):
                from_y(t, step_z).wait_recv()
                to_core(t, step_z, 1).start()
        for t in range(2):
            for step_z in range(planes):
                for x in range(2):
                    from_core(t, step_z, x).wait_recv()
        for t in range(2):
            outs(t).start()
        for member in range(batches):
            row_copy(0, member, 1).start()
            row_copy(0, member, 3).start()
        small_ref[...] = jnp.transpose(attn_ref[:, 3 * width : 3 * width + LANES].astype(F32))[0 : kinds + 8, :]

    def between():
        @pl.when(step == 0)
        def _():
            for j in range(3):
                for k, step_z in enumerate((planes - 1, 1)):
                    ffn_from_z(j, k).wait_recv()
                    ffn_pass_z(j, k).start()
                    ffn_to_core(j, step_z).start()

    sequence_forward(
        x_ref,
        seg_row_ref,
        seg_col_ref,
        routes_ref.at[pl.ds(step, 1)],
        prev_ref,
        map_ref,
        small_ref,
        attn_ref.at[:, 0:width],
        attn_ref.at[:, width : 2 * width],
        attn_ref.at[:, 2 * width : 3 * width],
        attn_o_ref,
        cos_ref,
        sin_ref,
        pos_ref.at[pl.ds(step, 1)],
        q_ref,
        k_ref,
        v_ref,
        o_ref,
        h_ref,
        lse_ref,
        aux_ref,
        [rows_ref.at[pl.ds(step, 1), number] for number in range(4)],
        bias_ref,
        proj_ref,
        here.expert,
        between,
    )
    for member in range(batches):

        @pl.when(step == member)
        def _():
            for number in range(4):
                row_copy(1, member, number).start()

    @pl.when(step == 0)
    def _():
        for j in range(3):
            for k in range(2):
                ffn_passed_z(j, k).wait_recv()
            ffn_to_core(j, 2).start()

    @pl.when(step == last)
    def _():
        for t in range(2):
            outs(t).wait()
            for k in range(2):
                to_z(t, k).wait_send()
                pass_z(t, k).wait_send()
            for step_z in range(planes):
                to_x(t, step_z).wait_send()
                to_y(t, step_z).wait_send()
                for x in range(2):
                    to_core(t, step_z, x).wait_send()
        for j in range(3):
            ffn_to_x(j).wait_send()
            for k in range(2):
                ffn_to_z(j, k).wait_send()
                ffn_pass_z(j, k).wait_send()
            for step_z in range(planes):
                ffn_to_core(j, step_z).wait_send()
                ffn_from_core(j, step_z).wait_recv()
        for kind in range(2):
            for member in range(batches):
                for number in range(4):
                    copy = row_copy(kind, member, number)
                    copy.wait()


def expert_kernel(
    a_ref,
    g_ref,
    gate_ref,
    up_ref,
    down_ref,
    v0,
    v1,
    v2,
    v3,
    d0,
    d1,
    d2,
    d3,
    grad_gate_ref,
    grad_up_ref,
    grad_down_ref,
    rows_ref,
    grads_ref,
    gates_ref,
    rows_t_ref,
    grads_t_ref,
    places_ref,
    acc_value_ref,
    acc_input_ref,
    acc_gate_ref,
    acc_up_ref,
    acc_down_ref,
    sems,
):
    step = pl.program_id(0)
    last = pl.num_programs(0) - 1
    batches, capacity, width = g_ref.shape[1:]
    blocks = 4 * batches

    @pl.when(step == 0)
    def _():
        copies = []
        for number in range(4):
            rows, grads = a_ref.at[number], g_ref.at[number]
            for member in range(batches):
                block = number * batches + member
                span = pl.ds(block * capacity, capacity)
                copies.append(
                    pltpu.make_async_copy(
                        rows.at[member, pl.ds(capacity, 16), pl.ds(0, capacity)],
                        gates_ref.at[block],
                        sems.at[3 * block],
                    )
                )
                copies.append(
                    pltpu.make_async_copy(
                        rows.at[member, pl.ds(0, capacity), :], rows_ref.at[span, :], sems.at[3 * block + 1]
                    )
                )
                copies.append(
                    pltpu.make_async_copy(grads.at[member], grads_ref.at[span, :], sems.at[3 * block + 2])
                )
        for copy in copies:
            copy.start()
        for copy in copies:
            copy.wait()
        same = iota((capacity, capacity), 0) == iota((capacity, capacity), 1)
        spare = jnp.zeros((capacity, width), BF16)
        rows_ref[blocks * capacity :, :] = spare
        grads_ref[blocks * capacity :, :] = spare

        def pack(block, place):
            span = pl.ds(pl.multiple_of(block * capacity, capacity), capacity)
            target = pl.ds(pl.multiple_of(place, 16), capacity)
            parts = gates_ref[block].astype(F32)
            count = jnp.max(parts[3:4, :]).astype(jnp.int32)
            line = jnp.sum(parts[0:3, :], axis=0, keepdims=True)
            column = jnp.sum(jnp.where(same, line, 0.0), axis=1, keepdims=True)
            rows = rows_ref[span, :]
            grads = (grads_ref[span, :].astype(F32) * column).astype(BF16)
            rows_ref[target, :] = rows
            grads_ref[target, :] = grads
            places_ref[block] = place
            return place + (count + 15) // 16 * 16

        total = lax.fori_loop(0, blocks, pack, 0)
        target = pl.ds(pl.multiple_of(total, 16), capacity)
        rows_ref[target, :] = spare
        grads_ref[target, :] = spare
        places_ref[blocks] = (total + capacity - 1) // capacity

        def turn(block, carry):
            span = pl.ds(pl.multiple_of(block * capacity, capacity), capacity)
            grads_t_ref[:, span] = jnp.transpose(grads_ref[span, :])
            rows_t_ref[:, span] = jnp.transpose(rows_ref[span, :])
            return carry

        lax.fori_loop(0, places_ref[blocks], turn, 0)

    acc_gate_ref[...] = jnp.zeros_like(acc_gate_ref)
    acc_up_ref[...] = jnp.zeros_like(acc_up_ref)
    acc_down_ref[...] = jnp.zeros_like(acc_down_ref)

    def work(block, carry):
        span = pl.ds(pl.multiple_of(block * capacity, capacity), capacity)
        rows = rows_ref[span, :]
        grads = grads_ref[span, :]
        gate = nn(rows, gate_ref[...])
        up = nn(rows, up_ref[...])
        back = nt(grads, down_ref[...])
        sig = 1.0 / (1.0 + jnp.exp(-gate))
        silu = gate * sig
        act = (silu * up).astype(BF16)
        grad_gate = (back * up * (sig * (1.0 + gate * (1.0 - sig)))).astype(BF16)
        grad_up = (back * silu).astype(BF16)
        value = nn(act, down_ref[...])
        grad_rows = nt(grad_gate, gate_ref[...]) + nt(grad_up, up_ref[...])
        rows_t = rows_t_ref[:, span]
        acc_gate_ref[...] += nn(rows_t, grad_gate)
        acc_up_ref[...] += nn(rows_t, grad_up)
        acc_down_ref[...] += nn(grads_t_ref[:, span], act)

        @pl.when(step == 0)
        def _():
            acc_value_ref[span, :] = value
            acc_input_ref[span, :] = grad_rows

        @pl.when((step > 0) & (step < last))
        def _():
            acc_value_ref[span, :] += value
            acc_input_ref[span, :] += grad_rows

        @pl.when(step == last)
        def _():
            rows_ref[span, :] = (acc_value_ref[span, :] + value).astype(BF16)
            grads_ref[span, :] = (acc_input_ref[span, :] + grad_rows).astype(BF16)

        return carry

    lax.fori_loop(0, places_ref[blocks], work, 0)
    grad_gate_ref[...] = acc_gate_ref[...].astype(BF16)
    grad_up_ref[...] = acc_up_ref[...].astype(BF16)
    grad_down_ref[...] = jnp.transpose(acc_down_ref[...].astype(BF16))

    @pl.when(step == last)
    def _():
        copies = []
        for number, (values, grads) in enumerate(zip((v0, v1, v2, v3), (d0, d1, d2, d3))):
            for member in range(batches):
                block = number * batches + member
                span = pl.ds(pl.multiple_of(places_ref[block], 16), capacity)
                copies.append(pltpu.make_async_copy(rows_ref.at[span, :], values.at[member], sems.at[3 * block]))
                copies.append(pltpu.make_async_copy(grads_ref.at[span, :], grads.at[member], sems.at[3 * block + 1]))
        for copy in copies:
            copy.start()
        for copy in copies:
            copy.wait()


def combine_kernel(
    own_ref,
    v0,
    v1,
    v2,
    v3,
    d0,
    d1,
    d2,
    d3,
    pos_ref,
    aux_ref,
    routes_ref,
    prev_ref,
    h_ref,
    g_ref,
    o_ref,
    small_ref,
    wo_ref,
    out_ref,
    dh_ref,
    dob_ref,
    grad_wo_ref,
    sgrad_ref,
    grad_map_ref,
    acc_ref,
    cols_ref,
):
    own = own_ref[0]
    step = pl.program_id(0)
    length, width = h_ref.shape[1:]
    kinds = pos_ref.shape[1]
    ffn = kinds - 4
    capacity = v0.shape[1]
    hidden = h_ref[0]
    inverse = rms_scale(hidden)
    gain = small_ref[kinds + 7 : kinds + 8, :]
    n2 = hidden * inverse * gain
    n2_high, n2_low = split2(n2)
    grad_low = g_ref[0]
    grad = grad_low.astype(F32)
    small = small_ref[...].astype(BF16)
    cols_ref[0:kinds, :] = pos_ref[0]
    cols_ref[kinds : kinds + 16, :] = aux_ref[0]
    cols_ref[kinds + 16 :, :] = jnp.zeros((LANES - kinds - 16, length), F32)
    cols = jnp.transpose(cols_ref[...])
    lane = iota((1, LANES), 1)

    def column(source, index):
        return jnp.sum(jnp.where(lane == index, source, 0.0), axis=1, keepdims=True)

    gate_one = column(cols, 2 * kinds)
    gate_two = column(cols, 2 * kinds + 1)
    hot_one = jnp.where(routes_ref[0, :, 0:1] == lane, 1.0, 0.0)
    hot_two = jnp.where(routes_ref[0, :, 1:2] == lane, 1.0, 0.0)

    result = hidden
    grad_n2 = jnp.zeros((length, width), F32)
    dws = jnp.zeros((length, LANES), F32)
    slot_lane = iota((1, capacity), 1).astype(F32)
    for number, (values, grads) in enumerate(zip((v0, v1, v2, v3), (d0, d1, d2, d3))):
        expert = own ^ number
        mask = jnp.where(column(cols, expert) == slot_lane, 1.0, 0.0).astype(BF16)
        taken = nn(mask, values[0])
        result = result + column(cols, kinds + expert) * taken
        dws = jnp.where(lane == expert, jnp.sum(grad * taken, axis=1, keepdims=True), dws)
        grad_n2 = grad_n2 + nn(mask, grads[0])

    mixes = nt(n2_high, small) + nt(n2_low, small)
    inner = nt(grad_low, small)
    with_n2 = jnp.sum(grad * n2, axis=1, keepdims=True)
    weight_copy = column(cols, kinds + ffn + 1)
    dws = jnp.where(lane == ffn + 1, with_n2, dws)
    share = weight_copy
    coefs = jnp.zeros((length, LANES), F32)
    for constant in range(2):
        weight = column(cols, kinds + ffn + 2 + constant)
        za = mixes[:, kinds + 2 * constant : kinds + 2 * constant + 1]
        zb = mixes[:, kinds + 2 * constant + 1 : kinds + 2 * constant + 2]
        top = jnp.maximum(za, zb)
        ea, eb = jnp.exp(za - top), jnp.exp(zb - top)
        alpha_a = ea / (ea + eb)
        alpha_b = eb / (ea + eb)
        with_vec = inner[:, kinds + 4 + constant : kinds + 5 + constant]
        vec = small_ref[kinds + 4 + constant : kinds + 5 + constant, :]
        result = result + (weight * alpha_b) * vec
        share = share + weight * alpha_a
        dws = jnp.where(lane == ffn + 2 + constant, alpha_a * with_n2 + alpha_b * with_vec, dws)
        da = weight * with_n2
        db = weight * with_vec
        mean = alpha_a * da + alpha_b * db
        coefs = jnp.where(lane == kinds + 2 * constant, alpha_a * (da - mean), coefs)
        coefs = jnp.where(lane == kinds + 2 * constant + 1, alpha_b * (db - mean), coefs)
        coefs = jnp.where(lane == kinds + 4 + constant, weight * alpha_b, coefs)
    out_ref[0] = result + share * n2

    dg_one = jnp.sum(dws * hot_one, axis=1, keepdims=True)
    dg_two = jnp.sum(dws * hot_two, axis=1, keepdims=True)
    mean = gate_one * dg_one + gate_two * dg_two
    dlogits = gate_one * (dg_one - mean) * hot_one + gate_two * (dg_two - mean) * hot_two
    coefs = jnp.where(lane < kinds, dlogits, coefs)
    back = jnp.where(lane < kinds + 4, coefs, 0.0)[:, 0:16]
    back_high, back_low = split2(back)
    grad_n2 = grad_n2 + nn(back_high, small) + nn(back_low, small) + share * grad

    coefs_t = jnp.transpose(coefs)[0:16, :]
    high, low = split2(coefs_t)
    by_n2 = nn(high, n2_high) + nn(low, n2_high)
    by_low = nn(high, n2_low)
    by_grad = nn(high, grad_low) + nn(low, grad_low)
    row = iota((16, 1), 0)
    parts = jnp.where(row < kinds, by_n2, jnp.where(row < kinds + 4, by_n2 + by_low, by_grad))
    gain_part = jnp.sum(grad_n2 * hidden * inverse, axis=0, keepdims=True)
    parts = jnp.where(row == kinds + 7, gain_part, jnp.where(row == kinds + 6, 0.0, parts))
    dlog_t = coefs_t[0:kinds, :]
    map_lane = iota((kinds, LANES), 1)
    map_part = jnp.zeros((kinds, LANES), F32)
    for j in range(kinds):
        map_part = jnp.where(
            map_lane == j, jnp.sum(dlog_t * prev_ref[0, j : j + 1, :], axis=1, keepdims=True), map_part
        )

    scaled = gain * grad_n2
    inner_mean = jnp.mean(scaled * hidden, axis=-1, keepdims=True)
    dh = grad + inverse * scaled - hidden * (inverse * inverse * inverse) * inner_mean
    dh_ref[0] = dh
    db = dh.astype(BF16)
    dob_ref[0] = nt(db, wo_ref[...]).astype(BF16)
    wo_part = nn(jnp.transpose(o_ref[0]), db)

    @pl.when(step == 0)
    def _():
        acc_ref[...] = wo_part
        sgrad_ref[...] = parts
        grad_map_ref[...] = map_part

    @pl.when(step > 0)
    def _():
        acc_ref[...] += wo_part
        sgrad_ref[...] += parts
        grad_map_ref[...] += map_part

    @pl.when(step == pl.num_programs(0) - 1)
    def _():
        grad_wo_ref[...] = acc_ref[...].astype(BF16)


def backward_kernel(
    depth,
    x_ref,
    seg_row_ref,
    seg_col_ref,
    q_ref,
    k_ref,
    v_ref,
    dob_ref,
    lse_ref,
    dh_ref,
    small_ref,
    wq_ref,
    wk_ref,
    wv_ref,
    cos_ref,
    sin_ref,
    grad_wo_ref,
    sgrad_ref,
    grad_map_ref,
    gin_ref,
    grad_w_ref,
    gain_ref,
    bias_ref,
    lse_t_ref,
    dqkv_ref,
    acc_ref,
):
    step = pl.program_id(0)
    length, width = x_ref.shape[1:]
    kinds = small_ref.shape[0] - 8
    pairs = width // LANES
    lane = iota((1, LANES), 1)
    low_half = (lane % HEAD_DIM) < (HEAD_DIM // 2)
    first_head = lane < HEAD_DIM
    mask_a = jnp.where(first_head, 1.0, 0.0).astype(BF16)
    mask_b = jnp.where(first_head, 0.0, 1.0).astype(BF16)
    allowed = (seg_col_ref[0] == seg_row_ref[0]) & (
        iota((length, length), 0) // BLOCK <= iota((length, length), 1) // BLOCK
    )
    bias_ref[...] = jnp.where(allowed, 0.0, NEG)
    lse_t_ref[...] = jnp.transpose(lse_ref[0])

    def pair(h, carry):
        cols = pl.ds(pl.multiple_of(h * LANES, LANES), LANES)
        keys_t = jnp.transpose(k_ref[0, :, cols])
        grad_keys = None
        grad_values = None
        grad_queries = []
        for begin in range(0, length, BLOCK):
            end = begin + BLOCK
            queries = q_ref[0, begin:end, cols]
            outs = dob_ref[0, begin:end, cols]
            keys = k_ref[0, 0:end, cols]
            values = v_ref[0, 0:end, cols]
            queries = jnp.concatenate([queries * mask_a, queries * mask_b], axis=0)
            outs = jnp.concatenate([outs * mask_a, outs * mask_b], axis=0)
            bias = bias_ref[0:end, begin:end]
            bias = jnp.concatenate([bias, bias], axis=1)
            line = jnp.concatenate(
                [lse_t_ref[pl.ds(2 * h, 1), begin:end], lse_t_ref[pl.ds(2 * h + 1, 1), begin:end]], axis=1
            )
            chances = jnp.exp(nt(keys, queries) + bias - line)
            grad_chances = nt(values, outs)
            delta = jnp.sum(chances * grad_chances, axis=0, keepdims=True)
            grad_scores = (chances * (grad_chances - delta)).astype(BF16)
            dv = nn(chances.astype(BF16), outs)
            dk = nn(grad_scores, queries)
            dq = jnp.transpose(nn(keys_t[:, 0:end], grad_scores))
            grad_queries.append(jnp.where(first_head, dq[0:BLOCK], dq[BLOCK:]))
            if grad_keys is None:
                grad_keys, grad_values = dk, dv
            else:
                grad_keys = jnp.concatenate([grad_keys + dk[0:begin], dk[begin:]], axis=0)
                grad_values = jnp.concatenate([grad_values + dv[0:begin], dv[begin:]], axis=0)
        dq = jnp.concatenate(grad_queries, axis=0) * 0.125
        dq = dq * cos_ref[...] - swap_halves(dq, low_half) * sin_ref[...]
        dk = grad_keys * cos_ref[...] - swap_halves(grad_keys, low_half) * sin_ref[...]
        dqkv_ref[:, cols] = dq.astype(BF16)
        dqkv_ref[:, pl.ds(pl.multiple_of(width + h * LANES, LANES), LANES)] = dk.astype(BF16)
        dqkv_ref[:, pl.ds(pl.multiple_of(2 * width + h * LANES, LANES), LANES)] = grad_values.astype(BF16)
        return carry

    lax.fori_loop(0, pairs, pair, 0)

    tokens = x_ref[0].astype(F32)
    inverse = rms_scale(tokens)
    gain = small_ref[kinds + 6 : kinds + 7, :]
    a1_t = jnp.transpose((tokens * inverse * gain).astype(BF16))
    dn1 = (
        nt(dqkv_ref[:, 0:width], wq_ref[...])
        + nt(dqkv_ref[:, width : 2 * width], wk_ref[...])
        + nt(dqkv_ref[:, 2 * width :], wv_ref[...])
    )
    scaled = gain * dn1
    inner_mean = jnp.mean(scaled * tokens, axis=-1, keepdims=True)
    gin_ref[0] = dh_ref[0] + inverse * scaled - tokens * (inverse * inverse * inverse) * inner_mean
    gain_part = jnp.broadcast_to(jnp.sum(dn1 * tokens * inverse, axis=0, keepdims=True), gain_ref.shape)

    @pl.when(step == 0)
    def _():
        acc_ref[...] = jnp.zeros_like(acc_ref)
        gain_ref[...] = gain_part

    @pl.when(step > 0)
    def _():
        gain_ref[...] += gain_part

    for part in range(3):
        span = slice(part * width, (part + 1) * width)
        acc_ref[:, span] += nn(a1_t, dqkv_ref[:, span])

    @pl.when(step == pl.num_programs(0) - 1)
    def _():
        grad_w_ref[:, 0 : 3 * width] = acc_ref[...].astype(BF16)
        grad_w_ref[:, 3 * width : 4 * width] = grad_wo_ref[...]
        row = iota((16, 1), 0)
        table = jnp.where(row == kinds + 6, gain_ref[0:1, :], sgrad_ref[...])
        chosen = jnp.where(iota((LANES, width), 1) % depth == iota((LANES, width), 0), 1.0, 0.0).astype(BF16)
        maps = nn(grad_map_ref[...].astype(BF16), chosen)
        table = jnp.concatenate([table, maps, jnp.zeros((LANES - 16 - kinds, width), F32)], axis=0)
        grad_w_ref[:, 4 * width : 4 * width + LANES] = jnp.transpose(table).astype(BF16)
        grad_w_ref[:, 4 * width + LANES :] = jnp.zeros((width, LANES), BF16)


def reduce_kernel(
    group,
    full_ref,
    out_ref,
    acc_ref,
    core_ref,
    y_first_ref,
    x_second_ref,
    x_first_ref,
    y_second_ref,
    z_ref,
    done_ref,
    other_ref,
    local_sem,
    send,
    recv,
    z_send,
    z_recv,
):
    here = Place(group)
    planes = here.planes
    near = planes // 2
    depth, columns = acc_ref.shape[2:]
    half = columns // 2
    x, y = here.x, here.y
    mine = pl.ds(pl.multiple_of(y * half, LANES), half)
    theirs = pl.ds(pl.multiple_of((1 - y) * half, LANES), half)
    here.barrier(
        [here.core_peer, here.x_peer, here.y_peer] + [here.z_peer(k) for k in range(1, planes)]
    )
    own = pltpu.make_async_copy(full_ref.at[:, :, here.core], acc_ref, local_sem)
    own.start()
    swap = remote(full_ref.at[:, :, 1 - here.core], core_ref, send.at[0], recv.at[0], here.core_peer)
    swap.start()
    own.wait()
    swap.wait_recv()

    def add(target, source):
        target[...] = (target[...].astype(F32) + source[...].astype(F32)).astype(BF16)

    def add_core(z, carry):
        for column in range(2):
            add(acc_ref.at[z, column], core_ref.at[z, column])
        return carry

    lax.fori_loop(0, planes, add_core, 0)
    y_first = remote(acc_ref.at[0:near, :, :, theirs], y_first_ref, send.at[1], recv.at[1], here.y_peer)
    x_first = remote(acc_ref.at[near:planes, 1 - x], x_first_ref, send.at[2], recv.at[2], here.x_peer)
    y_first.start()
    x_first.start()
    y_first.wait_recv()
    for z in range(near):
        for column in range(2):
            add(acc_ref.at[z, column, :, mine], y_first_ref.at[z, column])
    x_second = remote(acc_ref.at[0:near, 1 - x, :, mine], x_second_ref, send.at[3], recv.at[3], here.x_peer)
    x_second.start()
    x_first.wait_recv()
    for z in range(near, planes):
        add(acc_ref.at[z, x], x_first_ref.at[z - near])
    y_second = remote(acc_ref.at[near:planes, x, :, theirs], y_second_ref, send.at[4], recv.at[4], here.y_peer)
    y_second.start()
    x_second.wait_recv()
    for z in range(near):
        add(acc_ref.at[z, x, :, mine], x_second_ref.at[z])
    y_second.wait_recv()
    for z in range(near, planes):
        add(acc_ref.at[z, x, :, mine], y_second_ref.at[z - near])
    along = []
    for k in range(1, planes):
        to = (here.z + k) % planes
        along.append(
            remote(acc_ref.at[to, x, :, mine], z_ref.at[k - 1], z_send.at[k - 1], z_recv.at[k - 1], here.z_peer(k))
        )
        along[-1].start()
    total = acc_ref[here.z, x, :, mine].astype(F32)
    for k in range(1, planes):
        along[k - 1].wait_recv()
        total = total + z_ref[k - 1].astype(F32)
    done_ref[...] = total.astype(BF16)
    back = remote(done_ref, other_ref, send.at[5], recv.at[5], here.y_peer)
    back.start()
    out_ref[:, mine] = done_ref[...].astype(F32)
    back.wait_recv()
    out_ref[:, theirs] = other_ref[...].astype(F32)
    for copy in [swap, y_first, x_first, x_second, y_second, back] + along:
        copy.wait_send()


def params(limit_mib):
    return pltpu.CompilerParams(vmem_limit_bytes=limit_mib * 1024 * 1024, dimension_semantics=("arbitrary",))


def rotary(length):
    halfway = HEAD_DIM // 2
    frequency = 10000.0 ** (-jnp.arange(halfway).astype(F32) / halfway)
    angles = jnp.arange(length).astype(F32)[:, None] * frequency[None, :]
    cosine, sine = jnp.cos(angles), jnp.sin(angles)
    return (
        jnp.concatenate([cosine] * 4, axis=1),
        jnp.concatenate([-sine, sine, -sine, sine], axis=1),
    )


def local(
    reps,
    group,
    block_input,
    prev_logits,
    routes,
    segments,
    grad_out,
    gain_attn,
    w_query,
    w_key,
    w_value,
    w_output,
    gain_mix,
    router,
    route_map,
    const_proj,
    const_vec,
    w_gate,
    w_up,
    w_down,
):
    batches, length = segments.shape
    width = block_input.shape[1]
    kinds = router.shape[1]
    ffn = w_gate.shape[1]
    hidden = w_gate.shape[2]
    rows_d = w_gate.shape[0]
    rows_f = w_down.shape[0]
    capacity = length // 2
    planes = group // 4
    assert reps == 2 and ffn == 4 and group % 4 == 0
    g = lax.axis_index("grp")
    y = lax.axis_index("rep")
    core = g % 2
    x = (g // 2) % 2
    z = g // 4
    own = (2 * y + x).astype(jnp.int32)
    own_arr = own.reshape(1)

    x_flip = [(i, i ^ 2) for i in range(group)]
    core_flip = [(i, i ^ 1) for i in range(group)]
    y_flip = [(0, 1), (1, 0)]
    xy_flip = [(r * group + i, (1 - r) * group + (i ^ 2)) for r in range(2) for i in range(group)]

    def z_shift(k):
        return [(i, (i + 4 * k) % group) for i in range(group)]

    def to_plane(parts):
        return [
            parts[0],
            lax.ppermute(parts[1], "grp", x_flip),
            lax.ppermute(parts[2], "rep", y_flip),
            lax.ppermute(parts[3], ("rep", "grp"), xy_flip),
        ]

    tokens = block_input.reshape(batches, length, width)
    grads = grad_out.reshape(batches, length, width)
    route_cols = routes.reshape(batches, length, 2)
    route_rows = route_cols.transpose(0, 2, 1)
    prev_rows = prev_logits.reshape(batches, length, kinds).transpose(0, 2, 1)
    seg_row = segments[:, None, :]
    seg_col = segments[:, :, None]
    cos, sin = rotary(length)

    def spec_w(j):
        return pl.BlockSpec((width, width), lambda b, *_: (0, j), pipeline_mode=pl.Buffered(1))

    row_shape = jax.ShapeDtypeStruct((batches, capacity, width), BF16)
    seq_bf16 = jax.ShapeDtypeStruct((batches, length, width), BF16)
    seq_f32 = jax.ShapeDtypeStruct((batches, length, width), F32)
    small_shard = jnp.concatenate(
        [router, const_proj, const_vec, gain_attn[:, None], gain_mix[:, None]], axis=1
    ).astype(BF16)
    small_shard = jnp.pad(small_shard, ((0, 0), (0, 2 * LANES - small_shard.shape[1])))
    shard = jnp.concatenate([w.astype(BF16) for w in (w_query, w_key, w_value)] + [small_shard], axis=1)
    shard_o = w_output.astype(BF16)
    if planes == 4 and rows_d % 16 == 0 and rows_f % 16 == 0:
        any_space = pl.BlockSpec(memory_space=pl.ANY)
        out_struct = jax.ShapeDtypeStruct
        (
            q, k, v, o, h1, lse, aux, pos, small, attn, attn_o, a_rows, grad_rows, gate_full, up_full, down_full,
        ) = pl.pallas_call(
            functools.partial(fused_forward_kernel, group),
            grid=(batches,),
            in_specs=[
                per_seq((length, width)),
                per_seq((1, length)),
                per_seq((length, 1)),
                whole((batches, 2, length)),
                per_seq((kinds, length)),
                whole((kinds, kinds)),
                whole((batches, length, width)),
                whole((length, LANES)),
                whole((length, LANES)),
            ]
            + [any_space] * 5,
            out_specs=[per_seq((length, width))] * 5
            + [
                per_seq((length, LANES)),
                per_seq((16, length)),
                whole((batches, kinds, length)),
                whole((kinds + 8, width)),
            ]
            + [any_space] * 7,
            scratch_shapes=[
                pltpu.VMEM((width, 3 * width + 2 * LANES), BF16),
                pltpu.VMEM((width, width), BF16),
                pltpu.VMEM((length, length), F32),
                pltpu.VMEM((length, width), F32),
                pltpu.VMEM((batches, 4, capacity + 16, width), BF16),
                pltpu.VMEM((batches, 4, capacity, width), BF16),
                pltpu.SemaphoreType.DMA((2,)),
                pltpu.SemaphoreType.DMA((2, 4 + 4 * planes)),
                pltpu.SemaphoreType.DMA((2, 4 + 4 * planes)),
                pltpu.SemaphoreType.DMA((3,)),
                pltpu.SemaphoreType.DMA((3, 5 + planes)),
                pltpu.SemaphoreType.DMA((3, 5 + planes)),
                pltpu.SemaphoreType.DMA((2,)),
                pltpu.SemaphoreType.DMA((2, batches)),
                pltpu.SemaphoreType.DMA((2, batches, 4)),
                pltpu.SemaphoreType.DMA((2, batches, 4)),
            ],
            out_shape=[seq_bf16] * 4
            + [
                seq_f32,
                out_struct((batches, length, LANES), F32),
                out_struct((batches, 16, length), F32),
                out_struct((batches, kinds, length), F32),
                out_struct((kinds + 8, width), F32),
                out_struct((width, 3 * width + 2 * LANES), BF16),
                out_struct((width, width), BF16),
                out_struct((4, batches, capacity + 16, width), BF16),
                out_struct((4, batches, capacity, width), BF16),
                out_struct((planes, 2, 2, rows_d, hidden), BF16),
                out_struct((planes, 2, 2, rows_d, hidden), BF16),
                out_struct((planes, 2, 2, rows_f, width), BF16),
            ],
            compiler_params=pltpu.CompilerParams(
                vmem_limit_bytes=58 * 1024 * 1024,
                dimension_semantics=("arbitrary",),
                collective_id=1,
                has_side_effects=True,
            ),
            cost_estimate=pl.CostEstimate(flops=40 * 10**9, bytes_accessed=60 * 10**6, transcendentals=10**7),
            name="fused_forward",
        )(
            tokens, seg_row, seg_col, route_rows, prev_rows, route_map.T, grads, cos, sin,
            shard, shard_o,
            w_gate.astype(BF16).transpose(1, 0, 2),
            w_up.astype(BF16).transpose(1, 0, 2),
            w_down.astype(BF16).transpose(1, 0, 2),
        )
        gate_full = gate_full.reshape(width, hidden)
        up_full = up_full.reshape(width, hidden)
        down_full = down_full.reshape(hidden, width)
    else:
        attn = lax.all_gather(shard, "grp", axis=0, tiled=True)
        attn_o = lax.all_gather(shard_o, "grp", axis=0, tiled=True)
        small = attn[:, 3 * width : 3 * width + kinds + 8].astype(F32).T

        def pick(array, expert):
            return lax.dynamic_index_in_dim(array, expert, axis=1, keepdims=False)

        def gather_expert(mine, other):
            crossed = lax.ppermute(other, "grp", x_flip)
            both = jnp.where(x == 0, jnp.stack([mine, crossed]), jnp.stack([crossed, mine]))
            pieces = [both] + [lax.ppermute(both, "grp", z_shift(k)) for k in range(1, planes)]
            stacked = jnp.stack(pieces)
            half = jnp.take(stacked, (z - jnp.arange(planes)) % planes, axis=0)
            swapped = lax.ppermute(half, "grp", core_flip)
            return jnp.where(core == 0, jnp.stack([half, swapped], axis=2), jnp.stack([swapped, half], axis=2))

        gate_up = gather_expert(
            jnp.stack([pick(w_gate, own), pick(w_up, own)]).astype(BF16),
            jnp.stack([pick(w_gate, own ^ 1), pick(w_up, own ^ 1)]).astype(BF16),
        )
        down = gather_expert(pick(w_down, own).astype(BF16), pick(w_down, own ^ 1).astype(BF16))
        gate_full = gate_up[:, :, :, 0].reshape(width, hidden)
        up_full = gate_up[:, :, :, 1].reshape(width, hidden)
        down_full = down.reshape(hidden, width)

        *grad_rows, pos = pl.pallas_call(
            grad_rows_kernel,
            grid_spec=pltpu.PrefetchScalarGridSpec(
                num_scalar_prefetch=1,
                grid=(batches,),
                in_specs=[per_seq((2, length)), per_seq((length, width))],
                out_specs=[per_seq((capacity, width))] * 4 + [per_seq((kinds, length))],
            ),
            out_shape=[row_shape] * 4 + [jax.ShapeDtypeStruct((batches, kinds, length), F32)],
            compiler_params=params(32),
            cost_estimate=pl.CostEstimate(flops=4 * 10**9, bytes_accessed=8 * 10**6, transcendentals=0),
            name="grad_rows",
        )(own_arr, route_rows, grads)
        grad_rows = to_plane(grad_rows)

        q, k, v, o, h1, lse, aux, *a_rows = pl.pallas_call(
            forward_kernel,
            grid_spec=pltpu.PrefetchScalarGridSpec(
                num_scalar_prefetch=1,
                grid=(batches,),
                in_specs=[
                    per_seq((length, width)),
                    per_seq((1, length)),
                    per_seq((length, 1)),
                    per_seq((2, length)),
                    per_seq((kinds, length)),
                    whole((kinds, kinds)),
                    whole((kinds + 8, width)),
                    spec_w(0),
                    spec_w(1),
                    spec_w(2),
                    spec_w(0),
                    whole((length, LANES)),
                    whole((length, LANES)),
                    per_seq((kinds, length)),
                ],
                out_specs=[per_seq((length, width))] * 5
                + [per_seq((length, LANES)), per_seq((16, length))]
                + [per_seq((capacity + 16, width))] * 4,
                scratch_shapes=[pltpu.VMEM((length, length), F32), pltpu.VMEM((length, width), F32)],
            ),
            out_shape=[seq_bf16] * 4
            + [
                seq_f32,
                jax.ShapeDtypeStruct((batches, length, LANES), F32),
                jax.ShapeDtypeStruct((batches, 16, length), F32),
            ]
            + [jax.ShapeDtypeStruct((batches, capacity + 16, width), BF16)] * 4,
            compiler_params=params(56),
            cost_estimate=pl.CostEstimate(flops=20 * 10**9, bytes_accessed=20 * 10**6, transcendentals=10**7),
            name="forward",
        )(own_arr, tokens, seg_row, seg_col, route_rows, prev_rows, route_map.T, small, attn, attn, attn, attn_o, cos, sin, pos)
        a_rows = to_plane(a_rows)

        a_rows = jnp.stack(a_rows)
        grad_rows = jnp.stack(grad_rows)

    tile = hidden // 4
    total = 4 * batches * capacity
    any_spec = pl.BlockSpec(memory_space=pl.ANY)
    outs = pl.pallas_call(
        expert_kernel,
        grid=(hidden // tile,),
        in_specs=[any_spec] * 2
        + [
            pl.BlockSpec((width, tile), lambda f: (0, f)),
            pl.BlockSpec((width, tile), lambda f: (0, f)),
            pl.BlockSpec((tile, width), lambda f: (f, 0)),
        ],
        out_specs=[any_spec] * 8
        + [
            pl.BlockSpec((width, tile), lambda f: (0, f)),
            pl.BlockSpec((width, tile), lambda f: (0, f)),
            pl.BlockSpec((tile, width), lambda f: (f, 0)),
        ],
        scratch_shapes=[
            pltpu.VMEM((total + capacity, width), BF16),
            pltpu.VMEM((total + capacity, width), BF16),
            pltpu.VMEM((4 * batches, 16, capacity), BF16),
            pltpu.VMEM((width, total), BF16),
            pltpu.VMEM((width, total), BF16),
            pltpu.SMEM((4 * batches + 1,), jnp.int32),
            pltpu.VMEM((total, width), F32),
            pltpu.VMEM((total, width), F32),
            pltpu.VMEM((width, tile), F32),
            pltpu.VMEM((width, tile), F32),
            pltpu.VMEM((width, tile), F32),
            pltpu.SemaphoreType.DMA((12 * batches,)),
        ],
        out_shape=[row_shape] * 8
        + [
            jax.ShapeDtypeStruct((width, hidden), BF16),
            jax.ShapeDtypeStruct((width, hidden), BF16),
            jax.ShapeDtypeStruct((hidden, width), BF16),
        ],
        compiler_params=params(60),
        cost_estimate=pl.CostEstimate(flops=58 * 10**9, bytes_accessed=40 * 10**6, transcendentals=10**7),
        name="expert",
    )(a_rows, grad_rows, gate_full, up_full, down_full)
    value_rows = to_plane(outs[0:4])
    input_rows = to_plane(outs[4:8])
    grad_gate_full, grad_up_full, grad_down_full = outs[8:]

    def scatter_expert(full):
        keep = lax.dynamic_index_in_dim(full, core, axis=2, keepdims=False)
        send = lax.dynamic_index_in_dim(full, 1 - core, axis=2, keepdims=False)
        half = (keep.astype(F32) + lax.ppermute(send, "grp", core_flip).astype(F32)).astype(BF16)
        summed = lax.dynamic_index_in_dim(half, z, axis=0, keepdims=False).astype(F32)
        for k in range(1, planes):
            part = lax.dynamic_index_in_dim(half, (z + k) % planes, axis=0, keepdims=False)
            summed = summed + lax.ppermute(part, "grp", z_shift(k)).astype(F32)
        summed = summed.astype(BF16)
        mine = lax.dynamic_index_in_dim(summed, x, axis=0, keepdims=False)
        other = lax.dynamic_index_in_dim(summed, 1 - x, axis=0, keepdims=False)
        arrived = to_plane([mine, other, mine, other])

        def order(first):
            return lambda: tuple(arrived[first ^ e] for e in range(4))

        return lax.switch(own, [order(i) for i in range(4)])

    grad_gate_up = scatter_expert(
        jnp.stack(
            [
                grad_gate_full.reshape(planes, 2, 2, rows_d, hidden),
                grad_up_full.reshape(planes, 2, 2, rows_d, hidden),
            ],
            axis=3,
        )
    )
    grad_down = scatter_expert(grad_down_full.reshape(planes, 2, 2, rows_f, width))
    grad_gate = jnp.stack([part[0] for part in grad_gate_up], axis=1).astype(F32)
    grad_up = jnp.stack([part[1] for part in grad_gate_up], axis=1).astype(F32)
    grad_down = jnp.stack(grad_down, axis=1).astype(F32)

    result, dh1, dob, grad_wo, sgrad, grad_map = pl.pallas_call(
        combine_kernel,
        grid_spec=pltpu.PrefetchScalarGridSpec(
            num_scalar_prefetch=1,
            grid=(batches,),
            in_specs=[per_seq((capacity, width))] * 8
            + [
                per_seq((kinds, length)),
                per_seq((16, length)),
                per_seq((length, 2)),
                per_seq((kinds, length)),
                per_seq((length, width)),
                per_seq((length, width)),
                per_seq((length, width)),
                whole((kinds + 8, width)),
                spec_w(0),
            ],
            out_specs=[per_seq((length, width))] * 3
            + [whole((width, width)), whole((16, width)), whole((kinds, LANES))],
            scratch_shapes=[pltpu.VMEM((width, width), F32), pltpu.VMEM((LANES, length), F32)],
        ),
        out_shape=[
            seq_f32,
            seq_f32,
            seq_bf16,
            jax.ShapeDtypeStruct((width, width), BF16),
            jax.ShapeDtypeStruct((16, width), F32),
            jax.ShapeDtypeStruct((kinds, LANES), F32),
        ],
        compiler_params=params(56),
        cost_estimate=pl.CostEstimate(flops=12 * 10**9, bytes_accessed=20 * 10**6, transcendentals=10**5),
        name="combine",
    )(own_arr, *value_rows, *input_rows, pos, aux, route_cols, prev_rows, h1, grads, o, small, attn_o)

    gin, grad_attn, gain_one = pl.pallas_call(
        functools.partial(backward_kernel, rows_d),
        grid=(batches,),
        in_specs=[
            per_seq((length, width)),
            per_seq((1, length)),
            per_seq((length, 1)),
            per_seq((length, width)),
            per_seq((length, width)),
            per_seq((length, width)),
            per_seq((length, width)),
            per_seq((length, LANES)),
            per_seq((length, width)),
            whole((kinds + 8, width)),
            spec_w(0),
            spec_w(1),
            spec_w(2),
            whole((length, LANES)),
            whole((length, LANES)),
            whole((width, width)),
            whole((16, width)),
            whole((kinds, LANES)),
        ],
        out_specs=[per_seq((length, width)), whole((width, 4 * width + 2 * LANES), 1), whole((8, width))],
        scratch_shapes=[
            pltpu.VMEM((length, length), F32),
            pltpu.VMEM((LANES, length), F32),
            pltpu.VMEM((length, 3 * width), BF16),
            pltpu.VMEM((width, 3 * width), F32),
        ],
        out_shape=[
            seq_f32,
            jax.ShapeDtypeStruct((width, 4 * width + 2 * LANES), BF16),
            jax.ShapeDtypeStruct((8, width), F32),
        ],
        compiler_params=params(56),
        cost_estimate=pl.CostEstimate(flops=30 * 10**9, bytes_accessed=20 * 10**6, transcendentals=10**7),
        name="backward",
    )(tokens, seg_row, seg_col, q, k, v, dob, lse, dh1, small, attn, attn, attn, cos, sin, grad_wo, sgrad, grad_map)

    if planes == 4 and rows_d % 16 == 0:
        columns = 4 * width + 2 * LANES
        near = planes // 2
        sums = pl.pallas_call(
            functools.partial(reduce_kernel, group),
            in_specs=[pl.BlockSpec(memory_space=pl.ANY)],
            out_specs=pl.BlockSpec(memory_space=pltpu.VMEM),
            out_shape=jax.ShapeDtypeStruct((rows_d, columns), F32),
            scratch_shapes=[
                pltpu.VMEM((planes, 2, rows_d, columns), BF16),
                pltpu.VMEM((planes, 2, rows_d, columns), BF16),
                pltpu.VMEM((near, 2, rows_d, columns // 2), BF16),
                pltpu.VMEM((near, rows_d, columns // 2), BF16),
                pltpu.VMEM((near, rows_d, columns), BF16),
                pltpu.VMEM((near, rows_d, columns // 2), BF16),
                pltpu.VMEM((planes - 1, rows_d, columns // 2), BF16),
                pltpu.VMEM((rows_d, columns // 2), BF16),
                pltpu.VMEM((rows_d, columns // 2), BF16),
                pltpu.SemaphoreType.DMA,
                pltpu.SemaphoreType.DMA((6,)),
                pltpu.SemaphoreType.DMA((6,)),
                pltpu.SemaphoreType.DMA((planes - 1,)),
                pltpu.SemaphoreType.DMA((planes - 1,)),
            ],
            compiler_params=pltpu.CompilerParams(
                vmem_limit_bytes=32 * 1024 * 1024, collective_id=2, has_side_effects=True
            ),
            name="reduce",
        )(grad_attn.reshape(planes, 2, 2, rows_d, columns))
        attn_total = sums[:, 0 : 4 * width]
        sums = sums[:, 4 * width :]
        map_total = sums[0:kinds, 16 : 16 + kinds]
    else:
        part = lax.psum_scatter(grad_attn[:, 0 : 4 * width], "grp", scatter_dimension=0, tiled=True)
        attn_total = lax.psum(part, "rep").astype(F32)
        sgrad = jnp.where(iota((16, 1), 0) == kinds + 6, gain_one[0:1], sgrad)
        packed = jnp.concatenate([sgrad, jnp.pad(grad_map, ((0, 0), (0, width - LANES)))], axis=0)
        packed = lax.psum(packed, ("rep", "grp"))
        sums = lax.dynamic_slice_in_dim(packed[0:16], g * rows_d, rows_d, axis=1).T
        map_total = packed[16:, 0:kinds].T
    return (
        result.reshape(batches * length, width),
        gin.reshape(batches * length, width),
        sums[:, kinds + 6],
        attn_total[:, 0:width],
        attn_total[:, width : 2 * width],
        attn_total[:, 2 * width : 3 * width],
        attn_total[:, 3 * width :],
        sums[:, kinds + 7],
        sums[:, 0:kinds],
        map_total,
        sums[:, kinds : kinds + 4],
        sums[:, kinds + 4 : kinds + 6],
        grad_gate,
        grad_up,
        grad_down,
    )


def solution(mesh):
    rows = P(("rep", "grp"), None)
    in_specs = (
        (rows,) * 5
        + (P("grp"),)
        + (P("grp", None),) * 4
        + (P("grp"), P("grp", None), P(), P("grp", None), P("grp", None))
        + (P("grp", None, None),) * 3
    )
    out_specs = (
        (rows,) * 2
        + (P("grp"),)
        + (P("grp", None),) * 4
        + (P("grp"), P("grp", None), P(), P("grp", None), P("grp", None))
        + (P("grp", None, None),) * 3
    )
    body = functools.partial(local, mesh.shape["rep"], mesh.shape["grp"])
    return jax.shard_map(body, mesh=mesh, in_specs=in_specs, out_specs=out_specs, check_vma=False)
```

```python
import functools

import jax
import jax.numpy as jnp
from jax import lax
from jax.experimental import pallas as pl
from jax.experimental.pallas import tpu as pltpu
from jax.sharding import PartitionSpec as P

HEAD_DIM = 64
BLOCK = 256
EPS = 1e-05
NEG = -1000000000.0
F32 = jnp.float32
BF16 = jnp.bfloat16
LANES = 128


def nn(a, b):
    return lax.dot_general(a, b, (((1,), (0,)), ((), ())), preferred_element_type=F32)


def nt(a, b):
    return lax.dot_general(a, b, (((1,), (1,)), ((), ())), preferred_element_type=F32)


def tn(a, b):
    return lax.dot_general(a, b, (((0,), (0,)), ((), ())), preferred_element_type=F32)


def iota(shape, dim):
    return lax.broadcasted_iota(jnp.int32, shape, dim)


def split2(values):
    high = values.astype(BF16)
    low = (values - high.astype(F32)).astype(BF16)
    return high, low


def whole(shape, buffers=None):
    zeros = (0,) * len(shape)
    if buffers:
        return pl.BlockSpec(shape, lambda *_: zeros, pipeline_mode=pl.Buffered(buffers))
    return pl.BlockSpec(shape, lambda *_: zeros)


def per_seq(shape):
    tail = (0,) * len(shape)
    return pl.BlockSpec((1,) + shape, lambda b, *_: (b,) + tail)


def rms_scale(values):
    return lax.rsqrt(jnp.mean(values * values, axis=-1, keepdims=True) + EPS)


def slot_mask(position_row, capacity):
    places = iota((capacity, position_row.shape[1]), 0).astype(F32)
    return jnp.where(places == position_row, 1.0, 0.0).astype(BF16)


def grad_rows_kernel(own_ref, routes_ref, grad_ref, r0, r1, r2, r3, pos_ref):
    own = own_ref[0]
    kinds, length = pos_ref.shape[1:]
    capacity = r0.shape[1]
    ids = iota((kinds, length), 0)
    first = routes_ref[0, 0:1, :] == ids
    second = routes_ref[0, 1:2, :] == ids
    hits = jnp.where(first | second, 1.0, 0.0)
    before = jnp.where(iota((length, length), 0) < iota((length, length), 1), 1.0, 0.0)
    slots = nn(hits.astype(BF16), before.astype(BF16))
    pos_ref[0] = jnp.where(hits > 0.0, slots, -1.0)
    for number, rows in enumerate((r0, r1, r2, r3)):
        line = pos_ref[0, pl.ds(own ^ number, 1), :]
        rows[0] = nn(slot_mask(line, capacity), grad_ref[0]).astype(BF16)


def swap_halves(values, low_half):
    return jnp.where(low_half, pltpu.roll(values, 96, 1), pltpu.roll(values, 32, 1))


def sequence_forward(
    x_ref,
    seg_row_ref,
    seg_col_ref,
    routes_ref,
    prev_ref,
    map_ref,
    small_ref,
    wq_ref,
    wk_ref,
    wv_ref,
    wo_ref,
    cos_ref,
    sin_ref,
    pos_ref,
    q_ref,
    k_ref,
    v_ref,
    o_ref,
    h_ref,
    lse_ref,
    aux_ref,
    rows_refs,
    bias_ref,
    proj_ref,
    expert_of,
    between=None,
):
    length, width = x_ref.shape[1:]
    kinds = pos_ref.shape[1]
    capacity = length // 2
    tokens = x_ref[0].astype(F32)
    gain_one = small_ref[kinds + 6 : kinds + 7, :]
    gain_two = small_ref[kinds + 7 : kinds + 8, :]
    a1 = (tokens * rms_scale(tokens) * gain_one).astype(BF16)
    lane = iota((1, LANES), 1)
    low_half = (lane % HEAD_DIM) < (HEAD_DIM // 2)
    first_head = lane < HEAD_DIM
    mask_a = jnp.where(first_head, 1.0, 0.0).astype(BF16)
    mask_b = jnp.where(first_head, 0.0, 1.0).astype(BF16)
    pairs = width // LANES

    for weights, target, scale in ((wq_ref, q_ref, 0.125), (wk_ref, k_ref, 1.0)):
        proj_ref[...] = nn(a1, weights[...])

        def turn(h, carry):
            cols = pl.ds(pl.multiple_of(h * LANES, LANES), LANES)
            part = proj_ref[:, cols]
            turned = part * cos_ref[...] + swap_halves(part, low_half) * sin_ref[...]
            target[0, :, cols] = turned.astype(BF16) * jnp.asarray(scale, BF16)
            return carry

        lax.fori_loop(0, pairs, turn, 0)
    v_ref[0] = nn(a1, wv_ref[...]).astype(BF16)

    allowed = (seg_col_ref[0] == seg_row_ref[0]) & (
        iota((length, length), 1) // BLOCK <= iota((length, length), 0) // BLOCK
    )
    bias_ref[...] = jnp.where(allowed, 0.0, NEG)
    lse_ref[...] = jnp.zeros_like(lse_ref)
    if between is not None:
        between()

    def pair(h, carry):
        cols = pl.ds(pl.multiple_of(h * LANES, LANES), LANES)
        for begin in range(0, length, BLOCK):
            end = begin + BLOCK
            queries = q_ref[0, begin:end, cols]
            keys = k_ref[0, 0:end, cols]
            values = v_ref[0, 0:end, cols]
            bias = bias_ref[begin:end, 0:end]
            sums = lse_ref[0, begin:end, :]
            outs = []
            for half, mask in enumerate((mask_a, mask_b)):
                scores = nt(queries * mask, keys) + bias
                top = jnp.max(scores, axis=-1, keepdims=True)
                grown = jnp.exp(scores - top)
                total = jnp.sum(grown, axis=-1, keepdims=True)
                chances = (grown * (1.0 / total)).astype(BF16)
                outs.append(nn(chances, values))
                sums = jnp.where(lane == 2 * h + half, top + jnp.log(total), sums)
            lse_ref[0, begin:end, :] = sums
            o_ref[0, begin:end, cols] = jnp.where(first_head, outs[0], outs[1]).astype(BF16)
        return carry

    lax.fori_loop(0, pairs, pair, 0)

    hidden = tokens + nn(o_ref[0], wo_ref[...])
    h_ref[0] = hidden
    a2 = (hidden * rms_scale(hidden) * gain_two).astype(BF16)
    logits = nt(small_ref[...].astype(BF16), a2)[0:kinds, :]
    for j in range(kinds):
        logits = logits + map_ref[:, j : j + 1] * prev_ref[0, j : j + 1, :]
    ids = iota((kinds, length), 0)
    first = jnp.where(routes_ref[0, 0:1, :] == ids, 1.0, 0.0)
    second = jnp.where(routes_ref[0, 1:2, :] == ids, 1.0, 0.0)
    one = jnp.sum(logits * first, axis=0, keepdims=True)
    two = jnp.sum(logits * second, axis=0, keepdims=True)
    top = jnp.maximum(one, two)
    grown_one, grown_two = jnp.exp(one - top), jnp.exp(two - top)
    gate_one = grown_one / (grown_one + grown_two)
    gate_two = grown_two / (grown_one + grown_two)
    aux_ref[0, 0:kinds, :] = gate_one * first + gate_two * second
    aux_ref[0, kinds : kinds + 1, :] = gate_one
    aux_ref[0, kinds + 1 : kinds + 2, :] = gate_two
    aux_ref[0, kinds + 2 :, :] = jnp.zeros((aux_ref.shape[1] - kinds - 2, length), F32)

    place = iota((16, length), 0)
    for number, rows in enumerate(rows_refs):
        mask = slot_mask(pos_ref[0, pl.ds(expert_of(number), 1), :], capacity)
        rows[0, 0:capacity, :] = nn(mask, a2).astype(BF16)
        line = aux_ref[0, pl.ds(expert_of(number), 1), :]
        high = line.astype(BF16).astype(F32)
        mid = (line - high).astype(BF16).astype(F32)
        low = line - high - mid
        parts = jnp.where(place == 0, high, jnp.where(place == 1, mid, jnp.where(place == 2, low, 0.0)))
        spread = nt(parts.astype(BF16), mask)
        filled = jnp.max(pos_ref[0, pl.ds(expert_of(number), 1), :], axis=1, keepdims=True) + 1.0
        spread = jnp.where(iota((16, 1), 0) == 3, filled, spread)
        rows[0, capacity:, 0:capacity] = spread.astype(BF16)
        rows[0, capacity:, capacity:] = jnp.zeros((16, width - capacity), BF16)


def forward_kernel(
    own_ref,
    x_ref,
    seg_row_ref,
    seg_col_ref,
    routes_ref,
    prev_ref,
    map_ref,
    small_ref,
    wq_ref,
    wk_ref,
    wv_ref,
    wo_ref,
    cos_ref,
    sin_ref,
    pos_ref,
    q_ref,
    k_ref,
    v_ref,
    o_ref,
    h_ref,
    lse_ref,
    aux_ref,
    r0,
    r1,
    r2,
    r3,
    bias_ref,
    proj_ref,
):
    own = own_ref[0]
    sequence_forward(
        x_ref,
        seg_row_ref,
        seg_col_ref,
        routes_ref,
        prev_ref,
        map_ref,
        small_ref,
        wq_ref,
        wk_ref,
        wv_ref,
        wo_ref,
        cos_ref,
        sin_ref,
        pos_ref,
        q_ref,
        k_ref,
        v_ref,
        o_ref,
        h_ref,
        lse_ref,
        aux_ref,
        (r0, r1, r2, r3),
        bias_ref,
        proj_ref,
        lambda number: own ^ number,
    )


MESH = pl.DeviceIdType.MESH


class Place:
    def __init__(self, group):
        self.group = group
        self.planes = group // 4
        self.g = lax.axis_index("grp")
        self.y = lax.axis_index("rep")
        self.core = self.g % 2
        self.x = (self.g // 2) % 2
        self.z = self.g // 4
        self.core_peer = (self.y, self.g + 1 - 2 * self.core)
        self.x_peer = (self.y, self.g + 2 - 4 * self.x)
        self.y_peer = (1 - self.y, self.g)
        self.xy_peer = (1 - self.y, self.g + 2 - 4 * self.x)
        self.plane_peers = (None, self.x_peer, self.y_peer, self.xy_peer)

    def z_peer(self, k):
        return (self.y, (self.g + 4 * k) % self.group)

    def block(self, z, x, core):
        return (z * 2 + x) * 2 + core

    def expert(self, number):
        y = self.y if number < 2 else 1 - self.y
        x = self.x if number % 2 == 0 else 1 - self.x
        return 2 * y + x

    def barrier(self, peers):
        semaphore = pltpu.get_barrier_semaphore()
        for peer in peers:
            pl.semaphore_signal(semaphore, inc=1, device_id=peer, device_id_type=MESH)
        pl.semaphore_wait(semaphore, len(peers))


def remote(src, dst, send, recv, peer):
    return pltpu.make_async_remote_copy(
        src_ref=src, dst_ref=dst, send_sem=send, recv_sem=recv, device_id=peer, device_id_type=MESH
    )


def fused_forward_kernel(
    group,
    x_ref,
    seg_row_ref,
    seg_col_ref,
    routes_ref,
    prev_ref,
    map_ref,
    grad_ref,
    cos_ref,
    sin_ref,
    shard_ref,
    shard_o_ref,
    gate4_ref,
    up4_ref,
    down4_ref,
    q_ref,
    k_ref,
    v_ref,
    o_ref,
    h_ref,
    lse_ref,
    aux_ref,
    pos_ref,
    small_ref,
    attn_out_ref,
    attn_o_out_ref,
    rows_in_ref,
    grads_in_ref,
    gate_full_ref,
    up_full_ref,
    down_full_ref,
    attn_ref,
    attn_o_ref,
    bias_ref,
    proj_ref,
    rows_ref,
    grows_ref,
    local_sem,
    attn_send,
    attn_recv,
    ffn_local,
    ffn_send,
    ffn_recv,
    out_sem,
    row_local,
    row_send,
    row_recv,
):
    step = pl.program_id(0)
    last = pl.num_programs(0) - 1
    here = Place(group)
    planes = here.planes
    batches, kinds, length = pos_ref.shape
    width = x_ref.shape[2]
    capacity = length // 2
    shards = ((shard_ref, attn_ref), (shard_o_ref, attn_o_ref))
    experts = ((gate4_ref, gate_full_ref), (up4_ref, up_full_ref), (down4_ref, down_full_ref))
    depth = shard_ref.shape[0]
    mine = here.block(here.z, here.x, here.core)

    def rows_of(block):
        return pl.ds(pl.multiple_of(block * depth, 16), depth)

    def attn_part(t, block, part):
        full = shards[t][1]
        half = full.shape[1] // 2
        if part is None:
            return full.at[rows_of(block), :]
        return full.at[rows_of(block), pl.ds(pl.multiple_of(part * half, LANES), half)]

    def attn_copy(t, slot, z, x, part, peer):
        ref = attn_part(t, here.block(z, x, here.core), part)
        return remote(ref, ref, attn_send.at[t, slot], attn_recv.at[t, slot], peer)

    def to_z(t, k):
        return attn_copy(t, k, here.z, here.x, None, here.z_peer(1 if k == 0 else planes - 1))

    def from_z(t, k):
        return attn_copy(t, k, z_at(planes - 1 if k == 0 else 1), here.x, None, here.x_peer)

    def pass_z(t, k):
        z = z_at(planes - 1 if k == 0 else 1)
        return attn_copy(t, 2 + k, z, here.x, k, here.z_peer(1 if k == 0 else planes - 1))

    def passed_z(t, k):
        return attn_copy(t, 2 + k, z_at(2), here.x, k, here.x_peer)

    def to_x(t, step_z):
        return attn_copy(t, 4 + step_z, z_at(step_z), here.x, here.y, here.x_peer)

    def from_x(t, step_z):
        return attn_copy(t, 4 + step_z, z_at(step_z), 1 - here.x, here.y, here.x_peer)

    def to_y(t, step_z):
        return attn_copy(t, 4 + planes + step_z, z_at(step_z), 1 - here.x, here.y, here.y_peer)

    def from_y(t, step_z):
        return attn_copy(t, 4 + planes + step_z, z_at(step_z), 1 - here.x, 1 - here.y, here.y_peer)

    def to_core(t, step_z, x):
        return attn_copy(t, 4 + 2 * planes + 2 * step_z + x, z_at(step_z), here.x if x == 0 else 1 - here.x, None, here.core_peer)

    def from_core(t, step_z, x):
        ref = attn_part(t, here.block(z_at(step_z), here.x if x == 0 else 1 - here.x, 1 - here.core), None)
        slot = 4 + 2 * planes + 2 * step_z + x
        return remote(ref, ref, attn_send.at[t, slot], attn_recv.at[t, slot], here.core_peer)

    def z_at(k):
        return (here.z + k) % planes

    def ffn_to_x(j):
        source, full = experts[j]
        return remote(
            source.at[here.expert(1)],
            full.at[here.z, here.x, here.core],
            ffn_send.at[j, 0],
            ffn_recv.at[j, 0],
            here.x_peer,
        )

    def ffn_from_x(j):
        source, full = experts[j]
        return remote(
            source.at[here.expert(1)],
            full.at[here.z, 1 - here.x, here.core],
            ffn_send.at[j, 0],
            ffn_recv.at[j, 0],
            here.x_peer,
        )

    def ffn_mine(j):
        source, full = experts[j]
        return pltpu.make_async_copy(source.at[here.expert(0)], full.at[here.z, here.x, here.core], ffn_local.at[j])

    def ffn_copy(j, slot, z, x, core, peer):
        full = experts[j][1]
        part = full.at[z, :, core] if x is None else full.at[z, x, core]
        return remote(part, part, ffn_send.at[j, slot], ffn_recv.at[j, slot], peer)

    def ffn_to_z(j, k):
        return ffn_copy(j, 1 + k, here.z, None, here.core, here.z_peer(1 if k == 0 else planes - 1))

    def ffn_from_z(j, k):
        return ffn_copy(j, 1 + k, z_at(planes - 1 if k == 0 else 1), None, here.core, here.x_peer)

    def ffn_pass_z(j, k):
        z = z_at(planes - 1 if k == 0 else 1)
        return ffn_copy(j, 3 + k, z, k, here.core, here.z_peer(1 if k == 0 else planes - 1))

    def ffn_passed_z(j, k):
        return ffn_copy(j, 3 + k, z_at(2), k, here.core, here.x_peer)

    def ffn_to_core(j, step_z):
        return ffn_copy(j, 5 + step_z, z_at(step_z), None, here.core, here.core_peer)

    def ffn_from_core(j, step_z):
        return ffn_copy(j, 5 + step_z, z_at(step_z), None, 1 - here.core, here.core_peer)

    def row_copy(kind, member, number):
        source, target = ((grows_ref, grads_in_ref), (rows_ref, rows_in_ref))[kind]
        src, dst = source.at[member, number], target.at[number, member]
        if number == 0:
            return pltpu.make_async_copy(src, dst, row_local.at[kind, member])
        return remote(
            src,
            dst,
            row_send.at[kind, member, number],
            row_recv.at[kind, member, number],
            here.plane_peers[number],
        )

    def outs(t):
        full, target = ((attn_ref, attn_out_ref), (attn_o_ref, attn_o_out_ref))[t]
        return pltpu.make_async_copy(full, target, out_sem.at[t])

    @pl.when(step == 0)
    def _():
        own_copies = [
            pltpu.make_async_copy(source, full.at[rows_of(mine), :], local_sem.at[t])
            for t, (source, full) in enumerate(shards)
        ]
        for copy in own_copies:
            copy.start()
        for j in range(3):
            ffn_mine(j).start()
        here.barrier(
            [here.core_peer, here.x_peer, here.y_peer, here.xy_peer, here.z_peer(1), here.z_peer(planes - 1)]
        )
        for copy in own_copies:
            copy.wait()
        for t in range(2):
            to_z(t, 0).start()
            to_z(t, 1).start()
            to_x(t, 0).start()
            to_core(t, 0, 0).start()
        for j in range(3):
            ffn_to_x(j).start()

        ids = iota((kinds, length), 0)
        before = jnp.where(iota((length, length), 0) < iota((length, length), 1), 1.0, 0.0).astype(BF16)
        for member in range(batches):
            first = routes_ref[member, 0:1, :] == ids
            second = routes_ref[member, 1:2, :] == ids
            hits = jnp.where(first | second, 1.0, 0.0)
            pos_ref[member] = jnp.where(hits > 0.0, nn(hits.astype(BF16), before), -1.0)
            for number in range(4):
                line = pos_ref[member, pl.ds(here.expert(number), 1), :]
                grows_ref[member, number] = nn(slot_mask(line, capacity), grad_ref[member]).astype(BF16)
            row_copy(0, member, 0).start()

        for t in range(2):
            for k, step_z in enumerate((planes - 1, 1)):
                from_z(t, k).wait_recv()
                pass_z(t, k).start()
                to_x(t, step_z).start()
                to_core(t, step_z, 0).start()
        for t in range(2):
            from_x(t, 0).wait_recv()
            to_y(t, 0).start()
        for j in range(3):
            ffn_mine(j).wait()
            ffn_from_x(j).wait_recv()
            ffn_to_z(j, 0).start()
            ffn_to_z(j, 1).start()
            ffn_to_core(j, 0).start()
        for t in range(2):
            passed_z(t, 0).wait_recv()
            passed_z(t, 1).wait_recv()
            to_x(t, 2).start()
            to_core(t, 2, 0).start()
        for member in range(batches):
            row_copy(0, member, 2).start()
        for t in range(2):
            for step_z in (planes - 1, 1, 2):
                from_x(t, step_z).wait_recv()
                to_y(t, step_z).start()
        for t in range(2):
            for step_z in (0, planes - 1, 1, 2):
                from_y(t, step_z).wait_recv()
                to_core(t, step_z, 1).start()
        for t in range(2):
            for step_z in range(planes):
                for x in range(2):
                    from_core(t, step_z, x).wait_recv()
        for t in range(2):
            outs(t).start()
        for member in range(batches):
            row_copy(0, member, 1).start()
            row_copy(0, member, 3).start()
        small_ref[...] = jnp.transpose(attn_ref[:, 3 * width : 3 * width + LANES].astype(F32))[0 : kinds + 8, :]

    def between():
        @pl.when(step == 0)
        def _():
            for j in range(3):
                for k, step_z in enumerate((planes - 1, 1)):
                    ffn_from_z(j, k).wait_recv()
                    ffn_pass_z(j, k).start()
                    ffn_to_core(j, step_z).start()

    sequence_forward(
        x_ref,
        seg_row_ref,
        seg_col_ref,
        routes_ref.at[pl.ds(step, 1)],
        prev_ref,
        map_ref,
        small_ref,
        attn_ref.at[:, 0:width],
        attn_ref.at[:, width : 2 * width],
        attn_ref.at[:, 2 * width : 3 * width],
        attn_o_ref,
        cos_ref,
        sin_ref,
        pos_ref.at[pl.ds(step, 1)],
        q_ref,
        k_ref,
        v_ref,
        o_ref,
        h_ref,
        lse_ref,
        aux_ref,
        [rows_ref.at[pl.ds(step, 1), number] for number in range(4)],
        bias_ref,
        proj_ref,
        here.expert,
        between,
    )
    for member in range(batches):

        @pl.when(step == member)
        def _():
            for number in range(4):
                row_copy(1, member, number).start()

    @pl.when(step == 0)
    def _():
        for j in range(3):
            for k in range(2):
                ffn_passed_z(j, k).wait_recv()
            ffn_to_core(j, 2).start()

    @pl.when(step == last)
    def _():
        for t in range(2):
            outs(t).wait()
            for k in range(2):
                to_z(t, k).wait_send()
                pass_z(t, k).wait_send()
            for step_z in range(planes):
                to_x(t, step_z).wait_send()
                to_y(t, step_z).wait_send()
                for x in range(2):
                    to_core(t, step_z, x).wait_send()
        for j in range(3):
            ffn_to_x(j).wait_send()
            for k in range(2):
                ffn_to_z(j, k).wait_send()
                ffn_pass_z(j, k).wait_send()
            for step_z in range(planes):
                ffn_to_core(j, step_z).wait_send()
                ffn_from_core(j, step_z).wait_recv()
        for kind in range(2):
            for member in range(batches):
                for number in range(4):
                    copy = row_copy(kind, member, number)
                    copy.wait()


def expert_kernel(
    a_ref,
    g_ref,
    gate_ref,
    up_ref,
    down_ref,
    v_ref,
    d_ref,
    grad_gate_ref,
    grad_up_ref,
    grad_down_ref,
    rows_ref,
    grads_ref,
    gates_ref,
    rows_t_ref,
    grads_t_ref,
    places_ref,
    acc_value_ref,
    acc_input_ref,
    acc_gate_ref,
    acc_up_ref,
    acc_down_ref,
    share_ref,
    sems,
):
    step = pl.program_id(0)
    last = pl.num_programs(0) - 1
    batches, capacity, width = g_ref.shape[1:]
    blocks = 4 * batches

    @pl.when(step == 0)
    def _():
        copies = []
        for number in range(4):
            rows, grads = a_ref.at[number], g_ref.at[number]
            for member in range(batches):
                block = number * batches + member
                span = pl.ds(block * capacity, capacity)
                copies.append(
                    pltpu.make_async_copy(
                        rows.at[member, pl.ds(capacity, 16), pl.ds(0, capacity)],
                        gates_ref.at[block],
                        sems.at[3 * block],
                    )
                )
                copies.append(
                    pltpu.make_async_copy(
                        rows.at[member, pl.ds(0, capacity), :], rows_ref.at[span, :], sems.at[3 * block + 1]
                    )
                )
                copies.append(
                    pltpu.make_async_copy(grads.at[member], grads_ref.at[span, :], sems.at[3 * block + 2])
                )
        for copy in copies:
            copy.start()
        for copy in copies:
            copy.wait()
        same = iota((capacity, capacity), 0) == iota((capacity, capacity), 1)
        spare = jnp.zeros((capacity, width), BF16)
        rows_ref[blocks * capacity :, :] = spare
        grads_ref[blocks * capacity :, :] = spare
        share_ref[...] = jnp.zeros_like(share_ref)

        def pack(block, place):
            span = pl.ds(pl.multiple_of(block * capacity, capacity), capacity)
            target = pl.ds(pl.multiple_of(place, 16), capacity)
            parts = gates_ref[block].astype(F32)
            count = jnp.max(parts[3:4, :]).astype(jnp.int32)
            line = jnp.sum(parts[0:3, :], axis=0, keepdims=True)
            column = jnp.sum(jnp.where(same, line, 0.0), axis=1, keepdims=True)
            rows = rows_ref[span, :]
            grads = (grads_ref[span, :].astype(F32) * column).astype(BF16)
            rows_ref[target, :] = rows
            grads_ref[target, :] = grads
            places_ref[block] = place
            return place + (count + 15) // 16 * 16

        total = lax.fori_loop(0, blocks, pack, 0)
        target = pl.ds(pl.multiple_of(total, 16), capacity)
        rows_ref[target, :] = spare
        grads_ref[target, :] = spare
        places_ref[blocks] = (total + capacity - 1) // capacity

        def turn(block, carry):
            span = pl.ds(pl.multiple_of(block * capacity, capacity), capacity)
            grads_t_ref[:, span] = jnp.transpose(grads_ref[span, :])
            rows_t_ref[:, span] = jnp.transpose(rows_ref[span, :])
            return carry

        lax.fori_loop(0, places_ref[blocks], turn, 0)

    acc_gate_ref[...] = jnp.zeros_like(acc_gate_ref)
    acc_up_ref[...] = jnp.zeros_like(acc_up_ref)
    acc_down_ref[...] = jnp.zeros_like(acc_down_ref)

    def work(block, carry):
        span = pl.ds(pl.multiple_of(block * capacity, capacity), capacity)
        rows = rows_ref[span, :]
        grads = grads_ref[span, :]
        gate = nn(rows, gate_ref[...])
        up = nn(rows, up_ref[...])
        back = nt(grads, down_ref[...])
        sig = 1.0 / (1.0 + jnp.exp(-gate))
        silu = gate * sig
        act = (silu * up).astype(BF16)
        grad_gate = (back * up * (sig * (1.0 + gate * (1.0 - sig)))).astype(BF16)
        grad_up = (back * silu).astype(BF16)
        value = nn(act, down_ref[...])
        grad_rows = nt(grad_gate, gate_ref[...]) + nt(grad_up, up_ref[...])
        rows_t = rows_t_ref[:, span]
        acc_gate_ref[...] += nn(rows_t, grad_gate)
        acc_up_ref[...] += nn(rows_t, grad_up)
        acc_down_ref[...] += nn(grads_t_ref[:, span], act)
        share = jnp.broadcast_to(
            jnp.sum(act.astype(F32) * back, axis=1, keepdims=True), (capacity, LANES)
        )

        @pl.when(step == 0)
        def _():
            share_ref[span, :] = share
            acc_value_ref[span, :] = value
            acc_input_ref[span, :] = grad_rows

        @pl.when(step > 0)
        def _():
            share_ref[span, :] += share

        @pl.when((step > 0) & (step < last))
        def _():
            acc_value_ref[span, :] += value
            acc_input_ref[span, :] += grad_rows

        @pl.when(step == last)
        def _():
            rows_ref[span, :] = (acc_value_ref[span, :] + value).astype(BF16)
            grads_ref[span, :] = (acc_input_ref[span, :] + grad_rows).astype(BF16)

        return carry

    lax.fori_loop(0, places_ref[blocks], work, 0)
    grad_gate_ref[...] = acc_gate_ref[...].astype(BF16)
    grad_up_ref[...] = acc_up_ref[...].astype(BF16)
    grad_down_ref[...] = jnp.transpose(acc_down_ref[...].astype(BF16))

    @pl.when(step == last)
    def _():
        same = iota((capacity, capacity), 0) == iota((capacity, capacity), 1)
        place = iota((16, capacity), 0)

        def shares(block, carry):
            column = share_ref[pl.ds(pl.multiple_of(places_ref[block], 16), capacity), 0:1]
            line = jnp.sum(jnp.where(same, column, 0.0), axis=0, keepdims=True)
            high = line.astype(BF16).astype(F32)
            mid = (line - high).astype(BF16).astype(F32)
            low = line - high - mid
            parts = jnp.where(place == 0, high, jnp.where(place == 1, mid, jnp.where(place == 2, low, 0.0)))
            gates_ref[block] = parts.astype(BF16)
            return carry

        lax.fori_loop(0, blocks, shares, 0)
        copies = []
        for number in range(4):
            values, grads = v_ref.at[number], d_ref.at[number]
            for member in range(batches):
                block = number * batches + member
                span = pl.ds(pl.multiple_of(places_ref[block], 16), capacity)
                copies.append(pltpu.make_async_copy(rows_ref.at[span, :], values.at[member], sems.at[3 * block]))
                copies.append(
                    pltpu.make_async_copy(
                        grads_ref.at[span, :], grads.at[member, pl.ds(0, capacity), :], sems.at[3 * block + 1]
                    )
                )
                copies.append(
                    pltpu.make_async_copy(
                        gates_ref.at[block],
                        grads.at[member, pl.ds(capacity, 16), pl.ds(0, capacity)],
                        sems.at[3 * block + 2],
                    )
                )
        for copy in copies:
            copy.start()
        for copy in copies:
            copy.wait()


def constant_mix(zs, index):
    za, zb = zs[:, index : index + 1], zs[:, index + 1 : index + 2]
    top = jnp.maximum(za, zb)
    ea, eb = jnp.exp(za - top), jnp.exp(zb - top)
    return ea / (ea + eb), eb / (ea + eb)


def token_columns(pos_ref, aux_ref, cols_ref):
    kinds, length = pos_ref.shape[1:]
    cols_ref[0:kinds, :] = pos_ref[0]
    cols_ref[kinds : kinds + 16, :] = aux_ref[0]
    cols_ref[kinds + 16 :, :] = jnp.zeros((LANES - kinds - 16, length), F32)
    return jnp.transpose(cols_ref[...])


def column(source, index):
    return jnp.sum(jnp.where(iota((1, LANES), 1) == index, source, 0.0), axis=1, keepdims=True)


def result_kernel(own_ref, v_ref, pos_ref, aux_ref, h_ref, small_ref, out_ref, cols_ref):
    own = own_ref[0]
    length, width = h_ref.shape[1:]
    kinds = pos_ref.shape[1]
    ffn = kinds - 4
    capacity = v_ref.shape[2]
    hidden = h_ref[0]
    n2 = hidden * rms_scale(hidden) * small_ref[kinds + 7 : kinds + 8, :]
    n2_high, n2_low = split2(n2)
    small = small_ref[...].astype(BF16)
    cols = token_columns(pos_ref, aux_ref, cols_ref)
    result = hidden
    slot_lane = iota((1, capacity), 1).astype(F32)
    for number in range(4):
        expert = own ^ number
        mask = jnp.where(column(cols, expert) == slot_lane, 1.0, 0.0).astype(BF16)
        result = result + column(cols, kinds + expert) * nn(mask, v_ref[number, 0])
    mixes = nt(n2_high, small) + nt(n2_low, small)
    share = column(cols, kinds + ffn + 1)
    for constant in range(2):
        weight = column(cols, kinds + ffn + 2 + constant)
        alpha_a, alpha_b = constant_mix(mixes, kinds + 2 * constant)
        result = result + (weight * alpha_b) * small_ref[kinds + 4 + constant : kinds + 5 + constant, :]
        share = share + weight * alpha_a
    out_ref[0] = result + share * n2


def sequence_combine(
    step,
    d_refs,
    pos_ref,
    aux_ref,
    routes_ref,
    prev_ref,
    h_ref,
    g_ref,
    o_ref,
    small_ref,
    wo_ref,
    dh_ref,
    dob_ref,
    sgrad_ref,
    grad_map_ref,
    acc_ref,
    cols_ref,
    expert_of,
):
    length, width = h_ref.shape[1:]
    kinds = pos_ref.shape[1]
    ffn = kinds - 4
    capacity = d_refs[0].shape[1] - 16
    hidden = h_ref[0]
    inverse = rms_scale(hidden)
    gain = small_ref[kinds + 7 : kinds + 8, :]
    n2 = hidden * inverse * gain
    n2_high, n2_low = split2(n2)
    grad_low = g_ref[0]
    grad = grad_low.astype(F32)
    small = small_ref[...].astype(BF16)
    cols = token_columns(pos_ref, aux_ref, cols_ref)
    lane = iota((1, LANES), 1)
    gate_one = column(cols, 2 * kinds)
    gate_two = column(cols, 2 * kinds + 1)
    hot_one = jnp.where(routes_ref[0, :, 0:1] == lane, 1.0, 0.0)
    hot_two = jnp.where(routes_ref[0, :, 1:2] == lane, 1.0, 0.0)

    grad_n2 = jnp.zeros((length, width), F32)
    shares = jnp.zeros((length, LANES), F32)
    slot_lane = iota((1, capacity), 1).astype(F32)
    for number, rows in enumerate(d_refs):
        expert = expert_of(number)
        mask = jnp.where(column(cols, expert) == slot_lane, 1.0, 0.0).astype(BF16)
        grad_n2 = grad_n2 + nn(mask, rows[0, 0:capacity, :])
        parts = nt(mask, rows[0, capacity:, 0:capacity])
        shares = jnp.where(lane == expert, jnp.sum(parts, axis=1, keepdims=True), shares)

    mixes = nt(n2_high, small) + nt(n2_low, small)
    inner = nt(grad_low, small)
    with_n2 = jnp.sum(grad * n2, axis=1, keepdims=True)
    weight_copy = column(cols, kinds + ffn + 1)
    shares = jnp.where(lane == ffn + 1, weight_copy * with_n2, shares)
    share = weight_copy
    coefs = jnp.zeros((length, LANES), F32)
    for constant in range(2):
        weight = column(cols, kinds + ffn + 2 + constant)
        alpha_a, alpha_b = constant_mix(mixes, kinds + 2 * constant)
        with_vec = inner[:, kinds + 4 + constant : kinds + 5 + constant]
        share = share + weight * alpha_a
        da = weight * with_n2
        db = weight * with_vec
        mean = alpha_a * da + alpha_b * db
        shares = jnp.where(lane == ffn + 2 + constant, mean, shares)
        coefs = jnp.where(lane == kinds + 2 * constant, alpha_a * (da - mean), coefs)
        coefs = jnp.where(lane == kinds + 2 * constant + 1, alpha_b * (db - mean), coefs)
        coefs = jnp.where(lane == kinds + 4 + constant, weight * alpha_b, coefs)

    share_one = jnp.sum(shares * hot_one, axis=1, keepdims=True)
    share_two = jnp.sum(shares * hot_two, axis=1, keepdims=True)
    both = share_one + share_two
    dlogits = (share_one - gate_one * both) * hot_one + (share_two - gate_two * both) * hot_two
    coefs = jnp.where(lane < kinds, dlogits, coefs)
    back = jnp.where(lane < kinds + 4, coefs, 0.0)[:, 0:16]
    back_high, back_low = split2(back)
    grad_n2 = grad_n2 + nn(back_high, small) + nn(back_low, small) + share * grad

    coefs_t = jnp.transpose(coefs)[0:16, :]
    high, low = split2(coefs_t)
    by_n2 = nn(high, n2_high) + nn(low, n2_high)
    by_low = nn(high, n2_low)
    by_grad = nn(high, grad_low) + nn(low, grad_low)
    row = iota((16, 1), 0)
    parts = jnp.where(row < kinds, by_n2, jnp.where(row < kinds + 4, by_n2 + by_low, by_grad))
    gain_part = jnp.sum(grad_n2 * hidden * inverse, axis=0, keepdims=True)
    parts = jnp.where(row == kinds + 7, gain_part, jnp.where(row == kinds + 6, 0.0, parts))
    dlog_t = coefs_t[0:kinds, :]
    map_lane = iota((kinds, LANES), 1)
    map_part = jnp.zeros((kinds, LANES), F32)
    for j in range(kinds):
        map_part = jnp.where(
            map_lane == j, jnp.sum(dlog_t * prev_ref[0, j : j + 1, :], axis=1, keepdims=True), map_part
        )

    scaled = gain * grad_n2
    inner_mean = jnp.mean(scaled * hidden, axis=-1, keepdims=True)
    dh = grad + inverse * scaled - hidden * (inverse * inverse * inverse) * inner_mean
    dh_ref[0] = dh
    db = dh.astype(BF16)
    dob_ref[0] = nt(db, wo_ref[...]).astype(BF16)
    wo_part = nn(jnp.transpose(o_ref[0]), db)

    @pl.when(step == 0)
    def _():
        acc_ref[...] = wo_part
        sgrad_ref[...] = parts
        grad_map_ref[...] = map_part

    @pl.when(step > 0)
    def _():
        acc_ref[...] += wo_part
        sgrad_ref[...] += parts
        grad_map_ref[...] += map_part


def combine_kernel(
    own_ref,
    d0,
    d1,
    d2,
    d3,
    pos_ref,
    aux_ref,
    routes_ref,
    prev_ref,
    h_ref,
    g_ref,
    o_ref,
    small_ref,
    wo_ref,
    dh_ref,
    dob_ref,
    grad_wo_ref,
    sgrad_ref,
    grad_map_ref,
    acc_ref,
    cols_ref,
):
    own = own_ref[0]
    step = pl.program_id(0)
    sequence_combine(
        step,
        (d0, d1, d2, d3),
        pos_ref,
        aux_ref,
        routes_ref,
        prev_ref,
        h_ref,
        g_ref,
        o_ref,
        small_ref,
        wo_ref,
        dh_ref,
        dob_ref,
        sgrad_ref,
        grad_map_ref,
        acc_ref,
        cols_ref,
        lambda number: own ^ number,
    )

    @pl.when(step == pl.num_programs(0) - 1)
    def _():
        grad_wo_ref[...] = acc_ref[...].astype(BF16)


def sequence_backward(
    step,
    x_ref,
    seg_row_ref,
    seg_col_ref,
    q_ref,
    k_ref,
    v_ref,
    dob_ref,
    lse_ref,
    dh_ref,
    small_ref,
    wq_ref,
    wk_ref,
    wv_ref,
    cos_ref,
    sin_ref,
    gin_ref,
    gain_ref,
    bias_ref,
    lse_t_ref,
    dqkv_ref,
    acc_ref,
):
    length, width = x_ref.shape[1:]
    kinds = small_ref.shape[0] - 8
    pairs = width // LANES
    lane = iota((1, LANES), 1)
    low_half = (lane % HEAD_DIM) < (HEAD_DIM // 2)
    first_head = lane < HEAD_DIM
    mask_a = jnp.where(first_head, 1.0, 0.0).astype(BF16)
    mask_b = jnp.where(first_head, 0.0, 1.0).astype(BF16)
    allowed = (seg_col_ref[0] == seg_row_ref[0]) & (
        iota((length, length), 0) // BLOCK <= iota((length, length), 1) // BLOCK
    )
    bias_ref[...] = jnp.where(allowed, 0.0, NEG)
    lse_t_ref[...] = jnp.transpose(lse_ref[0])

    def pair(h, carry):
        cols = pl.ds(pl.multiple_of(h * LANES, LANES), LANES)
        keys_t = jnp.transpose(k_ref[0, :, cols])
        grad_keys = None
        grad_values = None
        grad_queries = []
        for begin in range(0, length, BLOCK):
            end = begin + BLOCK
            queries = q_ref[0, begin:end, cols]
            outs = dob_ref[0, begin:end, cols]
            keys = k_ref[0, 0:end, cols]
            values = v_ref[0, 0:end, cols]
            queries = jnp.concatenate([queries * mask_a, queries * mask_b], axis=0)
            outs = jnp.concatenate([outs * mask_a, outs * mask_b], axis=0)
            bias = bias_ref[0:end, begin:end]
            bias = jnp.concatenate([bias, bias], axis=1)
            line = jnp.concatenate(
                [lse_t_ref[pl.ds(2 * h, 1), begin:end], lse_t_ref[pl.ds(2 * h + 1, 1), begin:end]], axis=1
            )
            chances = jnp.exp(nt(keys, queries) + bias - line)
            grad_chances = nt(values, outs)
            delta = jnp.sum(chances * grad_chances, axis=0, keepdims=True)
            grad_scores = (chances * (grad_chances - delta)).astype(BF16)
            dv = nn(chances.astype(BF16), outs)
            dk = nn(grad_scores, queries)
            dq = jnp.transpose(nn(keys_t[:, 0:end], grad_scores))
            grad_queries.append(jnp.where(first_head, dq[0:BLOCK], dq[BLOCK:]))
            if grad_keys is None:
                grad_keys, grad_values = dk, dv
            else:
                grad_keys = jnp.concatenate([grad_keys + dk[0:begin], dk[begin:]], axis=0)
                grad_values = jnp.concatenate([grad_values + dv[0:begin], dv[begin:]], axis=0)
        dq = jnp.concatenate(grad_queries, axis=0) * 0.125
        dq = dq * cos_ref[...] - swap_halves(dq, low_half) * sin_ref[...]
        dk = grad_keys * cos_ref[...] - swap_halves(grad_keys, low_half) * sin_ref[...]
        dqkv_ref[:, cols] = dq.astype(BF16)
        dqkv_ref[:, pl.ds(pl.multiple_of(width + h * LANES, LANES), LANES)] = dk.astype(BF16)
        dqkv_ref[:, pl.ds(pl.multiple_of(2 * width + h * LANES, LANES), LANES)] = grad_values.astype(BF16)
        return carry

    lax.fori_loop(0, pairs, pair, 0)

    tokens = x_ref[0].astype(F32)
    inverse = rms_scale(tokens)
    gain = small_ref[kinds + 6 : kinds + 7, :]
    a1_t = jnp.transpose((tokens * inverse * gain).astype(BF16))
    dn1 = (
        nt(dqkv_ref[:, 0:width], wq_ref[...])
        + nt(dqkv_ref[:, width : 2 * width], wk_ref[...])
        + nt(dqkv_ref[:, 2 * width :], wv_ref[...])
    )
    scaled = gain * dn1
    inner_mean = jnp.mean(scaled * tokens, axis=-1, keepdims=True)
    gin_ref[0] = dh_ref[0] + inverse * scaled - tokens * (inverse * inverse * inverse) * inner_mean
    gain_part = jnp.broadcast_to(jnp.sum(dn1 * tokens * inverse, axis=0, keepdims=True), gain_ref.shape)

    @pl.when(step == 0)
    def _():
        acc_ref[...] = jnp.zeros_like(acc_ref)
        gain_ref[...] = gain_part

    @pl.when(step > 0)
    def _():
        gain_ref[...] += gain_part

    for part in range(3):
        span = slice(part * width, (part + 1) * width)
        acc_ref[:, span] += nn(a1_t, dqkv_ref[:, span])


def small_table(depth, sgrad_ref, grad_map_ref, gain_ref):
    kinds = grad_map_ref.shape[0]
    width = sgrad_ref.shape[1]
    row = iota((16, 1), 0)
    table = jnp.where(row == kinds + 6, gain_ref[0:1, :], sgrad_ref[...])
    chosen = jnp.where(iota((LANES, width), 1) % depth == iota((LANES, width), 0), 1.0, 0.0).astype(BF16)
    maps = nn(grad_map_ref[...].astype(BF16), chosen)
    table = jnp.concatenate([table, maps, jnp.zeros((LANES - 16 - kinds, width), F32)], axis=0)
    return jnp.transpose(table).astype(BF16)


def backward_kernel(
    x_ref,
    seg_row_ref,
    seg_col_ref,
    q_ref,
    k_ref,
    v_ref,
    dob_ref,
    lse_ref,
    dh_ref,
    small_ref,
    wq_ref,
    wk_ref,
    wv_ref,
    cos_ref,
    sin_ref,
    gin_ref,
    grad_w_ref,
    gain_ref,
    bias_ref,
    lse_t_ref,
    dqkv_ref,
    acc_ref,
):
    step = pl.program_id(0)
    sequence_backward(
        step,
        x_ref,
        seg_row_ref,
        seg_col_ref,
        q_ref,
        k_ref,
        v_ref,
        dob_ref,
        lse_ref,
        dh_ref,
        small_ref,
        wq_ref,
        wk_ref,
        wv_ref,
        cos_ref,
        sin_ref,
        gin_ref,
        gain_ref,
        bias_ref,
        lse_t_ref,
        dqkv_ref,
        acc_ref,
    )

    @pl.when(step == pl.num_programs(0) - 1)
    def _():
        grad_w_ref[...] = acc_ref[...].astype(BF16)


def fused_backward_kernel(
    group,
    depth,
    pos_ref,
    aux_ref,
    routes_ref,
    prev_ref,
    h_ref,
    g_ref,
    o_ref,
    x_ref,
    seg_row_ref,
    seg_col_ref,
    q_ref,
    k_ref,
    v_ref,
    lse_ref,
    small_ref,
    wq_ref,
    wk_ref,
    wv_ref,
    wo_ref,
    cos_ref,
    sin_ref,
    d_ref,
    val_ref,
    gate_ref,
    up_ref,
    down_ref,
    gin_ref,
    acc_ref,
    acc_wo_ref,
    table_ref,
    d_in_ref,
    val_in_ref,
    gate_out_ref,
    up_out_ref,
    down_out_ref,
    cols_ref,
    dh_ref,
    dob_ref,
    sgrad_ref,
    grad_map_ref,
    gain_ref,
    bias_ref,
    lse_t_ref,
    dqkv_ref,
    rows_ref,
    gate_own,
    up_own,
    down_own,
    gate_swap,
    up_swap,
    down_swap,
    gate_near,
    up_near,
    down_near,
    gate_far,
    up_far,
    down_far,
    row_local,
    row_send,
    row_recv,
    ffn_local,
    ffn_send,
    ffn_recv,
):
    step = pl.program_id(0)
    last = pl.num_programs(0) - 1
    here = Place(group)
    planes = here.planes
    batches = d_ref.shape[1]
    grads = (gate_ref, up_ref, down_ref)
    owns = (gate_own, up_own, down_own)
    swaps = (gate_swap, up_swap, down_swap)
    nears = (gate_near, up_near, down_near)
    fars = (gate_far, up_far, down_far)
    outs = (gate_out_ref, up_out_ref, down_out_ref)
    side = (here.z_peer(1), here.z_peer(planes - 1))

    def z_at(k):
        return (here.z + k) % planes

    def row_copy(kind, member, number):
        source, target = ((d_ref, d_in_ref), (val_ref, val_in_ref))[kind]
        src, dst = source.at[number, member], target.at[number, member]
        if number == 0:
            return pltpu.make_async_copy(src, dst, row_local.at[batches * 4 + member])
        return remote(
            src, dst, row_send.at[kind, member, number], row_recv.at[kind, member, number], here.plane_peers[number]
        )

    def load_rows(member, number):
        source = d_ref if number == 0 else d_in_ref
        return pltpu.make_async_copy(
            source.at[number, member], rows_ref.at[number, 0], row_local.at[member * 4 + number]
        )

    def own_copy(j):
        return pltpu.make_async_copy(grads[j].at[:, :, here.core], owns[j], ffn_local.at[j, 0])

    def swap_copy(j):
        return remote(
            grads[j].at[:, :, 1 - here.core], swaps[j], ffn_send.at[j, 0], ffn_recv.at[j, 0], here.core_peer
        )

    def near_copy(j, k):
        return remote(
            owns[j].at[z_at(2), k], nears[j].at[k], ffn_send.at[j, 1 + k], ffn_recv.at[j, 1 + k], side[k]
        )

    def far_copy(j, k):
        return remote(
            owns[j].at[z_at(1 if k == 0 else planes - 1)],
            fars[j].at[k],
            ffn_send.at[j, 3 + k],
            ffn_recv.at[j, 3 + k],
            side[k],
        )

    def plane_copy(j, number):
        x = here.x if number % 2 == 0 else 1 - here.x
        src, dst = owns[j].at[here.z, x], outs[j].at[here.expert(0)]
        if number == 0:
            return pltpu.make_async_copy(src, dst, ffn_local.at[j, 1])
        return remote(
            src, dst, ffn_send.at[j, 4 + number], ffn_recv.at[j, 4 + number], here.plane_peers[number]
        )

    def plane_arrival(j, number):
        dst = outs[j].at[here.expert(number)]
        return remote(
            dst, dst, ffn_send.at[j, 4 + number], ffn_recv.at[j, 4 + number], here.plane_peers[number]
        )

    def add(target, *sources):
        value = target[...].astype(F32)
        for source in sources:
            value = value + source[...].astype(F32)
        target[...] = value.astype(BF16)

    @pl.when(step == 0)
    def _():
        for j in range(3):
            own_copy(j).start()
        here.barrier([here.core_peer, here.x_peer, here.y_peer, here.xy_peer, side[0], side[1]])
        for number in range(1, 4):
            row_copy(0, 0, number).start()
        for j in range(3):
            swap_copy(j).start()
        for j in range(3):
            own_copy(j).wait()
            swap_copy(j).wait_recv()
            for x in range(2):

                def add_core(z, carry):
                    add(owns[j].at[z, x], swaps[j].at[z, x])
                    return carry

                lax.fori_loop(0, planes, add_core, 0)
            near_copy(j, 0).start()
            near_copy(j, 1).start()

    for member in range(batches):

        @pl.when(step == member)
        def _():
            for number in range(1, 4):
                row_copy(0, member, number).wait_recv()
            if member + 1 < batches:
                for number in range(1, 4):
                    row_copy(0, member + 1, number).start()
            else:
                for each in range(batches):
                    for number in range(4):
                        row_copy(1, each, number).start()
            for number in range(4):
                load_rows(member, number).start()
            for number in range(4):
                load_rows(member, number).wait()

    sequence_combine(
        step,
        [rows_ref.at[number] for number in range(4)],
        pos_ref,
        aux_ref,
        routes_ref,
        prev_ref,
        h_ref,
        g_ref,
        o_ref,
        small_ref,
        wo_ref,
        dh_ref,
        dob_ref,
        sgrad_ref,
        grad_map_ref,
        acc_wo_ref,
        cols_ref,
        here.expert,
    )

    @pl.when(step == 0)
    def _():
        for j in range(3):
            for k in range(2):
                near_copy(j, k).wait_recv()
                add(owns[j].at[z_at(1 if k == 0 else planes - 1), k], nears[j].at[k])
                far_copy(j, k).start()

    @pl.when(step == last)
    def _():
        for j in range(3):
            for k in range(2):
                far_copy(j, k).wait_recv()
            for x in range(2):
                add(owns[j].at[here.z, x], fars[j].at[0, x], fars[j].at[1, x])
            for number in range(4):
                plane_copy(j, number).start()

    sequence_backward(
        step,
        x_ref,
        seg_row_ref,
        seg_col_ref,
        q_ref,
        k_ref,
        v_ref,
        dob_ref,
        lse_ref,
        dh_ref,
        small_ref,
        wq_ref,
        wk_ref,
        wv_ref,
        cos_ref,
        sin_ref,
        gin_ref,
        gain_ref,
        bias_ref,
        lse_t_ref,
        dqkv_ref,
        acc_ref,
    )

    @pl.when(step == last)
    def _():
        table_ref[...] = small_table(depth, sgrad_ref, grad_map_ref, gain_ref)
        for j in range(3):
            swap_copy(j).wait_send()
            for k in range(2):
                near_copy(j, k).wait_send()
                far_copy(j, k).wait_send()
            plane_copy(j, 0).wait()
            for number in range(1, 4):
                plane_copy(j, number).wait_send()
                plane_arrival(j, number).wait_recv()
        for member in range(batches):
            row_copy(1, member, 0).wait()
            for number in range(1, 4):
                row_copy(0, member, number).wait_send()
                row_copy(1, member, number).wait()


def reduce_kernel(
    group,
    qkv_ref,
    wo_ref,
    small_ref,
    out_ref,
    full_ref,
    acc_ref,
    core_ref,
    y_first_ref,
    x_second_ref,
    x_first_ref,
    y_second_ref,
    z_ref,
    done_ref,
    other_ref,
    send,
    recv,
    z_send,
    z_recv,
):
    here = Place(group)
    planes = here.planes
    near = planes // 2
    depth, columns = acc_ref.shape[2:]
    half = columns // 2
    x, y = here.x, here.y
    mine = pl.ds(pl.multiple_of(y * half, LANES), half)
    theirs = pl.ds(pl.multiple_of((1 - y) * half, LANES), half)
    here.barrier(
        [here.core_peer, here.x_peer, here.y_peer] + [here.z_peer(k) for k in range(1, planes)]
    )
    width = wo_ref.shape[0]

    def lower(block, carry):
        rows = pl.ds(pl.multiple_of(block * depth, 16), depth)
        z, column, core = block // 4, (block // 2) % 2, block % 2
        full_ref[z, column, core, :, 0 : 3 * width] = qkv_ref[rows, :].astype(BF16)
        full_ref[z, column, core, :, 3 * width : 4 * width] = wo_ref[rows, :].astype(BF16)
        full_ref[z, column, core, :, 4 * width : 4 * width + LANES] = small_ref[rows, :]
        full_ref[z, column, core, :, 4 * width + LANES :] = jnp.zeros((depth, LANES), BF16)
        return carry

    lax.fori_loop(0, group, lower, 0)
    swap = remote(full_ref.at[:, :, 1 - here.core], core_ref, send.at[0], recv.at[0], here.core_peer)
    swap.start()
    swap.wait_recv()

    def add(target, source):
        target[...] = (target[...].astype(F32) + source[...].astype(F32)).astype(BF16)

    def add_core(z, carry):
        for column in range(2):
            mine_now = full_ref[z, column, here.core].astype(F32)
            acc_ref[z, column] = (mine_now + core_ref[z, column].astype(F32)).astype(BF16)
        return carry

    lax.fori_loop(0, planes, add_core, 0)
    y_first = remote(acc_ref.at[0:near, :, :, theirs], y_first_ref, send.at[1], recv.at[1], here.y_peer)
    x_first = remote(acc_ref.at[near:planes, 1 - x], x_first_ref, send.at[2], recv.at[2], here.x_peer)
    y_first.start()
    x_first.start()
    y_first.wait_recv()
    for z in range(near):
        for column in range(2):
            add(acc_ref.at[z, column, :, mine], y_first_ref.at[z, column])
    x_second = remote(acc_ref.at[0:near, 1 - x, :, mine], x_second_ref, send.at[3], recv.at[3], here.x_peer)
    x_second.start()
    x_first.wait_recv()
    for z in range(near, planes):
        add(acc_ref.at[z, x], x_first_ref.at[z - near])
    y_second = remote(acc_ref.at[near:planes, x, :, theirs], y_second_ref, send.at[4], recv.at[4], here.y_peer)
    y_second.start()
    x_second.wait_recv()
    for z in range(near):
        add(acc_ref.at[z, x, :, mine], x_second_ref.at[z])
    y_second.wait_recv()
    for z in range(near, planes):
        add(acc_ref.at[z, x, :, mine], y_second_ref.at[z - near])
    along = []
    for k in range(1, planes):
        to = (here.z + k) % planes
        along.append(
            remote(acc_ref.at[to, x, :, mine], z_ref.at[k - 1], z_send.at[k - 1], z_recv.at[k - 1], here.z_peer(k))
        )
        along[-1].start()
    total = acc_ref[here.z, x, :, mine].astype(F32)
    for k in range(1, planes):
        along[k - 1].wait_recv()
        total = total + z_ref[k - 1].astype(F32)
    done_ref[...] = total.astype(BF16)
    back = remote(done_ref, other_ref, send.at[5], recv.at[5], here.y_peer)
    back.start()
    out_ref[:, mine] = done_ref[...].astype(F32)
    back.wait_recv()
    out_ref[:, theirs] = other_ref[...].astype(F32)
    for copy in [swap, y_first, x_first, x_second, y_second, back] + along:
        copy.wait_send()


def params(limit_mib):
    return pltpu.CompilerParams(vmem_limit_bytes=limit_mib * 1024 * 1024, dimension_semantics=("arbitrary",))


def rotary(length):
    halfway = HEAD_DIM // 2
    frequency = 10000.0 ** (-jnp.arange(halfway).astype(F32) / halfway)
    angles = jnp.arange(length).astype(F32)[:, None] * frequency[None, :]
    cosine, sine = jnp.cos(angles), jnp.sin(angles)
    return (
        jnp.concatenate([cosine] * 4, axis=1),
        jnp.concatenate([-sine, sine, -sine, sine], axis=1),
    )


def local(
    reps,
    group,
    block_input,
    prev_logits,
    routes,
    segments,
    grad_out,
    gain_attn,
    w_query,
    w_key,
    w_value,
    w_output,
    gain_mix,
    router,
    route_map,
    const_proj,
    const_vec,
    w_gate,
    w_up,
    w_down,
):
    batches, length = segments.shape
    width = block_input.shape[1]
    kinds = router.shape[1]
    ffn = w_gate.shape[1]
    hidden = w_gate.shape[2]
    rows_d = w_gate.shape[0]
    rows_f = w_down.shape[0]
    capacity = length // 2
    planes = group // 4
    assert reps == 2 and ffn == 4 and group % 4 == 0
    g = lax.axis_index("grp")
    y = lax.axis_index("rep")
    core = g % 2
    x = (g // 2) % 2
    z = g // 4
    own = (2 * y + x).astype(jnp.int32)
    own_arr = own.reshape(1)

    x_flip = [(i, i ^ 2) for i in range(group)]
    core_flip = [(i, i ^ 1) for i in range(group)]
    y_flip = [(0, 1), (1, 0)]
    xy_flip = [(r * group + i, (1 - r) * group + (i ^ 2)) for r in range(2) for i in range(group)]

    def z_shift(k):
        return [(i, (i + 4 * k) % group) for i in range(group)]

    def to_plane(parts):
        return [
            parts[0],
            lax.ppermute(parts[1], "grp", x_flip),
            lax.ppermute(parts[2], "rep", y_flip),
            lax.ppermute(parts[3], ("rep", "grp"), xy_flip),
        ]

    tokens = block_input.reshape(batches, length, width)
    grads = grad_out.reshape(batches, length, width)
    route_cols = routes.reshape(batches, length, 2)
    route_rows = route_cols.transpose(0, 2, 1)
    prev_rows = prev_logits.reshape(batches, length, kinds).transpose(0, 2, 1)
    seg_row = segments[:, None, :]
    seg_col = segments[:, :, None]
    cos, sin = rotary(length)

    def spec_w(j):
        return pl.BlockSpec((width, width), lambda b, *_: (0, j), pipeline_mode=pl.Buffered(1))

    row_shape = jax.ShapeDtypeStruct((batches, capacity, width), BF16)
    seq_bf16 = jax.ShapeDtypeStruct((batches, length, width), BF16)
    seq_f32 = jax.ShapeDtypeStruct((batches, length, width), F32)
    small_shard = jnp.concatenate(
        [router, const_proj, const_vec, gain_attn[:, None], gain_mix[:, None]], axis=1
    ).astype(BF16)
    small_shard = jnp.pad(small_shard, ((0, 0), (0, 2 * LANES - small_shard.shape[1])))
    shard = jnp.concatenate([w.astype(BF16) for w in (w_query, w_key, w_value)] + [small_shard], axis=1)
    shard_o = w_output.astype(BF16)
    fused = planes == 4 and rows_d % 16 == 0 and rows_f % 16 == 0
    if fused:
        any_space = pl.BlockSpec(memory_space=pl.ANY)
        out_struct = jax.ShapeDtypeStruct
        (
            q, k, v, o, h1, lse, aux, pos, small, attn, attn_o, a_rows, grad_rows, gate_full, up_full, down_full,
        ) = pl.pallas_call(
            functools.partial(fused_forward_kernel, group),
            grid=(batches,),
            in_specs=[
                per_seq((length, width)),
                per_seq((1, length)),
                per_seq((length, 1)),
                whole((batches, 2, length)),
                per_seq((kinds, length)),
                whole((kinds, kinds)),
                whole((batches, length, width)),
                whole((length, LANES)),
                whole((length, LANES)),
            ]
            + [any_space] * 5,
            out_specs=[per_seq((length, width))] * 5
            + [
                per_seq((length, LANES)),
                per_seq((16, length)),
                whole((batches, kinds, length)),
                whole((kinds + 8, width)),
            ]
            + [any_space] * 7,
            scratch_shapes=[
                pltpu.VMEM((width, 3 * width + 2 * LANES), BF16),
                pltpu.VMEM((width, width), BF16),
                pltpu.VMEM((length, length), F32),
                pltpu.VMEM((length, width), F32),
                pltpu.VMEM((batches, 4, capacity + 16, width), BF16),
                pltpu.VMEM((batches, 4, capacity, width), BF16),
                pltpu.SemaphoreType.DMA((2,)),
                pltpu.SemaphoreType.DMA((2, 4 + 4 * planes)),
                pltpu.SemaphoreType.DMA((2, 4 + 4 * planes)),
                pltpu.SemaphoreType.DMA((3,)),
                pltpu.SemaphoreType.DMA((3, 5 + planes)),
                pltpu.SemaphoreType.DMA((3, 5 + planes)),
                pltpu.SemaphoreType.DMA((2,)),
                pltpu.SemaphoreType.DMA((2, batches)),
                pltpu.SemaphoreType.DMA((2, batches, 4)),
                pltpu.SemaphoreType.DMA((2, batches, 4)),
            ],
            out_shape=[seq_bf16] * 4
            + [
                seq_f32,
                out_struct((batches, length, LANES), F32),
                out_struct((batches, 16, length), F32),
                out_struct((batches, kinds, length), F32),
                out_struct((kinds + 8, width), F32),
                out_struct((width, 3 * width + 2 * LANES), BF16),
                out_struct((width, width), BF16),
                out_struct((4, batches, capacity + 16, width), BF16),
                out_struct((4, batches, capacity, width), BF16),
                out_struct((planes, 2, 2, rows_d, hidden), BF16),
                out_struct((planes, 2, 2, rows_d, hidden), BF16),
                out_struct((planes, 2, 2, rows_f, width), BF16),
            ],
            compiler_params=pltpu.CompilerParams(
                vmem_limit_bytes=58 * 1024 * 1024,
                dimension_semantics=("arbitrary",),
                collective_id=1,
                has_side_effects=True,
            ),
            cost_estimate=pl.CostEstimate(flops=40 * 10**9, bytes_accessed=60 * 10**6, transcendentals=10**7),
            name="fused_forward",
        )(
            tokens, seg_row, seg_col, route_rows, prev_rows, route_map.T, grads, cos, sin,
            shard, shard_o,
            w_gate.astype(BF16).transpose(1, 0, 2),
            w_up.astype(BF16).transpose(1, 0, 2),
            w_down.astype(BF16).transpose(1, 0, 2),
        )
        gate_full = gate_full.reshape(width, hidden)
        up_full = up_full.reshape(width, hidden)
        down_full = down_full.reshape(hidden, width)
    else:
        attn = lax.all_gather(shard, "grp", axis=0, tiled=True)
        attn_o = lax.all_gather(shard_o, "grp", axis=0, tiled=True)
        small = attn[:, 3 * width : 3 * width + kinds + 8].astype(F32).T

        def pick(array, expert):
            return lax.dynamic_index_in_dim(array, expert, axis=1, keepdims=False)

        def gather_expert(mine, other):
            crossed = lax.ppermute(other, "grp", x_flip)
            both = jnp.where(x == 0, jnp.stack([mine, crossed]), jnp.stack([crossed, mine]))
            pieces = [both] + [lax.ppermute(both, "grp", z_shift(k)) for k in range(1, planes)]
            stacked = jnp.stack(pieces)
            half = jnp.take(stacked, (z - jnp.arange(planes)) % planes, axis=0)
            swapped = lax.ppermute(half, "grp", core_flip)
            return jnp.where(core == 0, jnp.stack([half, swapped], axis=2), jnp.stack([swapped, half], axis=2))

        gate_up = gather_expert(
            jnp.stack([pick(w_gate, own), pick(w_up, own)]).astype(BF16),
            jnp.stack([pick(w_gate, own ^ 1), pick(w_up, own ^ 1)]).astype(BF16),
        )
        down = gather_expert(pick(w_down, own).astype(BF16), pick(w_down, own ^ 1).astype(BF16))
        gate_full = gate_up[:, :, :, 0].reshape(width, hidden)
        up_full = gate_up[:, :, :, 1].reshape(width, hidden)
        down_full = down.reshape(hidden, width)

        *grad_rows, pos = pl.pallas_call(
            grad_rows_kernel,
            grid_spec=pltpu.PrefetchScalarGridSpec(
                num_scalar_prefetch=1,
                grid=(batches,),
                in_specs=[per_seq((2, length)), per_seq((length, width))],
                out_specs=[per_seq((capacity, width))] * 4 + [per_seq((kinds, length))],
            ),
            out_shape=[row_shape] * 4 + [jax.ShapeDtypeStruct((batches, kinds, length), F32)],
            compiler_params=params(32),
            cost_estimate=pl.CostEstimate(flops=4 * 10**9, bytes_accessed=8 * 10**6, transcendentals=0),
            name="grad_rows",
        )(own_arr, route_rows, grads)
        grad_rows = to_plane(grad_rows)

        q, k, v, o, h1, lse, aux, *a_rows = pl.pallas_call(
            forward_kernel,
            grid_spec=pltpu.PrefetchScalarGridSpec(
                num_scalar_prefetch=1,
                grid=(batches,),
                in_specs=[
                    per_seq((length, width)),
                    per_seq((1, length)),
                    per_seq((length, 1)),
                    per_seq((2, length)),
                    per_seq((kinds, length)),
                    whole((kinds, kinds)),
                    whole((kinds + 8, width)),
                    spec_w(0),
                    spec_w(1),
                    spec_w(2),
                    spec_w(0),
                    whole((length, LANES)),
                    whole((length, LANES)),
                    per_seq((kinds, length)),
                ],
                out_specs=[per_seq((length, width))] * 5
                + [per_seq((length, LANES)), per_seq((16, length))]
                + [per_seq((capacity + 16, width))] * 4,
                scratch_shapes=[pltpu.VMEM((length, length), F32), pltpu.VMEM((length, width), F32)],
            ),
            out_shape=[seq_bf16] * 4
            + [
                seq_f32,
                jax.ShapeDtypeStruct((batches, length, LANES), F32),
                jax.ShapeDtypeStruct((batches, 16, length), F32),
            ]
            + [jax.ShapeDtypeStruct((batches, capacity + 16, width), BF16)] * 4,
            compiler_params=params(56),
            cost_estimate=pl.CostEstimate(flops=20 * 10**9, bytes_accessed=20 * 10**6, transcendentals=10**7),
            name="forward",
        )(own_arr, tokens, seg_row, seg_col, route_rows, prev_rows, route_map.T, small, attn, attn, attn, attn_o, cos, sin, pos)
        a_rows = to_plane(a_rows)

        a_rows = jnp.stack(a_rows)
        grad_rows = jnp.stack(grad_rows)

    tile = hidden // 4
    total = 4 * batches * capacity
    any_spec = pl.BlockSpec(memory_space=pl.ANY)
    values, input_rows, grad_gate_full, grad_up_full, grad_down_full = pl.pallas_call(
        expert_kernel,
        grid=(hidden // tile,),
        in_specs=[any_spec] * 2
        + [
            pl.BlockSpec((width, tile), lambda f: (0, f)),
            pl.BlockSpec((width, tile), lambda f: (0, f)),
            pl.BlockSpec((tile, width), lambda f: (f, 0)),
        ],
        out_specs=[any_spec] * 2
        + [
            pl.BlockSpec((width, tile), lambda f: (0, f)),
            pl.BlockSpec((width, tile), lambda f: (0, f)),
            pl.BlockSpec((tile, width), lambda f: (f, 0)),
        ],
        scratch_shapes=[
            pltpu.VMEM((total + capacity, width), BF16),
            pltpu.VMEM((total + capacity, width), BF16),
            pltpu.VMEM((4 * batches, 16, capacity), BF16),
            pltpu.VMEM((width, total), BF16),
            pltpu.VMEM((width, total), BF16),
            pltpu.SMEM((4 * batches + 1,), jnp.int32),
            pltpu.VMEM((total, width), F32),
            pltpu.VMEM((total, width), F32),
            pltpu.VMEM((width, tile), F32),
            pltpu.VMEM((width, tile), F32),
            pltpu.VMEM((width, tile), F32),
            pltpu.VMEM((total + capacity, LANES), F32),
            pltpu.SemaphoreType.DMA((12 * batches,)),
        ],
        out_shape=[
            jax.ShapeDtypeStruct((4, batches, capacity, width), BF16),
            jax.ShapeDtypeStruct((4, batches, capacity + 16, width), BF16),
        ]
        + [
            jax.ShapeDtypeStruct((width, hidden), BF16),
            jax.ShapeDtypeStruct((width, hidden), BF16),
            jax.ShapeDtypeStruct((hidden, width), BF16),
        ],
        compiler_params=params(60),
        cost_estimate=pl.CostEstimate(flops=58 * 10**9, bytes_accessed=40 * 10**6, transcendentals=10**7),
        name="expert",
    )(a_rows, grad_rows, gate_full, up_full, down_full)
    if fused:
        columns = 4 * width + 2 * LANES
        once = lambda shape: pl.BlockSpec(
            (1,) + shape, lambda b, *_: (b, 0, 0), pipeline_mode=pl.Buffered(1)
        )
        wide = ((rows_d, hidden), (rows_d, hidden), (rows_f, width))
        gin, grad_qkv, grad_wo, grad_small, _, values_in, grad_gate, grad_up, grad_down = pl.pallas_call(
            functools.partial(fused_backward_kernel, group, rows_d),
            grid=(batches,),
            in_specs=[
                per_seq((kinds, length)),
                per_seq((16, length)),
                per_seq((length, 2)),
                per_seq((kinds, length)),
                once((length, width)),
                once((length, width)),
                once((length, width)),
                once((length, width)),
                per_seq((1, length)),
                per_seq((length, 1)),
                once((length, width)),
                once((length, width)),
                once((length, width)),
                per_seq((length, LANES)),
                whole((kinds + 8, width), 1),
                spec_w(0),
                spec_w(1),
                spec_w(2),
                spec_w(0),
                whole((length, LANES), 1),
                whole((length, LANES), 1),
            ]
            + [any_spec] * 5,
            out_specs=[
                per_seq((length, width)),
                whole((width, 3 * width), 1),
                whole((width, width), 1),
                whole((width, LANES), 1),
            ]
            + [any_spec] * 5,
            out_shape=[
                seq_f32,
                jax.ShapeDtypeStruct((width, 3 * width), F32),
                jax.ShapeDtypeStruct((width, width), F32),
                jax.ShapeDtypeStruct((width, LANES), BF16),
                jax.ShapeDtypeStruct((4, batches, capacity + 16, width), BF16),
                jax.ShapeDtypeStruct((4, batches, capacity, width), BF16),
            ]
            + [jax.ShapeDtypeStruct((4,) + shape, BF16) for shape in wide],
            scratch_shapes=[
                pltpu.VMEM((LANES, length), F32),
                pltpu.VMEM((1, length, width), F32),
                pltpu.VMEM((1, length, width), BF16),
                pltpu.VMEM((16, width), F32),
                pltpu.VMEM((kinds, LANES), F32),
                pltpu.VMEM((8, width), F32),
                pltpu.VMEM((length, length), F32),
                pltpu.VMEM((LANES, length), F32),
                pltpu.VMEM((length, 3 * width), BF16),
                pltpu.VMEM((4, 1, capacity + 16, width), BF16),
            ]
            + [pltpu.VMEM((planes, 2) + shape, BF16) for shape in wide]
            + [pltpu.VMEM((planes, 2) + shape, BF16) for shape in wide]
            + [pltpu.VMEM((2,) + shape, BF16) for shape in wide]
            + [pltpu.VMEM((2, 2) + shape, BF16) for shape in wide]
            + [
                pltpu.SemaphoreType.DMA((5 * batches,)),
                pltpu.SemaphoreType.DMA((2, batches, 4)),
                pltpu.SemaphoreType.DMA((2, batches, 4)),
                pltpu.SemaphoreType.DMA((3, 2)),
                pltpu.SemaphoreType.DMA((3, 8)),
                pltpu.SemaphoreType.DMA((3, 8)),
            ],
            compiler_params=pltpu.CompilerParams(
                vmem_limit_bytes=60 * 1024 * 1024,
                dimension_semantics=("arbitrary",),
                collective_id=3,
                has_side_effects=True,
            ),
            cost_estimate=pl.CostEstimate(flops=60 * 10**9, bytes_accessed=60 * 10**6, transcendentals=10**7),
            name="fused_backward",
        )(
            pos, aux, route_cols, prev_rows, h1, grads, o, tokens, seg_row, seg_col, q, k, v, lse, small,
            attn, attn, attn, attn_o, cos, sin, input_rows, values,
            grad_gate_full.reshape(planes, 2, 2, rows_d, hidden),
            grad_up_full.reshape(planes, 2, 2, rows_d, hidden),
            grad_down_full.reshape(planes, 2, 2, rows_f, width),
        )
        grad_gate = grad_gate.transpose(1, 0, 2).astype(F32)
        grad_up = grad_up.transpose(1, 0, 2).astype(F32)
        grad_down = grad_down.transpose(1, 0, 2).astype(F32)
    else:
        values_in = jnp.stack(to_plane([values[i] for i in range(4)]))
        def scatter_expert(full):
            keep = lax.dynamic_index_in_dim(full, core, axis=2, keepdims=False)
            send = lax.dynamic_index_in_dim(full, 1 - core, axis=2, keepdims=False)
            half = (keep.astype(F32) + lax.ppermute(send, "grp", core_flip).astype(F32)).astype(BF16)
            summed = lax.dynamic_index_in_dim(half, z, axis=0, keepdims=False).astype(F32)
            for k in range(1, planes):
                part = lax.dynamic_index_in_dim(half, (z + k) % planes, axis=0, keepdims=False)
                summed = summed + lax.ppermute(part, "grp", z_shift(k)).astype(F32)
            summed = summed.astype(BF16)
            mine = lax.dynamic_index_in_dim(summed, x, axis=0, keepdims=False)
            other = lax.dynamic_index_in_dim(summed, 1 - x, axis=0, keepdims=False)
            arrived = to_plane([mine, other, mine, other])

            def order(first):
                return lambda: tuple(arrived[first ^ e] for e in range(4))

            return lax.switch(own, [order(i) for i in range(4)])

        grad_gate_up = scatter_expert(
            jnp.stack(
                [
                    grad_gate_full.reshape(planes, 2, 2, rows_d, hidden),
                    grad_up_full.reshape(planes, 2, 2, rows_d, hidden),
                ],
                axis=3,
            )
        )
        grad_down = scatter_expert(grad_down_full.reshape(planes, 2, 2, rows_f, width))
        grad_gate = jnp.stack([part[0] for part in grad_gate_up], axis=1).astype(F32)
        grad_up = jnp.stack([part[1] for part in grad_gate_up], axis=1).astype(F32)
        grad_down = jnp.stack(grad_down, axis=1).astype(F32)

        dh1, dob, grad_wo, sgrad, grad_map = pl.pallas_call(
            combine_kernel,
            grid_spec=pltpu.PrefetchScalarGridSpec(
                num_scalar_prefetch=1,
                grid=(batches,),
                in_specs=[per_seq((capacity + 16, width))] * 4
                + [
                    per_seq((kinds, length)),
                    per_seq((16, length)),
                    per_seq((length, 2)),
                    per_seq((kinds, length)),
                    per_seq((length, width)),
                    per_seq((length, width)),
                    per_seq((length, width)),
                    whole((kinds + 8, width)),
                    spec_w(0),
                ],
                out_specs=[per_seq((length, width))] * 2
                + [whole((width, width)), whole((16, width)), whole((kinds, LANES))],
                scratch_shapes=[pltpu.VMEM((width, width), F32), pltpu.VMEM((LANES, length), F32)],
            ),
            out_shape=[
                seq_f32,
                seq_bf16,
                jax.ShapeDtypeStruct((width, width), BF16),
                jax.ShapeDtypeStruct((16, width), F32),
                jax.ShapeDtypeStruct((kinds, LANES), F32),
            ],
            compiler_params=params(56),
            cost_estimate=pl.CostEstimate(flops=12 * 10**9, bytes_accessed=20 * 10**6, transcendentals=10**5),
            name="combine",
        )(own_arr, *to_plane([input_rows[i] for i in range(4)]), pos, aux, route_cols, prev_rows, h1, grads, o, small, attn_o)

        gin, grad_attn, gain_one = pl.pallas_call(
            backward_kernel,
            grid=(batches,),
            in_specs=[
                per_seq((length, width)),
                per_seq((1, length)),
                per_seq((length, 1)),
                per_seq((length, width)),
                per_seq((length, width)),
                per_seq((length, width)),
                per_seq((length, width)),
                per_seq((length, LANES)),
                per_seq((length, width)),
                whole((kinds + 8, width)),
                spec_w(0),
                spec_w(1),
                spec_w(2),
                whole((length, LANES)),
                whole((length, LANES)),
            ],
            out_specs=[per_seq((length, width)), whole((width, 3 * width)), whole((8, width))],
            scratch_shapes=[
                pltpu.VMEM((length, length), F32),
                pltpu.VMEM((LANES, length), F32),
                pltpu.VMEM((length, 3 * width), BF16),
                pltpu.VMEM((width, 3 * width), F32),
            ],
            out_shape=[
                seq_f32,
                jax.ShapeDtypeStruct((width, 3 * width), BF16),
                jax.ShapeDtypeStruct((8, width), F32),
            ],
            compiler_params=params(56),
            cost_estimate=pl.CostEstimate(flops=30 * 10**9, bytes_accessed=20 * 10**6, transcendentals=10**7),
            name="backward",
        )(tokens, seg_row, seg_col, q, k, v, dob, lse, dh1, small, attn, attn, attn, cos, sin)

    result = pl.pallas_call(
        result_kernel,
        grid_spec=pltpu.PrefetchScalarGridSpec(
            num_scalar_prefetch=1,
            grid=(batches,),
            in_specs=[
                pl.BlockSpec((4, 1, capacity, width), lambda b, *_: (0, b, 0, 0)),
                per_seq((kinds, length)),
                per_seq((16, length)),
                per_seq((length, width)),
                whole((kinds + 8, width)),
            ],
            out_specs=per_seq((length, width)),
            scratch_shapes=[pltpu.VMEM((LANES, length), F32)],
        ),
        out_shape=seq_f32,
        compiler_params=params(40),
        cost_estimate=pl.CostEstimate(flops=4 * 10**9, bytes_accessed=12 * 10**6, transcendentals=0),
        name="result",
    )(own_arr, values_in, pos, aux, h1, small)

    if fused:
        near = planes // 2
        sums = pl.pallas_call(
            functools.partial(reduce_kernel, group),
            in_specs=[pl.BlockSpec(memory_space=pltpu.VMEM)] * 3,
            out_specs=pl.BlockSpec(memory_space=pltpu.VMEM),
            out_shape=jax.ShapeDtypeStruct((rows_d, columns), F32),
            scratch_shapes=[
                pltpu.VMEM((planes, 2, 2, rows_d, columns), BF16),
                pltpu.VMEM((planes, 2, rows_d, columns), BF16),
                pltpu.VMEM((planes, 2, rows_d, columns), BF16),
                pltpu.VMEM((near, 2, rows_d, columns // 2), BF16),
                pltpu.VMEM((near, rows_d, columns // 2), BF16),
                pltpu.VMEM((near, rows_d, columns), BF16),
                pltpu.VMEM((near, rows_d, columns // 2), BF16),
                pltpu.VMEM((planes - 1, rows_d, columns // 2), BF16),
                pltpu.VMEM((rows_d, columns // 2), BF16),
                pltpu.VMEM((rows_d, columns // 2), BF16),
                pltpu.SemaphoreType.DMA((6,)),
                pltpu.SemaphoreType.DMA((6,)),
                pltpu.SemaphoreType.DMA((planes - 1,)),
                pltpu.SemaphoreType.DMA((planes - 1,)),
            ],
            compiler_params=pltpu.CompilerParams(
                vmem_limit_bytes=40 * 1024 * 1024, collective_id=2, has_side_effects=True
            ),
            name="reduce",
        )(grad_qkv, grad_wo, grad_small)
        attn_total = sums[:, 0 : 4 * width]
        sums = sums[:, 4 * width :]
        map_total = sums[0:kinds, 16 : 16 + kinds]
    else:
        part = lax.psum_scatter(jnp.concatenate([grad_attn, grad_wo], axis=1), "grp", scatter_dimension=0, tiled=True)
        attn_total = lax.psum(part, "rep").astype(F32)
        sgrad = jnp.where(iota((16, 1), 0) == kinds + 6, gain_one[0:1], sgrad)
        packed = jnp.concatenate([sgrad, jnp.pad(grad_map, ((0, 0), (0, width - LANES)))], axis=0)
        packed = lax.psum(packed, ("rep", "grp"))
        sums = lax.dynamic_slice_in_dim(packed[0:16], g * rows_d, rows_d, axis=1).T
        map_total = packed[16:, 0:kinds].T
    return (
        result.reshape(batches * length, width),
        gin.reshape(batches * length, width),
        sums[:, kinds + 6],
        attn_total[:, 0:width],
        attn_total[:, width : 2 * width],
        attn_total[:, 2 * width : 3 * width],
        attn_total[:, 3 * width :],
        sums[:, kinds + 7],
        sums[:, 0:kinds],
        map_total,
        sums[:, kinds : kinds + 4],
        sums[:, kinds + 4 : kinds + 6],
        grad_gate,
        grad_up,
        grad_down,
    )


def solution(mesh):
    rows = P(("rep", "grp"), None)
    in_specs = (
        (rows,) * 5
        + (P("grp"),)
        + (P("grp", None),) * 4
        + (P("grp"), P("grp", None), P(), P("grp", None), P("grp", None))
        + (P("grp", None, None),) * 3
    )
    out_specs = (
        (rows,) * 2
        + (P("grp"),)
        + (P("grp", None),) * 4
        + (P("grp"), P("grp", None), P(), P("grp", None), P("grp", None))
        + (P("grp", None, None),) * 3
    )
    body = functools.partial(local, mesh.shape["rep"], mesh.shape["grp"])
    return jax.shard_map(body, mesh=mesh, in_specs=in_specs, out_specs=out_specs, check_vma=False)
```

```python
import functools

import jax
import jax.numpy as jnp
from jax import lax
from jax.experimental import pallas as pl
from jax.experimental.pallas import tpu as pltpu
from jax.sharding import PartitionSpec as P

HEAD_DIM = 64
BLOCK = 256
EPS = 1e-05
NEG = -1000000000.0
F32 = jnp.float32
BF16 = jnp.bfloat16
LANES = 128


def nn(a, b):
    return lax.dot_general(a, b, (((1,), (0,)), ((), ())), preferred_element_type=F32)


def nt(a, b):
    return lax.dot_general(a, b, (((1,), (1,)), ((), ())), preferred_element_type=F32)


def tn(a, b):
    return lax.dot_general(a, b, (((0,), (0,)), ((), ())), preferred_element_type=F32)


def iota(shape, dim):
    return lax.broadcasted_iota(jnp.int32, shape, dim)


def split2(values):
    high = values.astype(BF16)
    low = (values - high.astype(F32)).astype(BF16)
    return high, low


def whole(shape, buffers=None):
    zeros = (0,) * len(shape)
    if buffers:
        return pl.BlockSpec(shape, lambda *_: zeros, pipeline_mode=pl.Buffered(buffers))
    return pl.BlockSpec(shape, lambda *_: zeros)


def per_seq(shape):
    tail = (0,) * len(shape)
    return pl.BlockSpec((1,) + shape, lambda b, *_: (b,) + tail)


def rms_scale(values):
    return lax.rsqrt(jnp.mean(values * values, axis=-1, keepdims=True) + EPS)


def slot_mask(position_row, capacity):
    places = iota((capacity, position_row.shape[1]), 0).astype(F32)
    return jnp.where(places == position_row, 1.0, 0.0).astype(BF16)


def grad_rows_kernel(own_ref, routes_ref, grad_ref, r0, r1, r2, r3, pos_ref):
    own = own_ref[0]
    kinds, length = pos_ref.shape[1:]
    capacity = r0.shape[1]
    ids = iota((kinds, length), 0)
    first = routes_ref[0, 0:1, :] == ids
    second = routes_ref[0, 1:2, :] == ids
    hits = jnp.where(first | second, 1.0, 0.0)
    before = jnp.where(iota((length, length), 0) < iota((length, length), 1), 1.0, 0.0)
    slots = nn(hits.astype(BF16), before.astype(BF16))
    pos_ref[0] = jnp.where(hits > 0.0, slots, -1.0)
    for number, rows in enumerate((r0, r1, r2, r3)):
        line = pos_ref[0, pl.ds(own ^ number, 1), :]
        rows[0] = nn(slot_mask(line, capacity), grad_ref[0]).astype(BF16)


def swap_halves(values, low_half):
    return jnp.where(low_half, pltpu.roll(values, 96, 1), pltpu.roll(values, 32, 1))


def sequence_forward(
    x_ref,
    seg_row_ref,
    seg_col_ref,
    routes_ref,
    prev_ref,
    map_ref,
    small_ref,
    wq_ref,
    wk_ref,
    wv_ref,
    wo_ref,
    cos_ref,
    sin_ref,
    pos_ref,
    q_ref,
    k_ref,
    v_ref,
    o_ref,
    h_ref,
    lse_ref,
    aux_ref,
    rows_refs,
    bias_ref,
    proj_ref,
    expert_of,
    between=None,
):
    length, width = x_ref.shape[1:]
    kinds = pos_ref.shape[1]
    capacity = length // 2
    tokens = x_ref[0].astype(F32)
    gain_one = small_ref[kinds + 6 : kinds + 7, :]
    gain_two = small_ref[kinds + 7 : kinds + 8, :]
    a1 = (tokens * rms_scale(tokens) * gain_one).astype(BF16)
    lane = iota((1, LANES), 1)
    low_half = (lane % HEAD_DIM) < (HEAD_DIM // 2)
    first_head = lane < HEAD_DIM
    mask_a = jnp.where(first_head, 1.0, 0.0).astype(BF16)
    mask_b = jnp.where(first_head, 0.0, 1.0).astype(BF16)
    pairs = width // LANES

    for weights, target, scale in ((wq_ref, q_ref, 0.125), (wk_ref, k_ref, 1.0)):
        proj_ref[...] = nn(a1, weights[...])

        def turn(h, carry):
            cols = pl.ds(pl.multiple_of(h * LANES, LANES), LANES)
            part = proj_ref[:, cols]
            turned = part * cos_ref[...] + swap_halves(part, low_half) * sin_ref[...]
            target[0, :, cols] = turned.astype(BF16) * jnp.asarray(scale, BF16)
            return carry

        lax.fori_loop(0, pairs, turn, 0)
    v_ref[0] = nn(a1, wv_ref[...]).astype(BF16)

    allowed = (seg_col_ref[0] == seg_row_ref[0]) & (
        iota((length, length), 1) // BLOCK <= iota((length, length), 0) // BLOCK
    )
    bias_ref[...] = jnp.where(allowed, 0.0, NEG)
    lse_ref[...] = jnp.zeros_like(lse_ref)
    if between is not None:
        between()

    def pair(h, carry):
        cols = pl.ds(pl.multiple_of(h * LANES, LANES), LANES)
        for begin in range(0, length, BLOCK):
            end = begin + BLOCK
            queries = q_ref[0, begin:end, cols]
            keys = k_ref[0, 0:end, cols]
            values = v_ref[0, 0:end, cols]
            bias = bias_ref[begin:end, 0:end]
            sums = lse_ref[0, begin:end, :]
            outs = []
            for half, mask in enumerate((mask_a, mask_b)):
                scores = nt(queries * mask, keys) + bias
                top = jnp.max(scores, axis=-1, keepdims=True)
                grown = jnp.exp(scores - top)
                total = jnp.sum(grown, axis=-1, keepdims=True)
                chances = (grown * (1.0 / total)).astype(BF16)
                outs.append(nn(chances, values))
                sums = jnp.where(lane == 2 * h + half, top + jnp.log(total), sums)
            lse_ref[0, begin:end, :] = sums
            o_ref[0, begin:end, cols] = jnp.where(first_head, outs[0], outs[1]).astype(BF16)
        return carry

    lax.fori_loop(0, pairs, pair, 0)

    hidden = tokens + nn(o_ref[0], wo_ref[...])
    h_ref[0] = hidden
    a2 = (hidden * rms_scale(hidden) * gain_two).astype(BF16)
    logits = nt(small_ref[...].astype(BF16), a2)[0:kinds, :]
    for j in range(kinds):
        logits = logits + map_ref[:, j : j + 1] * prev_ref[0, j : j + 1, :]
    ids = iota((kinds, length), 0)
    first = jnp.where(routes_ref[0, 0:1, :] == ids, 1.0, 0.0)
    second = jnp.where(routes_ref[0, 1:2, :] == ids, 1.0, 0.0)
    one = jnp.sum(logits * first, axis=0, keepdims=True)
    two = jnp.sum(logits * second, axis=0, keepdims=True)
    top = jnp.maximum(one, two)
    grown_one, grown_two = jnp.exp(one - top), jnp.exp(two - top)
    gate_one = grown_one / (grown_one + grown_two)
    gate_two = grown_two / (grown_one + grown_two)
    aux_ref[0, 0:kinds, :] = gate_one * first + gate_two * second
    aux_ref[0, kinds : kinds + 1, :] = gate_one
    aux_ref[0, kinds + 1 : kinds + 2, :] = gate_two
    aux_ref[0, kinds + 2 :, :] = jnp.zeros((aux_ref.shape[1] - kinds - 2, length), F32)

    place = iota((16, length), 0)
    for number, rows in enumerate(rows_refs):
        mask = slot_mask(pos_ref[0, pl.ds(expert_of(number), 1), :], capacity)
        rows[0, 0:capacity, :] = nn(mask, a2).astype(BF16)
        line = aux_ref[0, pl.ds(expert_of(number), 1), :]
        high = line.astype(BF16).astype(F32)
        mid = (line - high).astype(BF16).astype(F32)
        low = line - high - mid
        parts = jnp.where(place == 0, high, jnp.where(place == 1, mid, jnp.where(place == 2, low, 0.0)))
        spread = nt(parts.astype(BF16), mask)
        filled = jnp.max(pos_ref[0, pl.ds(expert_of(number), 1), :], axis=1, keepdims=True) + 1.0
        spread = jnp.where(iota((16, 1), 0) == 3, filled, spread)
        rows[0, capacity:, 0:capacity] = spread.astype(BF16)
        rows[0, capacity:, capacity:] = jnp.zeros((16, width - capacity), BF16)


def forward_kernel(
    own_ref,
    x_ref,
    seg_row_ref,
    seg_col_ref,
    routes_ref,
    prev_ref,
    map_ref,
    small_ref,
    wq_ref,
    wk_ref,
    wv_ref,
    wo_ref,
    cos_ref,
    sin_ref,
    pos_ref,
    q_ref,
    k_ref,
    v_ref,
    o_ref,
    h_ref,
    lse_ref,
    aux_ref,
    r0,
    r1,
    r2,
    r3,
    bias_ref,
    proj_ref,
):
    own = own_ref[0]
    sequence_forward(
        x_ref,
        seg_row_ref,
        seg_col_ref,
        routes_ref,
        prev_ref,
        map_ref,
        small_ref,
        wq_ref,
        wk_ref,
        wv_ref,
        wo_ref,
        cos_ref,
        sin_ref,
        pos_ref,
        q_ref,
        k_ref,
        v_ref,
        o_ref,
        h_ref,
        lse_ref,
        aux_ref,
        (r0, r1, r2, r3),
        bias_ref,
        proj_ref,
        lambda number: own ^ number,
    )


MESH = pl.DeviceIdType.MESH


class Place:
    def __init__(self, group):
        self.group = group
        self.planes = group // 4
        self.g = lax.axis_index("grp")
        self.y = lax.axis_index("rep")
        self.core = self.g % 2
        self.x = (self.g // 2) % 2
        self.z = self.g // 4
        self.core_peer = (self.y, self.g + 1 - 2 * self.core)
        self.x_peer = (self.y, self.g + 2 - 4 * self.x)
        self.y_peer = (1 - self.y, self.g)
        self.xy_peer = (1 - self.y, self.g + 2 - 4 * self.x)
        self.plane_peers = (None, self.x_peer, self.y_peer, self.xy_peer)

    def z_peer(self, k):
        return (self.y, (self.g + 4 * k) % self.group)

    def block(self, z, x, core):
        return (z * 2 + x) * 2 + core

    def expert(self, number):
        y = self.y if number < 2 else 1 - self.y
        x = self.x if number % 2 == 0 else 1 - self.x
        return 2 * y + x

    def barrier(self, peers):
        semaphore = pltpu.get_barrier_semaphore()
        for peer in peers:
            pl.semaphore_signal(semaphore, inc=1, device_id=peer, device_id_type=MESH)
        pl.semaphore_wait(semaphore, len(peers))


def remote(src, dst, send, recv, peer):
    return pltpu.make_async_remote_copy(
        src_ref=src, dst_ref=dst, send_sem=send, recv_sem=recv, device_id=peer, device_id_type=MESH
    )


def fused_forward_kernel(
    group,
    x_ref,
    seg_row_ref,
    seg_col_ref,
    routes_ref,
    prev_ref,
    map_ref,
    grad_ref,
    cos_ref,
    sin_ref,
    shard_ref,
    shard_o_ref,
    gate4_ref,
    up4_ref,
    down4_ref,
    q_ref,
    k_ref,
    v_ref,
    o_ref,
    h_ref,
    lse_ref,
    aux_ref,
    pos_ref,
    small_ref,
    attn_out_ref,
    attn_o_out_ref,
    rows_in_ref,
    grads_in_ref,
    gate_full_ref,
    up_full_ref,
    down_full_ref,
    attn_ref,
    attn_o_ref,
    bias_ref,
    proj_ref,
    rows_ref,
    grows_ref,
    local_sem,
    attn_send,
    attn_recv,
    ffn_local,
    ffn_send,
    ffn_recv,
    out_sem,
    row_local,
    row_send,
    row_recv,
):
    step = pl.program_id(0)
    last = pl.num_programs(0) - 1
    here = Place(group)
    planes = here.planes
    batches, kinds, length = pos_ref.shape
    width = x_ref.shape[2]
    capacity = length // 2
    shards = ((shard_ref, attn_ref), (shard_o_ref, attn_o_ref))
    experts = ((gate4_ref, gate_full_ref), (up4_ref, up_full_ref), (down4_ref, down_full_ref))
    depth = shard_ref.shape[0]
    mine = here.block(here.z, here.x, here.core)

    def rows_of(block):
        return pl.ds(pl.multiple_of(block * depth, 16), depth)

    def attn_part(t, block, part):
        full = shards[t][1]
        half = full.shape[1] // 2
        if part is None:
            return full.at[rows_of(block), :]
        return full.at[rows_of(block), pl.ds(pl.multiple_of(part * half, LANES), half)]

    def attn_copy(t, slot, z, x, part, peer):
        ref = attn_part(t, here.block(z, x, here.core), part)
        return remote(ref, ref, attn_send.at[t, slot], attn_recv.at[t, slot], peer)

    def to_z(t, k):
        return attn_copy(t, k, here.z, here.x, None, here.z_peer(1 if k == 0 else planes - 1))

    def from_z(t, k):
        return attn_copy(t, k, z_at(planes - 1 if k == 0 else 1), here.x, None, here.x_peer)

    def pass_z(t, k):
        z = z_at(planes - 1 if k == 0 else 1)
        return attn_copy(t, 2 + k, z, here.x, k, here.z_peer(1 if k == 0 else planes - 1))

    def passed_z(t, k):
        return attn_copy(t, 2 + k, z_at(2), here.x, k, here.x_peer)

    def to_x(t, step_z):
        return attn_copy(t, 4 + step_z, z_at(step_z), here.x, here.y, here.x_peer)

    def from_x(t, step_z):
        return attn_copy(t, 4 + step_z, z_at(step_z), 1 - here.x, here.y, here.x_peer)

    def to_y(t, step_z):
        return attn_copy(t, 4 + planes + step_z, z_at(step_z), 1 - here.x, here.y, here.y_peer)

    def from_y(t, step_z):
        return attn_copy(t, 4 + planes + step_z, z_at(step_z), 1 - here.x, 1 - here.y, here.y_peer)

    def to_core(t, step_z, x):
        return attn_copy(t, 4 + 2 * planes + 2 * step_z + x, z_at(step_z), here.x if x == 0 else 1 - here.x, None, here.core_peer)

    def from_core(t, step_z, x):
        ref = attn_part(t, here.block(z_at(step_z), here.x if x == 0 else 1 - here.x, 1 - here.core), None)
        slot = 4 + 2 * planes + 2 * step_z + x
        return remote(ref, ref, attn_send.at[t, slot], attn_recv.at[t, slot], here.core_peer)

    def z_at(k):
        return (here.z + k) % planes

    def ffn_to_x(j):
        source, full = experts[j]
        return remote(
            source.at[here.expert(1)],
            full.at[here.z, here.x, here.core],
            ffn_send.at[j, 0],
            ffn_recv.at[j, 0],
            here.x_peer,
        )

    def ffn_from_x(j):
        source, full = experts[j]
        return remote(
            source.at[here.expert(1)],
            full.at[here.z, 1 - here.x, here.core],
            ffn_send.at[j, 0],
            ffn_recv.at[j, 0],
            here.x_peer,
        )

    def ffn_mine(j):
        source, full = experts[j]
        return pltpu.make_async_copy(source.at[here.expert(0)], full.at[here.z, here.x, here.core], ffn_local.at[j])

    def ffn_copy(j, slot, z, x, core, peer):
        full = experts[j][1]
        part = full.at[z, :, core] if x is None else full.at[z, x, core]
        return remote(part, part, ffn_send.at[j, slot], ffn_recv.at[j, slot], peer)

    def ffn_to_z(j, k):
        return ffn_copy(j, 1 + k, here.z, None, here.core, here.z_peer(1 if k == 0 else planes - 1))

    def ffn_from_z(j, k):
        return ffn_copy(j, 1 + k, z_at(planes - 1 if k == 0 else 1), None, here.core, here.x_peer)

    def ffn_pass_z(j, k):
        z = z_at(planes - 1 if k == 0 else 1)
        return ffn_copy(j, 3 + k, z, k, here.core, here.z_peer(1 if k == 0 else planes - 1))

    def ffn_passed_z(j, k):
        return ffn_copy(j, 3 + k, z_at(2), k, here.core, here.x_peer)

    def ffn_to_core(j, step_z):
        return ffn_copy(j, 5 + step_z, z_at(step_z), None, here.core, here.core_peer)

    def ffn_from_core(j, step_z):
        return ffn_copy(j, 5 + step_z, z_at(step_z), None, 1 - here.core, here.core_peer)

    def row_copy(kind, member, number):
        source, target = ((grows_ref, grads_in_ref), (rows_ref, rows_in_ref))[kind]
        src, dst = source.at[member, number], target.at[number, member]
        if number == 0:
            return pltpu.make_async_copy(src, dst, row_local.at[kind, member])
        return remote(
            src,
            dst,
            row_send.at[kind, member, number],
            row_recv.at[kind, member, number],
            here.plane_peers[number],
        )

    def outs(t):
        full, target = ((attn_ref, attn_out_ref), (attn_o_ref, attn_o_out_ref))[t]
        return pltpu.make_async_copy(full, target, out_sem.at[t])

    @pl.when(step == 0)
    def _():
        own_copies = [
            pltpu.make_async_copy(source, full.at[rows_of(mine), :], local_sem.at[t])
            for t, (source, full) in enumerate(shards)
        ]
        for copy in own_copies:
            copy.start()
        for j in range(3):
            ffn_mine(j).start()
        here.barrier(
            [here.core_peer, here.x_peer, here.y_peer, here.xy_peer, here.z_peer(1), here.z_peer(planes - 1)]
        )
        for copy in own_copies:
            copy.wait()
        for t in range(2):
            to_z(t, 0).start()
            to_z(t, 1).start()
            to_x(t, 0).start()
            to_core(t, 0, 0).start()
        for j in range(3):
            ffn_to_x(j).start()

        ids = iota((kinds, length), 0)
        before = jnp.where(iota((length, length), 0) < iota((length, length), 1), 1.0, 0.0).astype(BF16)
        for member in range(batches):
            first = routes_ref[member, 0:1, :] == ids
            second = routes_ref[member, 1:2, :] == ids
            hits = jnp.where(first | second, 1.0, 0.0)
            pos_ref[member] = jnp.where(hits > 0.0, nn(hits.astype(BF16), before), -1.0)
            for number in range(4):
                line = pos_ref[member, pl.ds(here.expert(number), 1), :]
                grows_ref[member, number] = nn(slot_mask(line, capacity), grad_ref[member]).astype(BF16)
            row_copy(0, member, 0).start()
            row_copy(0, member, 2).start()

        for t in range(2):
            for k, step_z in enumerate((planes - 1, 1)):
                from_z(t, k).wait_recv()
                pass_z(t, k).start()
                to_x(t, step_z).start()
                to_core(t, step_z, 0).start()
        for t in range(2):
            from_x(t, 0).wait_recv()
            to_y(t, 0).start()
        for j in range(3):
            ffn_mine(j).wait()
            ffn_from_x(j).wait_recv()
            ffn_to_z(j, 0).start()
            ffn_to_z(j, 1).start()
            ffn_to_core(j, 0).start()
        for t in range(2):
            passed_z(t, 0).wait_recv()
            passed_z(t, 1).wait_recv()
            to_x(t, 2).start()
            to_core(t, 2, 0).start()
        for member in range(batches):
            row_copy(0, member, 1).start()
            row_copy(0, member, 3).start()
        for t in range(2):
            for step_z in (planes - 1, 1, 2):
                from_x(t, step_z).wait_recv()
                to_y(t, step_z).start()
        for t in range(2):
            for step_z in (0, planes - 1, 1, 2):
                from_y(t, step_z).wait_recv()
                to_core(t, step_z, 1).start()
        for t in range(2):
            for step_z in range(planes):
                for x in range(2):
                    from_core(t, step_z, x).wait_recv()
        for t in range(2):
            outs(t).start()
        small_ref[...] = jnp.transpose(attn_ref[:, 3 * width : 3 * width + LANES].astype(F32))[0 : kinds + 8, :]

    def between():
        @pl.when(step == 0)
        def _():
            for j in range(3):
                for k, step_z in enumerate((planes - 1, 1)):
                    ffn_from_z(j, k).wait_recv()
                    ffn_pass_z(j, k).start()
                    ffn_to_core(j, step_z).start()

    sequence_forward(
        x_ref,
        seg_row_ref,
        seg_col_ref,
        routes_ref.at[pl.ds(step, 1)],
        prev_ref,
        map_ref,
        small_ref,
        attn_ref.at[:, 0:width],
        attn_ref.at[:, width : 2 * width],
        attn_ref.at[:, 2 * width : 3 * width],
        attn_o_ref,
        cos_ref,
        sin_ref,
        pos_ref.at[pl.ds(step, 1)],
        q_ref,
        k_ref,
        v_ref,
        o_ref,
        h_ref,
        lse_ref,
        aux_ref,
        [rows_ref.at[pl.ds(step, 1), number] for number in range(4)],
        bias_ref,
        proj_ref,
        here.expert,
        between,
    )
    for member in range(batches):

        @pl.when(step == member)
        def _():
            for number in range(4):
                row_copy(1, member, number).start()

    @pl.when(step == 0)
    def _():
        for j in range(3):
            for k in range(2):
                ffn_passed_z(j, k).wait_recv()
            ffn_to_core(j, 2).start()

    @pl.when(step == last)
    def _():
        for t in range(2):
            outs(t).wait()
            for k in range(2):
                to_z(t, k).wait_send()
                pass_z(t, k).wait_send()
            for step_z in range(planes):
                to_x(t, step_z).wait_send()
                to_y(t, step_z).wait_send()
                for x in range(2):
                    to_core(t, step_z, x).wait_send()
        for j in range(3):
            ffn_to_x(j).wait_send()
            for k in range(2):
                ffn_to_z(j, k).wait_send()
                ffn_pass_z(j, k).wait_send()
            for step_z in range(planes):
                ffn_to_core(j, step_z).wait_send()
                ffn_from_core(j, step_z).wait_recv()
        for kind in range(2):
            for member in range(batches):
                for number in range(4):
                    copy = row_copy(kind, member, number)
                    copy.wait()


def expert_kernel(
    a_ref,
    g_ref,
    gate_ref,
    up_ref,
    down_ref,
    v_ref,
    d_ref,
    grad_gate_ref,
    grad_up_ref,
    grad_down_ref,
    rows_ref,
    grads_ref,
    gates_ref,
    rows_t_ref,
    grads_t_ref,
    places_ref,
    acc_value_ref,
    acc_input_ref,
    acc_gate_ref,
    acc_up_ref,
    acc_down_ref,
    share_ref,
    sems,
):
    step = pl.program_id(0)
    last = pl.num_programs(0) - 1
    batches, capacity, width = g_ref.shape[1:]
    blocks = 4 * batches

    @pl.when(step == 0)
    def _():
        copies = []
        for number in range(4):
            rows, grads = a_ref.at[number], g_ref.at[number]
            for member in range(batches):
                block = number * batches + member
                span = pl.ds(block * capacity, capacity)
                copies.append(
                    pltpu.make_async_copy(
                        rows.at[member, pl.ds(capacity, 16), pl.ds(0, capacity)],
                        gates_ref.at[block],
                        sems.at[3 * block],
                    )
                )
                copies.append(
                    pltpu.make_async_copy(
                        rows.at[member, pl.ds(0, capacity), :], rows_ref.at[span, :], sems.at[3 * block + 1]
                    )
                )
                copies.append(
                    pltpu.make_async_copy(grads.at[member], grads_ref.at[span, :], sems.at[3 * block + 2])
                )
        for copy in copies:
            copy.start()
        for copy in copies:
            copy.wait()
        same = iota((capacity, capacity), 0) == iota((capacity, capacity), 1)
        spare = jnp.zeros((capacity, width), BF16)
        rows_ref[blocks * capacity :, :] = spare
        grads_ref[blocks * capacity :, :] = spare
        share_ref[...] = jnp.zeros_like(share_ref)

        def pack(block, place):
            span = pl.ds(pl.multiple_of(block * capacity, capacity), capacity)
            target = pl.ds(pl.multiple_of(place, 16), capacity)
            parts = gates_ref[block].astype(F32)
            count = jnp.max(parts[3:4, :]).astype(jnp.int32)
            line = jnp.sum(parts[0:3, :], axis=0, keepdims=True)
            column = jnp.sum(jnp.where(same, line, 0.0), axis=1, keepdims=True)
            rows = rows_ref[span, :]
            grads = (grads_ref[span, :].astype(F32) * column).astype(BF16)
            rows_ref[target, :] = rows
            grads_ref[target, :] = grads
            places_ref[block] = place
            return place + (count + 15) // 16 * 16

        total = lax.fori_loop(0, blocks, pack, 0)
        target = pl.ds(pl.multiple_of(total, 16), capacity)
        rows_ref[target, :] = spare
        grads_ref[target, :] = spare
        places_ref[blocks] = (total + capacity - 1) // capacity

        def turn(block, carry):
            span = pl.ds(pl.multiple_of(block * capacity, capacity), capacity)
            grads_t_ref[:, span] = jnp.transpose(grads_ref[span, :])
            rows_t_ref[:, span] = jnp.transpose(rows_ref[span, :])
            return carry

        lax.fori_loop(0, places_ref[blocks], turn, 0)

    acc_gate_ref[...] = jnp.zeros_like(acc_gate_ref)
    acc_up_ref[...] = jnp.zeros_like(acc_up_ref)
    acc_down_ref[...] = jnp.zeros_like(acc_down_ref)

    def work(block, carry):
        span = pl.ds(pl.multiple_of(block * capacity, capacity), capacity)
        rows = rows_ref[span, :]
        grads = grads_ref[span, :]
        gate = nn(rows, gate_ref[...])
        up = nn(rows, up_ref[...])
        back = nt(grads, down_ref[...])
        sig = 1.0 / (1.0 + jnp.exp(-gate))
        silu = gate * sig
        act = (silu * up).astype(BF16)
        grad_gate = (back * up * (sig * (1.0 + gate * (1.0 - sig)))).astype(BF16)
        grad_up = (back * silu).astype(BF16)
        value = nn(act, down_ref[...])
        grad_rows = nt(grad_gate, gate_ref[...]) + nt(grad_up, up_ref[...])
        rows_t = rows_t_ref[:, span]
        acc_gate_ref[...] += nn(rows_t, grad_gate)
        acc_up_ref[...] += nn(rows_t, grad_up)
        acc_down_ref[...] += nn(grads_t_ref[:, span], act)
        share = jnp.broadcast_to(
            jnp.sum(act.astype(F32) * back, axis=1, keepdims=True), (capacity, LANES)
        )

        @pl.when(step == 0)
        def _():
            share_ref[span, :] = share
            acc_value_ref[span, :] = value
            acc_input_ref[span, :] = grad_rows

        @pl.when(step > 0)
        def _():
            share_ref[span, :] += share

        @pl.when((step > 0) & (step < last))
        def _():
            acc_value_ref[span, :] += value
            acc_input_ref[span, :] += grad_rows

        @pl.when(step == last)
        def _():
            rows_ref[span, :] = (acc_value_ref[span, :] + value).astype(BF16)
            grads_ref[span, :] = (acc_input_ref[span, :] + grad_rows).astype(BF16)

        return carry

    lax.fori_loop(0, places_ref[blocks], work, 0)
    grad_gate_ref[...] = acc_gate_ref[...].astype(BF16)
    grad_up_ref[...] = acc_up_ref[...].astype(BF16)
    grad_down_ref[...] = jnp.transpose(acc_down_ref[...].astype(BF16))

    @pl.when(step == last)
    def _():
        same = iota((capacity, capacity), 0) == iota((capacity, capacity), 1)
        place = iota((16, capacity), 0)

        def shares(block, carry):
            column = share_ref[pl.ds(pl.multiple_of(places_ref[block], 16), capacity), 0:1]
            line = jnp.sum(jnp.where(same, column, 0.0), axis=0, keepdims=True)
            high = line.astype(BF16).astype(F32)
            mid = (line - high).astype(BF16).astype(F32)
            low = line - high - mid
            parts = jnp.where(place == 0, high, jnp.where(place == 1, mid, jnp.where(place == 2, low, 0.0)))
            gates_ref[block] = parts.astype(BF16)
            return carry

        lax.fori_loop(0, blocks, shares, 0)
        copies = []
        for number in range(4):
            values, grads = v_ref.at[number], d_ref.at[number]
            for member in range(batches):
                block = number * batches + member
                span = pl.ds(pl.multiple_of(places_ref[block], 16), capacity)
                copies.append(pltpu.make_async_copy(rows_ref.at[span, :], values.at[member], sems.at[3 * block]))
                copies.append(
                    pltpu.make_async_copy(
                        grads_ref.at[span, :], grads.at[member, pl.ds(0, capacity), :], sems.at[3 * block + 1]
                    )
                )
                copies.append(
                    pltpu.make_async_copy(
                        gates_ref.at[block],
                        grads.at[member, pl.ds(capacity, 16), pl.ds(0, capacity)],
                        sems.at[3 * block + 2],
                    )
                )
        for copy in copies:
            copy.start()
        for copy in copies:
            copy.wait()


def constant_mix(zs, index):
    za, zb = zs[:, index : index + 1], zs[:, index + 1 : index + 2]
    top = jnp.maximum(za, zb)
    ea, eb = jnp.exp(za - top), jnp.exp(zb - top)
    return ea / (ea + eb), eb / (ea + eb)


def token_columns(pos_ref, aux_ref, cols_ref):
    kinds, length = pos_ref.shape[1:]
    cols_ref[0:kinds, :] = pos_ref[0]
    cols_ref[kinds : kinds + 16, :] = aux_ref[0]
    cols_ref[kinds + 16 :, :] = jnp.zeros((LANES - kinds - 16, length), F32)
    return jnp.transpose(cols_ref[...])


def column(source, index):
    return jnp.sum(jnp.where(iota((1, LANES), 1) == index, source, 0.0), axis=1, keepdims=True)


def result_kernel(own_ref, v_ref, pos_ref, aux_ref, h_ref, small_ref, out_ref, cols_ref):
    own = own_ref[0]
    length, width = h_ref.shape[1:]
    kinds = pos_ref.shape[1]
    ffn = kinds - 4
    capacity = v_ref.shape[2]
    hidden = h_ref[0]
    n2 = hidden * rms_scale(hidden) * small_ref[kinds + 7 : kinds + 8, :]
    n2_high, n2_low = split2(n2)
    small = small_ref[...].astype(BF16)
    cols = token_columns(pos_ref, aux_ref, cols_ref)
    result = hidden
    slot_lane = iota((1, capacity), 1).astype(F32)
    for number in range(4):
        expert = own ^ number
        mask = jnp.where(column(cols, expert) == slot_lane, 1.0, 0.0).astype(BF16)
        result = result + column(cols, kinds + expert) * nn(mask, v_ref[number, 0])
    mixes = nt(n2_high, small) + nt(n2_low, small)
    share = column(cols, kinds + ffn + 1)
    for constant in range(2):
        weight = column(cols, kinds + ffn + 2 + constant)
        alpha_a, alpha_b = constant_mix(mixes, kinds + 2 * constant)
        result = result + (weight * alpha_b) * small_ref[kinds + 4 + constant : kinds + 5 + constant, :]
        share = share + weight * alpha_a
    out_ref[0] = result + share * n2


def sequence_combine(
    step,
    d_refs,
    pos_ref,
    aux_ref,
    routes_ref,
    prev_ref,
    h_ref,
    g_ref,
    o_ref,
    small_ref,
    wo_ref,
    dh_ref,
    dob_ref,
    sgrad_ref,
    grad_map_ref,
    acc_ref,
    cols_ref,
    expert_of,
):
    length, width = h_ref.shape[1:]
    kinds = pos_ref.shape[1]
    ffn = kinds - 4
    capacity = d_refs[0].shape[1] - 16
    hidden = h_ref[0]
    inverse = rms_scale(hidden)
    gain = small_ref[kinds + 7 : kinds + 8, :]
    n2 = hidden * inverse * gain
    n2_high, n2_low = split2(n2)
    grad_low = g_ref[0]
    grad = grad_low.astype(F32)
    small = small_ref[...].astype(BF16)
    cols = token_columns(pos_ref, aux_ref, cols_ref)
    lane = iota((1, LANES), 1)
    gate_one = column(cols, 2 * kinds)
    gate_two = column(cols, 2 * kinds + 1)
    hot_one = jnp.where(routes_ref[0, :, 0:1] == lane, 1.0, 0.0)
    hot_two = jnp.where(routes_ref[0, :, 1:2] == lane, 1.0, 0.0)

    grad_n2 = jnp.zeros((length, width), F32)
    shares = jnp.zeros((length, LANES), F32)
    slot_lane = iota((1, capacity), 1).astype(F32)
    for number, rows in enumerate(d_refs):
        expert = expert_of(number)
        mask = jnp.where(column(cols, expert) == slot_lane, 1.0, 0.0).astype(BF16)
        grad_n2 = grad_n2 + nn(mask, rows[0, 0:capacity, :])
        parts = nt(mask, rows[0, capacity:, 0:capacity])
        shares = jnp.where(lane == expert, jnp.sum(parts, axis=1, keepdims=True), shares)

    mixes = nt(n2_high, small) + nt(n2_low, small)
    inner = nt(grad_low, small)
    with_n2 = jnp.sum(grad * n2, axis=1, keepdims=True)
    weight_copy = column(cols, kinds + ffn + 1)
    shares = jnp.where(lane == ffn + 1, weight_copy * with_n2, shares)
    share = weight_copy
    coefs = jnp.zeros((length, LANES), F32)
    for constant in range(2):
        weight = column(cols, kinds + ffn + 2 + constant)
        alpha_a, alpha_b = constant_mix(mixes, kinds + 2 * constant)
        with_vec = inner[:, kinds + 4 + constant : kinds + 5 + constant]
        share = share + weight * alpha_a
        da = weight * with_n2
        db = weight * with_vec
        mean = alpha_a * da + alpha_b * db
        shares = jnp.where(lane == ffn + 2 + constant, mean, shares)
        coefs = jnp.where(lane == kinds + 2 * constant, alpha_a * (da - mean), coefs)
        coefs = jnp.where(lane == kinds + 2 * constant + 1, alpha_b * (db - mean), coefs)
        coefs = jnp.where(lane == kinds + 4 + constant, weight * alpha_b, coefs)

    share_one = jnp.sum(shares * hot_one, axis=1, keepdims=True)
    share_two = jnp.sum(shares * hot_two, axis=1, keepdims=True)
    both = share_one + share_two
    dlogits = (share_one - gate_one * both) * hot_one + (share_two - gate_two * both) * hot_two
    coefs = jnp.where(lane < kinds, dlogits, coefs)
    back = jnp.where(lane < kinds + 4, coefs, 0.0)[:, 0:16]
    back_high, back_low = split2(back)
    grad_n2 = grad_n2 + nn(back_high, small) + nn(back_low, small) + share * grad

    coefs_t = jnp.transpose(coefs)[0:16, :]
    high, low = split2(coefs_t)
    by_n2 = nn(high, n2_high) + nn(low, n2_high)
    by_low = nn(high, n2_low)
    by_grad = nn(high, grad_low) + nn(low, grad_low)
    row = iota((16, 1), 0)
    parts = jnp.where(row < kinds, by_n2, jnp.where(row < kinds + 4, by_n2 + by_low, by_grad))
    gain_part = jnp.sum(grad_n2 * hidden * inverse, axis=0, keepdims=True)
    parts = jnp.where(row == kinds + 7, gain_part, jnp.where(row == kinds + 6, 0.0, parts))
    dlog_t = coefs_t[0:kinds, :]
    map_lane = iota((kinds, LANES), 1)
    map_part = jnp.zeros((kinds, LANES), F32)
    for j in range(kinds):
        map_part = jnp.where(
            map_lane == j, jnp.sum(dlog_t * prev_ref[0, j : j + 1, :], axis=1, keepdims=True), map_part
        )

    scaled = gain * grad_n2
    inner_mean = jnp.mean(scaled * hidden, axis=-1, keepdims=True)
    dh = grad + inverse * scaled - hidden * (inverse * inverse * inverse) * inner_mean
    dh_ref[0] = dh
    db = dh.astype(BF16)
    dob_ref[0] = nt(db, wo_ref[...]).astype(BF16)
    wo_part = nn(jnp.transpose(o_ref[0]), db)

    @pl.when(step == 0)
    def _():
        acc_ref[...] = wo_part
        sgrad_ref[...] = parts
        grad_map_ref[...] = map_part

    @pl.when(step > 0)
    def _():
        acc_ref[...] += wo_part
        sgrad_ref[...] += parts
        grad_map_ref[...] += map_part


def combine_kernel(
    own_ref,
    d0,
    d1,
    d2,
    d3,
    pos_ref,
    aux_ref,
    routes_ref,
    prev_ref,
    h_ref,
    g_ref,
    o_ref,
    small_ref,
    wo_ref,
    dh_ref,
    dob_ref,
    grad_wo_ref,
    sgrad_ref,
    grad_map_ref,
    acc_ref,
    cols_ref,
):
    own = own_ref[0]
    step = pl.program_id(0)
    sequence_combine(
        step,
        (d0, d1, d2, d3),
        pos_ref,
        aux_ref,
        routes_ref,
        prev_ref,
        h_ref,
        g_ref,
        o_ref,
        small_ref,
        wo_ref,
        dh_ref,
        dob_ref,
        sgrad_ref,
        grad_map_ref,
        acc_ref,
        cols_ref,
        lambda number: own ^ number,
    )

    @pl.when(step == pl.num_programs(0) - 1)
    def _():
        grad_wo_ref[...] = acc_ref[...].astype(BF16)


def sequence_backward(
    step,
    x_ref,
    seg_row_ref,
    seg_col_ref,
    q_ref,
    k_ref,
    v_ref,
    dob_ref,
    lse_ref,
    dh_ref,
    small_ref,
    wq_ref,
    wk_ref,
    wv_ref,
    cos_ref,
    sin_ref,
    gin_ref,
    gain_ref,
    bias_ref,
    lse_t_ref,
    dqkv_ref,
    acc_ref,
):
    length, width = x_ref.shape[1:]
    kinds = small_ref.shape[0] - 8
    pairs = width // LANES
    lane = iota((1, LANES), 1)
    low_half = (lane % HEAD_DIM) < (HEAD_DIM // 2)
    first_head = lane < HEAD_DIM
    mask_a = jnp.where(first_head, 1.0, 0.0).astype(BF16)
    mask_b = jnp.where(first_head, 0.0, 1.0).astype(BF16)
    allowed = (seg_col_ref[0] == seg_row_ref[0]) & (
        iota((length, length), 0) // BLOCK <= iota((length, length), 1) // BLOCK
    )
    bias_ref[...] = jnp.where(allowed, 0.0, NEG)
    lse_t_ref[...] = jnp.transpose(lse_ref[0])

    def pair(h, carry):
        cols = pl.ds(pl.multiple_of(h * LANES, LANES), LANES)
        keys_t = jnp.transpose(k_ref[0, :, cols])
        grad_keys = None
        grad_values = None
        grad_queries = []
        for begin in range(0, length, BLOCK):
            end = begin + BLOCK
            queries = q_ref[0, begin:end, cols]
            outs = dob_ref[0, begin:end, cols]
            keys = k_ref[0, 0:end, cols]
            values = v_ref[0, 0:end, cols]
            queries = jnp.concatenate([queries * mask_a, queries * mask_b], axis=0)
            outs = jnp.concatenate([outs * mask_a, outs * mask_b], axis=0)
            bias = bias_ref[0:end, begin:end]
            bias = jnp.concatenate([bias, bias], axis=1)
            line = jnp.concatenate(
                [lse_t_ref[pl.ds(2 * h, 1), begin:end], lse_t_ref[pl.ds(2 * h + 1, 1), begin:end]], axis=1
            )
            chances = jnp.exp(nt(keys, queries) + bias - line)
            grad_chances = nt(values, outs)
            delta = jnp.sum(chances * grad_chances, axis=0, keepdims=True)
            grad_scores = (chances * (grad_chances - delta)).astype(BF16)
            dv = nn(chances.astype(BF16), outs)
            dk = nn(grad_scores, queries)
            dq = jnp.transpose(nn(keys_t[:, 0:end], grad_scores))
            grad_queries.append(jnp.where(first_head, dq[0:BLOCK], dq[BLOCK:]))
            if grad_keys is None:
                grad_keys, grad_values = dk, dv
            else:
                grad_keys = jnp.concatenate([grad_keys + dk[0:begin], dk[begin:]], axis=0)
                grad_values = jnp.concatenate([grad_values + dv[0:begin], dv[begin:]], axis=0)
        dq = jnp.concatenate(grad_queries, axis=0) * 0.125
        dq = dq * cos_ref[...] - swap_halves(dq, low_half) * sin_ref[...]
        dk = grad_keys * cos_ref[...] - swap_halves(grad_keys, low_half) * sin_ref[...]
        dqkv_ref[:, cols] = dq.astype(BF16)
        dqkv_ref[:, pl.ds(pl.multiple_of(width + h * LANES, LANES), LANES)] = dk.astype(BF16)
        dqkv_ref[:, pl.ds(pl.multiple_of(2 * width + h * LANES, LANES), LANES)] = grad_values.astype(BF16)
        return carry

    lax.fori_loop(0, pairs, pair, 0)

    tokens = x_ref[0].astype(F32)
    inverse = rms_scale(tokens)
    gain = small_ref[kinds + 6 : kinds + 7, :]
    a1_t = jnp.transpose((tokens * inverse * gain).astype(BF16))
    dn1 = (
        nt(dqkv_ref[:, 0:width], wq_ref[...])
        + nt(dqkv_ref[:, width : 2 * width], wk_ref[...])
        + nt(dqkv_ref[:, 2 * width :], wv_ref[...])
    )
    scaled = gain * dn1
    inner_mean = jnp.mean(scaled * tokens, axis=-1, keepdims=True)
    gin_ref[0] = dh_ref[0] + inverse * scaled - tokens * (inverse * inverse * inverse) * inner_mean
    gain_part = jnp.broadcast_to(jnp.sum(dn1 * tokens * inverse, axis=0, keepdims=True), gain_ref.shape)

    @pl.when(step == 0)
    def _():
        acc_ref[...] = jnp.zeros_like(acc_ref)
        gain_ref[...] = gain_part

    @pl.when(step > 0)
    def _():
        gain_ref[...] += gain_part

    for part in range(3):
        span = slice(part * width, (part + 1) * width)
        acc_ref[:, span] += nn(a1_t, dqkv_ref[:, span])


def small_table(depth, sgrad_ref, grad_map_ref, gain_ref):
    kinds = grad_map_ref.shape[0]
    width = sgrad_ref.shape[1]
    row = iota((16, 1), 0)
    table = jnp.where(row == kinds + 6, gain_ref[0:1, :], sgrad_ref[...])
    chosen = jnp.where(iota((LANES, width), 1) % depth == iota((LANES, width), 0), 1.0, 0.0).astype(BF16)
    maps = nn(grad_map_ref[...].astype(BF16), chosen)
    table = jnp.concatenate([table, maps, jnp.zeros((LANES - 16 - kinds, width), F32)], axis=0)
    return jnp.transpose(table).astype(BF16)


def backward_kernel(
    x_ref,
    seg_row_ref,
    seg_col_ref,
    q_ref,
    k_ref,
    v_ref,
    dob_ref,
    lse_ref,
    dh_ref,
    small_ref,
    wq_ref,
    wk_ref,
    wv_ref,
    cos_ref,
    sin_ref,
    gin_ref,
    grad_w_ref,
    gain_ref,
    bias_ref,
    lse_t_ref,
    dqkv_ref,
    acc_ref,
):
    step = pl.program_id(0)
    sequence_backward(
        step,
        x_ref,
        seg_row_ref,
        seg_col_ref,
        q_ref,
        k_ref,
        v_ref,
        dob_ref,
        lse_ref,
        dh_ref,
        small_ref,
        wq_ref,
        wk_ref,
        wv_ref,
        cos_ref,
        sin_ref,
        gin_ref,
        gain_ref,
        bias_ref,
        lse_t_ref,
        dqkv_ref,
        acc_ref,
    )

    @pl.when(step == pl.num_programs(0) - 1)
    def _():
        grad_w_ref[...] = acc_ref[...].astype(BF16)


def reduce_attention(here, depth, value_of, sends, cores, buffers, out_ref, free_sem, send, recv, z_send, z_recv):
    planes = here.planes
    near = planes // 2
    x, y = here.x, here.y
    chunks = range(len(sends))
    halves = [sends[t].shape[3] // 2 for t in chunks]
    wide = [sends[t].shape[3] for t in chunks]
    mine = [pl.ds(pl.multiple_of(y * halves[t], LANES), halves[t]) for t in chunks]
    theirs = [pl.ds(pl.multiple_of((1 - y) * halves[t], LANES), halves[t]) for t in chunks]

    def rows_of(z, column, core):
        return pl.ds(pl.multiple_of(here.block(z, column, core) * depth, 16), depth)

    def add(target, source):
        target[...] = (target[...].astype(F32) + source[...].astype(F32)).astype(BF16)

    swaps = []
    for t in chunks:

        def lower(z, carry):
            for column in range(2):
                sends[t][z, column] = value_of(t, rows_of(z, column, 1 - here.core)).astype(BF16)
            return carry

        lax.fori_loop(0, planes, lower, 0)
        swaps.append(remote(sends[t], cores[t], send.at[t, 0], recv.at[t, 0], here.core_peer))
    pl.semaphore_wait(free_sem, 1)
    for t in chunks:
        swaps[t].start()
    y_first, x_first, x_second, y_second, along = [], [], [], [], []
    for t in chunks:
        swaps[t].wait_recv()

        def add_core(z, carry):
            for column in range(2):
                own = value_of(t, rows_of(z, column, here.core)).astype(F32)
                cores[t][z, column] = (own + cores[t][z, column].astype(F32)).astype(BF16)
            return carry

        lax.fori_loop(0, planes, add_core, 0)
        acc = cores[t]
        y_first.append(
            remote(acc.at[0:near, :, :, theirs[t]], buffers[t][0], send.at[t, 1], recv.at[t, 1], here.y_peer)
        )
        x_first.append(
            remote(acc.at[near:planes, 1 - x], buffers[t][1], send.at[t, 2], recv.at[t, 2], here.x_peer)
        )
        y_first[t].start()
        x_first[t].start()
    for t in chunks:
        acc = cores[t]
        y_first[t].wait_recv()
        for z in range(near):
            for column in range(2):
                add(acc.at[z, column, :, mine[t]], buffers[t][0].at[z, column])
        x_second.append(
            remote(acc.at[0:near, 1 - x, :, mine[t]], buffers[t][2], send.at[t, 3], recv.at[t, 3], here.x_peer)
        )
        x_second[t].start()
        x_first[t].wait_recv()
        for z in range(near, planes):
            add(acc.at[z, x], buffers[t][1].at[z - near])
        y_second.append(
            remote(acc.at[near:planes, x, :, theirs[t]], buffers[t][3], send.at[t, 4], recv.at[t, 4], here.y_peer)
        )
        y_second[t].start()
    for t in chunks:
        acc = cores[t]
        x_second[t].wait_recv()
        for z in range(near):
            add(acc.at[z, x, :, mine[t]], buffers[t][2].at[z])
        y_second[t].wait_recv()
        for z in range(near, planes):
            add(acc.at[z, x, :, mine[t]], buffers[t][3].at[z - near])
        hops = []
        for k in range(1, planes):
            hops.append(
                remote(
                    acc.at[(here.z + k) % planes, x, :, mine[t]],
                    buffers[t][4].at[k - 1],
                    z_send.at[t, k - 1],
                    z_recv.at[t, k - 1],
                    here.z_peer(k),
                )
            )
            hops[-1].start()
        along.append(hops)
    back = []
    for t in chunks:
        total = cores[t][here.z, x, :, mine[t]].astype(F32)
        for k in range(1, planes):
            along[t][k - 1].wait_recv()
            total = total + buffers[t][4][k - 1].astype(F32)
        buffers[t][5][...] = total.astype(BF16)
        back.append(remote(buffers[t][5], buffers[t][6], send.at[t, 5], recv.at[t, 5], here.y_peer))
        back[t].start()
    for t in chunks:
        begin = sum(wide[:t])
        back[t].wait_recv()
        spot = pl.ds(pl.multiple_of(begin + y * halves[t], LANES), halves[t])
        other = pl.ds(pl.multiple_of(begin + (1 - y) * halves[t], LANES), halves[t])
        out_ref[:, spot] = buffers[t][5][...].astype(F32)
        out_ref[:, other] = buffers[t][6][...].astype(F32)
        for copy in [swaps[t], y_first[t], x_first[t], x_second[t], y_second[t], back[t]] + along[t]:
            copy.wait_send()


def fused_backward_kernel(
    group,
    depth,
    pos_ref,
    aux_ref,
    routes_ref,
    prev_ref,
    h_ref,
    g_ref,
    o_ref,
    x_ref,
    seg_row_ref,
    seg_col_ref,
    q_ref,
    k_ref,
    v_ref,
    lse_ref,
    small_ref,
    wq_ref,
    wk_ref,
    wv_ref,
    wo_ref,
    cos_ref,
    sin_ref,
    d_ref,
    val_ref,
    gate_ref,
    up_ref,
    down_ref,
    gin_ref,
    sums_ref,
    d_in_ref,
    val_in_ref,
    gate_out_ref,
    up_out_ref,
    down_out_ref,
    acc_ref,
    acc_wo_ref,
    table_ref,
    send_a,
    send_b,
    buffers_a,
    buffers_b,
    cols_ref,
    dh_ref,
    dob_ref,
    sgrad_ref,
    grad_map_ref,
    gain_ref,
    bias_ref,
    lse_t_ref,
    dqkv_ref,
    rows_ref,
    gate_own,
    up_own,
    down_own,
    gate_swap,
    up_swap,
    down_swap,
    gate_near,
    up_near,
    down_near,
    gate_far,
    up_far,
    down_far,
    row_local,
    row_send,
    row_recv,
    ffn_local,
    ffn_send,
    ffn_recv,
    free_sem,
    reduce_send,
    reduce_recv,
    reduce_z_send,
    reduce_z_recv,
):
    step = pl.program_id(0)
    last = pl.num_programs(0) - 1
    here = Place(group)
    planes = here.planes
    batches = d_ref.shape[1]
    width = x_ref.shape[2]
    grads = (gate_ref, up_ref, down_ref)
    owns = (gate_own, up_own, down_own)
    swaps = (gate_swap, up_swap, down_swap)
    nears = (gate_near, up_near, down_near)
    fars = (gate_far, up_far, down_far)
    outs = (gate_out_ref, up_out_ref, down_out_ref)
    side = (here.z_peer(1), here.z_peer(planes - 1))

    def z_at(k):
        return (here.z + k) % planes

    def row_copy(kind, member, number):
        source, target = ((d_ref, d_in_ref), (val_ref, val_in_ref))[kind]
        src, dst = source.at[number, member], target.at[number, member]
        if number == 0:
            return pltpu.make_async_copy(src, dst, row_local.at[batches * 4 + member])
        return remote(
            src, dst, row_send.at[kind, member, number], row_recv.at[kind, member, number], here.plane_peers[number]
        )

    def load_rows(member, number):
        source = d_ref if number == 0 else d_in_ref
        return pltpu.make_async_copy(
            source.at[number, member], rows_ref.at[number, 0], row_local.at[member * 4 + number]
        )

    def own_copy(j):
        return pltpu.make_async_copy(grads[j].at[:, :, here.core], owns[j], ffn_local.at[j, 0])

    def swap_copy(j):
        return remote(
            grads[j].at[:, :, 1 - here.core], swaps[j], ffn_send.at[j, 0], ffn_recv.at[j, 0], here.core_peer
        )

    def near_copy(j, k):
        return remote(
            owns[j].at[z_at(2), k], nears[j].at[k], ffn_send.at[j, 1 + k], ffn_recv.at[j, 1 + k], side[k]
        )

    def far_copy(j, k):
        return remote(
            owns[j].at[z_at(1 if k == 0 else planes - 1)],
            fars[j].at[k],
            ffn_send.at[j, 3 + k],
            ffn_recv.at[j, 3 + k],
            side[k],
        )

    def plane_copy(j, number):
        x = here.x if number % 2 == 0 else 1 - here.x
        src, dst = owns[j].at[here.z, x], outs[j].at[here.expert(0)]
        if number == 0:
            return pltpu.make_async_copy(src, dst, ffn_local.at[j, 1])
        return remote(
            src, dst, ffn_send.at[j, 4 + number], ffn_recv.at[j, 4 + number], here.plane_peers[number]
        )

    def plane_arrival(j, number):
        dst = outs[j].at[here.expert(number)]
        return remote(
            dst, dst, ffn_send.at[j, 4 + number], ffn_recv.at[j, 4 + number], here.plane_peers[number]
        )

    def add(target, *sources):
        value = target[...].astype(F32)
        for source in sources:
            value = value + source[...].astype(F32)
        target[...] = value.astype(BF16)

    @pl.when(step == 0)
    def _():
        for j in range(3):
            own_copy(j).start()
        here.barrier(
            [here.core_peer, here.x_peer, here.y_peer, here.xy_peer] + [here.z_peer(k) for k in range(1, planes)]
        )
        for number in range(1, 4):
            row_copy(0, 0, number).start()
        for j in range(3):
            swap_copy(j).start()
        for j in range(3):
            own_copy(j).wait()
            swap_copy(j).wait_recv()
            for x in range(2):

                def add_core(z, carry):
                    add(owns[j].at[z, x], swaps[j].at[z, x])
                    return carry

                lax.fori_loop(0, planes, add_core, 0)
            near_copy(j, 0).start()
            near_copy(j, 1).start()
        pl.semaphore_signal(free_sem, inc=1, device_id=here.core_peer, device_id_type=MESH)

    for member in range(batches):

        @pl.when(step == member)
        def _():
            for number in range(1, 4):
                row_copy(0, member, number).wait_recv()
            if member + 1 < batches:
                for number in range(1, 4):
                    row_copy(0, member + 1, number).start()
            for number in range(4):
                row_copy(1, member, number).start()
            for number in range(4):
                load_rows(member, number).start()
            for number in range(4):
                load_rows(member, number).wait()

    sequence_combine(
        step,
        [rows_ref.at[number] for number in range(4)],
        pos_ref,
        aux_ref,
        routes_ref,
        prev_ref,
        h_ref,
        g_ref,
        o_ref,
        small_ref,
        wo_ref,
        dh_ref,
        dob_ref,
        sgrad_ref,
        grad_map_ref,
        acc_wo_ref,
        cols_ref,
        here.expert,
    )

    @pl.when(step == 0)
    def _():
        for j in range(3):
            for k in range(2):
                near_copy(j, k).wait_recv()
                add(owns[j].at[z_at(1 if k == 0 else planes - 1), k], nears[j].at[k])
                far_copy(j, k).start()

    @pl.when(step == last)
    def _():
        for j in range(3):
            for k in range(2):
                far_copy(j, k).wait_recv()
            for x in range(2):
                add(owns[j].at[here.z, x], fars[j].at[0, x], fars[j].at[1, x])
            for number in range(4):
                plane_copy(j, number).start()

    sequence_backward(
        step,
        x_ref,
        seg_row_ref,
        seg_col_ref,
        q_ref,
        k_ref,
        v_ref,
        dob_ref,
        lse_ref,
        dh_ref,
        small_ref,
        wq_ref,
        wk_ref,
        wv_ref,
        cos_ref,
        sin_ref,
        gin_ref,
        gain_ref,
        bias_ref,
        lse_t_ref,
        dqkv_ref,
        acc_ref,
    )

    @pl.when(step == last)
    def _():
        table_ref[...] = small_table(depth, sgrad_ref, grad_map_ref, gain_ref)
        split = gate_swap.shape[3]

        def value_of(t, rows):
            if t == 0:
                return acc_ref[rows, 0:split]
            return jnp.concatenate(
                [
                    acc_ref[rows, split:],
                    acc_wo_ref[rows, :],
                    table_ref[rows, :].astype(F32),
                    jnp.zeros((depth, LANES), F32),
                ],
                axis=1,
            )

        reduce_attention(
            here,
            depth,
            value_of,
            (send_a, send_b),
            (gate_swap, up_swap.at[:, :, :, 0 : send_b.shape[3]]),
            (buffers_a, buffers_b),
            sums_ref,
            free_sem,
            reduce_send,
            reduce_recv,
            reduce_z_send,
            reduce_z_recv,
        )
        for j in range(3):
            swap_copy(j).wait_send()
            for k in range(2):
                near_copy(j, k).wait_send()
                far_copy(j, k).wait_send()
            plane_copy(j, 0).wait()
            for number in range(1, 4):
                plane_copy(j, number).wait_send()
                plane_arrival(j, number).wait_recv()
        for member in range(batches):
            row_copy(1, member, 0).wait()
            for number in range(1, 4):
                row_copy(0, member, number).wait_send()
                row_copy(1, member, number).wait()


def params(limit_mib):
    return pltpu.CompilerParams(vmem_limit_bytes=limit_mib * 1024 * 1024, dimension_semantics=("arbitrary",))


def rotary(length):
    halfway = HEAD_DIM // 2
    frequency = 10000.0 ** (-jnp.arange(halfway).astype(F32) / halfway)
    angles = jnp.arange(length).astype(F32)[:, None] * frequency[None, :]
    cosine, sine = jnp.cos(angles), jnp.sin(angles)
    return (
        jnp.concatenate([cosine] * 4, axis=1),
        jnp.concatenate([-sine, sine, -sine, sine], axis=1),
    )


def local(
    reps,
    group,
    block_input,
    prev_logits,
    routes,
    segments,
    grad_out,
    gain_attn,
    w_query,
    w_key,
    w_value,
    w_output,
    gain_mix,
    router,
    route_map,
    const_proj,
    const_vec,
    w_gate,
    w_up,
    w_down,
):
    batches, length = segments.shape
    width = block_input.shape[1]
    kinds = router.shape[1]
    ffn = w_gate.shape[1]
    hidden = w_gate.shape[2]
    rows_d = w_gate.shape[0]
    rows_f = w_down.shape[0]
    capacity = length // 2
    planes = group // 4
    assert reps == 2 and ffn == 4 and group % 4 == 0
    g = lax.axis_index("grp")
    y = lax.axis_index("rep")
    core = g % 2
    x = (g // 2) % 2
    z = g // 4
    own = (2 * y + x).astype(jnp.int32)
    own_arr = own.reshape(1)

    x_flip = [(i, i ^ 2) for i in range(group)]
    core_flip = [(i, i ^ 1) for i in range(group)]
    y_flip = [(0, 1), (1, 0)]
    xy_flip = [(r * group + i, (1 - r) * group + (i ^ 2)) for r in range(2) for i in range(group)]

    def z_shift(k):
        return [(i, (i + 4 * k) % group) for i in range(group)]

    def to_plane(parts):
        return [
            parts[0],
            lax.ppermute(parts[1], "grp", x_flip),
            lax.ppermute(parts[2], "rep", y_flip),
            lax.ppermute(parts[3], ("rep", "grp"), xy_flip),
        ]

    tokens = block_input.reshape(batches, length, width)
    grads = grad_out.reshape(batches, length, width)
    route_cols = routes.reshape(batches, length, 2)
    route_rows = route_cols.transpose(0, 2, 1)
    prev_rows = prev_logits.reshape(batches, length, kinds).transpose(0, 2, 1)
    seg_row = segments[:, None, :]
    seg_col = segments[:, :, None]
    cos, sin = rotary(length)

    def spec_w(j):
        return pl.BlockSpec((width, width), lambda b, *_: (0, j), pipeline_mode=pl.Buffered(1))

    row_shape = jax.ShapeDtypeStruct((batches, capacity, width), BF16)
    seq_bf16 = jax.ShapeDtypeStruct((batches, length, width), BF16)
    seq_f32 = jax.ShapeDtypeStruct((batches, length, width), F32)
    small_shard = jnp.concatenate(
        [router, const_proj, const_vec, gain_attn[:, None], gain_mix[:, None]], axis=1
    ).astype(BF16)
    small_shard = jnp.pad(small_shard, ((0, 0), (0, 2 * LANES - small_shard.shape[1])))
    shard = jnp.concatenate([w.astype(BF16) for w in (w_query, w_key, w_value)] + [small_shard], axis=1)
    shard_o = w_output.astype(BF16)
    fused = planes == 4 and rows_d % 16 == 0 and rows_f % 16 == 0
    if fused:
        any_space = pl.BlockSpec(memory_space=pl.ANY)
        out_struct = jax.ShapeDtypeStruct
        (
            q, k, v, o, h1, lse, aux, pos, small, attn, attn_o, a_rows, grad_rows, gate_full, up_full, down_full,
        ) = pl.pallas_call(
            functools.partial(fused_forward_kernel, group),
            grid=(batches,),
            in_specs=[
                per_seq((length, width)),
                per_seq((1, length)),
                per_seq((length, 1)),
                whole((batches, 2, length)),
                per_seq((kinds, length)),
                whole((kinds, kinds)),
                whole((batches, length, width)),
                whole((length, LANES)),
                whole((length, LANES)),
            ]
            + [any_space] * 5,
            out_specs=[per_seq((length, width))] * 5
            + [
                per_seq((length, LANES)),
                per_seq((16, length)),
                whole((batches, kinds, length)),
                whole((kinds + 8, width)),
            ]
            + [any_space] * 7,
            scratch_shapes=[
                pltpu.VMEM((width, 3 * width + 2 * LANES), BF16),
                pltpu.VMEM((width, width), BF16),
                pltpu.VMEM((length, length), F32),
                pltpu.VMEM((length, width), F32),
                pltpu.VMEM((batches, 4, capacity + 16, width), BF16),
                pltpu.VMEM((batches, 4, capacity, width), BF16),
                pltpu.SemaphoreType.DMA((2,)),
                pltpu.SemaphoreType.DMA((2, 4 + 4 * planes)),
                pltpu.SemaphoreType.DMA((2, 4 + 4 * planes)),
                pltpu.SemaphoreType.DMA((3,)),
                pltpu.SemaphoreType.DMA((3, 5 + planes)),
                pltpu.SemaphoreType.DMA((3, 5 + planes)),
                pltpu.SemaphoreType.DMA((2,)),
                pltpu.SemaphoreType.DMA((2, batches)),
                pltpu.SemaphoreType.DMA((2, batches, 4)),
                pltpu.SemaphoreType.DMA((2, batches, 4)),
            ],
            out_shape=[seq_bf16] * 4
            + [
                seq_f32,
                out_struct((batches, length, LANES), F32),
                out_struct((batches, 16, length), F32),
                out_struct((batches, kinds, length), F32),
                out_struct((kinds + 8, width), F32),
                out_struct((width, 3 * width + 2 * LANES), BF16),
                out_struct((width, width), BF16),
                out_struct((4, batches, capacity + 16, width), BF16),
                out_struct((4, batches, capacity, width), BF16),
                out_struct((planes, 2, 2, rows_d, hidden), BF16),
                out_struct((planes, 2, 2, rows_d, hidden), BF16),
                out_struct((planes, 2, 2, rows_f, width), BF16),
            ],
            compiler_params=pltpu.CompilerParams(
                vmem_limit_bytes=58 * 1024 * 1024,
                dimension_semantics=("arbitrary",),
                collective_id=1,
                has_side_effects=True,
            ),
            cost_estimate=pl.CostEstimate(flops=40 * 10**9, bytes_accessed=60 * 10**6, transcendentals=10**7),
            name="fused_forward",
        )(
            tokens, seg_row, seg_col, route_rows, prev_rows, route_map.T, grads, cos, sin,
            shard, shard_o,
            w_gate.astype(BF16).transpose(1, 0, 2),
            w_up.astype(BF16).transpose(1, 0, 2),
            w_down.astype(BF16).transpose(1, 0, 2),
        )
        gate_full = gate_full.reshape(width, hidden)
        up_full = up_full.reshape(width, hidden)
        down_full = down_full.reshape(hidden, width)
    else:
        attn = lax.all_gather(shard, "grp", axis=0, tiled=True)
        attn_o = lax.all_gather(shard_o, "grp", axis=0, tiled=True)
        small = attn[:, 3 * width : 3 * width + kinds + 8].astype(F32).T

        def pick(array, expert):
            return lax.dynamic_index_in_dim(array, expert, axis=1, keepdims=False)

        def gather_expert(mine, other):
            crossed = lax.ppermute(other, "grp", x_flip)
            both = jnp.where(x == 0, jnp.stack([mine, crossed]), jnp.stack([crossed, mine]))
            pieces = [both] + [lax.ppermute(both, "grp", z_shift(k)) for k in range(1, planes)]
            stacked = jnp.stack(pieces)
            half = jnp.take(stacked, (z - jnp.arange(planes)) % planes, axis=0)
            swapped = lax.ppermute(half, "grp", core_flip)
            return jnp.where(core == 0, jnp.stack([half, swapped], axis=2), jnp.stack([swapped, half], axis=2))

        gate_up = gather_expert(
            jnp.stack([pick(w_gate, own), pick(w_up, own)]).astype(BF16),
            jnp.stack([pick(w_gate, own ^ 1), pick(w_up, own ^ 1)]).astype(BF16),
        )
        down = gather_expert(pick(w_down, own).astype(BF16), pick(w_down, own ^ 1).astype(BF16))
        gate_full = gate_up[:, :, :, 0].reshape(width, hidden)
        up_full = gate_up[:, :, :, 1].reshape(width, hidden)
        down_full = down.reshape(hidden, width)

        *grad_rows, pos = pl.pallas_call(
            grad_rows_kernel,
            grid_spec=pltpu.PrefetchScalarGridSpec(
                num_scalar_prefetch=1,
                grid=(batches,),
                in_specs=[per_seq((2, length)), per_seq((length, width))],
                out_specs=[per_seq((capacity, width))] * 4 + [per_seq((kinds, length))],
            ),
            out_shape=[row_shape] * 4 + [jax.ShapeDtypeStruct((batches, kinds, length), F32)],
            compiler_params=params(32),
            cost_estimate=pl.CostEstimate(flops=4 * 10**9, bytes_accessed=8 * 10**6, transcendentals=0),
            name="grad_rows",
        )(own_arr, route_rows, grads)
        grad_rows = to_plane(grad_rows)

        q, k, v, o, h1, lse, aux, *a_rows = pl.pallas_call(
            forward_kernel,
            grid_spec=pltpu.PrefetchScalarGridSpec(
                num_scalar_prefetch=1,
                grid=(batches,),
                in_specs=[
                    per_seq((length, width)),
                    per_seq((1, length)),
                    per_seq((length, 1)),
                    per_seq((2, length)),
                    per_seq((kinds, length)),
                    whole((kinds, kinds)),
                    whole((kinds + 8, width)),
                    spec_w(0),
                    spec_w(1),
                    spec_w(2),
                    spec_w(0),
                    whole((length, LANES)),
                    whole((length, LANES)),
                    per_seq((kinds, length)),
                ],
                out_specs=[per_seq((length, width))] * 5
                + [per_seq((length, LANES)), per_seq((16, length))]
                + [per_seq((capacity + 16, width))] * 4,
                scratch_shapes=[pltpu.VMEM((length, length), F32), pltpu.VMEM((length, width), F32)],
            ),
            out_shape=[seq_bf16] * 4
            + [
                seq_f32,
                jax.ShapeDtypeStruct((batches, length, LANES), F32),
                jax.ShapeDtypeStruct((batches, 16, length), F32),
            ]
            + [jax.ShapeDtypeStruct((batches, capacity + 16, width), BF16)] * 4,
            compiler_params=params(56),
            cost_estimate=pl.CostEstimate(flops=20 * 10**9, bytes_accessed=20 * 10**6, transcendentals=10**7),
            name="forward",
        )(own_arr, tokens, seg_row, seg_col, route_rows, prev_rows, route_map.T, small, attn, attn, attn, attn_o, cos, sin, pos)
        a_rows = to_plane(a_rows)

        a_rows = jnp.stack(a_rows)
        grad_rows = jnp.stack(grad_rows)

    tile = hidden // 4
    total = 4 * batches * capacity
    any_spec = pl.BlockSpec(memory_space=pl.ANY)
    values, input_rows, grad_gate_full, grad_up_full, grad_down_full = pl.pallas_call(
        expert_kernel,
        grid=(hidden // tile,),
        in_specs=[any_spec] * 2
        + [
            pl.BlockSpec((width, tile), lambda f: (0, f)),
            pl.BlockSpec((width, tile), lambda f: (0, f)),
            pl.BlockSpec((tile, width), lambda f: (f, 0)),
        ],
        out_specs=[any_spec] * 2
        + [
            pl.BlockSpec((width, tile), lambda f: (0, f)),
            pl.BlockSpec((width, tile), lambda f: (0, f)),
            pl.BlockSpec((tile, width), lambda f: (f, 0)),
        ],
        scratch_shapes=[
            pltpu.VMEM((total + capacity, width), BF16),
            pltpu.VMEM((total + capacity, width), BF16),
            pltpu.VMEM((4 * batches, 16, capacity), BF16),
            pltpu.VMEM((width, total), BF16),
            pltpu.VMEM((width, total), BF16),
            pltpu.SMEM((4 * batches + 1,), jnp.int32),
            pltpu.VMEM((total, width), F32),
            pltpu.VMEM((total, width), F32),
            pltpu.VMEM((width, tile), F32),
            pltpu.VMEM((width, tile), F32),
            pltpu.VMEM((width, tile), F32),
            pltpu.VMEM((total + capacity, LANES), F32),
            pltpu.SemaphoreType.DMA((12 * batches,)),
        ],
        out_shape=[
            jax.ShapeDtypeStruct((4, batches, capacity, width), BF16),
            jax.ShapeDtypeStruct((4, batches, capacity + 16, width), BF16),
        ]
        + [
            jax.ShapeDtypeStruct((width, hidden), BF16),
            jax.ShapeDtypeStruct((width, hidden), BF16),
            jax.ShapeDtypeStruct((hidden, width), BF16),
        ],
        compiler_params=params(60),
        cost_estimate=pl.CostEstimate(flops=58 * 10**9, bytes_accessed=40 * 10**6, transcendentals=10**7),
        name="expert",
    )(a_rows, grad_rows, gate_full, up_full, down_full)
    if fused:
        columns = 4 * width + 2 * LANES
        once = lambda shape: pl.BlockSpec(
            (1,) + shape, lambda b, *_: (b, 0, 0), pipeline_mode=pl.Buffered(1)
        )
        wide = ((rows_d, hidden), (rows_d, hidden), (rows_f, width))
        near = planes // 2
        parts = (hidden, columns - hidden)
        gin, sums, _, values_in, grad_gate, grad_up, grad_down = pl.pallas_call(
            functools.partial(fused_backward_kernel, group, rows_d),
            grid=(batches,),
            in_specs=[
                per_seq((kinds, length)),
                per_seq((16, length)),
                per_seq((length, 2)),
                per_seq((kinds, length)),
                once((length, width)),
                once((length, width)),
                once((length, width)),
                once((length, width)),
                per_seq((1, length)),
                per_seq((length, 1)),
                once((length, width)),
                once((length, width)),
                once((length, width)),
                once((length, LANES)),
                whole((kinds + 8, width), 1),
                spec_w(0),
                spec_w(1),
                spec_w(2),
                spec_w(0),
                whole((length, LANES), 1),
                whole((length, LANES), 1),
            ]
            + [any_spec] * 5,
            out_specs=[once((length, width)), whole((rows_d, columns), 1)] + [any_spec] * 5,
            out_shape=[
                seq_f32,
                jax.ShapeDtypeStruct((rows_d, columns), F32),
                jax.ShapeDtypeStruct((4, batches, capacity + 16, width), BF16),
                jax.ShapeDtypeStruct((4, batches, capacity, width), BF16),
            ]
            + [jax.ShapeDtypeStruct((4,) + shape, BF16) for shape in wide],
            scratch_shapes=[
                pltpu.VMEM((width, 3 * width), F32),
                pltpu.VMEM((width, width), F32),
                pltpu.VMEM((width, LANES), BF16),
            ]
            + [pltpu.VMEM((planes, 2, rows_d, part), BF16) for part in parts]
            + [
                [
                    pltpu.VMEM((near, 2, rows_d, part // 2), BF16),
                    pltpu.VMEM((near, rows_d, part), BF16),
                    pltpu.VMEM((near, rows_d, part // 2), BF16),
                    pltpu.VMEM((near, rows_d, part // 2), BF16),
                    pltpu.VMEM((planes - 1, rows_d, part // 2), BF16),
                    pltpu.VMEM((rows_d, part // 2), BF16),
                    pltpu.VMEM((rows_d, part // 2), BF16),
                ]
                for part in parts
            ]
            + [
                pltpu.VMEM((LANES, length), F32),
                pltpu.VMEM((1, length, width), F32),
                pltpu.VMEM((1, length, width), BF16),
                pltpu.VMEM((16, width), F32),
                pltpu.VMEM((kinds, LANES), F32),
                pltpu.VMEM((8, width), F32),
                pltpu.VMEM((length, length), F32),
                pltpu.VMEM((LANES, length), F32),
                pltpu.VMEM((length, 3 * width), BF16),
                pltpu.VMEM((4, 1, capacity + 16, width), BF16),
            ]
            + [pltpu.VMEM((planes, 2) + shape, BF16) for shape in wide]
            + [pltpu.VMEM((planes, 2) + shape, BF16) for shape in wide]
            + [pltpu.VMEM((2,) + shape, BF16) for shape in wide]
            + [pltpu.VMEM((2, 2) + shape, BF16) for shape in wide]
            + [
                pltpu.SemaphoreType.DMA((5 * batches,)),
                pltpu.SemaphoreType.DMA((2, batches, 4)),
                pltpu.SemaphoreType.DMA((2, batches, 4)),
                pltpu.SemaphoreType.DMA((3, 2)),
                pltpu.SemaphoreType.DMA((3, 8)),
                pltpu.SemaphoreType.DMA((3, 8)),
                pltpu.SemaphoreType.REGULAR,
                pltpu.SemaphoreType.DMA((2, 6)),
                pltpu.SemaphoreType.DMA((2, 6)),
                pltpu.SemaphoreType.DMA((2, planes - 1)),
                pltpu.SemaphoreType.DMA((2, planes - 1)),
            ],
            compiler_params=pltpu.CompilerParams(
                vmem_limit_bytes=63 * 1024 * 1024,
                dimension_semantics=("arbitrary",),
                collective_id=3,
                has_side_effects=True,
            ),
            cost_estimate=pl.CostEstimate(flops=60 * 10**9, bytes_accessed=60 * 10**6, transcendentals=10**7),
            name="fused_backward",
        )(
            pos, aux, route_cols, prev_rows, h1, grads, o, tokens, seg_row, seg_col, q, k, v, lse, small,
            attn, attn, attn, attn_o, cos, sin, input_rows, values,
            grad_gate_full.reshape(planes, 2, 2, rows_d, hidden),
            grad_up_full.reshape(planes, 2, 2, rows_d, hidden),
            grad_down_full.reshape(planes, 2, 2, rows_f, width),
        )
        grad_gate = grad_gate.transpose(1, 0, 2).astype(F32)
        grad_up = grad_up.transpose(1, 0, 2).astype(F32)
        grad_down = grad_down.transpose(1, 0, 2).astype(F32)
    else:
        values_in = jnp.stack(to_plane([values[i] for i in range(4)]))
        def scatter_expert(full):
            keep = lax.dynamic_index_in_dim(full, core, axis=2, keepdims=False)
            send = lax.dynamic_index_in_dim(full, 1 - core, axis=2, keepdims=False)
            half = (keep.astype(F32) + lax.ppermute(send, "grp", core_flip).astype(F32)).astype(BF16)
            summed = lax.dynamic_index_in_dim(half, z, axis=0, keepdims=False).astype(F32)
            for k in range(1, planes):
                part = lax.dynamic_index_in_dim(half, (z + k) % planes, axis=0, keepdims=False)
                summed = summed + lax.ppermute(part, "grp", z_shift(k)).astype(F32)
            summed = summed.astype(BF16)
            mine = lax.dynamic_index_in_dim(summed, x, axis=0, keepdims=False)
            other = lax.dynamic_index_in_dim(summed, 1 - x, axis=0, keepdims=False)
            arrived = to_plane([mine, other, mine, other])

            def order(first):
                return lambda: tuple(arrived[first ^ e] for e in range(4))

            return lax.switch(own, [order(i) for i in range(4)])

        grad_gate_up = scatter_expert(
            jnp.stack(
                [
                    grad_gate_full.reshape(planes, 2, 2, rows_d, hidden),
                    grad_up_full.reshape(planes, 2, 2, rows_d, hidden),
                ],
                axis=3,
            )
        )
        grad_down = scatter_expert(grad_down_full.reshape(planes, 2, 2, rows_f, width))
        grad_gate = jnp.stack([part[0] for part in grad_gate_up], axis=1).astype(F32)
        grad_up = jnp.stack([part[1] for part in grad_gate_up], axis=1).astype(F32)
        grad_down = jnp.stack(grad_down, axis=1).astype(F32)

        dh1, dob, grad_wo, sgrad, grad_map = pl.pallas_call(
            combine_kernel,
            grid_spec=pltpu.PrefetchScalarGridSpec(
                num_scalar_prefetch=1,
                grid=(batches,),
                in_specs=[per_seq((capacity + 16, width))] * 4
                + [
                    per_seq((kinds, length)),
                    per_seq((16, length)),
                    per_seq((length, 2)),
                    per_seq((kinds, length)),
                    per_seq((length, width)),
                    per_seq((length, width)),
                    per_seq((length, width)),
                    whole((kinds + 8, width)),
                    spec_w(0),
                ],
                out_specs=[per_seq((length, width))] * 2
                + [whole((width, width)), whole((16, width)), whole((kinds, LANES))],
                scratch_shapes=[pltpu.VMEM((width, width), F32), pltpu.VMEM((LANES, length), F32)],
            ),
            out_shape=[
                seq_f32,
                seq_bf16,
                jax.ShapeDtypeStruct((width, width), BF16),
                jax.ShapeDtypeStruct((16, width), F32),
                jax.ShapeDtypeStruct((kinds, LANES), F32),
            ],
            compiler_params=params(56),
            cost_estimate=pl.CostEstimate(flops=12 * 10**9, bytes_accessed=20 * 10**6, transcendentals=10**5),
            name="combine",
        )(own_arr, *to_plane([input_rows[i] for i in range(4)]), pos, aux, route_cols, prev_rows, h1, grads, o, small, attn_o)

        gin, grad_attn, gain_one = pl.pallas_call(
            backward_kernel,
            grid=(batches,),
            in_specs=[
                per_seq((length, width)),
                per_seq((1, length)),
                per_seq((length, 1)),
                per_seq((length, width)),
                per_seq((length, width)),
                per_seq((length, width)),
                per_seq((length, width)),
                per_seq((length, LANES)),
                per_seq((length, width)),
                whole((kinds + 8, width)),
                spec_w(0),
                spec_w(1),
                spec_w(2),
                whole((length, LANES)),
                whole((length, LANES)),
            ],
            out_specs=[per_seq((length, width)), whole((width, 3 * width)), whole((8, width))],
            scratch_shapes=[
                pltpu.VMEM((length, length), F32),
                pltpu.VMEM((LANES, length), F32),
                pltpu.VMEM((length, 3 * width), BF16),
                pltpu.VMEM((width, 3 * width), F32),
            ],
            out_shape=[
                seq_f32,
                jax.ShapeDtypeStruct((width, 3 * width), BF16),
                jax.ShapeDtypeStruct((8, width), F32),
            ],
            compiler_params=params(56),
            cost_estimate=pl.CostEstimate(flops=30 * 10**9, bytes_accessed=20 * 10**6, transcendentals=10**7),
            name="backward",
        )(tokens, seg_row, seg_col, q, k, v, dob, lse, dh1, small, attn, attn, attn, cos, sin)

    result = pl.pallas_call(
        result_kernel,
        grid_spec=pltpu.PrefetchScalarGridSpec(
            num_scalar_prefetch=1,
            grid=(batches,),
            in_specs=[
                pl.BlockSpec((4, 1, capacity, width), lambda b, *_: (0, b, 0, 0)),
                per_seq((kinds, length)),
                per_seq((16, length)),
                per_seq((length, width)),
                whole((kinds + 8, width)),
            ],
            out_specs=per_seq((length, width)),
            scratch_shapes=[pltpu.VMEM((LANES, length), F32)],
        ),
        out_shape=seq_f32,
        compiler_params=params(40),
        cost_estimate=pl.CostEstimate(flops=4 * 10**9, bytes_accessed=12 * 10**6, transcendentals=0),
        name="result",
    )(own_arr, values_in, pos, aux, h1, small)

    if fused:
        attn_total = sums[:, 0 : 4 * width]
        sums = sums[:, 4 * width :]
        map_total = sums[0:kinds, 16 : 16 + kinds]
    else:
        part = lax.psum_scatter(jnp.concatenate([grad_attn, grad_wo], axis=1), "grp", scatter_dimension=0, tiled=True)
        attn_total = lax.psum(part, "rep").astype(F32)
        sgrad = jnp.where(iota((16, 1), 0) == kinds + 6, gain_one[0:1], sgrad)
        packed = jnp.concatenate([sgrad, jnp.pad(grad_map, ((0, 0), (0, width - LANES)))], axis=0)
        packed = lax.psum(packed, ("rep", "grp"))
        sums = lax.dynamic_slice_in_dim(packed[0:16], g * rows_d, rows_d, axis=1).T
        map_total = packed[16:, 0:kinds].T
    return (
        result.reshape(batches * length, width),
        gin.reshape(batches * length, width),
        sums[:, kinds + 6],
        attn_total[:, 0:width],
        attn_total[:, width : 2 * width],
        attn_total[:, 2 * width : 3 * width],
        attn_total[:, 3 * width :],
        sums[:, kinds + 7],
        sums[:, 0:kinds],
        map_total,
        sums[:, kinds : kinds + 4],
        sums[:, kinds + 4 : kinds + 6],
        grad_gate,
        grad_up,
        grad_down,
    )


def solution(mesh):
    rows = P(("rep", "grp"), None)
    in_specs = (
        (rows,) * 5
        + (P("grp"),)
        + (P("grp", None),) * 4
        + (P("grp"), P("grp", None), P(), P("grp", None), P("grp", None))
        + (P("grp", None, None),) * 3
    )
    out_specs = (
        (rows,) * 2
        + (P("grp"),)
        + (P("grp", None),) * 4
        + (P("grp"), P("grp", None), P(), P("grp", None), P("grp", None))
        + (P("grp", None, None),) * 3
    )
    body = functools.partial(local, mesh.shape["rep"], mesh.shape["grp"])
    return jax.shard_map(body, mesh=mesh, in_specs=in_specs, out_specs=out_specs, check_vma=False)
```

```python
import functools

import jax
import jax.numpy as jnp
from jax import lax
from jax.experimental import pallas as pl
from jax.experimental.pallas import tpu as pltpu
from jax.sharding import PartitionSpec as P

HEAD_DIM = 64
BLOCK = 256
EPS = 1e-05
NEG = -1000000000.0
F32 = jnp.float32
BF16 = jnp.bfloat16
LANES = 128


def nn(a, b):
    return lax.dot_general(a, b, (((1,), (0,)), ((), ())), preferred_element_type=F32)


def nt(a, b):
    return lax.dot_general(a, b, (((1,), (1,)), ((), ())), preferred_element_type=F32)


def tn(a, b):
    return lax.dot_general(a, b, (((0,), (0,)), ((), ())), preferred_element_type=F32)


def iota(shape, dim):
    return lax.broadcasted_iota(jnp.int32, shape, dim)


def split2(values):
    high = values.astype(BF16)
    low = (values - high.astype(F32)).astype(BF16)
    return high, low


def whole(shape, buffers=None):
    zeros = (0,) * len(shape)
    if buffers:
        return pl.BlockSpec(shape, lambda *_: zeros, pipeline_mode=pl.Buffered(buffers))
    return pl.BlockSpec(shape, lambda *_: zeros)


def per_seq(shape):
    tail = (0,) * len(shape)
    return pl.BlockSpec((1,) + shape, lambda b, *_: (b,) + tail)


def rms_scale(values):
    return lax.rsqrt(jnp.mean(values * values, axis=-1, keepdims=True) + EPS)


def slot_mask(position_row, capacity):
    places = iota((capacity, position_row.shape[1]), 0).astype(F32)
    return jnp.where(places == position_row, 1.0, 0.0).astype(BF16)


def grad_rows_kernel(own_ref, routes_ref, grad_ref, r0, r1, r2, r3, pos_ref):
    own = own_ref[0]
    kinds, length = pos_ref.shape[1:]
    capacity = r0.shape[1]
    ids = iota((kinds, length), 0)
    first = routes_ref[0, 0:1, :] == ids
    second = routes_ref[0, 1:2, :] == ids
    hits = jnp.where(first | second, 1.0, 0.0)
    before = jnp.where(iota((length, length), 0) < iota((length, length), 1), 1.0, 0.0)
    slots = nn(hits.astype(BF16), before.astype(BF16))
    pos_ref[0] = jnp.where(hits > 0.0, slots, -1.0)
    for number, rows in enumerate((r0, r1, r2, r3)):
        line = pos_ref[0, pl.ds(own ^ number, 1), :]
        rows[0] = nn(slot_mask(line, capacity), grad_ref[0]).astype(BF16)


def swap_halves(values, low_half):
    return jnp.where(low_half, pltpu.roll(values, 96, 1), pltpu.roll(values, 32, 1))


def sequence_forward(
    x_ref,
    seg_row_ref,
    seg_col_ref,
    routes_ref,
    prev_ref,
    map_ref,
    small_ref,
    wq_ref,
    wk_ref,
    wv_ref,
    wo_ref,
    cos_ref,
    sin_ref,
    pos_ref,
    q_ref,
    k_ref,
    v_ref,
    o_ref,
    h_ref,
    lse_ref,
    aux_ref,
    rows_refs,
    bias_ref,
    proj_ref,
    expert_of,
    between=None,
):
    length, width = x_ref.shape[1:]
    kinds = pos_ref.shape[1]
    capacity = length // 2
    tokens = x_ref[0].astype(F32)
    gain_one = small_ref[kinds + 6 : kinds + 7, :]
    gain_two = small_ref[kinds + 7 : kinds + 8, :]
    a1 = (tokens * rms_scale(tokens) * gain_one).astype(BF16)
    lane = iota((1, LANES), 1)
    low_half = (lane % HEAD_DIM) < (HEAD_DIM // 2)
    first_head = lane < HEAD_DIM
    mask_a = jnp.where(first_head, 1.0, 0.0).astype(BF16)
    mask_b = jnp.where(first_head, 0.0, 1.0).astype(BF16)
    pairs = width // LANES

    for weights, target, scale in ((wq_ref, q_ref, 0.125), (wk_ref, k_ref, 1.0)):
        proj_ref[...] = nn(a1, weights[...])

        def turn(h, carry):
            cols = pl.ds(pl.multiple_of(h * LANES, LANES), LANES)
            part = proj_ref[:, cols]
            turned = part * cos_ref[...] + swap_halves(part, low_half) * sin_ref[...]
            target[0, :, cols] = turned.astype(BF16) * jnp.asarray(scale, BF16)
            return carry

        lax.fori_loop(0, pairs, turn, 0)
    v_ref[0] = nn(a1, wv_ref[...]).astype(BF16)

    allowed = (seg_col_ref[0] == seg_row_ref[0]) & (
        iota((length, length), 1) // BLOCK <= iota((length, length), 0) // BLOCK
    )
    bias_ref[...] = jnp.where(allowed, 0.0, NEG)
    lse_ref[...] = jnp.zeros_like(lse_ref)
    if between is not None:
        between()

    def pair(h, carry):
        cols = pl.ds(pl.multiple_of(h * LANES, LANES), LANES)
        for begin in range(0, length, BLOCK):
            end = begin + BLOCK
            queries = q_ref[0, begin:end, cols]
            keys = k_ref[0, 0:end, cols]
            values = v_ref[0, 0:end, cols]
            bias = bias_ref[begin:end, 0:end]
            sums = lse_ref[0, begin:end, :]
            outs = []
            for half, mask in enumerate((mask_a, mask_b)):
                scores = nt(queries * mask, keys) + bias
                top = jnp.max(scores, axis=-1, keepdims=True)
                grown = jnp.exp(scores - top)
                total = jnp.sum(grown, axis=-1, keepdims=True)
                chances = (grown * (1.0 / total)).astype(BF16)
                outs.append(nn(chances, values))
                sums = jnp.where(lane == 2 * h + half, top + jnp.log(total), sums)
            lse_ref[0, begin:end, :] = sums
            o_ref[0, begin:end, cols] = jnp.where(first_head, outs[0], outs[1]).astype(BF16)
        return carry

    lax.fori_loop(0, pairs, pair, 0)

    hidden = tokens + nn(o_ref[0], wo_ref[...])
    h_ref[0] = hidden
    a2 = (hidden * rms_scale(hidden) * gain_two).astype(BF16)
    logits = nt(small_ref[...].astype(BF16), a2)[0:kinds, :]
    for j in range(kinds):
        logits = logits + map_ref[:, j : j + 1] * prev_ref[0, j : j + 1, :]
    ids = iota((kinds, length), 0)
    first = jnp.where(routes_ref[0, 0:1, :] == ids, 1.0, 0.0)
    second = jnp.where(routes_ref[0, 1:2, :] == ids, 1.0, 0.0)
    one = jnp.sum(logits * first, axis=0, keepdims=True)
    two = jnp.sum(logits * second, axis=0, keepdims=True)
    top = jnp.maximum(one, two)
    grown_one, grown_two = jnp.exp(one - top), jnp.exp(two - top)
    gate_one = grown_one / (grown_one + grown_two)
    gate_two = grown_two / (grown_one + grown_two)
    aux_ref[0, 0:kinds, :] = gate_one * first + gate_two * second
    aux_ref[0, kinds : kinds + 1, :] = gate_one
    aux_ref[0, kinds + 1 : kinds + 2, :] = gate_two
    aux_ref[0, kinds + 2 :, :] = jnp.zeros((aux_ref.shape[1] - kinds - 2, length), F32)

    place = iota((16, length), 0)
    for number, rows in enumerate(rows_refs):
        mask = slot_mask(pos_ref[0, pl.ds(expert_of(number), 1), :], capacity)
        rows[0, 0:capacity, :] = nn(mask, a2).astype(BF16)
        line = aux_ref[0, pl.ds(expert_of(number), 1), :]
        high = line.astype(BF16).astype(F32)
        mid = (line - high).astype(BF16).astype(F32)
        low = line - high - mid
        parts = jnp.where(place == 0, high, jnp.where(place == 1, mid, jnp.where(place == 2, low, 0.0)))
        spread = nt(parts.astype(BF16), mask)
        filled = jnp.max(pos_ref[0, pl.ds(expert_of(number), 1), :], axis=1, keepdims=True) + 1.0
        spread = jnp.where(iota((16, 1), 0) == 3, filled, spread)
        rows[0, capacity:, 0:capacity] = spread.astype(BF16)
        rows[0, capacity:, capacity:] = jnp.zeros((16, width - capacity), BF16)


def forward_kernel(
    own_ref,
    x_ref,
    seg_row_ref,
    seg_col_ref,
    routes_ref,
    prev_ref,
    map_ref,
    small_ref,
    wq_ref,
    wk_ref,
    wv_ref,
    wo_ref,
    cos_ref,
    sin_ref,
    pos_ref,
    q_ref,
    k_ref,
    v_ref,
    o_ref,
    h_ref,
    lse_ref,
    aux_ref,
    r0,
    r1,
    r2,
    r3,
    bias_ref,
    proj_ref,
):
    own = own_ref[0]
    sequence_forward(
        x_ref,
        seg_row_ref,
        seg_col_ref,
        routes_ref,
        prev_ref,
        map_ref,
        small_ref,
        wq_ref,
        wk_ref,
        wv_ref,
        wo_ref,
        cos_ref,
        sin_ref,
        pos_ref,
        q_ref,
        k_ref,
        v_ref,
        o_ref,
        h_ref,
        lse_ref,
        aux_ref,
        (r0, r1, r2, r3),
        bias_ref,
        proj_ref,
        lambda number: own ^ number,
    )


MESH = pl.DeviceIdType.MESH


class Place:
    def __init__(self, group):
        self.group = group
        self.planes = group // 4
        self.g = lax.axis_index("grp")
        self.y = lax.axis_index("rep")
        self.core = self.g % 2
        self.x = (self.g // 2) % 2
        self.z = self.g // 4
        self.core_peer = (self.y, self.g + 1 - 2 * self.core)
        self.x_peer = (self.y, self.g + 2 - 4 * self.x)
        self.y_peer = (1 - self.y, self.g)
        self.xy_peer = (1 - self.y, self.g + 2 - 4 * self.x)
        self.plane_peers = (None, self.x_peer, self.y_peer, self.xy_peer)

    def z_peer(self, k):
        return (self.y, (self.g + 4 * k) % self.group)

    def block(self, z, x, core):
        return (z * 2 + x) * 2 + core

    def expert(self, number):
        y = self.y if number < 2 else 1 - self.y
        x = self.x if number % 2 == 0 else 1 - self.x
        return 2 * y + x

    def barrier(self, peers):
        semaphore = pltpu.get_barrier_semaphore()
        for peer in peers:
            pl.semaphore_signal(semaphore, inc=1, device_id=peer, device_id_type=MESH)
        pl.semaphore_wait(semaphore, len(peers))


def remote(src, dst, send, recv, peer):
    return pltpu.make_async_remote_copy(
        src_ref=src, dst_ref=dst, send_sem=send, recv_sem=recv, device_id=peer, device_id_type=MESH
    )


def fused_forward_kernel(
    group,
    x_ref,
    seg_row_ref,
    seg_col_ref,
    routes_ref,
    prev_ref,
    map_ref,
    grad_ref,
    cos_ref,
    sin_ref,
    shard_ref,
    shard_o_ref,
    gate4_ref,
    up4_ref,
    down4_ref,
    q_ref,
    k_ref,
    v_ref,
    o_ref,
    h_ref,
    lse_ref,
    aux_ref,
    pos_ref,
    small_ref,
    attn_out_ref,
    attn_o_out_ref,
    rows_in_ref,
    grads_in_ref,
    gate_full_ref,
    up_full_ref,
    down_full_ref,
    attn_ref,
    attn_o_ref,
    bias_ref,
    proj_ref,
    rows_ref,
    grows_ref,
    local_sem,
    attn_send,
    attn_recv,
    ffn_local,
    ffn_send,
    ffn_recv,
    out_sem,
    row_local,
    row_send,
    row_recv,
):
    step = pl.program_id(0)
    last = pl.num_programs(0) - 1
    here = Place(group)
    planes = here.planes
    batches, kinds, length = pos_ref.shape
    width = x_ref.shape[2]
    capacity = length // 2
    shards = ((shard_ref, attn_ref), (shard_o_ref, attn_o_ref))
    experts = ((gate4_ref, gate_full_ref), (up4_ref, up_full_ref), (down4_ref, down_full_ref))
    depth = shard_ref.shape[0]
    mine = here.block(here.z, here.x, here.core)

    def rows_of(block):
        return pl.ds(pl.multiple_of(block * depth, 16), depth)

    def attn_part(t, block, part):
        full = shards[t][1]
        half = full.shape[1] // 2
        if part is None:
            return full.at[rows_of(block), :]
        return full.at[rows_of(block), pl.ds(pl.multiple_of(part * half, LANES), half)]

    def attn_copy(t, slot, z, x, part, peer):
        ref = attn_part(t, here.block(z, x, here.core), part)
        return remote(ref, ref, attn_send.at[t, slot], attn_recv.at[t, slot], peer)

    def to_z(t, k):
        return attn_copy(t, k, here.z, here.x, None, here.z_peer(1 if k == 0 else planes - 1))

    def from_z(t, k):
        return attn_copy(t, k, z_at(planes - 1 if k == 0 else 1), here.x, None, here.x_peer)

    def pass_z(t, k):
        z = z_at(planes - 1 if k == 0 else 1)
        return attn_copy(t, 2 + k, z, here.x, k, here.z_peer(1 if k == 0 else planes - 1))

    def passed_z(t, k):
        return attn_copy(t, 2 + k, z_at(2), here.x, k, here.x_peer)

    def to_x(t, step_z):
        return attn_copy(t, 4 + step_z, z_at(step_z), here.x, here.y, here.x_peer)

    def from_x(t, step_z):
        return attn_copy(t, 4 + step_z, z_at(step_z), 1 - here.x, here.y, here.x_peer)

    def to_y(t, step_z):
        return attn_copy(t, 4 + planes + step_z, z_at(step_z), 1 - here.x, here.y, here.y_peer)

    def from_y(t, step_z):
        return attn_copy(t, 4 + planes + step_z, z_at(step_z), 1 - here.x, 1 - here.y, here.y_peer)

    def to_core(t, step_z, x):
        return attn_copy(t, 4 + 2 * planes + 2 * step_z + x, z_at(step_z), here.x if x == 0 else 1 - here.x, None, here.core_peer)

    def from_core(t, step_z, x):
        ref = attn_part(t, here.block(z_at(step_z), here.x if x == 0 else 1 - here.x, 1 - here.core), None)
        slot = 4 + 2 * planes + 2 * step_z + x
        return remote(ref, ref, attn_send.at[t, slot], attn_recv.at[t, slot], here.core_peer)

    def z_at(k):
        return (here.z + k) % planes

    def ffn_to_x(j):
        source, full = experts[j]
        return remote(
            source.at[here.expert(1)],
            full.at[here.z, here.x, here.core],
            ffn_send.at[j, 0],
            ffn_recv.at[j, 0],
            here.x_peer,
        )

    def ffn_from_x(j):
        source, full = experts[j]
        return remote(
            source.at[here.expert(1)],
            full.at[here.z, 1 - here.x, here.core],
            ffn_send.at[j, 0],
            ffn_recv.at[j, 0],
            here.x_peer,
        )

    def ffn_mine(j):
        source, full = experts[j]
        return pltpu.make_async_copy(source.at[here.expert(0)], full.at[here.z, here.x, here.core], ffn_local.at[j])

    def ffn_copy(j, slot, z, x, core, peer):
        full = experts[j][1]
        part = full.at[z, :, core] if x is None else full.at[z, x, core]
        return remote(part, part, ffn_send.at[j, slot], ffn_recv.at[j, slot], peer)

    def ffn_to_z(j, k):
        return ffn_copy(j, 1 + k, here.z, None, here.core, here.z_peer(1 if k == 0 else planes - 1))

    def ffn_from_z(j, k):
        return ffn_copy(j, 1 + k, z_at(planes - 1 if k == 0 else 1), None, here.core, here.x_peer)

    def ffn_pass_z(j, k):
        z = z_at(planes - 1 if k == 0 else 1)
        return ffn_copy(j, 3 + k, z, k, here.core, here.z_peer(1 if k == 0 else planes - 1))

    def ffn_passed_z(j, k):
        return ffn_copy(j, 3 + k, z_at(2), k, here.core, here.x_peer)

    def ffn_to_core(j, step_z):
        return ffn_copy(j, 5 + step_z, z_at(step_z), None, here.core, here.core_peer)

    def ffn_from_core(j, step_z):
        return ffn_copy(j, 5 + step_z, z_at(step_z), None, 1 - here.core, here.core_peer)

    def row_copy(kind, member, number):
        source, target = ((grows_ref, grads_in_ref), (rows_ref, rows_in_ref))[kind]
        src, dst = source.at[member, number], target.at[number, member]
        if number == 0:
            return pltpu.make_async_copy(src, dst, row_local.at[kind, member])
        return remote(
            src,
            dst,
            row_send.at[kind, member, number],
            row_recv.at[kind, member, number],
            here.plane_peers[number],
        )

    def outs(t):
        full, target = ((attn_ref, attn_out_ref), (attn_o_ref, attn_o_out_ref))[t]
        return pltpu.make_async_copy(full, target, out_sem.at[t])

    @pl.when(step == 0)
    def _():
        own_copies = [
            pltpu.make_async_copy(source, full.at[rows_of(mine), :], local_sem.at[t])
            for t, (source, full) in enumerate(shards)
        ]
        for copy in own_copies:
            copy.start()
        for j in range(3):
            ffn_mine(j).start()
        here.barrier(
            [here.core_peer, here.x_peer, here.y_peer, here.xy_peer, here.z_peer(1), here.z_peer(planes - 1)]
        )
        for copy in own_copies:
            copy.wait()
        for t in range(2):
            to_z(t, 0).start()
            to_z(t, 1).start()
            to_x(t, 0).start()
            to_core(t, 0, 0).start()
        for j in range(3):
            ffn_to_x(j).start()

        ids = iota((kinds, length), 0)
        before = jnp.where(iota((length, length), 0) < iota((length, length), 1), 1.0, 0.0).astype(BF16)
        for member in range(batches):
            first = routes_ref[member, 0:1, :] == ids
            second = routes_ref[member, 1:2, :] == ids
            hits = jnp.where(first | second, 1.0, 0.0)
            pos_ref[member] = jnp.where(hits > 0.0, nn(hits.astype(BF16), before), -1.0)
            for number in range(4):
                line = pos_ref[member, pl.ds(here.expert(number), 1), :]
                grows_ref[member, number] = nn(slot_mask(line, capacity), grad_ref[member]).astype(BF16)
            row_copy(0, member, 0).start()
            row_copy(0, member, 2).start()

        for t in range(2):
            for k, step_z in enumerate((planes - 1, 1)):
                from_z(t, k).wait_recv()
                pass_z(t, k).start()
                to_x(t, step_z).start()
                to_core(t, step_z, 0).start()
        for t in range(2):
            from_x(t, 0).wait_recv()
            to_y(t, 0).start()
        for j in range(3):
            ffn_mine(j).wait()
            ffn_from_x(j).wait_recv()
            ffn_to_z(j, 0).start()
            ffn_to_z(j, 1).start()
            ffn_to_core(j, 0).start()
        for t in range(2):
            passed_z(t, 0).wait_recv()
            passed_z(t, 1).wait_recv()
            to_x(t, 2).start()
            to_core(t, 2, 0).start()
        for member in range(batches):
            row_copy(0, member, 1).start()
            row_copy(0, member, 3).start()
        for t in range(2):
            for step_z in (planes - 1, 1, 2):
                from_x(t, step_z).wait_recv()
                to_y(t, step_z).start()
        for t in range(2):
            for step_z in (0, planes - 1, 1, 2):
                from_y(t, step_z).wait_recv()
                to_core(t, step_z, 1).start()
        for t in range(2):
            for step_z in range(planes):
                for x in range(2):
                    from_core(t, step_z, x).wait_recv()
        for t in range(2):
            outs(t).start()
        small_ref[...] = jnp.transpose(attn_ref[:, 3 * width : 3 * width + LANES].astype(F32))[0 : kinds + 8, :]

    def between():
        @pl.when(step == last)
        def _():
            for j in range(3):
                for k, step_z in enumerate((planes - 1, 1)):
                    ffn_from_z(j, k).wait_recv()
                    ffn_pass_z(j, k).start()
                    ffn_to_core(j, step_z).start()

    sequence_forward(
        x_ref,
        seg_row_ref,
        seg_col_ref,
        routes_ref.at[pl.ds(step, 1)],
        prev_ref,
        map_ref,
        small_ref,
        attn_ref.at[:, 0:width],
        attn_ref.at[:, width : 2 * width],
        attn_ref.at[:, 2 * width : 3 * width],
        attn_o_ref,
        cos_ref,
        sin_ref,
        pos_ref.at[pl.ds(step, 1)],
        q_ref,
        k_ref,
        v_ref,
        o_ref,
        h_ref,
        lse_ref,
        aux_ref,
        [rows_ref.at[pl.ds(step, 1), number] for number in range(4)],
        bias_ref,
        proj_ref,
        here.expert,
        between,
    )
    for member in range(batches):

        @pl.when(step == member)
        def _():
            for number in range(4):
                row_copy(1, member, number).start()

    @pl.when(step == last)
    def _():
        for j in range(3):
            for k in range(2):
                ffn_passed_z(j, k).wait_recv()
            ffn_to_core(j, 2).start()
        for t in range(2):
            outs(t).wait()
            for k in range(2):
                to_z(t, k).wait_send()
                pass_z(t, k).wait_send()
            for step_z in range(planes):
                to_x(t, step_z).wait_send()
                to_y(t, step_z).wait_send()
                for x in range(2):
                    to_core(t, step_z, x).wait_send()
        for j in range(3):
            ffn_to_x(j).wait_send()
            for k in range(2):
                ffn_to_z(j, k).wait_send()
                ffn_pass_z(j, k).wait_send()
            for step_z in range(planes):
                ffn_to_core(j, step_z).wait_send()
                ffn_from_core(j, step_z).wait_recv()
        for kind in range(2):
            for member in range(batches):
                for number in range(4):
                    copy = row_copy(kind, member, number)
                    copy.wait()


def expert_kernel(
    a_ref,
    g_ref,
    gate_ref,
    up_ref,
    down_ref,
    v_ref,
    d_ref,
    grad_gate_ref,
    grad_up_ref,
    grad_down_ref,
    rows_ref,
    grads_ref,
    gates_ref,
    rows_t_ref,
    grads_t_ref,
    places_ref,
    acc_value_ref,
    acc_input_ref,
    acc_gate_ref,
    acc_up_ref,
    acc_down_ref,
    share_ref,
    sems,
):
    step = pl.program_id(0)
    last = pl.num_programs(0) - 1
    batches, capacity, width = g_ref.shape[1:]
    blocks = 4 * batches

    @pl.when(step == 0)
    def _():
        copies = []
        for number in range(4):
            rows, grads = a_ref.at[number], g_ref.at[number]
            for member in range(batches):
                block = number * batches + member
                span = pl.ds(block * capacity, capacity)
                copies.append(
                    pltpu.make_async_copy(
                        rows.at[member, pl.ds(capacity, 16), pl.ds(0, capacity)],
                        gates_ref.at[block],
                        sems.at[3 * block],
                    )
                )
                copies.append(
                    pltpu.make_async_copy(
                        rows.at[member, pl.ds(0, capacity), :], rows_ref.at[span, :], sems.at[3 * block + 1]
                    )
                )
                copies.append(
                    pltpu.make_async_copy(grads.at[member], grads_ref.at[span, :], sems.at[3 * block + 2])
                )
        for copy in copies:
            copy.start()
        for copy in copies:
            copy.wait()
        same = iota((capacity, capacity), 0) == iota((capacity, capacity), 1)
        spare = jnp.zeros((capacity, width), BF16)
        rows_ref[blocks * capacity :, :] = spare
        grads_ref[blocks * capacity :, :] = spare
        share_ref[...] = jnp.zeros_like(share_ref)

        def pack(block, place):
            span = pl.ds(pl.multiple_of(block * capacity, capacity), capacity)
            target = pl.ds(pl.multiple_of(place, 16), capacity)
            parts = gates_ref[block].astype(F32)
            count = jnp.max(parts[3:4, :]).astype(jnp.int32)
            line = jnp.sum(parts[0:3, :], axis=0, keepdims=True)
            column = jnp.sum(jnp.where(same, line, 0.0), axis=1, keepdims=True)
            rows = rows_ref[span, :]
            grads = (grads_ref[span, :].astype(F32) * column).astype(BF16)
            rows_ref[target, :] = rows
            grads_ref[target, :] = grads
            places_ref[block] = place
            return place + (count + 15) // 16 * 16

        total = lax.fori_loop(0, blocks, pack, 0)
        target = pl.ds(pl.multiple_of(total, 16), capacity)
        rows_ref[target, :] = spare
        grads_ref[target, :] = spare
        places_ref[blocks] = (total + capacity - 1) // capacity

        def turn(block, carry):
            span = pl.ds(pl.multiple_of(block * capacity, capacity), capacity)
            grads_t_ref[:, span] = jnp.transpose(grads_ref[span, :])
            rows_t_ref[:, span] = jnp.transpose(rows_ref[span, :])
            return carry

        lax.fori_loop(0, places_ref[blocks], turn, 0)

    acc_gate_ref[...] = jnp.zeros_like(acc_gate_ref)
    acc_up_ref[...] = jnp.zeros_like(acc_up_ref)
    acc_down_ref[...] = jnp.zeros_like(acc_down_ref)

    def work(block, carry):
        span = pl.ds(pl.multiple_of(block * capacity, capacity), capacity)
        rows = rows_ref[span, :]
        grads = grads_ref[span, :]
        gate = nn(rows, gate_ref[...])
        up = nn(rows, up_ref[...])
        back = nt(grads, down_ref[...])
        sig = 1.0 / (1.0 + jnp.exp(-gate))
        silu = gate * sig
        act = (silu * up).astype(BF16)
        grad_gate = (back * up * (sig * (1.0 + gate * (1.0 - sig)))).astype(BF16)
        grad_up = (back * silu).astype(BF16)
        value = nn(act, down_ref[...])
        grad_rows = nt(grad_gate, gate_ref[...]) + nt(grad_up, up_ref[...])
        rows_t = rows_t_ref[:, span]
        acc_gate_ref[...] += nn(rows_t, grad_gate)
        acc_up_ref[...] += nn(rows_t, grad_up)
        acc_down_ref[...] += nn(grads_t_ref[:, span], act)
        share = jnp.broadcast_to(
            jnp.sum(act.astype(F32) * back, axis=1, keepdims=True), (capacity, LANES)
        )

        @pl.when(step == 0)
        def _():
            share_ref[span, :] = share
            acc_value_ref[span, :] = value
            acc_input_ref[span, :] = grad_rows

        @pl.when(step > 0)
        def _():
            share_ref[span, :] += share

        @pl.when((step > 0) & (step < last))
        def _():
            acc_value_ref[span, :] += value
            acc_input_ref[span, :] += grad_rows

        @pl.when(step == last)
        def _():
            rows_ref[span, :] = (acc_value_ref[span, :] + value).astype(BF16)
            grads_ref[span, :] = (acc_input_ref[span, :] + grad_rows).astype(BF16)

        return carry

    lax.fori_loop(0, places_ref[blocks], work, 0)
    grad_gate_ref[...] = acc_gate_ref[...].astype(BF16)
    grad_up_ref[...] = acc_up_ref[...].astype(BF16)
    grad_down_ref[...] = jnp.transpose(acc_down_ref[...].astype(BF16))

    @pl.when(step == last)
    def _():
        same = iota((capacity, capacity), 0) == iota((capacity, capacity), 1)
        place = iota((16, capacity), 0)

        def shares(block, carry):
            column = share_ref[pl.ds(pl.multiple_of(places_ref[block], 16), capacity), 0:1]
            line = jnp.sum(jnp.where(same, column, 0.0), axis=0, keepdims=True)
            high = line.astype(BF16).astype(F32)
            mid = (line - high).astype(BF16).astype(F32)
            low = line - high - mid
            parts = jnp.where(place == 0, high, jnp.where(place == 1, mid, jnp.where(place == 2, low, 0.0)))
            gates_ref[block] = parts.astype(BF16)
            return carry

        lax.fori_loop(0, blocks, shares, 0)
        copies = []
        for number in range(4):
            values, grads = v_ref.at[number], d_ref.at[number]
            for member in range(batches):
                block = number * batches + member
                span = pl.ds(pl.multiple_of(places_ref[block], 16), capacity)
                copies.append(pltpu.make_async_copy(rows_ref.at[span, :], values.at[member], sems.at[3 * block]))
                copies.append(
                    pltpu.make_async_copy(
                        grads_ref.at[span, :], grads.at[member, pl.ds(0, capacity), :], sems.at[3 * block + 1]
                    )
                )
                copies.append(
                    pltpu.make_async_copy(
                        gates_ref.at[block],
                        grads.at[member, pl.ds(capacity, 16), pl.ds(0, capacity)],
                        sems.at[3 * block + 2],
                    )
                )
        for copy in copies:
            copy.start()
        for copy in copies:
            copy.wait()


def constant_mix(zs, index):
    za, zb = zs[:, index : index + 1], zs[:, index + 1 : index + 2]
    top = jnp.maximum(za, zb)
    ea, eb = jnp.exp(za - top), jnp.exp(zb - top)
    return ea / (ea + eb), eb / (ea + eb)


def token_columns(pos_ref, aux_ref, cols_ref):
    kinds, length = pos_ref.shape[1:]
    cols_ref[0:kinds, :] = pos_ref[0]
    cols_ref[kinds : kinds + 16, :] = aux_ref[0]
    cols_ref[kinds + 16 :, :] = jnp.zeros((LANES - kinds - 16, length), F32)
    return jnp.transpose(cols_ref[...])


def column(source, index):
    return jnp.sum(jnp.where(iota((1, LANES), 1) == index, source, 0.0), axis=1, keepdims=True)


def result_kernel(own_ref, v_ref, pos_ref, aux_ref, h_ref, small_ref, out_ref, cols_ref):
    own = own_ref[0]
    length, width = h_ref.shape[1:]
    kinds = pos_ref.shape[1]
    ffn = kinds - 4
    capacity = v_ref.shape[2]
    hidden = h_ref[0]
    n2 = hidden * rms_scale(hidden) * small_ref[kinds + 7 : kinds + 8, :]
    n2_high, n2_low = split2(n2)
    small = small_ref[...].astype(BF16)
    cols = token_columns(pos_ref, aux_ref, cols_ref)
    result = hidden
    slot_lane = iota((1, capacity), 1).astype(F32)
    for number in range(4):
        expert = own ^ number
        mask = jnp.where(column(cols, expert) == slot_lane, 1.0, 0.0).astype(BF16)
        result = result + column(cols, kinds + expert) * nn(mask, v_ref[number, 0])
    mixes = nt(n2_high, small) + nt(n2_low, small)
    share = column(cols, kinds + ffn + 1)
    for constant in range(2):
        weight = column(cols, kinds + ffn + 2 + constant)
        alpha_a, alpha_b = constant_mix(mixes, kinds + 2 * constant)
        result = result + (weight * alpha_b) * small_ref[kinds + 4 + constant : kinds + 5 + constant, :]
        share = share + weight * alpha_a
    out_ref[0] = result + share * n2


def sequence_combine(
    step,
    d_refs,
    pos_ref,
    aux_ref,
    routes_ref,
    prev_ref,
    h_ref,
    g_ref,
    o_ref,
    small_ref,
    wo_ref,
    dh_ref,
    dob_ref,
    sgrad_ref,
    grad_map_ref,
    acc_ref,
    cols_ref,
    expert_of,
):
    length, width = h_ref.shape[1:]
    kinds = pos_ref.shape[1]
    ffn = kinds - 4
    capacity = d_refs[0].shape[1] - 16
    hidden = h_ref[0]
    inverse = rms_scale(hidden)
    gain = small_ref[kinds + 7 : kinds + 8, :]
    n2 = hidden * inverse * gain
    n2_high, n2_low = split2(n2)
    grad_low = g_ref[0]
    grad = grad_low.astype(F32)
    small = small_ref[...].astype(BF16)
    cols = token_columns(pos_ref, aux_ref, cols_ref)
    lane = iota((1, LANES), 1)
    gate_one = column(cols, 2 * kinds)
    gate_two = column(cols, 2 * kinds + 1)
    hot_one = jnp.where(routes_ref[0, :, 0:1] == lane, 1.0, 0.0)
    hot_two = jnp.where(routes_ref[0, :, 1:2] == lane, 1.0, 0.0)

    grad_n2 = jnp.zeros((length, width), F32)
    shares = jnp.zeros((length, LANES), F32)
    slot_lane = iota((1, capacity), 1).astype(F32)
    for number, rows in enumerate(d_refs):
        expert = expert_of(number)
        mask = jnp.where(column(cols, expert) == slot_lane, 1.0, 0.0).astype(BF16)
        grad_n2 = grad_n2 + nn(mask, rows[0, 0:capacity, :])
        parts = nt(mask, rows[0, capacity:, 0:capacity])
        shares = jnp.where(lane == expert, jnp.sum(parts, axis=1, keepdims=True), shares)

    mixes = nt(n2_high, small) + nt(n2_low, small)
    inner = nt(grad_low, small)
    with_n2 = jnp.sum(grad * n2, axis=1, keepdims=True)
    weight_copy = column(cols, kinds + ffn + 1)
    shares = jnp.where(lane == ffn + 1, weight_copy * with_n2, shares)
    share = weight_copy
    coefs = jnp.zeros((length, LANES), F32)
    for constant in range(2):
        weight = column(cols, kinds + ffn + 2 + constant)
        alpha_a, alpha_b = constant_mix(mixes, kinds + 2 * constant)
        with_vec = inner[:, kinds + 4 + constant : kinds + 5 + constant]
        share = share + weight * alpha_a
        da = weight * with_n2
        db = weight * with_vec
        mean = alpha_a * da + alpha_b * db
        shares = jnp.where(lane == ffn + 2 + constant, mean, shares)
        coefs = jnp.where(lane == kinds + 2 * constant, alpha_a * (da - mean), coefs)
        coefs = jnp.where(lane == kinds + 2 * constant + 1, alpha_b * (db - mean), coefs)
        coefs = jnp.where(lane == kinds + 4 + constant, weight * alpha_b, coefs)

    share_one = jnp.sum(shares * hot_one, axis=1, keepdims=True)
    share_two = jnp.sum(shares * hot_two, axis=1, keepdims=True)
    both = share_one + share_two
    dlogits = (share_one - gate_one * both) * hot_one + (share_two - gate_two * both) * hot_two
    coefs = jnp.where(lane < kinds, dlogits, coefs)
    back = jnp.where(lane < kinds + 4, coefs, 0.0)[:, 0:16]
    back_high, back_low = split2(back)
    grad_n2 = grad_n2 + nn(back_high, small) + nn(back_low, small) + share * grad

    coefs_t = jnp.transpose(coefs)[0:16, :]
    high, low = split2(coefs_t)
    by_n2 = nn(high, n2_high) + nn(low, n2_high)
    by_low = nn(high, n2_low)
    by_grad = nn(high, grad_low) + nn(low, grad_low)
    row = iota((16, 1), 0)
    parts = jnp.where(row < kinds, by_n2, jnp.where(row < kinds + 4, by_n2 + by_low, by_grad))
    gain_part = jnp.sum(grad_n2 * hidden * inverse, axis=0, keepdims=True)
    parts = jnp.where(row == kinds + 7, gain_part, jnp.where(row == kinds + 6, 0.0, parts))
    dlog_t = coefs_t[0:kinds, :]
    map_lane = iota((kinds, LANES), 1)
    map_part = jnp.zeros((kinds, LANES), F32)
    for j in range(kinds):
        map_part = jnp.where(
            map_lane == j, jnp.sum(dlog_t * prev_ref[0, j : j + 1, :], axis=1, keepdims=True), map_part
        )

    scaled = gain * grad_n2
    inner_mean = jnp.mean(scaled * hidden, axis=-1, keepdims=True)
    dh = grad + inverse * scaled - hidden * (inverse * inverse * inverse) * inner_mean
    dh_ref[0] = dh
    db = dh.astype(BF16)
    dob_ref[0] = nt(db, wo_ref[...]).astype(BF16)
    wo_part = nn(jnp.transpose(o_ref[0]), db)

    @pl.when(step == 0)
    def _():
        acc_ref[...] = wo_part
        sgrad_ref[...] = parts
        grad_map_ref[...] = map_part

    @pl.when(step > 0)
    def _():
        acc_ref[...] += wo_part
        sgrad_ref[...] += parts
        grad_map_ref[...] += map_part


def combine_kernel(
    own_ref,
    d0,
    d1,
    d2,
    d3,
    pos_ref,
    aux_ref,
    routes_ref,
    prev_ref,
    h_ref,
    g_ref,
    o_ref,
    small_ref,
    wo_ref,
    dh_ref,
    dob_ref,
    grad_wo_ref,
    sgrad_ref,
    grad_map_ref,
    acc_ref,
    cols_ref,
):
    own = own_ref[0]
    step = pl.program_id(0)
    sequence_combine(
        step,
        (d0, d1, d2, d3),
        pos_ref,
        aux_ref,
        routes_ref,
        prev_ref,
        h_ref,
        g_ref,
        o_ref,
        small_ref,
        wo_ref,
        dh_ref,
        dob_ref,
        sgrad_ref,
        grad_map_ref,
        acc_ref,
        cols_ref,
        lambda number: own ^ number,
    )

    @pl.when(step == pl.num_programs(0) - 1)
    def _():
        grad_wo_ref[...] = acc_ref[...].astype(BF16)


def sequence_backward(
    step,
    x_ref,
    seg_row_ref,
    seg_col_ref,
    q_ref,
    k_ref,
    v_ref,
    dob_ref,
    lse_ref,
    dh_ref,
    small_ref,
    wq_ref,
    wk_ref,
    wv_ref,
    cos_ref,
    sin_ref,
    gin_ref,
    gain_ref,
    bias_ref,
    lse_t_ref,
    dqkv_ref,
    acc_ref,
):
    length, width = x_ref.shape[1:]
    kinds = small_ref.shape[0] - 8
    pairs = width // LANES
    lane = iota((1, LANES), 1)
    low_half = (lane % HEAD_DIM) < (HEAD_DIM // 2)
    first_head = lane < HEAD_DIM
    mask_a = jnp.where(first_head, 1.0, 0.0).astype(BF16)
    mask_b = jnp.where(first_head, 0.0, 1.0).astype(BF16)
    allowed = (seg_col_ref[0] == seg_row_ref[0]) & (
        iota((length, length), 0) // BLOCK <= iota((length, length), 1) // BLOCK
    )
    bias_ref[...] = jnp.where(allowed, 0.0, NEG)
    lse_t_ref[...] = jnp.transpose(lse_ref[0])

    def pair(h, carry):
        cols = pl.ds(pl.multiple_of(h * LANES, LANES), LANES)
        keys_t = jnp.transpose(k_ref[0, :, cols])
        grad_keys = None
        grad_values = None
        grad_queries = []
        for begin in range(0, length, BLOCK):
            end = begin + BLOCK
            queries = q_ref[0, begin:end, cols]
            outs = dob_ref[0, begin:end, cols]
            keys = k_ref[0, 0:end, cols]
            values = v_ref[0, 0:end, cols]
            queries = jnp.concatenate([queries * mask_a, queries * mask_b], axis=0)
            outs = jnp.concatenate([outs * mask_a, outs * mask_b], axis=0)
            bias = bias_ref[0:end, begin:end]
            bias = jnp.concatenate([bias, bias], axis=1)
            line = jnp.concatenate(
                [lse_t_ref[pl.ds(2 * h, 1), begin:end], lse_t_ref[pl.ds(2 * h + 1, 1), begin:end]], axis=1
            )
            chances = jnp.exp(nt(keys, queries) + bias - line)
            grad_chances = nt(values, outs)
            delta = jnp.sum(chances * grad_chances, axis=0, keepdims=True)
            grad_scores = (chances * (grad_chances - delta)).astype(BF16)
            dv = nn(chances.astype(BF16), outs)
            dk = nn(grad_scores, queries)
            dq = jnp.transpose(nn(keys_t[:, 0:end], grad_scores))
            grad_queries.append(jnp.where(first_head, dq[0:BLOCK], dq[BLOCK:]))
            if grad_keys is None:
                grad_keys, grad_values = dk, dv
            else:
                grad_keys = jnp.concatenate([grad_keys + dk[0:begin], dk[begin:]], axis=0)
                grad_values = jnp.concatenate([grad_values + dv[0:begin], dv[begin:]], axis=0)
        dq = jnp.concatenate(grad_queries, axis=0) * 0.125
        dq = dq * cos_ref[...] - swap_halves(dq, low_half) * sin_ref[...]
        dk = grad_keys * cos_ref[...] - swap_halves(grad_keys, low_half) * sin_ref[...]
        dqkv_ref[:, cols] = dq.astype(BF16)
        dqkv_ref[:, pl.ds(pl.multiple_of(width + h * LANES, LANES), LANES)] = dk.astype(BF16)
        dqkv_ref[:, pl.ds(pl.multiple_of(2 * width + h * LANES, LANES), LANES)] = grad_values.astype(BF16)
        return carry

    lax.fori_loop(0, pairs, pair, 0)

    tokens = x_ref[0].astype(F32)
    inverse = rms_scale(tokens)
    gain = small_ref[kinds + 6 : kinds + 7, :]
    a1_t = jnp.transpose((tokens * inverse * gain).astype(BF16))
    dn1 = (
        nt(dqkv_ref[:, 0:width], wq_ref[...])
        + nt(dqkv_ref[:, width : 2 * width], wk_ref[...])
        + nt(dqkv_ref[:, 2 * width :], wv_ref[...])
    )
    scaled = gain * dn1
    inner_mean = jnp.mean(scaled * tokens, axis=-1, keepdims=True)
    gin_ref[0] = dh_ref[0] + inverse * scaled - tokens * (inverse * inverse * inverse) * inner_mean
    gain_part = jnp.broadcast_to(jnp.sum(dn1 * tokens * inverse, axis=0, keepdims=True), gain_ref.shape)

    @pl.when(step == 0)
    def _():
        acc_ref[...] = jnp.zeros_like(acc_ref)
        gain_ref[...] = gain_part

    @pl.when(step > 0)
    def _():
        gain_ref[...] += gain_part

    for part in range(3):
        span = slice(part * width, (part + 1) * width)
        acc_ref[:, span] += nn(a1_t, dqkv_ref[:, span])


def small_table(depth, sgrad_ref, grad_map_ref, gain_ref):
    kinds = grad_map_ref.shape[0]
    width = sgrad_ref.shape[1]
    row = iota((16, 1), 0)
    table = jnp.where(row == kinds + 6, gain_ref[0:1, :], sgrad_ref[...])
    chosen = jnp.where(iota((LANES, width), 1) % depth == iota((LANES, width), 0), 1.0, 0.0).astype(BF16)
    maps = nn(grad_map_ref[...].astype(BF16), chosen)
    table = jnp.concatenate([table, maps, jnp.zeros((LANES - 16 - kinds, width), F32)], axis=0)
    return jnp.transpose(table).astype(BF16)


def backward_kernel(
    x_ref,
    seg_row_ref,
    seg_col_ref,
    q_ref,
    k_ref,
    v_ref,
    dob_ref,
    lse_ref,
    dh_ref,
    small_ref,
    wq_ref,
    wk_ref,
    wv_ref,
    cos_ref,
    sin_ref,
    gin_ref,
    grad_w_ref,
    gain_ref,
    bias_ref,
    lse_t_ref,
    dqkv_ref,
    acc_ref,
):
    step = pl.program_id(0)
    sequence_backward(
        step,
        x_ref,
        seg_row_ref,
        seg_col_ref,
        q_ref,
        k_ref,
        v_ref,
        dob_ref,
        lse_ref,
        dh_ref,
        small_ref,
        wq_ref,
        wk_ref,
        wv_ref,
        cos_ref,
        sin_ref,
        gin_ref,
        gain_ref,
        bias_ref,
        lse_t_ref,
        dqkv_ref,
        acc_ref,
    )

    @pl.when(step == pl.num_programs(0) - 1)
    def _():
        grad_w_ref[...] = acc_ref[...].astype(BF16)


class ReducedChunk:
    def __init__(self, here, depth, begin, value_of, send_buffer, core_buffer, buffers, out_ref, sems):
        self.here, self.depth, self.begin, self.value_of = here, depth, begin, value_of
        self.send_buffer, self.acc, self.out_ref = send_buffer, core_buffer, out_ref
        y_first, x_first, x_second, y_second, self.z_buffer, self.done, self.other = buffers
        send, recv, z_send, z_recv = sems
        planes, x, y = here.planes, here.x, here.y
        near = planes // 2
        self.half = send_buffer.shape[3] // 2
        self.mine = pl.ds(pl.multiple_of(y * self.half, LANES), self.half)
        theirs = pl.ds(pl.multiple_of((1 - y) * self.half, LANES), self.half)
        self.received = (y_first, x_first, x_second, y_second)
        acc = core_buffer
        self.swap = remote(send_buffer, acc, send.at[0], recv.at[0], here.core_peer)
        self.y_first = remote(acc.at[0:near, :, :, theirs], y_first, send.at[1], recv.at[1], here.y_peer)
        self.x_first = remote(acc.at[near:planes, 1 - x], x_first, send.at[2], recv.at[2], here.x_peer)
        self.x_second = remote(acc.at[0:near, 1 - x, :, self.mine], x_second, send.at[3], recv.at[3], here.x_peer)
        self.y_second = remote(acc.at[near:planes, x, :, theirs], y_second, send.at[4], recv.at[4], here.y_peer)
        self.along = [
            remote(
                acc.at[(here.z + k) % planes, x, :, self.mine],
                self.z_buffer.at[k - 1],
                z_send.at[k - 1],
                z_recv.at[k - 1],
                here.z_peer(k),
            )
            for k in range(1, planes)
        ]
        self.back = remote(self.done, self.other, send.at[5], recv.at[5], here.y_peer)
        self.phases = (self.first, self.second, self.third, self.fourth, self.fifth)

    def rows_of(self, z, column, core):
        return pl.ds(pl.multiple_of(self.here.block(z, column, core) * self.depth, 16), self.depth)

    def lower(self):
        def body(z, carry):
            for column in range(2):
                rows = self.rows_of(z, column, 1 - self.here.core)
                self.send_buffer[z, column] = self.value_of(rows).astype(BF16)
            return carry

        lax.fori_loop(0, self.here.planes, body, 0)

    def add(self, target, source):
        target[...] = (target[...].astype(F32) + source[...].astype(F32)).astype(BF16)

    def first(self):
        self.swap.wait_recv()

        def body(z, carry):
            for column in range(2):
                own = self.value_of(self.rows_of(z, column, self.here.core)).astype(F32)
                self.acc[z, column] = (own + self.acc[z, column].astype(F32)).astype(BF16)
            return carry

        lax.fori_loop(0, self.here.planes, body, 0)
        self.y_first.start()
        self.x_first.start()

    def second(self):
        planes = self.here.planes
        self.y_first.wait_recv()
        for z in range(planes // 2):
            for column in range(2):
                self.add(self.acc.at[z, column, :, self.mine], self.received[0].at[z, column])
        self.x_second.start()
        self.x_first.wait_recv()
        for z in range(planes // 2, planes):
            self.add(self.acc.at[z, self.here.x], self.received[1].at[z - planes // 2])
        self.y_second.start()

    def third(self):
        planes = self.here.planes
        self.x_second.wait_recv()
        for z in range(planes // 2):
            self.add(self.acc.at[z, self.here.x, :, self.mine], self.received[2].at[z])
        self.y_second.wait_recv()
        for z in range(planes // 2, planes):
            self.add(self.acc.at[z, self.here.x, :, self.mine], self.received[3].at[z - planes // 2])
        for copy in self.along:
            copy.start()

    def fourth(self):
        total = self.acc[self.here.z, self.here.x, :, self.mine].astype(F32)
        for k, copy in enumerate(self.along):
            copy.wait_recv()
            total = total + self.z_buffer[k].astype(F32)
        self.done[...] = total.astype(BF16)
        self.back.start()

    def fifth(self):
        self.back.wait_recv()
        y = self.here.y
        spot = pl.ds(pl.multiple_of(self.begin + y * self.half, LANES), self.half)
        other = pl.ds(pl.multiple_of(self.begin + (1 - y) * self.half, LANES), self.half)
        self.out_ref[:, spot] = self.done[...].astype(F32)
        self.out_ref[:, other] = self.other[...].astype(F32)
        for copy in [self.swap, self.y_first, self.x_first, self.x_second, self.y_second, self.back] + self.along:
            copy.wait_send()


def attention_columns(acc_ref, acc_wo_ref, table_ref, begin, columns, rows):
    pieces = []
    width = acc_wo_ref.shape[1]
    for start, size, ref in (
        (0, 3 * width, acc_ref),
        (3 * width, width, acc_wo_ref),
        (4 * width, LANES, table_ref),
        (4 * width + LANES, LANES, None),
    ):
        low, high = max(begin, start) - start, min(begin + columns, start + size) - start
        if low < high:
            if ref is None:
                pieces.append(jnp.zeros((rows.size, high - low), F32))
            else:
                pieces.append(ref[rows, low:high].astype(F32))
    return pieces[0] if len(pieces) == 1 else jnp.concatenate(pieces, axis=1)


def reduce_attention(chunks, free_sem):
    chunks[0].lower()
    pl.semaphore_wait(free_sem, 1)
    chunks[0].swap.start()
    for chunk in chunks[1:]:
        chunk.lower()
        chunk.swap.start()
    phases = len(chunks[0].phases)
    for step in range(len(chunks) + phases - 1):
        for number, chunk in enumerate(chunks):
            if 0 <= step - number < phases:
                chunk.phases[step - number]()


def fused_backward_kernel(
    group,
    depth,
    pos_ref,
    aux_ref,
    routes_ref,
    prev_ref,
    h_ref,
    g_ref,
    o_ref,
    x_ref,
    seg_row_ref,
    seg_col_ref,
    q_ref,
    k_ref,
    v_ref,
    lse_ref,
    small_ref,
    wq_ref,
    wk_ref,
    wv_ref,
    wo_ref,
    cos_ref,
    sin_ref,
    d_ref,
    val_ref,
    gate_ref,
    up_ref,
    down_ref,
    gin_ref,
    sums_ref,
    d_in_ref,
    val_in_ref,
    gate_out_ref,
    up_out_ref,
    down_out_ref,
    acc_ref,
    acc_wo_ref,
    table_ref,
    send_buffers,
    chunk_buffers,
    cols_ref,
    dh_ref,
    dob_ref,
    sgrad_ref,
    grad_map_ref,
    gain_ref,
    bias_ref,
    lse_t_ref,
    dqkv_ref,
    rows_ref,
    gate_own,
    up_own,
    down_own,
    gate_swap,
    up_swap,
    down_swap,
    gate_near,
    up_near,
    down_near,
    gate_far,
    up_far,
    down_far,
    row_local,
    row_send,
    row_recv,
    ffn_local,
    ffn_send,
    ffn_recv,
    free_sem,
    reduce_send,
    reduce_recv,
    reduce_z_send,
    reduce_z_recv,
):
    step = pl.program_id(0)
    last = pl.num_programs(0) - 1
    here = Place(group)
    planes = here.planes
    batches = d_ref.shape[1]
    width = x_ref.shape[2]
    grads = (gate_ref, up_ref, down_ref)
    owns = (gate_own, up_own, down_own)
    swaps = (gate_swap, up_swap, down_swap)
    nears = (gate_near, up_near, down_near)
    fars = (gate_far, up_far, down_far)
    outs = (gate_out_ref, up_out_ref, down_out_ref)
    side = (here.z_peer(1), here.z_peer(planes - 1))

    def z_at(k):
        return (here.z + k) % planes

    def row_copy(kind, member, number):
        source, target = ((d_ref, d_in_ref), (val_ref, val_in_ref))[kind]
        src, dst = source.at[number, member], target.at[number, member]
        if number == 0:
            return pltpu.make_async_copy(src, dst, row_local.at[batches * 4 + member])
        return remote(
            src, dst, row_send.at[kind, member, number], row_recv.at[kind, member, number], here.plane_peers[number]
        )

    def load_rows(member, number):
        source = d_ref if number == 0 else d_in_ref
        return pltpu.make_async_copy(
            source.at[number, member], rows_ref.at[number, 0], row_local.at[member * 4 + number]
        )

    def own_copy(j):
        return pltpu.make_async_copy(grads[j].at[:, :, here.core], owns[j], ffn_local.at[j, 0])

    def swap_copy(j):
        return remote(
            grads[j].at[:, :, 1 - here.core], swaps[j], ffn_send.at[j, 0], ffn_recv.at[j, 0], here.core_peer
        )

    def near_copy(j, k):
        return remote(
            owns[j].at[z_at(2), k], nears[j].at[k], ffn_send.at[j, 1 + k], ffn_recv.at[j, 1 + k], side[k]
        )

    def far_copy(j, k):
        return remote(
            owns[j].at[z_at(1 if k == 0 else planes - 1)],
            fars[j].at[k],
            ffn_send.at[j, 3 + k],
            ffn_recv.at[j, 3 + k],
            side[k],
        )

    def plane_copy(j, number):
        x = here.x if number % 2 == 0 else 1 - here.x
        src, dst = owns[j].at[here.z, x], outs[j].at[here.expert(0)]
        if number == 0:
            return pltpu.make_async_copy(src, dst, ffn_local.at[j, 1])
        return remote(
            src, dst, ffn_send.at[j, 4 + number], ffn_recv.at[j, 4 + number], here.plane_peers[number]
        )

    def plane_arrival(j, number):
        dst = outs[j].at[here.expert(number)]
        return remote(
            dst, dst, ffn_send.at[j, 4 + number], ffn_recv.at[j, 4 + number], here.plane_peers[number]
        )

    def add(target, *sources):
        value = target[...].astype(F32)
        for source in sources:
            value = value + source[...].astype(F32)
        target[...] = value.astype(BF16)

    @pl.when(step == 0)
    def _():
        for j in range(3):
            own_copy(j).start()
        here.barrier(
            [here.core_peer, here.x_peer, here.y_peer, here.xy_peer] + [here.z_peer(k) for k in range(1, planes)]
        )
        for number in range(1, 4):
            row_copy(0, 0, number).start()
        for j in range(3):
            swap_copy(j).start()
        for j in range(3):
            own_copy(j).wait()
            swap_copy(j).wait_recv()
            for x in range(2):

                def add_core(z, carry):
                    add(owns[j].at[z, x], swaps[j].at[z, x])
                    return carry

                lax.fori_loop(0, planes, add_core, 0)
            near_copy(j, 0).start()
            near_copy(j, 1).start()
        pl.semaphore_signal(free_sem, inc=1, device_id=here.core_peer, device_id_type=MESH)

    for member in range(batches):

        @pl.when(step == member)
        def _():
            for number in range(1, 4):
                row_copy(0, member, number).wait_recv()
            if member + 1 < batches:
                for number in range(1, 4):
                    row_copy(0, member + 1, number).start()
            for number in range(4):
                row_copy(1, member, number).start()
            for number in range(4):
                load_rows(member, number).start()
            for number in range(4):
                load_rows(member, number).wait()

    sequence_combine(
        step,
        [rows_ref.at[number] for number in range(4)],
        pos_ref,
        aux_ref,
        routes_ref,
        prev_ref,
        h_ref,
        g_ref,
        o_ref,
        small_ref,
        wo_ref,
        dh_ref,
        dob_ref,
        sgrad_ref,
        grad_map_ref,
        acc_wo_ref,
        cols_ref,
        here.expert,
    )

    @pl.when(step == 0)
    def _():
        for j in range(3):
            for k in range(2):
                near_copy(j, k).wait_recv()
                add(owns[j].at[z_at(1 if k == 0 else planes - 1), k], nears[j].at[k])
                far_copy(j, k).start()

    @pl.when(step == last)
    def _():
        for j in range(3):
            for k in range(2):
                far_copy(j, k).wait_recv()
            for x in range(2):
                add(owns[j].at[here.z, x], fars[j].at[0, x], fars[j].at[1, x])
            for number in range(4):
                plane_copy(j, number).start()

    sequence_backward(
        step,
        x_ref,
        seg_row_ref,
        seg_col_ref,
        q_ref,
        k_ref,
        v_ref,
        dob_ref,
        lse_ref,
        dh_ref,
        small_ref,
        wq_ref,
        wk_ref,
        wv_ref,
        cos_ref,
        sin_ref,
        gin_ref,
        gain_ref,
        bias_ref,
        lse_t_ref,
        dqkv_ref,
        acc_ref,
    )

    @pl.when(step == last)
    def _():
        table_ref[...] = small_table(depth, sgrad_ref, grad_map_ref, gain_ref)
        chunks = []
        begin = 0
        for number, (send_buffer, buffers) in enumerate(zip(send_buffers, chunk_buffers)):
            columns = send_buffer.shape[3]
            home, place = (gate_swap, begin) if begin < gate_swap.shape[3] else (up_swap, begin - gate_swap.shape[3])
            chunks.append(
                ReducedChunk(
                    here,
                    depth,
                    begin,
                    functools.partial(attention_columns, acc_ref, acc_wo_ref, table_ref, begin, columns),
                    send_buffer,
                    home.at[:, :, :, place : place + columns],
                    buffers,
                    sums_ref,
                    (
                        reduce_send.at[number],
                        reduce_recv.at[number],
                        reduce_z_send.at[number],
                        reduce_z_recv.at[number],
                    ),
                )
            )
            begin += columns
        reduce_attention(chunks, free_sem)
        for j in range(3):
            swap_copy(j).wait_send()
            for k in range(2):
                near_copy(j, k).wait_send()
                far_copy(j, k).wait_send()
            plane_copy(j, 0).wait()
            for number in range(1, 4):
                plane_copy(j, number).wait_send()
                plane_arrival(j, number).wait_recv()
        for member in range(batches):
            row_copy(1, member, 0).wait()
            for number in range(1, 4):
                row_copy(0, member, number).wait_send()
                row_copy(1, member, number).wait()


def params(limit_mib):
    return pltpu.CompilerParams(vmem_limit_bytes=limit_mib * 1024 * 1024, dimension_semantics=("arbitrary",))


def rotary(length):
    halfway = HEAD_DIM // 2
    frequency = 10000.0 ** (-jnp.arange(halfway).astype(F32) / halfway)
    angles = jnp.arange(length).astype(F32)[:, None] * frequency[None, :]
    cosine, sine = jnp.cos(angles), jnp.sin(angles)
    return (
        jnp.concatenate([cosine] * 4, axis=1),
        jnp.concatenate([-sine, sine, -sine, sine], axis=1),
    )


def local(
    reps,
    group,
    block_input,
    prev_logits,
    routes,
    segments,
    grad_out,
    gain_attn,
    w_query,
    w_key,
    w_value,
    w_output,
    gain_mix,
    router,
    route_map,
    const_proj,
    const_vec,
    w_gate,
    w_up,
    w_down,
):
    batches, length = segments.shape
    width = block_input.shape[1]
    kinds = router.shape[1]
    ffn = w_gate.shape[1]
    hidden = w_gate.shape[2]
    rows_d = w_gate.shape[0]
    rows_f = w_down.shape[0]
    capacity = length // 2
    planes = group // 4
    assert reps == 2 and ffn == 4 and group % 4 == 0
    g = lax.axis_index("grp")
    y = lax.axis_index("rep")
    core = g % 2
    x = (g // 2) % 2
    z = g // 4
    own = (2 * y + x).astype(jnp.int32)
    own_arr = own.reshape(1)

    x_flip = [(i, i ^ 2) for i in range(group)]
    core_flip = [(i, i ^ 1) for i in range(group)]
    y_flip = [(0, 1), (1, 0)]
    xy_flip = [(r * group + i, (1 - r) * group + (i ^ 2)) for r in range(2) for i in range(group)]

    def z_shift(k):
        return [(i, (i + 4 * k) % group) for i in range(group)]

    def to_plane(parts):
        return [
            parts[0],
            lax.ppermute(parts[1], "grp", x_flip),
            lax.ppermute(parts[2], "rep", y_flip),
            lax.ppermute(parts[3], ("rep", "grp"), xy_flip),
        ]

    tokens = block_input.reshape(batches, length, width)
    grads = grad_out.reshape(batches, length, width)
    route_cols = routes.reshape(batches, length, 2)
    route_rows = route_cols.transpose(0, 2, 1)
    prev_rows = prev_logits.reshape(batches, length, kinds).transpose(0, 2, 1)
    seg_row = segments[:, None, :]
    seg_col = segments[:, :, None]
    cos, sin = rotary(length)

    def spec_w(j):
        return pl.BlockSpec((width, width), lambda b, *_: (0, j), pipeline_mode=pl.Buffered(1))

    row_shape = jax.ShapeDtypeStruct((batches, capacity, width), BF16)
    seq_bf16 = jax.ShapeDtypeStruct((batches, length, width), BF16)
    seq_f32 = jax.ShapeDtypeStruct((batches, length, width), F32)
    small_shard = jnp.concatenate(
        [router, const_proj, const_vec, gain_attn[:, None], gain_mix[:, None]], axis=1
    ).astype(BF16)
    small_shard = jnp.pad(small_shard, ((0, 0), (0, 2 * LANES - small_shard.shape[1])))
    shard = jnp.concatenate([w.astype(BF16) for w in (w_query, w_key, w_value)] + [small_shard], axis=1)
    shard_o = w_output.astype(BF16)
    fused = planes == 4 and rows_d % 16 == 0 and rows_f % 16 == 0
    if fused:
        any_space = pl.BlockSpec(memory_space=pl.ANY)
        out_struct = jax.ShapeDtypeStruct
        (
            q, k, v, o, h1, lse, aux, pos, small, attn, attn_o, a_rows, grad_rows, gate_full, up_full, down_full,
        ) = pl.pallas_call(
            functools.partial(fused_forward_kernel, group),
            grid=(batches,),
            in_specs=[
                per_seq((length, width)),
                per_seq((1, length)),
                per_seq((length, 1)),
                whole((batches, 2, length)),
                per_seq((kinds, length)),
                whole((kinds, kinds)),
                whole((batches, length, width)),
                whole((length, LANES)),
                whole((length, LANES)),
            ]
            + [any_space] * 5,
            out_specs=[per_seq((length, width))] * 5
            + [
                per_seq((length, LANES)),
                per_seq((16, length)),
                whole((batches, kinds, length)),
                whole((kinds + 8, width)),
            ]
            + [any_space] * 7,
            scratch_shapes=[
                pltpu.VMEM((width, 3 * width + 2 * LANES), BF16),
                pltpu.VMEM((width, width), BF16),
                pltpu.VMEM((length, length), F32),
                pltpu.VMEM((length, width), F32),
                pltpu.VMEM((batches, 4, capacity + 16, width), BF16),
                pltpu.VMEM((batches, 4, capacity, width), BF16),
                pltpu.SemaphoreType.DMA((2,)),
                pltpu.SemaphoreType.DMA((2, 4 + 4 * planes)),
                pltpu.SemaphoreType.DMA((2, 4 + 4 * planes)),
                pltpu.SemaphoreType.DMA((3,)),
                pltpu.SemaphoreType.DMA((3, 5 + planes)),
                pltpu.SemaphoreType.DMA((3, 5 + planes)),
                pltpu.SemaphoreType.DMA((2,)),
                pltpu.SemaphoreType.DMA((2, batches)),
                pltpu.SemaphoreType.DMA((2, batches, 4)),
                pltpu.SemaphoreType.DMA((2, batches, 4)),
            ],
            out_shape=[seq_bf16] * 4
            + [
                seq_f32,
                out_struct((batches, length, LANES), F32),
                out_struct((batches, 16, length), F32),
                out_struct((batches, kinds, length), F32),
                out_struct((kinds + 8, width), F32),
                out_struct((width, 3 * width + 2 * LANES), BF16),
                out_struct((width, width), BF16),
                out_struct((4, batches, capacity + 16, width), BF16),
                out_struct((4, batches, capacity, width), BF16),
                out_struct((planes, 2, 2, rows_d, hidden), BF16),
                out_struct((planes, 2, 2, rows_d, hidden), BF16),
                out_struct((planes, 2, 2, rows_f, width), BF16),
            ],
            compiler_params=pltpu.CompilerParams(
                vmem_limit_bytes=58 * 1024 * 1024,
                dimension_semantics=("arbitrary",),
                collective_id=1,
                has_side_effects=True,
            ),
            cost_estimate=pl.CostEstimate(flops=40 * 10**9, bytes_accessed=60 * 10**6, transcendentals=10**7),
            name="fused_forward",
        )(
            tokens, seg_row, seg_col, route_rows, prev_rows, route_map.T, grads, cos, sin,
            shard, shard_o,
            w_gate.astype(BF16).transpose(1, 0, 2),
            w_up.astype(BF16).transpose(1, 0, 2),
            w_down.astype(BF16).transpose(1, 0, 2),
        )
        gate_full = gate_full.reshape(width, hidden)
        up_full = up_full.reshape(width, hidden)
        down_full = down_full.reshape(hidden, width)
    else:
        attn = lax.all_gather(shard, "grp", axis=0, tiled=True)
        attn_o = lax.all_gather(shard_o, "grp", axis=0, tiled=True)
        small = attn[:, 3 * width : 3 * width + kinds + 8].astype(F32).T

        def pick(array, expert):
            return lax.dynamic_index_in_dim(array, expert, axis=1, keepdims=False)

        def gather_expert(mine, other):
            crossed = lax.ppermute(other, "grp", x_flip)
            both = jnp.where(x == 0, jnp.stack([mine, crossed]), jnp.stack([crossed, mine]))
            pieces = [both] + [lax.ppermute(both, "grp", z_shift(k)) for k in range(1, planes)]
            stacked = jnp.stack(pieces)
            half = jnp.take(stacked, (z - jnp.arange(planes)) % planes, axis=0)
            swapped = lax.ppermute(half, "grp", core_flip)
            return jnp.where(core == 0, jnp.stack([half, swapped], axis=2), jnp.stack([swapped, half], axis=2))

        gate_up = gather_expert(
            jnp.stack([pick(w_gate, own), pick(w_up, own)]).astype(BF16),
            jnp.stack([pick(w_gate, own ^ 1), pick(w_up, own ^ 1)]).astype(BF16),
        )
        down = gather_expert(pick(w_down, own).astype(BF16), pick(w_down, own ^ 1).astype(BF16))
        gate_full = gate_up[:, :, :, 0].reshape(width, hidden)
        up_full = gate_up[:, :, :, 1].reshape(width, hidden)
        down_full = down.reshape(hidden, width)

        *grad_rows, pos = pl.pallas_call(
            grad_rows_kernel,
            grid_spec=pltpu.PrefetchScalarGridSpec(
                num_scalar_prefetch=1,
                grid=(batches,),
                in_specs=[per_seq((2, length)), per_seq((length, width))],
                out_specs=[per_seq((capacity, width))] * 4 + [per_seq((kinds, length))],
            ),
            out_shape=[row_shape] * 4 + [jax.ShapeDtypeStruct((batches, kinds, length), F32)],
            compiler_params=params(32),
            cost_estimate=pl.CostEstimate(flops=4 * 10**9, bytes_accessed=8 * 10**6, transcendentals=0),
            name="grad_rows",
        )(own_arr, route_rows, grads)
        grad_rows = to_plane(grad_rows)

        q, k, v, o, h1, lse, aux, *a_rows = pl.pallas_call(
            forward_kernel,
            grid_spec=pltpu.PrefetchScalarGridSpec(
                num_scalar_prefetch=1,
                grid=(batches,),
                in_specs=[
                    per_seq((length, width)),
                    per_seq((1, length)),
                    per_seq((length, 1)),
                    per_seq((2, length)),
                    per_seq((kinds, length)),
                    whole((kinds, kinds)),
                    whole((kinds + 8, width)),
                    spec_w(0),
                    spec_w(1),
                    spec_w(2),
                    spec_w(0),
                    whole((length, LANES)),
                    whole((length, LANES)),
                    per_seq((kinds, length)),
                ],
                out_specs=[per_seq((length, width))] * 5
                + [per_seq((length, LANES)), per_seq((16, length))]
                + [per_seq((capacity + 16, width))] * 4,
                scratch_shapes=[pltpu.VMEM((length, length), F32), pltpu.VMEM((length, width), F32)],
            ),
            out_shape=[seq_bf16] * 4
            + [
                seq_f32,
                jax.ShapeDtypeStruct((batches, length, LANES), F32),
                jax.ShapeDtypeStruct((batches, 16, length), F32),
            ]
            + [jax.ShapeDtypeStruct((batches, capacity + 16, width), BF16)] * 4,
            compiler_params=params(56),
            cost_estimate=pl.CostEstimate(flops=20 * 10**9, bytes_accessed=20 * 10**6, transcendentals=10**7),
            name="forward",
        )(own_arr, tokens, seg_row, seg_col, route_rows, prev_rows, route_map.T, small, attn, attn, attn, attn_o, cos, sin, pos)
        a_rows = to_plane(a_rows)

        a_rows = jnp.stack(a_rows)
        grad_rows = jnp.stack(grad_rows)

    tile = hidden // 4
    total = 4 * batches * capacity
    any_spec = pl.BlockSpec(memory_space=pl.ANY)
    values, input_rows, grad_gate_full, grad_up_full, grad_down_full = pl.pallas_call(
        expert_kernel,
        grid=(hidden // tile,),
        in_specs=[any_spec] * 2
        + [
            pl.BlockSpec((width, tile), lambda f: (0, f)),
            pl.BlockSpec((width, tile), lambda f: (0, f)),
            pl.BlockSpec((tile, width), lambda f: (f, 0)),
        ],
        out_specs=[any_spec] * 2
        + [
            pl.BlockSpec((width, tile), lambda f: (0, f)),
            pl.BlockSpec((width, tile), lambda f: (0, f)),
            pl.BlockSpec((tile, width), lambda f: (f, 0)),
        ],
        scratch_shapes=[
            pltpu.VMEM((total + capacity, width), BF16),
            pltpu.VMEM((total + capacity, width), BF16),
            pltpu.VMEM((4 * batches, 16, capacity), BF16),
            pltpu.VMEM((width, total), BF16),
            pltpu.VMEM((width, total), BF16),
            pltpu.SMEM((4 * batches + 1,), jnp.int32),
            pltpu.VMEM((total, width), F32),
            pltpu.VMEM((total, width), F32),
            pltpu.VMEM((width, tile), F32),
            pltpu.VMEM((width, tile), F32),
            pltpu.VMEM((width, tile), F32),
            pltpu.VMEM((total + capacity, LANES), F32),
            pltpu.SemaphoreType.DMA((12 * batches,)),
        ],
        out_shape=[
            jax.ShapeDtypeStruct((4, batches, capacity, width), BF16),
            jax.ShapeDtypeStruct((4, batches, capacity + 16, width), BF16),
        ]
        + [
            jax.ShapeDtypeStruct((width, hidden), BF16),
            jax.ShapeDtypeStruct((width, hidden), BF16),
            jax.ShapeDtypeStruct((hidden, width), BF16),
        ],
        compiler_params=params(60),
        cost_estimate=pl.CostEstimate(flops=58 * 10**9, bytes_accessed=40 * 10**6, transcendentals=10**7),
        name="expert",
    )(a_rows, grad_rows, gate_full, up_full, down_full)
    if fused:
        columns = 4 * width + 2 * LANES
        once = lambda shape: pl.BlockSpec(
            (1,) + shape, lambda b, *_: (b, 0, 0), pipeline_mode=pl.Buffered(1)
        )
        wide = ((rows_d, hidden), (rows_d, hidden), (rows_f, width))
        near = planes // 2
        parts = (hidden // 2, hidden // 2, width, columns - hidden - width)
        gin, sums, _, values_in, grad_gate, grad_up, grad_down = pl.pallas_call(
            functools.partial(fused_backward_kernel, group, rows_d),
            grid=(batches,),
            in_specs=[
                per_seq((kinds, length)),
                per_seq((16, length)),
                per_seq((length, 2)),
                per_seq((kinds, length)),
                once((length, width)),
                once((length, width)),
                once((length, width)),
                once((length, width)),
                per_seq((1, length)),
                per_seq((length, 1)),
                once((length, width)),
                once((length, width)),
                once((length, width)),
                once((length, LANES)),
                whole((kinds + 8, width), 1),
                spec_w(0),
                spec_w(1),
                spec_w(2),
                spec_w(0),
                whole((length, LANES), 1),
                whole((length, LANES), 1),
            ]
            + [any_spec] * 5,
            out_specs=[once((length, width)), whole((rows_d, columns), 1)] + [any_spec] * 5,
            out_shape=[
                seq_f32,
                jax.ShapeDtypeStruct((rows_d, columns), F32),
                jax.ShapeDtypeStruct((4, batches, capacity + 16, width), BF16),
                jax.ShapeDtypeStruct((4, batches, capacity, width), BF16),
            ]
            + [jax.ShapeDtypeStruct((4,) + shape, BF16) for shape in wide],
            scratch_shapes=[
                pltpu.VMEM((width, 3 * width), F32),
                pltpu.VMEM((width, width), F32),
                pltpu.VMEM((width, LANES), BF16),
            ]
            + [[pltpu.VMEM((planes, 2, rows_d, part), BF16) for part in parts]]
            + [
                [[
                    pltpu.VMEM((near, 2, rows_d, part // 2), BF16),
                    pltpu.VMEM((near, rows_d, part), BF16),
                    pltpu.VMEM((near, rows_d, part // 2), BF16),
                    pltpu.VMEM((near, rows_d, part // 2), BF16),
                    pltpu.VMEM((planes - 1, rows_d, part // 2), BF16),
                    pltpu.VMEM((rows_d, part // 2), BF16),
                    pltpu.VMEM((rows_d, part // 2), BF16),
                ] for part in parts]
            ]
            + [
                pltpu.VMEM((LANES, length), F32),
                pltpu.VMEM((1, length, width), F32),
                pltpu.VMEM((1, length, width), BF16),
                pltpu.VMEM((16, width), F32),
                pltpu.VMEM((kinds, LANES), F32),
                pltpu.VMEM((8, width), F32),
                pltpu.VMEM((length, length), F32),
                pltpu.VMEM((LANES, length), F32),
                pltpu.VMEM((length, 3 * width), BF16),
                pltpu.VMEM((4, 1, capacity + 16, width), BF16),
            ]
            + [pltpu.VMEM((planes, 2) + shape, BF16) for shape in wide]
            + [pltpu.VMEM((planes, 2) + shape, BF16) for shape in wide]
            + [pltpu.VMEM((2,) + shape, BF16) for shape in wide]
            + [pltpu.VMEM((2, 2) + shape, BF16) for shape in wide]
            + [
                pltpu.SemaphoreType.DMA((5 * batches,)),
                pltpu.SemaphoreType.DMA((2, batches, 4)),
                pltpu.SemaphoreType.DMA((2, batches, 4)),
                pltpu.SemaphoreType.DMA((3, 2)),
                pltpu.SemaphoreType.DMA((3, 8)),
                pltpu.SemaphoreType.DMA((3, 8)),
                pltpu.SemaphoreType.REGULAR,
                pltpu.SemaphoreType.DMA((len(parts), 6)),
                pltpu.SemaphoreType.DMA((len(parts), 6)),
                pltpu.SemaphoreType.DMA((len(parts), planes - 1)),
                pltpu.SemaphoreType.DMA((len(parts), planes - 1)),
            ],
            compiler_params=pltpu.CompilerParams(
                vmem_limit_bytes=63 * 1024 * 1024,
                dimension_semantics=("arbitrary",),
                collective_id=3,
                has_side_effects=True,
            ),
            cost_estimate=pl.CostEstimate(flops=60 * 10**9, bytes_accessed=60 * 10**6, transcendentals=10**7),
            name="fused_backward",
        )(
            pos, aux, route_cols, prev_rows, h1, grads, o, tokens, seg_row, seg_col, q, k, v, lse, small,
            attn, attn, attn, attn_o, cos, sin, input_rows, values,
            grad_gate_full.reshape(planes, 2, 2, rows_d, hidden),
            grad_up_full.reshape(planes, 2, 2, rows_d, hidden),
            grad_down_full.reshape(planes, 2, 2, rows_f, width),
        )
        grad_gate = grad_gate.transpose(1, 0, 2).astype(F32)
        grad_up = grad_up.transpose(1, 0, 2).astype(F32)
        grad_down = grad_down.transpose(1, 0, 2).astype(F32)
    else:
        values_in = jnp.stack(to_plane([values[i] for i in range(4)]))
        def scatter_expert(full):
            keep = lax.dynamic_index_in_dim(full, core, axis=2, keepdims=False)
            send = lax.dynamic_index_in_dim(full, 1 - core, axis=2, keepdims=False)
            half = (keep.astype(F32) + lax.ppermute(send, "grp", core_flip).astype(F32)).astype(BF16)
            summed = lax.dynamic_index_in_dim(half, z, axis=0, keepdims=False).astype(F32)
            for k in range(1, planes):
                part = lax.dynamic_index_in_dim(half, (z + k) % planes, axis=0, keepdims=False)
                summed = summed + lax.ppermute(part, "grp", z_shift(k)).astype(F32)
            summed = summed.astype(BF16)
            mine = lax.dynamic_index_in_dim(summed, x, axis=0, keepdims=False)
            other = lax.dynamic_index_in_dim(summed, 1 - x, axis=0, keepdims=False)
            arrived = to_plane([mine, other, mine, other])

            def order(first):
                return lambda: tuple(arrived[first ^ e] for e in range(4))

            return lax.switch(own, [order(i) for i in range(4)])

        grad_gate_up = scatter_expert(
            jnp.stack(
                [
                    grad_gate_full.reshape(planes, 2, 2, rows_d, hidden),
                    grad_up_full.reshape(planes, 2, 2, rows_d, hidden),
                ],
                axis=3,
            )
        )
        grad_down = scatter_expert(grad_down_full.reshape(planes, 2, 2, rows_f, width))
        grad_gate = jnp.stack([part[0] for part in grad_gate_up], axis=1).astype(F32)
        grad_up = jnp.stack([part[1] for part in grad_gate_up], axis=1).astype(F32)
        grad_down = jnp.stack(grad_down, axis=1).astype(F32)

        dh1, dob, grad_wo, sgrad, grad_map = pl.pallas_call(
            combine_kernel,
            grid_spec=pltpu.PrefetchScalarGridSpec(
                num_scalar_prefetch=1,
                grid=(batches,),
                in_specs=[per_seq((capacity + 16, width))] * 4
                + [
                    per_seq((kinds, length)),
                    per_seq((16, length)),
                    per_seq((length, 2)),
                    per_seq((kinds, length)),
                    per_seq((length, width)),
                    per_seq((length, width)),
                    per_seq((length, width)),
                    whole((kinds + 8, width)),
                    spec_w(0),
                ],
                out_specs=[per_seq((length, width))] * 2
                + [whole((width, width)), whole((16, width)), whole((kinds, LANES))],
                scratch_shapes=[pltpu.VMEM((width, width), F32), pltpu.VMEM((LANES, length), F32)],
            ),
            out_shape=[
                seq_f32,
                seq_bf16,
                jax.ShapeDtypeStruct((width, width), BF16),
                jax.ShapeDtypeStruct((16, width), F32),
                jax.ShapeDtypeStruct((kinds, LANES), F32),
            ],
            compiler_params=params(56),
            cost_estimate=pl.CostEstimate(flops=12 * 10**9, bytes_accessed=20 * 10**6, transcendentals=10**5),
            name="combine",
        )(own_arr, *to_plane([input_rows[i] for i in range(4)]), pos, aux, route_cols, prev_rows, h1, grads, o, small, attn_o)

        gin, grad_attn, gain_one = pl.pallas_call(
            backward_kernel,
            grid=(batches,),
            in_specs=[
                per_seq((length, width)),
                per_seq((1, length)),
                per_seq((length, 1)),
                per_seq((length, width)),
                per_seq((length, width)),
                per_seq((length, width)),
                per_seq((length, width)),
                per_seq((length, LANES)),
                per_seq((length, width)),
                whole((kinds + 8, width)),
                spec_w(0),
                spec_w(1),
                spec_w(2),
                whole((length, LANES)),
                whole((length, LANES)),
            ],
            out_specs=[per_seq((length, width)), whole((width, 3 * width)), whole((8, width))],
            scratch_shapes=[
                pltpu.VMEM((length, length), F32),
                pltpu.VMEM((LANES, length), F32),
                pltpu.VMEM((length, 3 * width), BF16),
                pltpu.VMEM((width, 3 * width), F32),
            ],
            out_shape=[
                seq_f32,
                jax.ShapeDtypeStruct((width, 3 * width), BF16),
                jax.ShapeDtypeStruct((8, width), F32),
            ],
            compiler_params=params(56),
            cost_estimate=pl.CostEstimate(flops=30 * 10**9, bytes_accessed=20 * 10**6, transcendentals=10**7),
            name="backward",
        )(tokens, seg_row, seg_col, q, k, v, dob, lse, dh1, small, attn, attn, attn, cos, sin)

    result = pl.pallas_call(
        result_kernel,
        grid_spec=pltpu.PrefetchScalarGridSpec(
            num_scalar_prefetch=1,
            grid=(batches,),
            in_specs=[
                pl.BlockSpec((4, 1, capacity, width), lambda b, *_: (0, b, 0, 0)),
                per_seq((kinds, length)),
                per_seq((16, length)),
                per_seq((length, width)),
                whole((kinds + 8, width)),
            ],
            out_specs=per_seq((length, width)),
            scratch_shapes=[pltpu.VMEM((LANES, length), F32)],
        ),
        out_shape=seq_f32,
        compiler_params=params(40),
        cost_estimate=pl.CostEstimate(flops=4 * 10**9, bytes_accessed=12 * 10**6, transcendentals=0),
        name="result",
    )(own_arr, values_in, pos, aux, h1, small)

    if fused:
        attn_total = sums[:, 0 : 4 * width]
        sums = sums[:, 4 * width :]
        map_total = sums[0:kinds, 16 : 16 + kinds]
    else:
        part = lax.psum_scatter(jnp.concatenate([grad_attn, grad_wo], axis=1), "grp", scatter_dimension=0, tiled=True)
        attn_total = lax.psum(part, "rep").astype(F32)
        sgrad = jnp.where(iota((16, 1), 0) == kinds + 6, gain_one[0:1], sgrad)
        packed = jnp.concatenate([sgrad, jnp.pad(grad_map, ((0, 0), (0, width - LANES)))], axis=0)
        packed = lax.psum(packed, ("rep", "grp"))
        sums = lax.dynamic_slice_in_dim(packed[0:16], g * rows_d, rows_d, axis=1).T
        map_total = packed[16:, 0:kinds].T
    return (
        result.reshape(batches * length, width),
        gin.reshape(batches * length, width),
        sums[:, kinds + 6],
        attn_total[:, 0:width],
        attn_total[:, width : 2 * width],
        attn_total[:, 2 * width : 3 * width],
        attn_total[:, 3 * width :],
        sums[:, kinds + 7],
        sums[:, 0:kinds],
        map_total,
        sums[:, kinds : kinds + 4],
        sums[:, kinds + 4 : kinds + 6],
        grad_gate,
        grad_up,
        grad_down,
    )


def solution(mesh):
    rows = P(("rep", "grp"), None)
    in_specs = (
        (rows,) * 5
        + (P("grp"),)
        + (P("grp", None),) * 4
        + (P("grp"), P("grp", None), P(), P("grp", None), P("grp", None))
        + (P("grp", None, None),) * 3
    )
    out_specs = (
        (rows,) * 2
        + (P("grp"),)
        + (P("grp", None),) * 4
        + (P("grp"), P("grp", None), P(), P("grp", None), P("grp", None))
        + (P("grp", None, None),) * 3
    )
    body = functools.partial(local, mesh.shape["rep"], mesh.shape["grp"])
    return jax.shard_map(body, mesh=mesh, in_specs=in_specs, out_specs=out_specs, check_vma=False)
```

```python
import functools

import jax
import jax.numpy as jnp
import numpy as np
from jax import lax
from jax.experimental import pallas as pl
from jax.experimental.pallas import tpu as pltpu
from jax.sharding import PartitionSpec as P

HEAD_DIM = 64
BLOCK = 256
EPS = 1e-05
NEG = -1000000000.0
F32 = jnp.float32
BF16 = jnp.bfloat16
LANES = 128


def nn(a, b):
    return lax.dot_general(a, b, (((1,), (0,)), ((), ())), preferred_element_type=F32)


def nt(a, b):
    return lax.dot_general(a, b, (((1,), (1,)), ((), ())), preferred_element_type=F32)


def tn(a, b):
    return lax.dot_general(a, b, (((0,), (0,)), ((), ())), preferred_element_type=F32)


def iota(shape, dim):
    return lax.broadcasted_iota(jnp.int32, shape, dim)


def split2(values):
    high = values.astype(BF16)
    low = (values - high.astype(F32)).astype(BF16)
    return high, low


def whole(shape, buffers=None):
    zeros = (0,) * len(shape)
    if buffers:
        return pl.BlockSpec(shape, lambda *_: zeros, pipeline_mode=pl.Buffered(buffers))
    return pl.BlockSpec(shape, lambda *_: zeros)


def per_seq(shape):
    tail = (0,) * len(shape)
    return pl.BlockSpec((1,) + shape, lambda b, *_: (b,) + tail)


def same_document(segments):
    hot = jnp.where(segments == iota((16, segments.shape[1]), 0), 1.0, 0.0).astype(BF16)
    return tn(hot, hot) > 0.5


def rms_scale(values):
    return lax.rsqrt(jnp.mean(values * values, axis=-1, keepdims=True) + EPS)


def slot_mask(position_row, capacity):
    places = iota((capacity, position_row.shape[1]), 0).astype(F32)
    return jnp.where(places == position_row, 1.0, 0.0).astype(BF16)


def grad_rows_kernel(own_ref, routes_ref, grad_ref, r0, r1, r2, r3, pos_ref):
    own = own_ref[0]
    kinds, length = pos_ref.shape[1:]
    capacity = r0.shape[1]
    ids = iota((kinds, length), 0)
    first = routes_ref[0:1, :] == ids
    second = routes_ref[1:2, :] == ids
    hits = jnp.where(first | second, 1.0, 0.0)
    before = jnp.where(iota((length, length), 0) < iota((length, length), 1), 1.0, 0.0)
    slots = nn(hits.astype(BF16), before.astype(BF16))
    pos_ref[0] = jnp.where(hits > 0.0, slots, -1.0)
    for number, rows in enumerate((r0, r1, r2, r3)):
        line = pos_ref[0, pl.ds(own ^ number, 1), :]
        rows[0] = nn(slot_mask(line, capacity), grad_ref[0]).astype(BF16)


def swap_halves(values, low_half):
    return jnp.where(low_half, pltpu.roll(values, 96, 1), pltpu.roll(values, 32, 1))


def sequence_forward(
    x_ref,
    segments,
    routes,
    prev_ref,
    map_ref,
    small_ref,
    wq_ref,
    wk_ref,
    wv_ref,
    wo_ref,
    cos_ref,
    sin_ref,
    pos_ref,
    q_ref,
    k_ref,
    v_ref,
    o_ref,
    h_ref,
    lse_ref,
    aux_ref,
    rows_refs,
    bias_ref,
    proj_ref,
    expert_of,
    between=None,
):
    length, width = x_ref.shape[1:]
    kinds = pos_ref.shape[1]
    capacity = length // 2
    tokens = x_ref[0].astype(F32)
    gain_one = small_ref[kinds + 6 : kinds + 7, :]
    gain_two = small_ref[kinds + 7 : kinds + 8, :]
    a1 = (tokens * rms_scale(tokens) * gain_one).astype(BF16)
    lane = iota((1, LANES), 1)
    low_half = (lane % HEAD_DIM) < (HEAD_DIM // 2)
    first_head = lane < HEAD_DIM
    mask_a = jnp.where(first_head, 1.0, 0.0).astype(BF16)
    mask_b = jnp.where(first_head, 0.0, 1.0).astype(BF16)
    pairs = width // LANES

    for weights, target, scale in ((wq_ref, q_ref, 0.125), (wk_ref, k_ref, 1.0)):
        proj_ref[...] = nn(a1, weights[...])

        def turn(h, carry):
            cols = pl.ds(pl.multiple_of(h * LANES, LANES), LANES)
            part = proj_ref[:, cols]
            turned = part * cos_ref[...] + swap_halves(part, low_half) * sin_ref[...]
            target[0, :, cols] = turned.astype(BF16) * jnp.asarray(scale, BF16)
            return carry

        lax.fori_loop(0, pairs, turn, 0)
    v_ref[0] = nn(a1, wv_ref[...]).astype(BF16)

    allowed = same_document(segments) & (
        iota((length, length), 1) // BLOCK <= iota((length, length), 0) // BLOCK
    )
    bias_ref[...] = jnp.where(allowed, 0.0, NEG)
    lse_ref[...] = jnp.zeros_like(lse_ref)
    if between is not None:
        between()

    def pair(h, carry):
        cols = pl.ds(pl.multiple_of(h * LANES, LANES), LANES)
        for begin in range(0, length, BLOCK):
            end = begin + BLOCK
            queries = q_ref[0, begin:end, cols]
            keys = k_ref[0, 0:end, cols]
            values = v_ref[0, 0:end, cols]
            bias = bias_ref[begin:end, 0:end]
            sums = lse_ref[0, begin:end, :]
            outs = []
            for half, mask in enumerate((mask_a, mask_b)):
                scores = nt(queries * mask, keys) + bias
                top = jnp.max(scores, axis=-1, keepdims=True)
                grown = jnp.exp(scores - top)
                total = jnp.sum(grown, axis=-1, keepdims=True)
                chances = (grown * (1.0 / total)).astype(BF16)
                outs.append(nn(chances, values))
                sums = jnp.where(lane == 2 * h + half, top + jnp.log(total), sums)
            lse_ref[0, begin:end, :] = sums
            o_ref[0, begin:end, cols] = jnp.where(first_head, outs[0], outs[1]).astype(BF16)
        return carry

    lax.fori_loop(0, pairs, pair, 0)

    hidden = tokens + nn(o_ref[0], wo_ref[...])
    h_ref[0] = hidden
    a2 = (hidden * rms_scale(hidden) * gain_two).astype(BF16)
    logits = nt(small_ref[...].astype(BF16), a2)[0:kinds, :]
    for j in range(kinds):
        logits = logits + map_ref[:, j : j + 1] * prev_ref[j : j + 1, :]
    ids = iota((kinds, length), 0)
    first = jnp.where(routes[0:1, :] == ids, 1.0, 0.0)
    second = jnp.where(routes[1:2, :] == ids, 1.0, 0.0)
    one = jnp.sum(logits * first, axis=0, keepdims=True)
    two = jnp.sum(logits * second, axis=0, keepdims=True)
    top = jnp.maximum(one, two)
    grown_one, grown_two = jnp.exp(one - top), jnp.exp(two - top)
    gate_one = grown_one / (grown_one + grown_two)
    gate_two = grown_two / (grown_one + grown_two)
    aux_ref[0, 0:kinds, :] = gate_one * first + gate_two * second
    aux_ref[0, kinds : kinds + 1, :] = gate_one
    aux_ref[0, kinds + 1 : kinds + 2, :] = gate_two
    aux_ref[0, kinds + 2 : kinds + 4, :] = routes.astype(F32)
    aux_ref[0, kinds + 4 :, :] = jnp.zeros((aux_ref.shape[1] - kinds - 4, length), F32)

    place = iota((16, length), 0)
    for number, rows in enumerate(rows_refs):
        mask = slot_mask(pos_ref[0, pl.ds(expert_of(number), 1), :], capacity)
        rows[0, 0:capacity, :] = nn(mask, a2).astype(BF16)
        line = aux_ref[0, pl.ds(expert_of(number), 1), :]
        high = line.astype(BF16).astype(F32)
        mid = (line - high).astype(BF16).astype(F32)
        low = line - high - mid
        parts = jnp.where(place == 0, high, jnp.where(place == 1, mid, jnp.where(place == 2, low, 0.0)))
        spread = nt(parts.astype(BF16), mask)
        filled = jnp.max(pos_ref[0, pl.ds(expert_of(number), 1), :], axis=1, keepdims=True) + 1.0
        spread = jnp.where(iota((16, 1), 0) == 3, filled, spread)
        rows[0, capacity:, 0:capacity] = spread.astype(BF16)
        rows[0, capacity:, capacity:] = jnp.zeros((16, width - capacity), BF16)


def forward_kernel(
    own_ref,
    x_ref,
    seg_ref,
    routes_ref,
    prev_ref,
    map_ref,
    small_ref,
    wq_ref,
    wk_ref,
    wv_ref,
    wo_ref,
    cos_ref,
    sin_ref,
    pos_ref,
    q_ref,
    k_ref,
    v_ref,
    o_ref,
    h_ref,
    lse_ref,
    aux_ref,
    r0,
    r1,
    r2,
    r3,
    bias_ref,
    proj_ref,
):
    own = own_ref[0]
    sequence_forward(
        x_ref,
        seg_ref[0],
        routes_ref[...],
        prev_ref,
        map_ref,
        small_ref,
        wq_ref,
        wk_ref,
        wv_ref,
        wo_ref,
        cos_ref,
        sin_ref,
        pos_ref,
        q_ref,
        k_ref,
        v_ref,
        o_ref,
        h_ref,
        lse_ref,
        aux_ref,
        (r0, r1, r2, r3),
        bias_ref,
        proj_ref,
        lambda number: own ^ number,
    )


MESH = pl.DeviceIdType.MESH


class Place:
    def __init__(self, group):
        self.group = group
        self.planes = group // 4
        self.g = lax.axis_index("grp")
        self.y = lax.axis_index("rep")
        self.core = self.g % 2
        self.x = (self.g // 2) % 2
        self.z = self.g // 4
        self.core_peer = (self.y, self.g + 1 - 2 * self.core)
        self.x_peer = (self.y, self.g + 2 - 4 * self.x)
        self.y_peer = (1 - self.y, self.g)
        self.xy_peer = (1 - self.y, self.g + 2 - 4 * self.x)
        self.plane_peers = (None, self.x_peer, self.y_peer, self.xy_peer)

    def z_peer(self, k):
        return (self.y, (self.g + 4 * k) % self.group)

    def block(self, z, x, core):
        return (z * 2 + x) * 2 + core

    def expert(self, number):
        y = self.y if number < 2 else 1 - self.y
        x = self.x if number % 2 == 0 else 1 - self.x
        return 2 * y + x

    def barrier(self, peers):
        semaphore = pltpu.get_barrier_semaphore()
        for peer in peers:
            pl.semaphore_signal(semaphore, inc=1, device_id=peer, device_id_type=MESH)
        pl.semaphore_wait(semaphore, len(peers))


def remote(src, dst, send, recv, peer):
    return pltpu.make_async_remote_copy(
        src_ref=src, dst_ref=dst, send_sem=send, recv_sem=recv, device_id=peer, device_id_type=MESH
    )


def fused_forward_kernel(
    group,
    x_ref,
    seg_ref,
    routes_ref,
    prev_ref,
    map_ref,
    grad_ref,
    coarse_ref,
    fine_ref,
    shard_refs,
    small_refs,
    gate4_ref,
    up4_ref,
    down4_ref,
    q_ref,
    k_ref,
    v_ref,
    o_ref,
    h_ref,
    lse_ref,
    aux_ref,
    pos_ref,
    small_ref,
    cos_ref,
    sin_ref,
    attn_out_ref,
    attn_o_out_ref,
    rows_in_ref,
    grads_in_ref,
    gate_full_ref,
    up_full_ref,
    down_full_ref,
    attn_ref,
    attn_o_ref,
    bias_ref,
    proj_ref,
    rows_ref,
    grows_ref,
    tile_ref,
    map_t_ref,
    attn_send,
    attn_recv,
    ffn_local,
    ffn_send,
    ffn_recv,
    out_sem,
    row_local,
    row_send,
    row_recv,
):
    step = pl.program_id(0)
    last = pl.num_programs(0) - 1
    here = Place(group)
    planes = here.planes
    batches, kinds, length = pos_ref.shape
    width = x_ref.shape[2]
    capacity = length // 2
    shards = (attn_ref, attn_o_ref)
    experts = ((gate4_ref, gate_full_ref), (up4_ref, up_full_ref), (down4_ref, down_full_ref))
    depth = shard_refs[0].shape[0]
    mine = here.block(here.z, here.x, here.core)

    def rows_of(block):
        return pl.ds(pl.multiple_of(block * depth, 16), depth)

    def attn_part(t, block, part):
        full = shards[t]
        half = full.shape[1] // 2
        if part is None:
            return full.at[rows_of(block), :]
        return full.at[rows_of(block), pl.ds(pl.multiple_of(part * half, LANES), half)]

    def attn_copy(t, slot, z, x, part, peer):
        ref = attn_part(t, here.block(z, x, here.core), part)
        return remote(ref, ref, attn_send.at[t, slot], attn_recv.at[t, slot], peer)

    def to_z(t, k):
        return attn_copy(t, k, here.z, here.x, None, here.z_peer(1 if k == 0 else planes - 1))

    def from_z(t, k):
        return attn_copy(t, k, z_at(planes - 1 if k == 0 else 1), here.x, None, here.x_peer)

    def pass_z(t, k):
        z = z_at(planes - 1 if k == 0 else 1)
        return attn_copy(t, 2 + k, z, here.x, k, here.z_peer(1 if k == 0 else planes - 1))

    def passed_z(t, k):
        return attn_copy(t, 2 + k, z_at(2), here.x, k, here.x_peer)

    def to_x(t, step_z):
        return attn_copy(t, 4 + step_z, z_at(step_z), here.x, here.y, here.x_peer)

    def from_x(t, step_z):
        return attn_copy(t, 4 + step_z, z_at(step_z), 1 - here.x, here.y, here.x_peer)

    def to_y(t, step_z):
        return attn_copy(t, 4 + planes + step_z, z_at(step_z), 1 - here.x, here.y, here.y_peer)

    def from_y(t, step_z):
        return attn_copy(t, 4 + planes + step_z, z_at(step_z), 1 - here.x, 1 - here.y, here.y_peer)

    def to_core(t, step_z, x):
        return attn_copy(t, 4 + 2 * planes + 2 * step_z + x, z_at(step_z), here.x if x == 0 else 1 - here.x, None, here.core_peer)

    def from_core(t, step_z, x):
        ref = attn_part(t, here.block(z_at(step_z), here.x if x == 0 else 1 - here.x, 1 - here.core), None)
        slot = 4 + 2 * planes + 2 * step_z + x
        return remote(ref, ref, attn_send.at[t, slot], attn_recv.at[t, slot], here.core_peer)

    def z_at(k):
        return (here.z + k) % planes

    def ffn_to_x(j):
        source, full = experts[j]
        return remote(
            source.at[here.expert(1)],
            full.at[here.z, here.x, here.core],
            ffn_send.at[j, 0],
            ffn_recv.at[j, 0],
            here.x_peer,
        )

    def ffn_from_x(j):
        source, full = experts[j]
        return remote(
            source.at[here.expert(1)],
            full.at[here.z, 1 - here.x, here.core],
            ffn_send.at[j, 0],
            ffn_recv.at[j, 0],
            here.x_peer,
        )

    def ffn_mine(j):
        source, full = experts[j]
        return pltpu.make_async_copy(source.at[here.expert(0)], full.at[here.z, here.x, here.core], ffn_local.at[j])

    def ffn_copy(j, slot, z, x, core, peer):
        full = experts[j][1]
        part = full.at[z, :, core] if x is None else full.at[z, x, core]
        return remote(part, part, ffn_send.at[j, slot], ffn_recv.at[j, slot], peer)

    def ffn_to_z(j, k):
        return ffn_copy(j, 1 + k, here.z, None, here.core, here.z_peer(1 if k == 0 else planes - 1))

    def ffn_from_z(j, k):
        return ffn_copy(j, 1 + k, z_at(planes - 1 if k == 0 else 1), None, here.core, here.x_peer)

    def ffn_pass_z(j, k):
        z = z_at(planes - 1 if k == 0 else 1)
        return ffn_copy(j, 3 + k, z, k, here.core, here.z_peer(1 if k == 0 else planes - 1))

    def ffn_passed_z(j, k):
        return ffn_copy(j, 3 + k, z_at(2), k, here.core, here.x_peer)

    def ffn_to_core(j, step_z):
        return ffn_copy(j, 5 + step_z, z_at(step_z), None, here.core, here.core_peer)

    def ffn_from_core(j, step_z):
        return ffn_copy(j, 5 + step_z, z_at(step_z), None, 1 - here.core, here.core_peer)

    def row_copy(kind, member, number):
        source, target = ((grows_ref, grads_in_ref), (rows_ref, rows_in_ref))[kind]
        src, dst = source.at[member, number], target.at[number, member]
        if number == 0:
            return pltpu.make_async_copy(src, dst, row_local.at[kind, member])
        return remote(
            src,
            dst,
            row_send.at[kind, member, number],
            row_recv.at[kind, member, number],
            here.plane_peers[number],
        )

    def outs(t):
        full, target = ((attn_ref, attn_out_ref), (attn_o_ref, attn_o_out_ref))[t]
        return pltpu.make_async_copy(full, target, out_sem.at[t])

    @pl.when(step == 0)
    def _():
        for j in range(3):
            ffn_mine(j).start()
        for part in range(3):
            attn_ref[rows_of(mine), part * width : (part + 1) * width] = shard_refs[part][...].astype(BF16)
        attn_o_ref[rows_of(mine), :] = shard_refs[3][...].astype(BF16)
        tile_ref[...] = jnp.zeros_like(tile_ref)
        at = 0
        for part in small_refs:
            tile_ref[at : at + part.shape[0], 0:depth] = part[...]
            at += part.shape[0]
        tile_ref[at : at + kinds, 0:kinds] = map_ref[...]
        turned = jnp.transpose(tile_ref[...])
        map_t_ref[...] = pltpu.roll(turned[0:kinds, :], LANES - kinds - 8, 1)
        attn_ref[rows_of(mine), 3 * width : 3 * width + LANES] = turned[0:depth, :].astype(BF16)
        attn_ref[rows_of(mine), 3 * width + LANES :] = jnp.zeros((depth, LANES), BF16)
        here.barrier(
            [here.core_peer, here.x_peer, here.y_peer, here.xy_peer, here.z_peer(1), here.z_peer(planes - 1)]
        )
        for t in range(2):
            to_z(t, 0).start()
            to_z(t, 1).start()
            to_x(t, 0).start()
            to_core(t, 0, 0).start()
        for j in range(3):
            ffn_to_x(j).start()

        ids = iota((kinds, length), 0)
        before = jnp.where(iota((length, length), 0) < iota((length, length), 1), 1.0, 0.0).astype(BF16)
        for member in range(batches):
            first = routes_ref[0:1, member * length : (member + 1) * length] == ids
            second = routes_ref[1:2, member * length : (member + 1) * length] == ids
            hits = jnp.where(first | second, 1.0, 0.0)
            pos_ref[member] = jnp.where(hits > 0.0, nn(hits.astype(BF16), before), -1.0)
            for number in range(4):
                line = pos_ref[member, pl.ds(here.expert(number), 1), :]
                grows_ref[member, number] = nn(slot_mask(line, capacity), grad_ref[member]).astype(BF16)
            row_copy(0, member, 0).start()
            row_copy(0, member, 2).start()

        for high in range(coarse_ref.shape[1]):
            rows = slice(high * fine_ref.shape[1], (high + 1) * fine_ref.shape[1])
            cos_high, sin_high = coarse_ref[0, high : high + 1, :], coarse_ref[1, high : high + 1, :]
            cos_ref[rows, :] = cos_high * fine_ref[0] - sin_high * fine_ref[1]
            sin_ref[rows, :] = (sin_high * fine_ref[0] + cos_high * fine_ref[1]) * fine_ref[2]

        for t in range(2):
            for k, step_z in enumerate((planes - 1, 1)):
                from_z(t, k).wait_recv()
                pass_z(t, k).start()
                to_x(t, step_z).start()
                to_core(t, step_z, 0).start()
        for t in range(2):
            from_x(t, 0).wait_recv()
            to_y(t, 0).start()
        for j in range(3):
            ffn_mine(j).wait()
            ffn_from_x(j).wait_recv()
            ffn_to_z(j, 0).start()
            ffn_to_z(j, 1).start()
            ffn_to_core(j, 0).start()
        for t in range(2):
            passed_z(t, 0).wait_recv()
            passed_z(t, 1).wait_recv()
            to_x(t, 2).start()
            to_core(t, 2, 0).start()
        for member in range(batches):
            row_copy(0, member, 1).start()
            row_copy(0, member, 3).start()
        for t in range(2):
            for step_z in (planes - 1, 1, 2):
                from_x(t, step_z).wait_recv()
                to_y(t, step_z).start()
        for t in range(2):
            for step_z in (0, planes - 1, 1, 2):
                from_y(t, step_z).wait_recv()
                to_core(t, step_z, 1).start()
        for t in range(2):
            for step_z in range(planes):
                for x in range(2):
                    from_core(t, step_z, x).wait_recv()
        for t in range(2):
            outs(t).start()
        small_ref[...] = jnp.transpose(attn_ref[:, 3 * width : 3 * width + LANES].astype(F32))[0 : kinds + 8, :]

    def between():
        @pl.when(step == last)
        def _():
            for j in range(3):
                for k, step_z in enumerate((planes - 1, 1)):
                    ffn_from_z(j, k).wait_recv()
                    ffn_pass_z(j, k).start()
                    ffn_to_core(j, step_z).start()

    sequence_forward(
        x_ref,
        seg_ref[pl.ds(step, 1), :],
        routes_ref[:, pl.ds(pl.multiple_of(step * length, LANES), length)],
        prev_ref,
        map_t_ref,
        small_ref,
        attn_ref.at[:, 0:width],
        attn_ref.at[:, width : 2 * width],
        attn_ref.at[:, 2 * width : 3 * width],
        attn_o_ref,
        cos_ref,
        sin_ref,
        pos_ref.at[pl.ds(step, 1)],
        q_ref,
        k_ref,
        v_ref,
        o_ref,
        h_ref,
        lse_ref,
        aux_ref,
        [rows_ref.at[pl.ds(step, 1), number] for number in range(4)],
        bias_ref,
        proj_ref,
        here.expert,
        between,
    )
    for member in range(batches):

        @pl.when(step == member)
        def _():
            for number in range(4):
                row_copy(1, member, number).start()

    @pl.when(step == last)
    def _():
        for j in range(3):
            for k in range(2):
                ffn_passed_z(j, k).wait_recv()
            ffn_to_core(j, 2).start()
        for t in range(2):
            outs(t).wait()
            for k in range(2):
                to_z(t, k).wait_send()
                pass_z(t, k).wait_send()
            for step_z in range(planes):
                to_x(t, step_z).wait_send()
                to_y(t, step_z).wait_send()
                for x in range(2):
                    to_core(t, step_z, x).wait_send()
        for j in range(3):
            ffn_to_x(j).wait_send()
            for k in range(2):
                ffn_to_z(j, k).wait_send()
                ffn_pass_z(j, k).wait_send()
            for step_z in range(planes):
                ffn_to_core(j, step_z).wait_send()
                ffn_from_core(j, step_z).wait_recv()
        for kind in range(2):
            for member in range(batches):
                for number in range(4):
                    copy = row_copy(kind, member, number)
                    copy.wait()


def expert_kernel(
    a_ref,
    g_ref,
    gate_ref,
    up_ref,
    down_ref,
    v_ref,
    d_ref,
    grad_gate_ref,
    grad_up_ref,
    grad_down_ref,
    rows_ref,
    grads_ref,
    gates_ref,
    rows_t_ref,
    grads_t_ref,
    places_ref,
    acc_value_ref,
    acc_input_ref,
    acc_gate_ref,
    acc_up_ref,
    acc_down_ref,
    share_ref,
    sems,
):
    step = pl.program_id(0)
    last = pl.num_programs(0) - 1
    batches, capacity, width = g_ref.shape[1:]
    blocks = 4 * batches

    @pl.when(step == 0)
    def _():
        copies = []
        for number in range(4):
            rows, grads = a_ref.at[number], g_ref.at[number]
            for member in range(batches):
                block = number * batches + member
                span = pl.ds(block * capacity, capacity)
                copies.append(
                    pltpu.make_async_copy(
                        rows.at[member, pl.ds(capacity, 16), pl.ds(0, capacity)],
                        gates_ref.at[block],
                        sems.at[3 * block],
                    )
                )
                copies.append(
                    pltpu.make_async_copy(
                        rows.at[member, pl.ds(0, capacity), :], rows_ref.at[span, :], sems.at[3 * block + 1]
                    )
                )
                copies.append(
                    pltpu.make_async_copy(grads.at[member], grads_ref.at[span, :], sems.at[3 * block + 2])
                )
        for copy in copies:
            copy.start()
        for copy in copies:
            copy.wait()
        same = iota((capacity, capacity), 0) == iota((capacity, capacity), 1)
        spare = jnp.zeros((capacity, width), BF16)
        rows_ref[blocks * capacity :, :] = spare
        grads_ref[blocks * capacity :, :] = spare
        share_ref[...] = jnp.zeros_like(share_ref)

        def pack(block, place):
            span = pl.ds(pl.multiple_of(block * capacity, capacity), capacity)
            target = pl.ds(pl.multiple_of(place, 16), capacity)
            parts = gates_ref[block].astype(F32)
            count = jnp.max(parts[3:4, :]).astype(jnp.int32)
            line = jnp.sum(parts[0:3, :], axis=0, keepdims=True)
            column = jnp.sum(jnp.where(same, line, 0.0), axis=1, keepdims=True)
            rows = rows_ref[span, :]
            grads = (grads_ref[span, :].astype(F32) * column).astype(BF16)
            rows_ref[target, :] = rows
            grads_ref[target, :] = grads
            places_ref[block] = place
            return place + (count + 15) // 16 * 16

        total = lax.fori_loop(0, blocks, pack, 0)
        target = pl.ds(pl.multiple_of(total, 16), capacity)
        rows_ref[target, :] = spare
        grads_ref[target, :] = spare
        places_ref[blocks] = (total + capacity - 1) // capacity

        def turn(block, carry):
            span = pl.ds(pl.multiple_of(block * capacity, capacity), capacity)
            grads_t_ref[:, span] = jnp.transpose(grads_ref[span, :])
            rows_t_ref[:, span] = jnp.transpose(rows_ref[span, :])
            return carry

        lax.fori_loop(0, places_ref[blocks], turn, 0)

    acc_gate_ref[...] = jnp.zeros_like(acc_gate_ref)
    acc_up_ref[...] = jnp.zeros_like(acc_up_ref)
    acc_down_ref[...] = jnp.zeros_like(acc_down_ref)

    def work(block, carry):
        span = pl.ds(pl.multiple_of(block * capacity, capacity), capacity)
        rows = rows_ref[span, :]
        grads = grads_ref[span, :]
        gate = nn(rows, gate_ref[...])
        up = nn(rows, up_ref[...])
        back = nt(grads, down_ref[...])
        sig = 1.0 / (1.0 + jnp.exp(-gate))
        silu = gate * sig
        act = (silu * up).astype(BF16)
        grad_gate = (back * up * (sig * (1.0 + gate * (1.0 - sig)))).astype(BF16)
        grad_up = (back * silu).astype(BF16)
        value = nn(act, down_ref[...])
        grad_rows = nt(grad_gate, gate_ref[...]) + nt(grad_up, up_ref[...])
        rows_t = rows_t_ref[:, span]
        acc_gate_ref[...] += nn(rows_t, grad_gate)
        acc_up_ref[...] += nn(rows_t, grad_up)
        acc_down_ref[...] += nn(grads_t_ref[:, span], act)
        share = jnp.broadcast_to(
            jnp.sum(act.astype(F32) * back, axis=1, keepdims=True), (capacity, LANES)
        )

        @pl.when(step == 0)
        def _():
            share_ref[span, :] = share
            acc_value_ref[span, :] = value
            acc_input_ref[span, :] = grad_rows

        @pl.when(step > 0)
        def _():
            share_ref[span, :] += share

        @pl.when((step > 0) & (step < last))
        def _():
            acc_value_ref[span, :] += value
            acc_input_ref[span, :] += grad_rows

        @pl.when(step == last)
        def _():
            rows_ref[span, :] = (acc_value_ref[span, :] + value).astype(BF16)
            grads_ref[span, :] = (acc_input_ref[span, :] + grad_rows).astype(BF16)

        return carry

    lax.fori_loop(0, places_ref[blocks], work, 0)
    grad_gate_ref[...] = acc_gate_ref[...].astype(BF16)
    grad_up_ref[...] = acc_up_ref[...].astype(BF16)
    grad_down_ref[...] = jnp.transpose(acc_down_ref[...].astype(BF16))

    @pl.when(step == last)
    def _():
        same = iota((capacity, capacity), 0) == iota((capacity, capacity), 1)
        place = iota((16, capacity), 0)

        def shares(block, carry):
            column = share_ref[pl.ds(pl.multiple_of(places_ref[block], 16), capacity), 0:1]
            line = jnp.sum(jnp.where(same, column, 0.0), axis=0, keepdims=True)
            high = line.astype(BF16).astype(F32)
            mid = (line - high).astype(BF16).astype(F32)
            low = line - high - mid
            parts = jnp.where(place == 0, high, jnp.where(place == 1, mid, jnp.where(place == 2, low, 0.0)))
            gates_ref[block] = parts.astype(BF16)
            return carry

        lax.fori_loop(0, blocks, shares, 0)
        copies = []
        for number in range(4):
            values, grads = v_ref.at[number], d_ref.at[number]
            for member in range(batches):
                block = number * batches + member
                span = pl.ds(pl.multiple_of(places_ref[block], 16), capacity)
                copies.append(pltpu.make_async_copy(rows_ref.at[span, :], values.at[member], sems.at[3 * block]))
                copies.append(
                    pltpu.make_async_copy(
                        grads_ref.at[span, :], grads.at[member, pl.ds(0, capacity), :], sems.at[3 * block + 1]
                    )
                )
                copies.append(
                    pltpu.make_async_copy(
                        gates_ref.at[block],
                        grads.at[member, pl.ds(capacity, 16), pl.ds(0, capacity)],
                        sems.at[3 * block + 2],
                    )
                )
        for copy in copies:
            copy.start()
        for copy in copies:
            copy.wait()


def constant_mix(zs, index):
    za, zb = zs[:, index : index + 1], zs[:, index + 1 : index + 2]
    top = jnp.maximum(za, zb)
    ea, eb = jnp.exp(za - top), jnp.exp(zb - top)
    return ea / (ea + eb), eb / (ea + eb)


def token_columns(pos_ref, aux_ref, cols_ref):
    kinds, length = pos_ref.shape[1:]
    cols_ref[0:kinds, :] = pos_ref[0]
    cols_ref[kinds : kinds + 16, :] = aux_ref[0]
    cols_ref[kinds + 16 :, :] = jnp.zeros((LANES - kinds - 16, length), F32)
    return jnp.transpose(cols_ref[...])


def column(source, index):
    return jnp.sum(jnp.where(iota((1, LANES), 1) == index, source, 0.0), axis=1, keepdims=True)


def result_kernel(own_ref, v_ref, pos_ref, aux_ref, h_ref, small_ref, out_ref, cols_ref):
    block_output(own_ref, v_ref, pos_ref, aux_ref, h_ref, small_ref, out_ref, cols_ref)


def finish_kernel(
    own_ref,
    v_ref,
    pos_ref,
    aux_ref,
    h_ref,
    small_ref,
    sums_ref,
    out_ref,
    gq_ref,
    gk_ref,
    gv_ref,
    go_ref,
    router_ref,
    proj_ref,
    vec_ref,
    gain_one_ref,
    gain_two_ref,
    map_ref,
    cols_ref,
    tile_ref,
):
    @pl.when(pl.program_id(0) == 0)
    def _():
        depth, width = gq_ref.shape
        kinds = pos_ref.shape[1]
        for part, ref in enumerate((gq_ref, gk_ref, gv_ref, go_ref)):
            ref[...] = sums_ref[:, part * width : (part + 1) * width]
        small = sums_ref[:, 4 * width : 4 * width + LANES]
        tile_ref[...] = jnp.zeros_like(tile_ref)
        tile_ref[0:depth, :] = small
        turned = jnp.transpose(tile_ref[...])
        at = 0
        for ref in (router_ref, proj_ref, vec_ref, gain_one_ref, gain_two_ref):
            ref[...] = turned[at : at + ref.shape[0], 0:depth]
            at += ref.shape[0]
        map_ref[...] = pltpu.roll(small[0:kinds, :], LANES - kinds - 8, 1)[:, 0:kinds]

    block_output(own_ref, v_ref, pos_ref, aux_ref, h_ref, small_ref, out_ref, cols_ref)


def block_output(own_ref, v_ref, pos_ref, aux_ref, h_ref, small_ref, out_ref, cols_ref):
    own = own_ref[0]
    length, width = h_ref.shape[1:]
    kinds = pos_ref.shape[1]
    ffn = kinds - 4
    capacity = v_ref.shape[2]
    hidden = h_ref[0]
    n2 = hidden * rms_scale(hidden) * small_ref[kinds + 7 : kinds + 8, :]
    n2_high, n2_low = split2(n2)
    small = small_ref[...].astype(BF16)
    cols = token_columns(pos_ref, aux_ref, cols_ref)
    result = hidden
    slot_lane = iota((1, capacity), 1).astype(F32)
    for number in range(4):
        expert = own ^ number
        mask = jnp.where(column(cols, expert) == slot_lane, 1.0, 0.0).astype(BF16)
        result = result + column(cols, kinds + expert) * nn(mask, v_ref[number, 0])
    mixes = nt(n2_high, small) + nt(n2_low, small)
    share = column(cols, kinds + ffn + 1)
    for constant in range(2):
        weight = column(cols, kinds + ffn + 2 + constant)
        alpha_a, alpha_b = constant_mix(mixes, kinds + 2 * constant)
        result = result + (weight * alpha_b) * small_ref[kinds + 4 + constant : kinds + 5 + constant, :]
        share = share + weight * alpha_a
    out_ref[0] = result + share * n2


def sequence_combine(
    step,
    d_refs,
    pos_ref,
    aux_ref,
    prev_ref,
    h_ref,
    g_ref,
    o_ref,
    small_ref,
    wo_ref,
    dh_ref,
    dob_ref,
    sgrad_ref,
    grad_map_ref,
    acc_ref,
    cols_ref,
    expert_of,
):
    length, width = h_ref.shape[1:]
    kinds = pos_ref.shape[1]
    ffn = kinds - 4
    capacity = d_refs[0].shape[1] - 16
    hidden = h_ref[0]
    inverse = rms_scale(hidden)
    gain = small_ref[kinds + 7 : kinds + 8, :]
    n2 = hidden * inverse * gain
    n2_high, n2_low = split2(n2)
    grad_low = g_ref[0]
    grad = grad_low.astype(F32)
    small = small_ref[...].astype(BF16)
    cols = token_columns(pos_ref, aux_ref, cols_ref)
    lane = iota((1, LANES), 1)
    gate_one = column(cols, 2 * kinds)
    gate_two = column(cols, 2 * kinds + 1)
    ids = lane.astype(F32)
    hot_one = jnp.where(column(cols, 2 * kinds + 2) == ids, 1.0, 0.0)
    hot_two = jnp.where(column(cols, 2 * kinds + 3) == ids, 1.0, 0.0)

    grad_n2 = jnp.zeros((length, width), F32)
    shares = jnp.zeros((length, LANES), F32)
    slot_lane = iota((1, capacity), 1).astype(F32)
    for number, rows in enumerate(d_refs):
        expert = expert_of(number)
        mask = jnp.where(column(cols, expert) == slot_lane, 1.0, 0.0).astype(BF16)
        grad_n2 = grad_n2 + nn(mask, rows[0, 0:capacity, :])
        parts = nt(mask, rows[0, capacity:, 0:capacity])
        shares = jnp.where(lane == expert, jnp.sum(parts, axis=1, keepdims=True), shares)

    mixes = nt(n2_high, small) + nt(n2_low, small)
    inner = nt(grad_low, small)
    with_n2 = jnp.sum(grad * n2, axis=1, keepdims=True)
    weight_copy = column(cols, kinds + ffn + 1)
    shares = jnp.where(lane == ffn + 1, weight_copy * with_n2, shares)
    share = weight_copy
    coefs = jnp.zeros((length, LANES), F32)
    for constant in range(2):
        weight = column(cols, kinds + ffn + 2 + constant)
        alpha_a, alpha_b = constant_mix(mixes, kinds + 2 * constant)
        with_vec = inner[:, kinds + 4 + constant : kinds + 5 + constant]
        share = share + weight * alpha_a
        da = weight * with_n2
        db = weight * with_vec
        mean = alpha_a * da + alpha_b * db
        shares = jnp.where(lane == ffn + 2 + constant, mean, shares)
        coefs = jnp.where(lane == kinds + 2 * constant, alpha_a * (da - mean), coefs)
        coefs = jnp.where(lane == kinds + 2 * constant + 1, alpha_b * (db - mean), coefs)
        coefs = jnp.where(lane == kinds + 4 + constant, weight * alpha_b, coefs)

    share_one = jnp.sum(shares * hot_one, axis=1, keepdims=True)
    share_two = jnp.sum(shares * hot_two, axis=1, keepdims=True)
    both = share_one + share_two
    dlogits = (share_one - gate_one * both) * hot_one + (share_two - gate_two * both) * hot_two
    coefs = jnp.where(lane < kinds, dlogits, coefs)
    back = jnp.where(lane < kinds + 4, coefs, 0.0)[:, 0:16]
    back_high, back_low = split2(back)
    grad_n2 = grad_n2 + nn(back_high, small) + nn(back_low, small) + share * grad

    coefs_t = jnp.transpose(coefs)[0:16, :]
    high, low = split2(coefs_t)
    by_n2 = nn(high, n2_high) + nn(low, n2_high)
    by_low = nn(high, n2_low)
    by_grad = nn(high, grad_low) + nn(low, grad_low)
    row = iota((16, 1), 0)
    parts = jnp.where(row < kinds, by_n2, jnp.where(row < kinds + 4, by_n2 + by_low, by_grad))
    gain_part = jnp.sum(grad_n2 * hidden * inverse, axis=0, keepdims=True)
    parts = jnp.where(row == kinds + 7, gain_part, jnp.where(row == kinds + 6, 0.0, parts))
    dlog_t = coefs_t[0:kinds, :]
    map_lane = iota((kinds, LANES), 1)
    map_part = jnp.zeros((kinds, LANES), F32)
    for j in range(kinds):
        map_part = jnp.where(
            map_lane == j, jnp.sum(dlog_t * prev_ref[j : j + 1, :], axis=1, keepdims=True), map_part
        )

    scaled = gain * grad_n2
    inner_mean = jnp.mean(scaled * hidden, axis=-1, keepdims=True)
    dh = grad + inverse * scaled - hidden * (inverse * inverse * inverse) * inner_mean
    dh_ref[0] = dh
    db = dh.astype(BF16)
    dob_ref[0] = nt(db, wo_ref[...]).astype(BF16)
    wo_part = nn(jnp.transpose(o_ref[0]), db)

    @pl.when(step == 0)
    def _():
        acc_ref[...] = wo_part
        sgrad_ref[...] = parts
        grad_map_ref[...] = map_part

    @pl.when(step > 0)
    def _():
        acc_ref[...] += wo_part
        sgrad_ref[...] += parts
        grad_map_ref[...] += map_part


def combine_kernel(
    own_ref,
    d0,
    d1,
    d2,
    d3,
    pos_ref,
    aux_ref,
    prev_ref,
    h_ref,
    g_ref,
    o_ref,
    small_ref,
    wo_ref,
    dh_ref,
    dob_ref,
    grad_wo_ref,
    sgrad_ref,
    grad_map_ref,
    acc_ref,
    cols_ref,
):
    own = own_ref[0]
    step = pl.program_id(0)
    sequence_combine(
        step,
        (d0, d1, d2, d3),
        pos_ref,
        aux_ref,
        prev_ref,
        h_ref,
        g_ref,
        o_ref,
        small_ref,
        wo_ref,
        dh_ref,
        dob_ref,
        sgrad_ref,
        grad_map_ref,
        acc_ref,
        cols_ref,
        lambda number: own ^ number,
    )

    @pl.when(step == pl.num_programs(0) - 1)
    def _():
        grad_wo_ref[...] = acc_ref[...].astype(BF16)


def sequence_backward(
    step,
    x_ref,
    segments,
    q_ref,
    k_ref,
    v_ref,
    dob_ref,
    lse_ref,
    dh_ref,
    small_ref,
    wq_ref,
    wk_ref,
    wv_ref,
    cos_ref,
    sin_ref,
    gin_ref,
    gain_ref,
    bias_ref,
    lse_t_ref,
    dqkv_ref,
    acc_ref,
):
    length, width = x_ref.shape[1:]
    kinds = small_ref.shape[0] - 8
    pairs = width // LANES
    lane = iota((1, LANES), 1)
    low_half = (lane % HEAD_DIM) < (HEAD_DIM // 2)
    first_head = lane < HEAD_DIM
    mask_a = jnp.where(first_head, 1.0, 0.0).astype(BF16)
    mask_b = jnp.where(first_head, 0.0, 1.0).astype(BF16)
    allowed = same_document(segments) & (
        iota((length, length), 0) // BLOCK <= iota((length, length), 1) // BLOCK
    )
    bias_ref[...] = jnp.where(allowed, 0.0, NEG)
    lse_t_ref[...] = jnp.transpose(lse_ref[0])

    def pair(h, carry):
        cols = pl.ds(pl.multiple_of(h * LANES, LANES), LANES)
        keys_t = jnp.transpose(k_ref[0, :, cols])
        grad_keys = None
        grad_values = None
        grad_queries = []
        for begin in range(0, length, BLOCK):
            end = begin + BLOCK
            queries = q_ref[0, begin:end, cols]
            outs = dob_ref[0, begin:end, cols]
            keys = k_ref[0, 0:end, cols]
            values = v_ref[0, 0:end, cols]
            queries = jnp.concatenate([queries * mask_a, queries * mask_b], axis=0)
            outs = jnp.concatenate([outs * mask_a, outs * mask_b], axis=0)
            bias = bias_ref[0:end, begin:end]
            bias = jnp.concatenate([bias, bias], axis=1)
            line = jnp.concatenate(
                [lse_t_ref[pl.ds(2 * h, 1), begin:end], lse_t_ref[pl.ds(2 * h + 1, 1), begin:end]], axis=1
            )
            chances = jnp.exp(nt(keys, queries) + bias - line)
            grad_chances = nt(values, outs)
            delta = jnp.sum(chances * grad_chances, axis=0, keepdims=True)
            grad_scores = (chances * (grad_chances - delta)).astype(BF16)
            dv = nn(chances.astype(BF16), outs)
            dk = nn(grad_scores, queries)
            dq = jnp.transpose(nn(keys_t[:, 0:end], grad_scores))
            grad_queries.append(jnp.where(first_head, dq[0:BLOCK], dq[BLOCK:]))
            if grad_keys is None:
                grad_keys, grad_values = dk, dv
            else:
                grad_keys = jnp.concatenate([grad_keys + dk[0:begin], dk[begin:]], axis=0)
                grad_values = jnp.concatenate([grad_values + dv[0:begin], dv[begin:]], axis=0)
        dq = jnp.concatenate(grad_queries, axis=0) * 0.125
        dq = dq * cos_ref[...] - swap_halves(dq, low_half) * sin_ref[...]
        dk = grad_keys * cos_ref[...] - swap_halves(grad_keys, low_half) * sin_ref[...]
        dqkv_ref[:, cols] = dq.astype(BF16)
        dqkv_ref[:, pl.ds(pl.multiple_of(width + h * LANES, LANES), LANES)] = dk.astype(BF16)
        dqkv_ref[:, pl.ds(pl.multiple_of(2 * width + h * LANES, LANES), LANES)] = grad_values.astype(BF16)
        return carry

    lax.fori_loop(0, pairs, pair, 0)

    tokens = x_ref[0].astype(F32)
    inverse = rms_scale(tokens)
    gain = small_ref[kinds + 6 : kinds + 7, :]
    a1_t = jnp.transpose((tokens * inverse * gain).astype(BF16))
    dn1 = (
        nt(dqkv_ref[:, 0:width], wq_ref[...])
        + nt(dqkv_ref[:, width : 2 * width], wk_ref[...])
        + nt(dqkv_ref[:, 2 * width :], wv_ref[...])
    )
    scaled = gain * dn1
    inner_mean = jnp.mean(scaled * tokens, axis=-1, keepdims=True)
    gin_ref[0] = dh_ref[0] + inverse * scaled - tokens * (inverse * inverse * inverse) * inner_mean
    gain_part = jnp.broadcast_to(jnp.sum(dn1 * tokens * inverse, axis=0, keepdims=True), gain_ref.shape)

    @pl.when(step == 0)
    def _():
        acc_ref[...] = jnp.zeros_like(acc_ref)
        gain_ref[...] = gain_part

    @pl.when(step > 0)
    def _():
        gain_ref[...] += gain_part

    for part in range(3):
        span = slice(part * width, (part + 1) * width)
        acc_ref[:, span] += nn(a1_t, dqkv_ref[:, span])


def small_table(depth, sgrad_ref, grad_map_ref, gain_ref):
    kinds = grad_map_ref.shape[0]
    width = sgrad_ref.shape[1]
    row = iota((16, 1), 0)
    table = jnp.where(row == kinds + 6, gain_ref[0:1, :], sgrad_ref[...])
    chosen = jnp.where(iota((LANES, width), 1) % depth == iota((LANES, width), 0), 1.0, 0.0).astype(BF16)
    maps = nn(grad_map_ref[...].astype(BF16), chosen)
    table = jnp.concatenate([table, maps, jnp.zeros((LANES - 16 - kinds, width), F32)], axis=0)
    return jnp.transpose(table).astype(BF16)


def backward_kernel(
    x_ref,
    seg_ref,
    q_ref,
    k_ref,
    v_ref,
    dob_ref,
    lse_ref,
    dh_ref,
    small_ref,
    wq_ref,
    wk_ref,
    wv_ref,
    cos_ref,
    sin_ref,
    gin_ref,
    grad_w_ref,
    gain_ref,
    bias_ref,
    lse_t_ref,
    dqkv_ref,
    acc_ref,
):
    step = pl.program_id(0)
    sequence_backward(
        step,
        x_ref,
        seg_ref[0],
        q_ref,
        k_ref,
        v_ref,
        dob_ref,
        lse_ref,
        dh_ref,
        small_ref,
        wq_ref,
        wk_ref,
        wv_ref,
        cos_ref,
        sin_ref,
        gin_ref,
        gain_ref,
        bias_ref,
        lse_t_ref,
        dqkv_ref,
        acc_ref,
    )

    @pl.when(step == pl.num_programs(0) - 1)
    def _():
        grad_w_ref[...] = acc_ref[...].astype(BF16)


class ReducedChunk:
    def __init__(self, here, depth, begin, value_of, send_buffer, core_buffer, buffers, out_ref, sems):
        self.here, self.depth, self.begin, self.value_of = here, depth, begin, value_of
        self.send_buffer, self.acc, self.out_ref = send_buffer, core_buffer, out_ref
        y_first, x_first, x_second, y_second, self.z_buffer, self.done, self.other = buffers
        send, recv, z_send, z_recv = sems
        planes, x, y = here.planes, here.x, here.y
        near = planes // 2
        self.half = send_buffer.shape[3] // 2
        self.mine = pl.ds(pl.multiple_of(y * self.half, LANES), self.half)
        theirs = pl.ds(pl.multiple_of((1 - y) * self.half, LANES), self.half)
        self.received = (y_first, x_first, x_second, y_second)
        acc = core_buffer
        self.swap = remote(send_buffer, acc, send.at[0], recv.at[0], here.core_peer)
        self.y_first = remote(acc.at[0:near, :, :, theirs], y_first, send.at[1], recv.at[1], here.y_peer)
        self.x_first = remote(acc.at[near:planes, 1 - x], x_first, send.at[2], recv.at[2], here.x_peer)
        self.x_second = remote(acc.at[0:near, 1 - x, :, self.mine], x_second, send.at[3], recv.at[3], here.x_peer)
        self.y_second = remote(acc.at[near:planes, x, :, theirs], y_second, send.at[4], recv.at[4], here.y_peer)
        self.along = [
            remote(
                acc.at[(here.z + k) % planes, x, :, self.mine],
                self.z_buffer.at[k - 1],
                z_send.at[k - 1],
                z_recv.at[k - 1],
                here.z_peer(k),
            )
            for k in range(1, planes)
        ]
        self.back = remote(self.done, self.other, send.at[5], recv.at[5], here.y_peer)
        self.phases = (self.first, self.second, self.third, self.fourth, self.fifth)

    def rows_of(self, z, column, core):
        return pl.ds(pl.multiple_of(self.here.block(z, column, core) * self.depth, 16), self.depth)

    def lower(self):
        def body(z, carry):
            for column in range(2):
                rows = self.rows_of(z, column, 1 - self.here.core)
                self.send_buffer[z, column] = self.value_of(rows).astype(BF16)
            return carry

        lax.fori_loop(0, self.here.planes, body, 0)

    def add(self, target, source):
        target[...] = (target[...].astype(F32) + source[...].astype(F32)).astype(BF16)

    def first(self):
        self.swap.wait_recv()

        def body(z, carry):
            for column in range(2):
                own = self.value_of(self.rows_of(z, column, self.here.core)).astype(F32)
                self.acc[z, column] = (own + self.acc[z, column].astype(F32)).astype(BF16)
            return carry

        lax.fori_loop(0, self.here.planes, body, 0)
        self.y_first.start()
        self.x_first.start()

    def second(self):
        planes = self.here.planes
        self.y_first.wait_recv()
        for z in range(planes // 2):
            for column in range(2):
                self.add(self.acc.at[z, column, :, self.mine], self.received[0].at[z, column])
        self.x_second.start()
        self.x_first.wait_recv()
        for z in range(planes // 2, planes):
            self.add(self.acc.at[z, self.here.x], self.received[1].at[z - planes // 2])
        self.y_second.start()

    def third(self):
        planes = self.here.planes
        self.x_second.wait_recv()
        for z in range(planes // 2):
            self.add(self.acc.at[z, self.here.x, :, self.mine], self.received[2].at[z])
        self.y_second.wait_recv()
        for z in range(planes // 2, planes):
            self.add(self.acc.at[z, self.here.x, :, self.mine], self.received[3].at[z - planes // 2])
        for copy in self.along:
            copy.start()

    def fourth(self):
        total = self.acc[self.here.z, self.here.x, :, self.mine].astype(F32)
        for k, copy in enumerate(self.along):
            copy.wait_recv()
            total = total + self.z_buffer[k].astype(F32)
        self.done[...] = total.astype(BF16)
        self.back.start()

    def fifth(self):
        self.back.wait_recv()
        y = self.here.y
        spot = pl.ds(pl.multiple_of(self.begin + y * self.half, LANES), self.half)
        other = pl.ds(pl.multiple_of(self.begin + (1 - y) * self.half, LANES), self.half)
        self.out_ref[:, spot] = self.done[...].astype(F32)
        self.out_ref[:, other] = self.other[...].astype(F32)
        for copy in [self.swap, self.y_first, self.x_first, self.x_second, self.y_second, self.back] + self.along:
            copy.wait_send()


def attention_columns(acc_ref, acc_wo_ref, table_ref, begin, columns, rows):
    pieces = []
    width = acc_wo_ref.shape[1]
    for start, size, ref in (
        (0, 3 * width, acc_ref),
        (3 * width, width, acc_wo_ref),
        (4 * width, LANES, table_ref),
        (4 * width + LANES, LANES, None),
    ):
        low, high = max(begin, start) - start, min(begin + columns, start + size) - start
        if low < high:
            if ref is None:
                pieces.append(jnp.zeros((rows.size, high - low), F32))
            else:
                pieces.append(ref[rows, low:high].astype(F32))
    return pieces[0] if len(pieces) == 1 else jnp.concatenate(pieces, axis=1)


def reduce_attention(chunks, free_sem):
    chunks[0].lower()
    pl.semaphore_wait(free_sem, 1)
    chunks[0].swap.start()
    for chunk in chunks[1:]:
        chunk.lower()
        chunk.swap.start()
    phases = len(chunks[0].phases)
    for step in range(len(chunks) + phases - 1):
        for number, chunk in enumerate(chunks):
            if 0 <= step - number < phases:
                chunk.phases[step - number]()


def fused_backward_kernel(
    group,
    depth,
    pos_ref,
    aux_ref,
    prev_ref,
    h_ref,
    g_ref,
    o_ref,
    x_ref,
    seg_ref,
    q_ref,
    k_ref,
    v_ref,
    lse_ref,
    small_ref,
    wq_ref,
    wk_ref,
    wv_ref,
    wo_ref,
    cos_ref,
    sin_ref,
    d_ref,
    val_ref,
    gate_ref,
    up_ref,
    down_ref,
    gin_ref,
    sums_ref,
    d_in_ref,
    val_in_ref,
    gate_out_ref,
    up_out_ref,
    down_out_ref,
    acc_ref,
    acc_wo_ref,
    table_ref,
    send_buffers,
    chunk_buffers,
    cols_ref,
    dh_ref,
    dob_ref,
    sgrad_ref,
    grad_map_ref,
    gain_ref,
    bias_ref,
    lse_t_ref,
    dqkv_ref,
    rows_ref,
    gate_own,
    up_own,
    down_own,
    gate_swap,
    up_swap,
    down_swap,
    gate_near,
    up_near,
    down_near,
    gate_far,
    up_far,
    down_far,
    row_local,
    row_send,
    row_recv,
    ffn_local,
    ffn_send,
    ffn_recv,
    free_sem,
    reduce_send,
    reduce_recv,
    reduce_z_send,
    reduce_z_recv,
):
    step = pl.program_id(0)
    last = pl.num_programs(0) - 1
    here = Place(group)
    planes = here.planes
    batches = d_ref.shape[1]
    width = x_ref.shape[2]
    grads = (gate_ref, up_ref, down_ref)
    owns = (gate_own, up_own, down_own)
    swaps = (gate_swap, up_swap, down_swap)
    nears = (gate_near, up_near, down_near)
    fars = (gate_far, up_far, down_far)
    outs = (gate_out_ref, up_out_ref, down_out_ref)
    side = (here.z_peer(1), here.z_peer(planes - 1))

    def z_at(k):
        return (here.z + k) % planes

    def row_copy(kind, member, number):
        source, target = ((d_ref, d_in_ref), (val_ref, val_in_ref))[kind]
        src, dst = source.at[number, member], target.at[number, member]
        if number == 0:
            return pltpu.make_async_copy(src, dst, row_local.at[batches * 4 + member])
        return remote(
            src, dst, row_send.at[kind, member, number], row_recv.at[kind, member, number], here.plane_peers[number]
        )

    def load_rows(member, number):
        source = d_ref if number == 0 else d_in_ref
        return pltpu.make_async_copy(
            source.at[number, member], rows_ref.at[number, 0], row_local.at[member * 4 + number]
        )

    def own_copy(j):
        return pltpu.make_async_copy(grads[j].at[:, :, here.core], owns[j], ffn_local.at[j, 0])

    def swap_copy(j):
        return remote(
            grads[j].at[:, :, 1 - here.core], swaps[j], ffn_send.at[j, 0], ffn_recv.at[j, 0], here.core_peer
        )

    def near_copy(j, k):
        return remote(
            owns[j].at[z_at(2), k], nears[j].at[k], ffn_send.at[j, 1 + k], ffn_recv.at[j, 1 + k], side[k]
        )

    def far_copy(j, k):
        return remote(
            owns[j].at[z_at(1 if k == 0 else planes - 1)],
            fars[j].at[k],
            ffn_send.at[j, 3 + k],
            ffn_recv.at[j, 3 + k],
            side[k],
        )

    def plane_copy(j, number):
        x = here.x if number % 2 == 0 else 1 - here.x
        src, dst = owns[j].at[here.z, x], outs[j].at[here.expert(0)]
        if number == 0:
            return pltpu.make_async_copy(src, dst, ffn_local.at[j, 1])
        return remote(
            src, dst, ffn_send.at[j, 4 + number], ffn_recv.at[j, 4 + number], here.plane_peers[number]
        )

    def plane_arrival(j, number):
        dst = outs[j].at[here.expert(number)]
        return remote(
            dst, dst, ffn_send.at[j, 4 + number], ffn_recv.at[j, 4 + number], here.plane_peers[number]
        )

    def add(target, *sources):
        value = target[...].astype(F32)
        for source in sources:
            value = value + source[...].astype(F32)
        target[...] = value.astype(BF16)

    @pl.when(step == 0)
    def _():
        for j in range(3):
            own_copy(j).start()
        here.barrier(
            [here.core_peer, here.x_peer, here.y_peer, here.xy_peer] + [here.z_peer(k) for k in range(1, planes)]
        )
        for number in range(1, 4):
            row_copy(0, 0, number).start()
        for j in range(3):
            swap_copy(j).start()
        for j in range(3):
            own_copy(j).wait()
            swap_copy(j).wait_recv()
            for x in range(2):

                def add_core(z, carry):
                    add(owns[j].at[z, x], swaps[j].at[z, x])
                    return carry

                lax.fori_loop(0, planes, add_core, 0)
            near_copy(j, 0).start()
            near_copy(j, 1).start()
        pl.semaphore_signal(free_sem, inc=1, device_id=here.core_peer, device_id_type=MESH)

    for member in range(batches):

        @pl.when(step == member)
        def _():
            for number in range(1, 4):
                row_copy(0, member, number).wait_recv()
            if member + 1 < batches:
                for number in range(1, 4):
                    row_copy(0, member + 1, number).start()
            for number in range(4):
                row_copy(1, member, number).start()
            for number in range(4):
                load_rows(member, number).start()
            for number in range(4):
                load_rows(member, number).wait()

    sequence_combine(
        step,
        [rows_ref.at[number] for number in range(4)],
        pos_ref,
        aux_ref,
        prev_ref,
        h_ref,
        g_ref,
        o_ref,
        small_ref,
        wo_ref,
        dh_ref,
        dob_ref,
        sgrad_ref,
        grad_map_ref,
        acc_wo_ref,
        cols_ref,
        here.expert,
    )

    @pl.when(step == 0)
    def _():
        for j in range(3):
            for k in range(2):
                near_copy(j, k).wait_recv()
                add(owns[j].at[z_at(1 if k == 0 else planes - 1), k], nears[j].at[k])
                far_copy(j, k).start()

    sequence_backward(
        step,
        x_ref,
        seg_ref[pl.ds(step, 1), :],
        q_ref,
        k_ref,
        v_ref,
        dob_ref,
        lse_ref,
        dh_ref,
        small_ref,
        wq_ref,
        wk_ref,
        wv_ref,
        cos_ref,
        sin_ref,
        gin_ref,
        gain_ref,
        bias_ref,
        lse_t_ref,
        dqkv_ref,
        acc_ref,
    )

    @pl.when(step == last)
    def _():
        table_ref[...] = small_table(depth, sgrad_ref, grad_map_ref, gain_ref)
        for j in range(3):
            for k in range(2):
                far_copy(j, k).wait_recv()
            for x in range(2):
                add(owns[j].at[here.z, x], fars[j].at[0, x], fars[j].at[1, x])
            for number in range(4):
                plane_copy(j, number).start()
        chunks = []
        begin = 0
        for number, (send_buffer, buffers) in enumerate(zip(send_buffers, chunk_buffers)):
            columns = send_buffer.shape[3]
            home, place = (gate_swap, begin) if begin < gate_swap.shape[3] else (up_swap, begin - gate_swap.shape[3])
            chunks.append(
                ReducedChunk(
                    here,
                    depth,
                    begin,
                    functools.partial(attention_columns, acc_ref, acc_wo_ref, table_ref, begin, columns),
                    send_buffer,
                    home.at[:, :, :, place : place + columns],
                    buffers,
                    sums_ref,
                    (
                        reduce_send.at[number],
                        reduce_recv.at[number],
                        reduce_z_send.at[number],
                        reduce_z_recv.at[number],
                    ),
                )
            )
            begin += columns
        reduce_attention(chunks, free_sem)
        for j in range(3):
            swap_copy(j).wait_send()
            for k in range(2):
                near_copy(j, k).wait_send()
                far_copy(j, k).wait_send()
            plane_copy(j, 0).wait()
            for number in range(1, 4):
                plane_copy(j, number).wait_send()
                plane_arrival(j, number).wait_recv()
        for member in range(batches):
            row_copy(1, member, 0).wait()
            for number in range(1, 4):
                row_copy(0, member, number).wait_send()
                row_copy(1, member, number).wait()


def params(limit_mib):
    return pltpu.CompilerParams(vmem_limit_bytes=limit_mib * 1024 * 1024, dimension_semantics=("arbitrary",))


def rotary(length):
    halfway = HEAD_DIM // 2
    frequency = 10000.0 ** (-jnp.arange(halfway).astype(F32) / halfway)
    angles = jnp.arange(length).astype(F32)[:, None] * frequency[None, :]
    cosine, sine = jnp.cos(angles), jnp.sin(angles)
    return (
        jnp.concatenate([cosine] * 4, axis=1),
        jnp.concatenate([-sine, sine, -sine, sine], axis=1),
    )


def rotary_parts(length):
    halfway = HEAD_DIM // 2
    frequency = 10000.0 ** (-np.arange(halfway) / halfway)
    step = 32
    sign = np.tile(np.repeat([-1.0, 1.0], halfway), LANES // HEAD_DIM)

    def table(positions):
        angles = np.tile(positions[:, None] * frequency[None, :], (1, LANES // halfway))
        return np.cos(angles), np.sin(angles)

    coarse = table(np.arange(0, length, step))
    fine = table(np.arange(step))
    signs = np.broadcast_to(sign, fine[0].shape)
    return jnp.asarray(np.stack(coarse), F32), jnp.asarray(np.stack(fine + (signs,)), F32)


def local(
    reps,
    group,
    block_input,
    prev_logits,
    routes,
    segments,
    grad_out,
    gain_attn,
    w_query,
    w_key,
    w_value,
    w_output,
    gain_mix,
    router,
    route_map,
    const_proj,
    const_vec,
    w_gate,
    w_up,
    w_down,
):
    batches, length = segments.shape
    width = block_input.shape[1]
    kinds = router.shape[1]
    ffn = w_gate.shape[1]
    hidden = w_gate.shape[2]
    rows_d = w_gate.shape[0]
    rows_f = w_down.shape[0]
    capacity = length // 2
    planes = group // 4
    assert reps == 2 and ffn == 4 and group % 4 == 0
    g = lax.axis_index("grp")
    y = lax.axis_index("rep")
    core = g % 2
    x = (g // 2) % 2
    z = g // 4
    own = (2 * y + x).astype(jnp.int32)
    own_arr = own.reshape(1)

    x_flip = [(i, i ^ 2) for i in range(group)]
    core_flip = [(i, i ^ 1) for i in range(group)]
    y_flip = [(0, 1), (1, 0)]
    xy_flip = [(r * group + i, (1 - r) * group + (i ^ 2)) for r in range(2) for i in range(group)]

    def z_shift(k):
        return [(i, (i + 4 * k) % group) for i in range(group)]

    def to_plane(parts):
        return [
            parts[0],
            lax.ppermute(parts[1], "grp", x_flip),
            lax.ppermute(parts[2], "rep", y_flip),
            lax.ppermute(parts[3], ("rep", "grp"), xy_flip),
        ]

    tokens = block_input.reshape(batches, length, width)
    grads = grad_out.reshape(batches, length, width)
    route_rows = routes.T
    prev_rows = prev_logits.T
    row_spec = pl.BlockSpec((2, length), lambda b, *_: (0, b))
    prev_spec = pl.BlockSpec((kinds, length), lambda b, *_: (0, b))

    def spec_w(j):
        return pl.BlockSpec((width, width), lambda b, *_: (0, j), pipeline_mode=pl.Buffered(1))

    row_shape = jax.ShapeDtypeStruct((batches, capacity, width), BF16)
    seq_bf16 = jax.ShapeDtypeStruct((batches, length, width), BF16)
    seq_f32 = jax.ShapeDtypeStruct((batches, length, width), F32)
    fused = planes == 4 and rows_d % 16 == 0 and rows_f % 16 == 0
    if fused:
        any_space = pl.BlockSpec(memory_space=pl.ANY)
        coarse, fine = rotary_parts(length)
        smalls = [router.T, const_proj.T, const_vec.T, gain_attn[None], gain_mix[None]]
        out_struct = jax.ShapeDtypeStruct
        (
            q, k, v, o, h1, lse, aux, pos, small, cos, sin, attn, attn_o, a_rows, grad_rows, gate_full, up_full, down_full,
        ) = pl.pallas_call(
            functools.partial(fused_forward_kernel, group),
            grid=(batches,),
            in_specs=[
                per_seq((length, width)),
                whole((batches, length)),
                whole((2, batches * length)),
                prev_spec,
                whole((kinds, kinds)),
                whole((batches, length, width)),
                whole(coarse.shape),
                whole(fine.shape),
                [whole((rows_d, width))] * 4,
                [whole(part.shape) for part in smalls],
            ]
            + [any_space] * 3,
            out_specs=[per_seq((length, width))] * 5
            + [
                per_seq((length, LANES)),
                per_seq((16, length)),
                whole((batches, kinds, length)),
                whole((kinds + 8, width)),
                whole((length, LANES)),
                whole((length, LANES)),
            ]
            + [any_space] * 7,
            scratch_shapes=[
                pltpu.VMEM((width, 3 * width + 2 * LANES), BF16),
                pltpu.VMEM((width, width), BF16),
                pltpu.VMEM((length, length), F32),
                pltpu.VMEM((length, width), F32),
                pltpu.VMEM((batches, 4, capacity + 16, width), BF16),
                pltpu.VMEM((batches, 4, capacity, width), BF16),
                pltpu.VMEM((LANES, LANES), F32),
                pltpu.VMEM((kinds, LANES), F32),
                pltpu.SemaphoreType.DMA((2, 4 + 4 * planes)),
                pltpu.SemaphoreType.DMA((2, 4 + 4 * planes)),
                pltpu.SemaphoreType.DMA((3,)),
                pltpu.SemaphoreType.DMA((3, 5 + planes)),
                pltpu.SemaphoreType.DMA((3, 5 + planes)),
                pltpu.SemaphoreType.DMA((2,)),
                pltpu.SemaphoreType.DMA((2, batches)),
                pltpu.SemaphoreType.DMA((2, batches, 4)),
                pltpu.SemaphoreType.DMA((2, batches, 4)),
            ],
            out_shape=[seq_bf16] * 4
            + [
                seq_f32,
                out_struct((batches, length, LANES), F32),
                out_struct((batches, 16, length), F32),
                out_struct((batches, kinds, length), F32),
                out_struct((kinds + 8, width), F32),
                out_struct((length, LANES), F32),
                out_struct((length, LANES), F32),
                out_struct((width, 3 * width + 2 * LANES), BF16),
                out_struct((width, width), BF16),
                out_struct((4, batches, capacity + 16, width), BF16),
                out_struct((4, batches, capacity, width), BF16),
                out_struct((planes, 2, 2, rows_d, hidden), BF16),
                out_struct((planes, 2, 2, rows_d, hidden), BF16),
                out_struct((planes, 2, 2, rows_f, width), BF16),
            ],
            compiler_params=pltpu.CompilerParams(
                vmem_limit_bytes=58 * 1024 * 1024,
                dimension_semantics=("arbitrary",),
                collective_id=1,
                has_side_effects=True,
            ),
            cost_estimate=pl.CostEstimate(flops=40 * 10**9, bytes_accessed=60 * 10**6, transcendentals=10**7),
            name="fused_forward",
        )(
            tokens, segments, route_rows, prev_rows, route_map, grads, coarse, fine,
            [w_query, w_key, w_value, w_output], smalls,
            w_gate.astype(BF16).transpose(1, 0, 2),
            w_up.astype(BF16).transpose(1, 0, 2),
            w_down.astype(BF16).transpose(1, 0, 2),
        )
        gate_full = gate_full.reshape(width, hidden)
        up_full = up_full.reshape(width, hidden)
        down_full = down_full.reshape(hidden, width)
    else:
        cos, sin = rotary(length)
        small_shard = jnp.concatenate(
            [router, const_proj, const_vec, gain_attn[:, None], gain_mix[:, None]], axis=1
        ).astype(BF16)
        small_shard = jnp.pad(small_shard, ((0, 0), (0, 2 * LANES - small_shard.shape[1])))
        shard = jnp.concatenate([w.astype(BF16) for w in (w_query, w_key, w_value)] + [small_shard], axis=1)
        shard_o = w_output.astype(BF16)
        attn = lax.all_gather(shard, "grp", axis=0, tiled=True)
        attn_o = lax.all_gather(shard_o, "grp", axis=0, tiled=True)
        small = attn[:, 3 * width : 3 * width + kinds + 8].astype(F32).T

        def pick(array, expert):
            return lax.dynamic_index_in_dim(array, expert, axis=1, keepdims=False)

        def gather_expert(mine, other):
            crossed = lax.ppermute(other, "grp", x_flip)
            both = jnp.where(x == 0, jnp.stack([mine, crossed]), jnp.stack([crossed, mine]))
            pieces = [both] + [lax.ppermute(both, "grp", z_shift(k)) for k in range(1, planes)]
            stacked = jnp.stack(pieces)
            half = jnp.take(stacked, (z - jnp.arange(planes)) % planes, axis=0)
            swapped = lax.ppermute(half, "grp", core_flip)
            return jnp.where(core == 0, jnp.stack([half, swapped], axis=2), jnp.stack([swapped, half], axis=2))

        gate_up = gather_expert(
            jnp.stack([pick(w_gate, own), pick(w_up, own)]).astype(BF16),
            jnp.stack([pick(w_gate, own ^ 1), pick(w_up, own ^ 1)]).astype(BF16),
        )
        down = gather_expert(pick(w_down, own).astype(BF16), pick(w_down, own ^ 1).astype(BF16))
        gate_full = gate_up[:, :, :, 0].reshape(width, hidden)
        up_full = gate_up[:, :, :, 1].reshape(width, hidden)
        down_full = down.reshape(hidden, width)

        *grad_rows, pos = pl.pallas_call(
            grad_rows_kernel,
            grid_spec=pltpu.PrefetchScalarGridSpec(
                num_scalar_prefetch=1,
                grid=(batches,),
                in_specs=[row_spec, per_seq((length, width))],
                out_specs=[per_seq((capacity, width))] * 4 + [per_seq((kinds, length))],
            ),
            out_shape=[row_shape] * 4 + [jax.ShapeDtypeStruct((batches, kinds, length), F32)],
            compiler_params=params(32),
            cost_estimate=pl.CostEstimate(flops=4 * 10**9, bytes_accessed=8 * 10**6, transcendentals=0),
            name="grad_rows",
        )(own_arr, route_rows, grads)
        grad_rows = to_plane(grad_rows)

        q, k, v, o, h1, lse, aux, *a_rows = pl.pallas_call(
            forward_kernel,
            grid_spec=pltpu.PrefetchScalarGridSpec(
                num_scalar_prefetch=1,
                grid=(batches,),
                in_specs=[
                    per_seq((length, width)),
                    per_seq((1, length)),
                    row_spec,
                    prev_spec,
                    whole((kinds, kinds)),
                    whole((kinds + 8, width)),
                    spec_w(0),
                    spec_w(1),
                    spec_w(2),
                    spec_w(0),
                    whole((length, LANES)),
                    whole((length, LANES)),
                    per_seq((kinds, length)),
                ],
                out_specs=[per_seq((length, width))] * 5
                + [per_seq((length, LANES)), per_seq((16, length))]
                + [per_seq((capacity + 16, width))] * 4,
                scratch_shapes=[pltpu.VMEM((length, length), F32), pltpu.VMEM((length, width), F32)],
            ),
            out_shape=[seq_bf16] * 4
            + [
                seq_f32,
                jax.ShapeDtypeStruct((batches, length, LANES), F32),
                jax.ShapeDtypeStruct((batches, 16, length), F32),
            ]
            + [jax.ShapeDtypeStruct((batches, capacity + 16, width), BF16)] * 4,
            compiler_params=params(56),
            cost_estimate=pl.CostEstimate(flops=20 * 10**9, bytes_accessed=20 * 10**6, transcendentals=10**7),
            name="forward",
        )(own_arr, tokens, segments[:, None], route_rows, prev_rows, route_map.T, small, attn, attn, attn, attn_o, cos, sin, pos)
        a_rows = to_plane(a_rows)

        a_rows = jnp.stack(a_rows)
        grad_rows = jnp.stack(grad_rows)

    tile = hidden // 4
    total = 4 * batches * capacity
    any_spec = pl.BlockSpec(memory_space=pl.ANY)
    values, input_rows, grad_gate_full, grad_up_full, grad_down_full = pl.pallas_call(
        expert_kernel,
        grid=(hidden // tile,),
        in_specs=[any_spec] * 2
        + [
            pl.BlockSpec((width, tile), lambda f: (0, f)),
            pl.BlockSpec((width, tile), lambda f: (0, f)),
            pl.BlockSpec((tile, width), lambda f: (f, 0)),
        ],
        out_specs=[any_spec] * 2
        + [
            pl.BlockSpec((width, tile), lambda f: (0, f)),
            pl.BlockSpec((width, tile), lambda f: (0, f)),
            pl.BlockSpec((tile, width), lambda f: (f, 0)),
        ],
        scratch_shapes=[
            pltpu.VMEM((total + capacity, width), BF16),
            pltpu.VMEM((total + capacity, width), BF16),
            pltpu.VMEM((4 * batches, 16, capacity), BF16),
            pltpu.VMEM((width, total), BF16),
            pltpu.VMEM((width, total), BF16),
            pltpu.SMEM((4 * batches + 1,), jnp.int32),
            pltpu.VMEM((total, width), F32),
            pltpu.VMEM((total, width), F32),
            pltpu.VMEM((width, tile), F32),
            pltpu.VMEM((width, tile), F32),
            pltpu.VMEM((width, tile), F32),
            pltpu.VMEM((total + capacity, LANES), F32),
            pltpu.SemaphoreType.DMA((12 * batches,)),
        ],
        out_shape=[
            jax.ShapeDtypeStruct((4, batches, capacity, width), BF16),
            jax.ShapeDtypeStruct((4, batches, capacity + 16, width), BF16),
        ]
        + [
            jax.ShapeDtypeStruct((width, hidden), BF16),
            jax.ShapeDtypeStruct((width, hidden), BF16),
            jax.ShapeDtypeStruct((hidden, width), BF16),
        ],
        compiler_params=params(60),
        cost_estimate=pl.CostEstimate(flops=58 * 10**9, bytes_accessed=40 * 10**6, transcendentals=10**7),
        name="expert",
    )(a_rows, grad_rows, gate_full, up_full, down_full)
    if fused:
        columns = 4 * width + 2 * LANES
        once = lambda shape: pl.BlockSpec(
            (1,) + shape, lambda b, *_: (b, 0, 0), pipeline_mode=pl.Buffered(1)
        )
        wide = ((rows_d, hidden), (rows_d, hidden), (rows_f, width))
        near = planes // 2
        parts = (hidden // 2, hidden // 2, width, columns - hidden - width)
        gin, sums, _, values_in, grad_gate, grad_up, grad_down = pl.pallas_call(
            functools.partial(fused_backward_kernel, group, rows_d),
            grid=(batches,),
            in_specs=[
                per_seq((kinds, length)),
                per_seq((16, length)),
                prev_spec,
                once((length, width)),
                once((length, width)),
                once((length, width)),
                once((length, width)),
                whole((batches, length)),
                once((length, width)),
                once((length, width)),
                once((length, width)),
                once((length, LANES)),
                whole((kinds + 8, width), 1),
                spec_w(0),
                spec_w(1),
                spec_w(2),
                spec_w(0),
                whole((length, LANES), 1),
                whole((length, LANES), 1),
            ]
            + [any_spec] * 5,
            out_specs=[once((length, width)), whole((rows_d, columns), 1)] + [any_spec] * 5,
            out_shape=[
                seq_f32,
                jax.ShapeDtypeStruct((rows_d, columns), F32),
                jax.ShapeDtypeStruct((4, batches, capacity + 16, width), BF16),
                jax.ShapeDtypeStruct((4, batches, capacity, width), BF16),
            ]
            + [jax.ShapeDtypeStruct((4,) + shape, BF16) for shape in wide],
            scratch_shapes=[
                pltpu.VMEM((width, 3 * width), F32),
                pltpu.VMEM((width, width), F32),
                pltpu.VMEM((width, LANES), BF16),
            ]
            + [[pltpu.VMEM((planes, 2, rows_d, part), BF16) for part in parts]]
            + [
                [[
                    pltpu.VMEM((near, 2, rows_d, part // 2), BF16),
                    pltpu.VMEM((near, rows_d, part), BF16),
                    pltpu.VMEM((near, rows_d, part // 2), BF16),
                    pltpu.VMEM((near, rows_d, part // 2), BF16),
                    pltpu.VMEM((planes - 1, rows_d, part // 2), BF16),
                    pltpu.VMEM((rows_d, part // 2), BF16),
                    pltpu.VMEM((rows_d, part // 2), BF16),
                ] for part in parts]
            ]
            + [
                pltpu.VMEM((LANES, length), F32),
                pltpu.VMEM((1, length, width), F32),
                pltpu.VMEM((1, length, width), BF16),
                pltpu.VMEM((16, width), F32),
                pltpu.VMEM((kinds, LANES), F32),
                pltpu.VMEM((8, width), F32),
                pltpu.VMEM((length, length), F32),
                pltpu.VMEM((LANES, length), F32),
                pltpu.VMEM((length, 3 * width), BF16),
                pltpu.VMEM((4, 1, capacity + 16, width), BF16),
            ]
            + [pltpu.VMEM((planes, 2) + shape, BF16) for shape in wide]
            + [pltpu.VMEM((planes, 2) + shape, BF16) for shape in wide]
            + [pltpu.VMEM((2,) + shape, BF16) for shape in wide]
            + [pltpu.VMEM((2, 2) + shape, BF16) for shape in wide]
            + [
                pltpu.SemaphoreType.DMA((5 * batches,)),
                pltpu.SemaphoreType.DMA((2, batches, 4)),
                pltpu.SemaphoreType.DMA((2, batches, 4)),
                pltpu.SemaphoreType.DMA((3, 2)),
                pltpu.SemaphoreType.DMA((3, 8)),
                pltpu.SemaphoreType.DMA((3, 8)),
                pltpu.SemaphoreType.REGULAR,
                pltpu.SemaphoreType.DMA((len(parts), 6)),
                pltpu.SemaphoreType.DMA((len(parts), 6)),
                pltpu.SemaphoreType.DMA((len(parts), planes - 1)),
                pltpu.SemaphoreType.DMA((len(parts), planes - 1)),
            ],
            compiler_params=pltpu.CompilerParams(
                vmem_limit_bytes=63 * 1024 * 1024,
                dimension_semantics=("arbitrary",),
                collective_id=3,
                has_side_effects=True,
            ),
            cost_estimate=pl.CostEstimate(flops=60 * 10**9, bytes_accessed=60 * 10**6, transcendentals=10**7),
            name="fused_backward",
        )(
            pos, aux, prev_rows, h1, grads, o, tokens, segments, q, k, v, lse, small,
            attn, attn, attn, attn_o, cos, sin, input_rows, values,
            grad_gate_full.reshape(planes, 2, 2, rows_d, hidden),
            grad_up_full.reshape(planes, 2, 2, rows_d, hidden),
            grad_down_full.reshape(planes, 2, 2, rows_f, width),
        )
        grad_gate = grad_gate.transpose(1, 0, 2).astype(F32)
        grad_up = grad_up.transpose(1, 0, 2).astype(F32)
        grad_down = grad_down.transpose(1, 0, 2).astype(F32)
    else:
        values_in = jnp.stack(to_plane([values[i] for i in range(4)]))
        def scatter_expert(full):
            keep = lax.dynamic_index_in_dim(full, core, axis=2, keepdims=False)
            send = lax.dynamic_index_in_dim(full, 1 - core, axis=2, keepdims=False)
            half = (keep.astype(F32) + lax.ppermute(send, "grp", core_flip).astype(F32)).astype(BF16)
            summed = lax.dynamic_index_in_dim(half, z, axis=0, keepdims=False).astype(F32)
            for k in range(1, planes):
                part = lax.dynamic_index_in_dim(half, (z + k) % planes, axis=0, keepdims=False)
                summed = summed + lax.ppermute(part, "grp", z_shift(k)).astype(F32)
            summed = summed.astype(BF16)
            mine = lax.dynamic_index_in_dim(summed, x, axis=0, keepdims=False)
            other = lax.dynamic_index_in_dim(summed, 1 - x, axis=0, keepdims=False)
            arrived = to_plane([mine, other, mine, other])

            def order(first):
                return lambda: tuple(arrived[first ^ e] for e in range(4))

            return lax.switch(own, [order(i) for i in range(4)])

        grad_gate_up = scatter_expert(
            jnp.stack(
                [
                    grad_gate_full.reshape(planes, 2, 2, rows_d, hidden),
                    grad_up_full.reshape(planes, 2, 2, rows_d, hidden),
                ],
                axis=3,
            )
        )
        grad_down = scatter_expert(grad_down_full.reshape(planes, 2, 2, rows_f, width))
        grad_gate = jnp.stack([part[0] for part in grad_gate_up], axis=1).astype(F32)
        grad_up = jnp.stack([part[1] for part in grad_gate_up], axis=1).astype(F32)
        grad_down = jnp.stack(grad_down, axis=1).astype(F32)

        dh1, dob, grad_wo, sgrad, grad_map = pl.pallas_call(
            combine_kernel,
            grid_spec=pltpu.PrefetchScalarGridSpec(
                num_scalar_prefetch=1,
                grid=(batches,),
                in_specs=[per_seq((capacity + 16, width))] * 4
                + [
                    per_seq((kinds, length)),
                    per_seq((16, length)),
                    prev_spec,
                    per_seq((length, width)),
                    per_seq((length, width)),
                    per_seq((length, width)),
                    whole((kinds + 8, width)),
                    spec_w(0),
                ],
                out_specs=[per_seq((length, width))] * 2
                + [whole((width, width)), whole((16, width)), whole((kinds, LANES))],
                scratch_shapes=[pltpu.VMEM((width, width), F32), pltpu.VMEM((LANES, length), F32)],
            ),
            out_shape=[
                seq_f32,
                seq_bf16,
                jax.ShapeDtypeStruct((width, width), BF16),
                jax.ShapeDtypeStruct((16, width), F32),
                jax.ShapeDtypeStruct((kinds, LANES), F32),
            ],
            compiler_params=params(56),
            cost_estimate=pl.CostEstimate(flops=12 * 10**9, bytes_accessed=20 * 10**6, transcendentals=10**5),
            name="combine",
        )(own_arr, *to_plane([input_rows[i] for i in range(4)]), pos, aux, prev_rows, h1, grads, o, small, attn_o)

        gin, grad_attn, gain_one = pl.pallas_call(
            backward_kernel,
            grid=(batches,),
            in_specs=[
                per_seq((length, width)),
                per_seq((1, length)),
                per_seq((length, width)),
                per_seq((length, width)),
                per_seq((length, width)),
                per_seq((length, width)),
                per_seq((length, LANES)),
                per_seq((length, width)),
                whole((kinds + 8, width)),
                spec_w(0),
                spec_w(1),
                spec_w(2),
                whole((length, LANES)),
                whole((length, LANES)),
            ],
            out_specs=[per_seq((length, width)), whole((width, 3 * width)), whole((8, width))],
            scratch_shapes=[
                pltpu.VMEM((length, length), F32),
                pltpu.VMEM((LANES, length), F32),
                pltpu.VMEM((length, 3 * width), BF16),
                pltpu.VMEM((width, 3 * width), F32),
            ],
            out_shape=[
                seq_f32,
                jax.ShapeDtypeStruct((width, 3 * width), BF16),
                jax.ShapeDtypeStruct((8, width), F32),
            ],
            compiler_params=params(56),
            cost_estimate=pl.CostEstimate(flops=30 * 10**9, bytes_accessed=20 * 10**6, transcendentals=10**7),
            name="backward",
        )(tokens, segments[:, None], q, k, v, dob, lse, dh1, small, attn, attn, attn, cos, sin)

    finish_specs = dict(
        num_scalar_prefetch=1,
        grid=(batches,),
    )
    finish_in = [
        pl.BlockSpec((4, 1, capacity, width), lambda b, *_: (0, b, 0, 0)),
        per_seq((kinds, length)),
        per_seq((16, length)),
        per_seq((length, width)),
        whole((kinds + 8, width)),
    ]
    finish_cost = pl.CostEstimate(flops=4 * 10**9, bytes_accessed=12 * 10**6, transcendentals=0)
    if fused:
        small_shapes = [(rows_d, width)] * 4 + [
            (kinds, rows_d), (4, rows_d), (2, rows_d), (1, rows_d), (1, rows_d), (kinds, kinds)
        ]
        result, gq, gk, gv, go, *small_sums = pl.pallas_call(
            finish_kernel,
            grid_spec=pltpu.PrefetchScalarGridSpec(
                in_specs=finish_in + [whole((rows_d, columns))],
                out_specs=[per_seq((length, width))] + [whole(shape) for shape in small_shapes],
                scratch_shapes=[pltpu.VMEM((LANES, length), F32), pltpu.VMEM((LANES, LANES), F32)],
                **finish_specs,
            ),
            out_shape=[seq_f32] + [jax.ShapeDtypeStruct(shape, F32) for shape in small_shapes],
            compiler_params=params(40),
            cost_estimate=finish_cost,
            name="finish",
        )(own_arr, values_in, pos, aux, h1, small, sums)
        grad_router, grad_proj, grad_vec, grad_one, grad_two, map_total = small_sums
        return (
            result.reshape(batches * length, width),
            gin.reshape(batches * length, width),
            grad_one[0],
            gq,
            gk,
            gv,
            go,
            grad_two[0],
            grad_router.T,
            map_total,
            grad_proj.T,
            grad_vec.T,
            grad_gate,
            grad_up,
            grad_down,
        )

    result = pl.pallas_call(
        result_kernel,
        grid_spec=pltpu.PrefetchScalarGridSpec(
            in_specs=finish_in,
            out_specs=per_seq((length, width)),
            scratch_shapes=[pltpu.VMEM((LANES, length), F32)],
            **finish_specs,
        ),
        out_shape=seq_f32,
        compiler_params=params(40),
        cost_estimate=finish_cost,
        name="result",
    )(own_arr, values_in, pos, aux, h1, small)

    part = lax.psum_scatter(jnp.concatenate([grad_attn, grad_wo], axis=1), "grp", scatter_dimension=0, tiled=True)
    attn_total = lax.psum(part, "rep").astype(F32)
    sgrad = jnp.where(iota((16, 1), 0) == kinds + 6, gain_one[0:1], sgrad)
    packed = jnp.concatenate([sgrad, jnp.pad(grad_map, ((0, 0), (0, width - LANES)))], axis=0)
    packed = lax.psum(packed, ("rep", "grp"))
    sums = lax.dynamic_slice_in_dim(packed[0:16], g * rows_d, rows_d, axis=1).T
    map_total = packed[16:, 0:kinds].T
    return (
        result.reshape(batches * length, width),
        gin.reshape(batches * length, width),
        sums[:, kinds + 6],
        attn_total[:, 0:width],
        attn_total[:, width : 2 * width],
        attn_total[:, 2 * width : 3 * width],
        attn_total[:, 3 * width :],
        sums[:, kinds + 7],
        sums[:, 0:kinds],
        map_total,
        sums[:, kinds : kinds + 4],
        sums[:, kinds + 4 : kinds + 6],
        grad_gate,
        grad_up,
        grad_down,
    )


def solution(mesh):
    rows = P(("rep", "grp"), None)
    in_specs = (
        (rows,) * 5
        + (P("grp"),)
        + (P("grp", None),) * 4
        + (P("grp"), P("grp", None), P(), P("grp", None), P("grp", None))
        + (P("grp", None, None),) * 3
    )
    out_specs = (
        (rows,) * 2
        + (P("grp"),)
        + (P("grp", None),) * 4
        + (P("grp"), P("grp", None), P(), P("grp", None), P("grp", None))
        + (P("grp", None, None),) * 3
    )
    body = functools.partial(local, mesh.shape["rep"], mesh.shape["grp"])
    return jax.shard_map(body, mesh=mesh, in_specs=in_specs, out_specs=out_specs, check_vma=False)
```

```python
import functools

import jax
import jax.numpy as jnp
import numpy as np
from jax import lax
from jax.experimental import pallas as pl
from jax.experimental.pallas import tpu as pltpu
from jax.sharding import PartitionSpec as P

HEAD_DIM = 64
BLOCK = 256
EPS = 1e-05
NEG = -1000000000.0
F32 = jnp.float32
BF16 = jnp.bfloat16
LANES = 128


def nn(a, b):
    return lax.dot_general(a, b, (((1,), (0,)), ((), ())), preferred_element_type=F32)


def nt(a, b):
    return lax.dot_general(a, b, (((1,), (1,)), ((), ())), preferred_element_type=F32)


def tn(a, b):
    return lax.dot_general(a, b, (((0,), (0,)), ((), ())), preferred_element_type=F32)


def iota(shape, dim):
    return lax.broadcasted_iota(jnp.int32, shape, dim)


def split2(values):
    high = values.astype(BF16)
    low = (values - high.astype(F32)).astype(BF16)
    return high, low


def whole(shape, buffers=None):
    zeros = (0,) * len(shape)
    if buffers:
        return pl.BlockSpec(shape, lambda *_: zeros, pipeline_mode=pl.Buffered(buffers))
    return pl.BlockSpec(shape, lambda *_: zeros)


def per_seq(shape):
    tail = (0,) * len(shape)
    return pl.BlockSpec((1,) + shape, lambda b, *_: (b,) + tail)


def same_document(segments):
    hot = jnp.where(segments == iota((16, segments.shape[1]), 0), 1.0, 0.0).astype(BF16)
    return tn(hot, hot) > 0.5


def rms_scale(values):
    return lax.rsqrt(jnp.mean(values * values, axis=-1, keepdims=True) + EPS)


def slot_mask(position_row, capacity):
    places = iota((capacity, position_row.shape[1]), 0).astype(F32)
    return jnp.where(places == position_row, 1.0, 0.0).astype(BF16)


def grad_rows_kernel(own_ref, routes_ref, grad_ref, r0, r1, r2, r3, pos_ref):
    own = own_ref[0]
    kinds, length = pos_ref.shape[1:]
    capacity = r0.shape[1]
    ids = iota((kinds, length), 0)
    first = routes_ref[0:1, :] == ids
    second = routes_ref[1:2, :] == ids
    hits = jnp.where(first | second, 1.0, 0.0)
    before = jnp.where(iota((length, length), 0) < iota((length, length), 1), 1.0, 0.0)
    slots = nn(hits.astype(BF16), before.astype(BF16))
    pos_ref[0] = jnp.where(hits > 0.0, slots, -1.0)
    for number, rows in enumerate((r0, r1, r2, r3)):
        line = pos_ref[0, pl.ds(own ^ number, 1), :]
        rows[0] = nn(slot_mask(line, capacity), grad_ref[0]).astype(BF16)


def swap_halves(values, low_half):
    return jnp.where(low_half, pltpu.roll(values, 96, 1), pltpu.roll(values, 32, 1))


def sequence_forward(
    x_ref,
    segments,
    routes,
    prev_ref,
    map_ref,
    small_ref,
    wq_ref,
    wk_ref,
    wv_ref,
    wo_ref,
    cos_ref,
    sin_ref,
    pos_ref,
    q_ref,
    k_ref,
    v_ref,
    o_ref,
    h_ref,
    lse_ref,
    aux_ref,
    rows_at,
    bias_ref,
    proj_ref,
    expert_of,
    between=None,
):
    length, width = x_ref.shape[1:]
    kinds = pos_ref.shape[1]
    capacity = length // 2
    tokens = x_ref[0].astype(F32)
    gain_one = small_ref[kinds + 6 : kinds + 7, :]
    gain_two = small_ref[kinds + 7 : kinds + 8, :]
    a1 = (tokens * rms_scale(tokens) * gain_one).astype(BF16)
    lane = iota((1, LANES), 1)
    low_half = (lane % HEAD_DIM) < (HEAD_DIM // 2)
    first_head = lane < HEAD_DIM
    mask_a = jnp.where(first_head, 1.0, 0.0).astype(BF16)
    mask_b = jnp.where(first_head, 0.0, 1.0).astype(BF16)
    pairs = width // LANES

    for weights, target, scale in ((wq_ref, q_ref, 0.125), (wk_ref, k_ref, 1.0)):
        proj_ref[...] = nn(a1, weights[...])

        def turn(h, carry):
            cols = pl.ds(pl.multiple_of(h * LANES, LANES), LANES)
            part = proj_ref[:, cols]
            turned = part * cos_ref[...] + swap_halves(part, low_half) * sin_ref[...]
            target[0, :, cols] = turned.astype(BF16) * jnp.asarray(scale, BF16)
            return carry

        lax.fori_loop(0, pairs, turn, 0)
    v_ref[0] = nn(a1, wv_ref[...]).astype(BF16)

    allowed = same_document(segments) & (
        iota((length, length), 1) // BLOCK <= iota((length, length), 0) // BLOCK
    )
    bias_ref[...] = jnp.where(allowed, 0.0, NEG)
    lse_ref[...] = jnp.zeros_like(lse_ref)
    if between is not None:
        between()

    def pair(h, carry):
        cols = pl.ds(pl.multiple_of(h * LANES, LANES), LANES)
        for begin in range(0, length, BLOCK):
            end = begin + BLOCK
            queries = q_ref[0, begin:end, cols]
            keys = k_ref[0, 0:end, cols]
            values = v_ref[0, 0:end, cols]
            bias = bias_ref[begin:end, 0:end]
            sums = lse_ref[0, begin:end, :]
            outs = []
            for half, mask in enumerate((mask_a, mask_b)):
                scores = nt(queries * mask, keys) + bias
                top = jnp.max(scores, axis=-1, keepdims=True)
                grown = jnp.exp(scores - top)
                total = jnp.sum(grown, axis=-1, keepdims=True)
                chances = (grown * (1.0 / total)).astype(BF16)
                outs.append(nn(chances, values))
                sums = jnp.where(lane == 2 * h + half, top + jnp.log(total), sums)
            lse_ref[0, begin:end, :] = sums
            o_ref[0, begin:end, cols] = jnp.where(first_head, outs[0], outs[1]).astype(BF16)
        return carry

    lax.fori_loop(0, pairs, pair, 0)

    hidden = tokens + nn(o_ref[0], wo_ref[...])
    h_ref[0] = hidden
    a2 = (hidden * rms_scale(hidden) * gain_two).astype(BF16)
    logits = nt(small_ref[...].astype(BF16), a2)[0:kinds, :]
    for j in range(kinds):
        logits = logits + map_ref[:, j : j + 1] * prev_ref[j : j + 1, :]
    ids = iota((kinds, length), 0)
    first = jnp.where(routes[0:1, :] == ids, 1.0, 0.0)
    second = jnp.where(routes[1:2, :] == ids, 1.0, 0.0)
    one = jnp.sum(logits * first, axis=0, keepdims=True)
    two = jnp.sum(logits * second, axis=0, keepdims=True)
    top = jnp.maximum(one, two)
    grown_one, grown_two = jnp.exp(one - top), jnp.exp(two - top)
    gate_one = grown_one / (grown_one + grown_two)
    gate_two = grown_two / (grown_one + grown_two)
    aux_ref[0, 0:kinds, :] = gate_one * first + gate_two * second
    aux_ref[0, kinds : kinds + 1, :] = gate_one
    aux_ref[0, kinds + 1 : kinds + 2, :] = gate_two
    aux_ref[0, kinds + 2 : kinds + 4, :] = routes.astype(F32)
    aux_ref[0, kinds + 4 :, :] = jnp.zeros((aux_ref.shape[1] - kinds - 4, length), F32)

    place = iota((16, length), 0)

    def send_rows(number, carry):
        rows = rows_at(number)
        mask = slot_mask(pos_ref[0, pl.ds(expert_of(number), 1), :], capacity)
        rows[0, 0:capacity, :] = nn(mask, a2).astype(BF16)
        line = aux_ref[0, pl.ds(expert_of(number), 1), :]
        high = line.astype(BF16).astype(F32)
        mid = (line - high).astype(BF16).astype(F32)
        low = line - high - mid
        parts = jnp.where(place == 0, high, jnp.where(place == 1, mid, jnp.where(place == 2, low, 0.0)))
        spread = nt(parts.astype(BF16), mask)
        filled = jnp.max(pos_ref[0, pl.ds(expert_of(number), 1), :], axis=1, keepdims=True) + 1.0
        spread = jnp.where(iota((16, 1), 0) == 3, filled, spread)
        rows[0, capacity:, 0:capacity] = spread.astype(BF16)
        rows[0, capacity:, capacity:] = jnp.zeros((16, width - capacity), BF16)
        return carry

    lax.fori_loop(0, 4, send_rows, 0)


def forward_kernel(
    own_ref,
    x_ref,
    seg_ref,
    routes_ref,
    prev_ref,
    map_ref,
    small_ref,
    wq_ref,
    wk_ref,
    wv_ref,
    wo_ref,
    cos_ref,
    sin_ref,
    pos_ref,
    q_ref,
    k_ref,
    v_ref,
    o_ref,
    h_ref,
    lse_ref,
    aux_ref,
    rows_ref,
    bias_ref,
    proj_ref,
):
    own = own_ref[0]
    sequence_forward(
        x_ref,
        seg_ref[0],
        routes_ref[...],
        prev_ref,
        map_ref,
        small_ref,
        wq_ref,
        wk_ref,
        wv_ref,
        wo_ref,
        cos_ref,
        sin_ref,
        pos_ref,
        q_ref,
        k_ref,
        v_ref,
        o_ref,
        h_ref,
        lse_ref,
        aux_ref,
        lambda number: rows_ref.at[number],
        bias_ref,
        proj_ref,
        lambda number: own ^ number,
    )


MESH = pl.DeviceIdType.MESH


class Place:
    def __init__(self, group):
        self.group = group
        self.planes = group // 4
        self.g = lax.axis_index("grp")
        self.y = lax.axis_index("rep")
        self.core = self.g % 2
        self.x = (self.g // 2) % 2
        self.z = self.g // 4
        self.core_peer = (self.y, self.g + 1 - 2 * self.core)
        self.x_peer = (self.y, self.g + 2 - 4 * self.x)
        self.y_peer = (1 - self.y, self.g)
        self.xy_peer = (1 - self.y, self.g + 2 - 4 * self.x)
        self.plane_peers = (None, self.x_peer, self.y_peer, self.xy_peer)

    def z_peer(self, k):
        return (self.y, (self.g + 4 * k) % self.group)

    def block(self, z, x, core):
        return (z * 2 + x) * 2 + core

    def expert(self, number):
        return 2 * ((self.y + number // 2) % 2) + (self.x + number % 2) % 2

    def barrier(self, peers):
        semaphore = pltpu.get_barrier_semaphore()
        for peer in peers:
            pl.semaphore_signal(semaphore, inc=1, device_id=peer, device_id_type=MESH)
        pl.semaphore_wait(semaphore, len(peers))


def remote(src, dst, send, recv, peer):
    return pltpu.make_async_remote_copy(
        src_ref=src, dst_ref=dst, send_sem=send, recv_sem=recv, device_id=peer, device_id_type=MESH
    )


def fused_forward_kernel(
    group,
    x_ref,
    seg_ref,
    routes_ref,
    prev_ref,
    map_ref,
    grad_ref,
    coarse_ref,
    fine_ref,
    shard_refs,
    small_refs,
    gate4_ref,
    up4_ref,
    down4_ref,
    q_ref,
    k_ref,
    v_ref,
    o_ref,
    h_ref,
    lse_ref,
    aux_ref,
    pos_ref,
    small_ref,
    cos_ref,
    sin_ref,
    attn_out_ref,
    attn_o_out_ref,
    rows_in_ref,
    grads_in_ref,
    gate_full_ref,
    up_full_ref,
    down_full_ref,
    attn_ref,
    attn_o_ref,
    bias_ref,
    proj_ref,
    rows_ref,
    grows_ref,
    tile_ref,
    map_t_ref,
    attn_send,
    attn_recv,
    ffn_local,
    ffn_send,
    ffn_recv,
    out_sem,
    row_local,
    row_send,
    row_recv,
):
    step = pl.program_id(0)
    last = pl.num_programs(0) - 1
    here = Place(group)
    planes = here.planes
    batches, kinds, length = pos_ref.shape
    width = x_ref.shape[2]
    capacity = length // 2
    shards = (attn_ref, attn_o_ref)
    experts = ((gate4_ref, gate_full_ref), (up4_ref, up_full_ref), (down4_ref, down_full_ref))
    depth = shard_refs[0].shape[0]
    mine = here.block(here.z, here.x, here.core)

    def rows_of(block):
        return pl.ds(pl.multiple_of(block * depth, 16), depth)

    def attn_part(t, block, part):
        full = shards[t]
        half = full.shape[1] // 2
        if part is None:
            return full.at[rows_of(block), :]
        return full.at[rows_of(block), pl.ds(pl.multiple_of(part * half, LANES), half)]

    def attn_copy(t, slot, z, x, part, peer):
        ref = attn_part(t, here.block(z, x, here.core), part)
        return remote(ref, ref, attn_send.at[t, slot], attn_recv.at[t, slot], peer)

    def to_z(t, k):
        return attn_copy(t, k, here.z, here.x, None, here.z_peer(1 if k == 0 else planes - 1))

    def from_z(t, k):
        return attn_copy(t, k, z_at(planes - 1 if k == 0 else 1), here.x, None, here.x_peer)

    def pass_z(t, k):
        z = z_at(planes - 1 if k == 0 else 1)
        return attn_copy(t, 2 + k, z, here.x, k, here.z_peer(1 if k == 0 else planes - 1))

    def passed_z(t, k):
        return attn_copy(t, 2 + k, z_at(2), here.x, k, here.x_peer)

    def to_x(t, step_z):
        return attn_copy(t, 4 + step_z, z_at(step_z), here.x, here.y, here.x_peer)

    def from_x(t, step_z):
        return attn_copy(t, 4 + step_z, z_at(step_z), 1 - here.x, here.y, here.x_peer)

    def to_y(t, step_z):
        return attn_copy(t, 4 + planes + step_z, z_at(step_z), 1 - here.x, here.y, here.y_peer)

    def from_y(t, step_z):
        return attn_copy(t, 4 + planes + step_z, z_at(step_z), 1 - here.x, 1 - here.y, here.y_peer)

    def to_core(t, step_z, x):
        return attn_copy(t, 4 + 2 * planes + 2 * step_z + x, z_at(step_z), here.x if x == 0 else 1 - here.x, None, here.core_peer)

    def from_core(t, step_z, x):
        ref = attn_part(t, here.block(z_at(step_z), here.x if x == 0 else 1 - here.x, 1 - here.core), None)
        slot = 4 + 2 * planes + 2 * step_z + x
        return remote(ref, ref, attn_send.at[t, slot], attn_recv.at[t, slot], here.core_peer)

    def z_at(k):
        return (here.z + k) % planes

    def ffn_to_x(j):
        source, full = experts[j]
        return remote(
            source.at[here.expert(1)],
            full.at[here.z, here.x, here.core],
            ffn_send.at[j, 0],
            ffn_recv.at[j, 0],
            here.x_peer,
        )

    def ffn_from_x(j):
        source, full = experts[j]
        return remote(
            source.at[here.expert(1)],
            full.at[here.z, 1 - here.x, here.core],
            ffn_send.at[j, 0],
            ffn_recv.at[j, 0],
            here.x_peer,
        )

    def ffn_mine(j):
        source, full = experts[j]
        return pltpu.make_async_copy(source.at[here.expert(0)], full.at[here.z, here.x, here.core], ffn_local.at[j])

    def ffn_copy(j, slot, z, x, core, peer):
        full = experts[j][1]
        part = full.at[z, :, core] if x is None else full.at[z, x, core]
        return remote(part, part, ffn_send.at[j, slot], ffn_recv.at[j, slot], peer)

    def ffn_to_z(j, k):
        return ffn_copy(j, 1 + k, here.z, None, here.core, here.z_peer(1 if k == 0 else planes - 1))

    def ffn_from_z(j, k):
        return ffn_copy(j, 1 + k, z_at(planes - 1 if k == 0 else 1), None, here.core, here.x_peer)

    def ffn_pass_z(j, k):
        z = z_at(planes - 1 if k == 0 else 1)
        return ffn_copy(j, 3 + k, z, k, here.core, here.z_peer(1 if k == 0 else planes - 1))

    def ffn_passed_z(j, k):
        return ffn_copy(j, 3 + k, z_at(2), k, here.core, here.x_peer)

    def ffn_to_core(j, step_z):
        return ffn_copy(j, 5 + step_z, z_at(step_z), None, here.core, here.core_peer)

    def ffn_from_core(j, step_z):
        return ffn_copy(j, 5 + step_z, z_at(step_z), None, 1 - here.core, here.core_peer)

    def row_copy(kind, member, number):
        source, target = ((grows_ref, grads_in_ref), (rows_ref, rows_in_ref))[kind]
        src, dst = source.at[member, number], target.at[number, member]
        if number == 0:
            return pltpu.make_async_copy(src, dst, row_local.at[kind, member])
        return remote(
            src,
            dst,
            row_send.at[kind, member, number],
            row_recv.at[kind, member, number],
            here.plane_peers[number],
        )

    def outs(t):
        full, target = ((attn_ref, attn_out_ref), (attn_o_ref, attn_o_out_ref))[t]
        return pltpu.make_async_copy(full, target, out_sem.at[t])

    @pl.when(step == 0)
    def _():
        for j in range(3):
            ffn_mine(j).start()
        for part in range(3):
            attn_ref[rows_of(mine), part * width : (part + 1) * width] = shard_refs[part][...].astype(BF16)
        attn_o_ref[rows_of(mine), :] = shard_refs[3][...].astype(BF16)
        tile_ref[...] = jnp.zeros_like(tile_ref)
        at = 0
        for part in small_refs:
            tile_ref[at : at + part.shape[0], 0:depth] = part[...]
            at += part.shape[0]
        tile_ref[at : at + kinds, 0:kinds] = map_ref[...]
        turned = jnp.transpose(tile_ref[...])
        map_t_ref[...] = pltpu.roll(turned[0:kinds, :], LANES - kinds - 8, 1)
        attn_ref[rows_of(mine), 3 * width : 3 * width + LANES] = turned[0:depth, :].astype(BF16)
        attn_ref[rows_of(mine), 3 * width + LANES :] = jnp.zeros((depth, LANES), BF16)
        here.barrier(
            [here.core_peer, here.x_peer, here.y_peer, here.xy_peer, here.z_peer(1), here.z_peer(planes - 1)]
        )
        for t in range(2):
            to_z(t, 0).start()
            to_z(t, 1).start()
            to_x(t, 0).start()
            to_core(t, 0, 0).start()
        for j in range(3):
            ffn_to_x(j).start()

        ids = iota((kinds, length), 0)
        before = jnp.where(iota((length, length), 0) < iota((length, length), 1), 1.0, 0.0).astype(BF16)
        for member in range(batches):
            first = routes_ref[0:1, member * length : (member + 1) * length] == ids
            second = routes_ref[1:2, member * length : (member + 1) * length] == ids
            hits = jnp.where(first | second, 1.0, 0.0)
            pos_ref[member] = jnp.where(hits > 0.0, nn(hits.astype(BF16), before), -1.0)

        def grad_rows(index, carry):
            member, number = index // 4, index % 4
            line = pos_ref[member, pl.ds(here.expert(number), 1), :]
            grows_ref[member, number] = nn(slot_mask(line, capacity), grad_ref[member]).astype(BF16)
            return carry

        lax.fori_loop(0, 4 * batches, grad_rows, 0)
        for member in range(batches):
            row_copy(0, member, 0).start()
            row_copy(0, member, 2).start()

        for high in range(coarse_ref.shape[1]):
            rows = slice(high * fine_ref.shape[1], (high + 1) * fine_ref.shape[1])
            cos_high, sin_high = coarse_ref[0, high : high + 1, :], coarse_ref[1, high : high + 1, :]
            cos_ref[rows, :] = cos_high * fine_ref[0] - sin_high * fine_ref[1]
            sin_ref[rows, :] = (sin_high * fine_ref[0] + cos_high * fine_ref[1]) * fine_ref[2]

        for t in range(2):
            for k, step_z in enumerate((planes - 1, 1)):
                from_z(t, k).wait_recv()
                pass_z(t, k).start()
                to_x(t, step_z).start()
                to_core(t, step_z, 0).start()
        for t in range(2):
            from_x(t, 0).wait_recv()
            to_y(t, 0).start()
        for j in range(3):
            ffn_mine(j).wait()
            ffn_from_x(j).wait_recv()
            ffn_to_z(j, 0).start()
            ffn_to_z(j, 1).start()
            ffn_to_core(j, 0).start()
        for t in range(2):
            passed_z(t, 0).wait_recv()
            passed_z(t, 1).wait_recv()
            to_x(t, 2).start()
            to_core(t, 2, 0).start()
        for member in range(batches):
            row_copy(0, member, 1).start()
            row_copy(0, member, 3).start()
        for t in range(2):
            for step_z in (planes - 1, 1, 2):
                from_x(t, step_z).wait_recv()
                to_y(t, step_z).start()
        for t in range(2):
            for step_z in (0, planes - 1, 1, 2):
                from_y(t, step_z).wait_recv()
                to_core(t, step_z, 1).start()
        for t in range(2):
            for step_z in range(planes):
                for x in range(2):
                    from_core(t, step_z, x).wait_recv()
        for t in range(2):
            outs(t).start()
        small_ref[...] = jnp.transpose(attn_ref[:, 3 * width : 3 * width + LANES].astype(F32))[0 : kinds + 8, :]

    def between():
        @pl.when(step == last)
        def _():
            for j in range(3):
                for k, step_z in enumerate((planes - 1, 1)):
                    ffn_from_z(j, k).wait_recv()
                    ffn_pass_z(j, k).start()
                    ffn_to_core(j, step_z).start()

    sequence_forward(
        x_ref,
        seg_ref[pl.ds(step, 1), :],
        routes_ref[:, pl.ds(pl.multiple_of(step * length, LANES), length)],
        prev_ref,
        map_t_ref,
        small_ref,
        attn_ref.at[:, 0:width],
        attn_ref.at[:, width : 2 * width],
        attn_ref.at[:, 2 * width : 3 * width],
        attn_o_ref,
        cos_ref,
        sin_ref,
        pos_ref.at[pl.ds(step, 1)],
        q_ref,
        k_ref,
        v_ref,
        o_ref,
        h_ref,
        lse_ref,
        aux_ref,
        lambda number: rows_ref.at[pl.ds(step, 1), number],
        bias_ref,
        proj_ref,
        here.expert,
        between,
    )
    for member in range(batches):

        @pl.when(step == member)
        def _():
            for number in range(4):
                row_copy(1, member, number).start()

    @pl.when(step == last)
    def _():
        for j in range(3):
            for k in range(2):
                ffn_passed_z(j, k).wait_recv()
            ffn_to_core(j, 2).start()
        for t in range(2):
            outs(t).wait()
            for k in range(2):
                to_z(t, k).wait_send()
                pass_z(t, k).wait_send()
            for step_z in range(planes):
                to_x(t, step_z).wait_send()
                to_y(t, step_z).wait_send()
                for x in range(2):
                    to_core(t, step_z, x).wait_send()
        for j in range(3):
            ffn_to_x(j).wait_send()
            for k in range(2):
                ffn_to_z(j, k).wait_send()
                ffn_pass_z(j, k).wait_send()
            for step_z in range(planes):
                ffn_to_core(j, step_z).wait_send()
                ffn_from_core(j, step_z).wait_recv()
        for kind in range(2):
            for member in range(batches):
                for number in range(4):
                    copy = row_copy(kind, member, number)
                    copy.wait()


def expert_kernel(
    a_ref,
    g_ref,
    gate_ref,
    up_ref,
    down_ref,
    v_ref,
    d_ref,
    grad_gate_ref,
    grad_up_ref,
    grad_down_ref,
    rows_ref,
    grads_ref,
    gates_ref,
    rows_t_ref,
    grads_t_ref,
    places_ref,
    acc_value_ref,
    acc_input_ref,
    acc_gate_ref,
    acc_up_ref,
    acc_down_ref,
    share_ref,
    sems,
):
    step = pl.program_id(0)
    last = pl.num_programs(0) - 1
    batches, capacity, width = g_ref.shape[1:]
    blocks = 4 * batches

    @pl.when(step == 0)
    def _():
        copies = []
        for number in range(4):
            rows, grads = a_ref.at[number], g_ref.at[number]
            for member in range(batches):
                block = number * batches + member
                span = pl.ds(block * capacity, capacity)
                copies.append(
                    pltpu.make_async_copy(
                        rows.at[member, pl.ds(capacity, 16), pl.ds(0, capacity)],
                        gates_ref.at[block],
                        sems.at[3 * block],
                    )
                )
                copies.append(
                    pltpu.make_async_copy(
                        rows.at[member, pl.ds(0, capacity), :], rows_ref.at[span, :], sems.at[3 * block + 1]
                    )
                )
                copies.append(
                    pltpu.make_async_copy(grads.at[member], grads_ref.at[span, :], sems.at[3 * block + 2])
                )
        for copy in copies:
            copy.start()
        for copy in copies:
            copy.wait()
        same = iota((capacity, capacity), 0) == iota((capacity, capacity), 1)
        spare = jnp.zeros((capacity, width), BF16)
        rows_ref[blocks * capacity :, :] = spare
        grads_ref[blocks * capacity :, :] = spare
        share_ref[...] = jnp.zeros_like(share_ref)

        def pack(block, place):
            span = pl.ds(pl.multiple_of(block * capacity, capacity), capacity)
            target = pl.ds(pl.multiple_of(place, 16), capacity)
            parts = gates_ref[block].astype(F32)
            count = jnp.max(parts[3:4, :]).astype(jnp.int32)
            line = jnp.sum(parts[0:3, :], axis=0, keepdims=True)
            column = jnp.sum(jnp.where(same, line, 0.0), axis=1, keepdims=True)
            rows = rows_ref[span, :]
            grads = (grads_ref[span, :].astype(F32) * column).astype(BF16)
            rows_ref[target, :] = rows
            grads_ref[target, :] = grads
            places_ref[block] = place
            return place + (count + 15) // 16 * 16

        total = lax.fori_loop(0, blocks, pack, 0)
        target = pl.ds(pl.multiple_of(total, 16), capacity)
        rows_ref[target, :] = spare
        grads_ref[target, :] = spare
        places_ref[blocks] = (total + capacity - 1) // capacity

        def turn(block, carry):
            span = pl.ds(pl.multiple_of(block * capacity, capacity), capacity)
            grads_t_ref[:, span] = jnp.transpose(grads_ref[span, :])
            rows_t_ref[:, span] = jnp.transpose(rows_ref[span, :])
            return carry

        lax.fori_loop(0, places_ref[blocks], turn, 0)

    acc_gate_ref[...] = jnp.zeros_like(acc_gate_ref)
    acc_up_ref[...] = jnp.zeros_like(acc_up_ref)
    acc_down_ref[...] = jnp.zeros_like(acc_down_ref)

    def work(block, carry):
        span = pl.ds(pl.multiple_of(block * capacity, capacity), capacity)
        rows = rows_ref[span, :]
        grads = grads_ref[span, :]
        gate = nn(rows, gate_ref[...])
        up = nn(rows, up_ref[...])
        back = nt(grads, down_ref[...])
        sig = 1.0 / (1.0 + jnp.exp(-gate))
        silu = gate * sig
        act = (silu * up).astype(BF16)
        grad_gate = (back * up * (sig * (1.0 + gate * (1.0 - sig)))).astype(BF16)
        grad_up = (back * silu).astype(BF16)
        value = nn(act, down_ref[...])
        grad_rows = nt(grad_gate, gate_ref[...]) + nt(grad_up, up_ref[...])
        rows_t = rows_t_ref[:, span]
        acc_gate_ref[...] += nn(rows_t, grad_gate)
        acc_up_ref[...] += nn(rows_t, grad_up)
        acc_down_ref[...] += nn(grads_t_ref[:, span], act)
        share = jnp.broadcast_to(
            jnp.sum(act.astype(F32) * back, axis=1, keepdims=True), (capacity, LANES)
        )

        @pl.when(step == 0)
        def _():
            share_ref[span, :] = share
            acc_value_ref[span, :] = value
            acc_input_ref[span, :] = grad_rows

        @pl.when(step > 0)
        def _():
            share_ref[span, :] += share

        @pl.when((step > 0) & (step < last))
        def _():
            acc_value_ref[span, :] += value
            acc_input_ref[span, :] += grad_rows

        @pl.when(step == last)
        def _():
            rows_ref[span, :] = (acc_value_ref[span, :] + value).astype(BF16)
            grads_ref[span, :] = (acc_input_ref[span, :] + grad_rows).astype(BF16)

        return carry

    lax.fori_loop(0, places_ref[blocks], work, 0)
    grad_gate_ref[...] = acc_gate_ref[...].astype(BF16)
    grad_up_ref[...] = acc_up_ref[...].astype(BF16)
    grad_down_ref[...] = jnp.transpose(acc_down_ref[...].astype(BF16))

    @pl.when(step == last)
    def _():
        same = iota((capacity, capacity), 0) == iota((capacity, capacity), 1)
        place = iota((16, capacity), 0)

        def shares(block, carry):
            column = share_ref[pl.ds(pl.multiple_of(places_ref[block], 16), capacity), 0:1]
            line = jnp.sum(jnp.where(same, column, 0.0), axis=0, keepdims=True)
            high = line.astype(BF16).astype(F32)
            mid = (line - high).astype(BF16).astype(F32)
            low = line - high - mid
            parts = jnp.where(place == 0, high, jnp.where(place == 1, mid, jnp.where(place == 2, low, 0.0)))
            gates_ref[block] = parts.astype(BF16)
            return carry

        lax.fori_loop(0, blocks, shares, 0)
        copies = []
        for number in range(4):
            values, grads = v_ref.at[number], d_ref.at[number]
            for member in range(batches):
                block = number * batches + member
                span = pl.ds(pl.multiple_of(places_ref[block], 16), capacity)
                copies.append(pltpu.make_async_copy(rows_ref.at[span, :], values.at[member], sems.at[3 * block]))
                copies.append(
                    pltpu.make_async_copy(
                        grads_ref.at[span, :], grads.at[member, pl.ds(0, capacity), :], sems.at[3 * block + 1]
                    )
                )
                copies.append(
                    pltpu.make_async_copy(
                        gates_ref.at[block],
                        grads.at[member, pl.ds(capacity, 16), pl.ds(0, capacity)],
                        sems.at[3 * block + 2],
                    )
                )
        for copy in copies:
            copy.start()
        for copy in copies:
            copy.wait()


def constant_mix(zs, index):
    za, zb = zs[:, index : index + 1], zs[:, index + 1 : index + 2]
    top = jnp.maximum(za, zb)
    ea, eb = jnp.exp(za - top), jnp.exp(zb - top)
    return ea / (ea + eb), eb / (ea + eb)


def token_columns(pos_ref, aux_ref, cols_ref):
    kinds, length = pos_ref.shape[1:]
    cols_ref[0:kinds, :] = pos_ref[0]
    cols_ref[kinds : kinds + 16, :] = aux_ref[0]
    cols_ref[kinds + 16 :, :] = jnp.zeros((LANES - kinds - 16, length), F32)
    return jnp.transpose(cols_ref[...])


def column(source, index):
    return jnp.sum(jnp.where(iota((1, LANES), 1) == index, source, 0.0), axis=1, keepdims=True)


def result_kernel(own_ref, v_ref, pos_ref, aux_ref, h_ref, small_ref, out_ref, cols_ref):
    block_output(own_ref, v_ref, pos_ref, aux_ref, h_ref, small_ref, out_ref, cols_ref)


def finish_kernel(
    own_ref,
    v_ref,
    pos_ref,
    aux_ref,
    h_ref,
    small_ref,
    sums_ref,
    out_ref,
    gq_ref,
    gk_ref,
    gv_ref,
    go_ref,
    router_ref,
    proj_ref,
    vec_ref,
    gain_one_ref,
    gain_two_ref,
    map_ref,
    cols_ref,
    tile_ref,
):
    @pl.when(pl.program_id(0) == 0)
    def _():
        depth, width = gq_ref.shape
        kinds = pos_ref.shape[1]
        for part, ref in enumerate((gq_ref, gk_ref, gv_ref, go_ref)):
            ref[...] = sums_ref[:, part * width : (part + 1) * width]
        small = sums_ref[:, 4 * width : 4 * width + LANES]
        tile_ref[...] = jnp.zeros_like(tile_ref)
        tile_ref[0:depth, :] = small
        turned = jnp.transpose(tile_ref[...])
        at = 0
        for ref in (router_ref, proj_ref, vec_ref, gain_one_ref, gain_two_ref):
            ref[...] = turned[at : at + ref.shape[0], 0:depth]
            at += ref.shape[0]
        map_ref[...] = pltpu.roll(small[0:kinds, :], LANES - kinds - 8, 1)[:, 0:kinds]

    block_output(own_ref, v_ref, pos_ref, aux_ref, h_ref, small_ref, out_ref, cols_ref)


def block_output(own_ref, v_ref, pos_ref, aux_ref, h_ref, small_ref, out_ref, cols_ref):
    own = own_ref[0]
    length, width = h_ref.shape[1:]
    kinds = pos_ref.shape[1]
    ffn = kinds - 4
    capacity = v_ref.shape[2]
    hidden = h_ref[0]
    n2 = hidden * rms_scale(hidden) * small_ref[kinds + 7 : kinds + 8, :]
    n2_high, n2_low = split2(n2)
    small = small_ref[...].astype(BF16)
    cols = token_columns(pos_ref, aux_ref, cols_ref)
    out_ref[0] = hidden
    slot_lane = iota((1, capacity), 1).astype(F32)

    def take(number, carry):
        expert = own ^ number
        mask = jnp.where(column(cols, expert) == slot_lane, 1.0, 0.0).astype(BF16)
        out_ref[0] += column(cols, kinds + expert) * nn(mask, v_ref[number, 0])
        return carry

    lax.fori_loop(0, 4, take, 0)
    result = out_ref[0]
    mixes = nt(n2_high, small) + nt(n2_low, small)
    share = column(cols, kinds + ffn + 1)
    for constant in range(2):
        weight = column(cols, kinds + ffn + 2 + constant)
        alpha_a, alpha_b = constant_mix(mixes, kinds + 2 * constant)
        result = result + (weight * alpha_b) * small_ref[kinds + 4 + constant : kinds + 5 + constant, :]
        share = share + weight * alpha_a
    out_ref[0] = result + share * n2


def sequence_combine(
    step,
    d_ref,
    pos_ref,
    aux_ref,
    prev_ref,
    h_ref,
    g_ref,
    o_ref,
    small_ref,
    wo_ref,
    dh_ref,
    dob_ref,
    sgrad_ref,
    grad_map_ref,
    acc_ref,
    cols_ref,
    expert_of,
):
    length, width = h_ref.shape[1:]
    kinds = pos_ref.shape[1]
    ffn = kinds - 4
    capacity = d_ref.shape[2] - 16
    hidden = h_ref[0]
    inverse = rms_scale(hidden)
    gain = small_ref[kinds + 7 : kinds + 8, :]
    n2 = hidden * inverse * gain
    n2_high, n2_low = split2(n2)
    grad_low = g_ref[0]
    grad = grad_low.astype(F32)
    small = small_ref[...].astype(BF16)
    cols = token_columns(pos_ref, aux_ref, cols_ref)
    lane = iota((1, LANES), 1)
    gate_one = column(cols, 2 * kinds)
    gate_two = column(cols, 2 * kinds + 1)
    ids = lane.astype(F32)
    hot_one = jnp.where(column(cols, 2 * kinds + 2) == ids, 1.0, 0.0)
    hot_two = jnp.where(column(cols, 2 * kinds + 3) == ids, 1.0, 0.0)

    dh_ref[0] = jnp.zeros((length, width), F32)
    slot_lane = iota((1, capacity), 1).astype(F32)

    def take(number, shares):
        expert = expert_of(number)
        mask = jnp.where(column(cols, expert) == slot_lane, 1.0, 0.0).astype(BF16)
        dh_ref[0] += nn(mask, d_ref[number, 0, 0:capacity, :])
        parts = nt(mask, d_ref[number, 0, capacity:, 0:capacity])
        return jnp.where(lane == expert, jnp.sum(parts, axis=1, keepdims=True), shares)

    shares = lax.fori_loop(0, 4, take, jnp.zeros((length, LANES), F32))
    grad_n2 = dh_ref[0]

    mixes = nt(n2_high, small) + nt(n2_low, small)
    inner = nt(grad_low, small)
    with_n2 = jnp.sum(grad * n2, axis=1, keepdims=True)
    weight_copy = column(cols, kinds + ffn + 1)
    shares = jnp.where(lane == ffn + 1, weight_copy * with_n2, shares)
    share = weight_copy
    coefs = jnp.zeros((length, LANES), F32)
    for constant in range(2):
        weight = column(cols, kinds + ffn + 2 + constant)
        alpha_a, alpha_b = constant_mix(mixes, kinds + 2 * constant)
        with_vec = inner[:, kinds + 4 + constant : kinds + 5 + constant]
        share = share + weight * alpha_a
        da = weight * with_n2
        db = weight * with_vec
        mean = alpha_a * da + alpha_b * db
        shares = jnp.where(lane == ffn + 2 + constant, mean, shares)
        coefs = jnp.where(lane == kinds + 2 * constant, alpha_a * (da - mean), coefs)
        coefs = jnp.where(lane == kinds + 2 * constant + 1, alpha_b * (db - mean), coefs)
        coefs = jnp.where(lane == kinds + 4 + constant, weight * alpha_b, coefs)

    share_one = jnp.sum(shares * hot_one, axis=1, keepdims=True)
    share_two = jnp.sum(shares * hot_two, axis=1, keepdims=True)
    both = share_one + share_two
    dlogits = (share_one - gate_one * both) * hot_one + (share_two - gate_two * both) * hot_two
    coefs = jnp.where(lane < kinds, dlogits, coefs)
    back = jnp.where(lane < kinds + 4, coefs, 0.0)[:, 0:16]
    back_high, back_low = split2(back)
    grad_n2 = grad_n2 + nn(back_high, small) + nn(back_low, small) + share * grad

    coefs_t = jnp.transpose(coefs)[0:16, :]
    high, low = split2(coefs_t)
    by_n2 = nn(high, n2_high) + nn(low, n2_high)
    by_low = nn(high, n2_low)
    by_grad = nn(high, grad_low) + nn(low, grad_low)
    row = iota((16, 1), 0)
    parts = jnp.where(row < kinds, by_n2, jnp.where(row < kinds + 4, by_n2 + by_low, by_grad))
    gain_part = jnp.sum(grad_n2 * hidden * inverse, axis=0, keepdims=True)
    parts = jnp.where(row == kinds + 7, gain_part, jnp.where(row == kinds + 6, 0.0, parts))
    dlog_t = coefs_t[0:kinds, :]
    map_lane = iota((kinds, LANES), 1)
    map_part = jnp.zeros((kinds, LANES), F32)
    for j in range(kinds):
        map_part = jnp.where(
            map_lane == j, jnp.sum(dlog_t * prev_ref[j : j + 1, :], axis=1, keepdims=True), map_part
        )

    scaled = gain * grad_n2
    inner_mean = jnp.mean(scaled * hidden, axis=-1, keepdims=True)
    dh = grad + inverse * scaled - hidden * (inverse * inverse * inverse) * inner_mean
    dh_ref[0] = dh
    db = dh.astype(BF16)
    dob_ref[0] = nt(db, wo_ref[...]).astype(BF16)
    wo_part = nn(jnp.transpose(o_ref[0]), db)

    @pl.when(step == 0)
    def _():
        acc_ref[...] = wo_part
        sgrad_ref[...] = parts
        grad_map_ref[...] = map_part

    @pl.when(step > 0)
    def _():
        acc_ref[...] += wo_part
        sgrad_ref[...] += parts
        grad_map_ref[...] += map_part


def combine_kernel(
    own_ref,
    d_ref,
    pos_ref,
    aux_ref,
    prev_ref,
    h_ref,
    g_ref,
    o_ref,
    small_ref,
    wo_ref,
    dh_ref,
    dob_ref,
    grad_wo_ref,
    sgrad_ref,
    grad_map_ref,
    acc_ref,
    cols_ref,
):
    own = own_ref[0]
    step = pl.program_id(0)
    sequence_combine(
        step,
        d_ref,
        pos_ref,
        aux_ref,
        prev_ref,
        h_ref,
        g_ref,
        o_ref,
        small_ref,
        wo_ref,
        dh_ref,
        dob_ref,
        sgrad_ref,
        grad_map_ref,
        acc_ref,
        cols_ref,
        lambda number: own ^ number,
    )

    @pl.when(step == pl.num_programs(0) - 1)
    def _():
        grad_wo_ref[...] = acc_ref[...].astype(BF16)


def sequence_backward(
    step,
    x_ref,
    segments,
    q_ref,
    k_ref,
    v_ref,
    dob_ref,
    lse_ref,
    dh_ref,
    small_ref,
    w_ref,
    cos_ref,
    sin_ref,
    gin_ref,
    gain_ref,
    bias_ref,
    lse_t_ref,
    dqkv_ref,
    acc_ref,
):
    length, width = x_ref.shape[1:]
    kinds = small_ref.shape[0] - 8
    pairs = width // LANES
    lane = iota((1, LANES), 1)
    low_half = (lane % HEAD_DIM) < (HEAD_DIM // 2)
    first_head = lane < HEAD_DIM
    mask_a = jnp.where(first_head, 1.0, 0.0).astype(BF16)
    mask_b = jnp.where(first_head, 0.0, 1.0).astype(BF16)
    allowed = same_document(segments) & (
        iota((length, length), 0) // BLOCK <= iota((length, length), 1) // BLOCK
    )
    bias_ref[...] = jnp.where(allowed, 0.0, NEG)
    lse_t_ref[...] = jnp.transpose(lse_ref[0])

    def pair(h, carry):
        cols = pl.ds(pl.multiple_of(h * LANES, LANES), LANES)
        keys_t = jnp.transpose(k_ref[0, :, cols])
        grad_keys = None
        grad_values = None
        grad_queries = []
        for begin in range(0, length, BLOCK):
            end = begin + BLOCK
            queries = q_ref[0, begin:end, cols]
            outs = dob_ref[0, begin:end, cols]
            keys = k_ref[0, 0:end, cols]
            values = v_ref[0, 0:end, cols]
            queries = jnp.concatenate([queries * mask_a, queries * mask_b], axis=0)
            outs = jnp.concatenate([outs * mask_a, outs * mask_b], axis=0)
            bias = bias_ref[0:end, begin:end]
            bias = jnp.concatenate([bias, bias], axis=1)
            line = jnp.concatenate(
                [lse_t_ref[pl.ds(2 * h, 1), begin:end], lse_t_ref[pl.ds(2 * h + 1, 1), begin:end]], axis=1
            )
            chances = jnp.exp(nt(keys, queries) + bias - line)
            grad_chances = nt(values, outs)
            delta = jnp.sum(chances * grad_chances, axis=0, keepdims=True)
            grad_scores = (chances * (grad_chances - delta)).astype(BF16)
            dv = nn(chances.astype(BF16), outs)
            dk = nn(grad_scores, queries)
            dq = jnp.transpose(nn(keys_t[:, 0:end], grad_scores))
            grad_queries.append(jnp.where(first_head, dq[0:BLOCK], dq[BLOCK:]))
            if grad_keys is None:
                grad_keys, grad_values = dk, dv
            else:
                grad_keys = jnp.concatenate([grad_keys + dk[0:begin], dk[begin:]], axis=0)
                grad_values = jnp.concatenate([grad_values + dv[0:begin], dv[begin:]], axis=0)
        dq = jnp.concatenate(grad_queries, axis=0) * 0.125
        dq = dq * cos_ref[...] - swap_halves(dq, low_half) * sin_ref[...]
        dk = grad_keys * cos_ref[...] - swap_halves(grad_keys, low_half) * sin_ref[...]
        dqkv_ref[:, cols] = dq.astype(BF16)
        dqkv_ref[:, pl.ds(pl.multiple_of(width + h * LANES, LANES), LANES)] = dk.astype(BF16)
        dqkv_ref[:, pl.ds(pl.multiple_of(2 * width + h * LANES, LANES), LANES)] = grad_values.astype(BF16)
        return carry

    lax.fori_loop(0, pairs, pair, 0)

    tokens = x_ref[0].astype(F32)
    inverse = rms_scale(tokens)
    gain = small_ref[kinds + 6 : kinds + 7, :]
    a1_t = jnp.transpose((tokens * inverse * gain).astype(BF16))

    @pl.when(step == 0)
    def _():
        acc_ref[...] = jnp.zeros_like(acc_ref)

    gin_ref[0] = jnp.zeros((length, width), F32)

    def project(part, carry):
        span = pl.ds(pl.multiple_of(part * width, LANES), width)
        gin_ref[0] += nt(dqkv_ref[:, span], w_ref[:, span])
        acc_ref[:, span] += nn(a1_t, dqkv_ref[:, span])
        return carry

    lax.fori_loop(0, 3, project, 0)
    dn1 = gin_ref[0]
    scaled = gain * dn1
    inner_mean = jnp.mean(scaled * tokens, axis=-1, keepdims=True)
    gin_ref[0] = dh_ref[0] + inverse * scaled - tokens * (inverse * inverse * inverse) * inner_mean
    gain_part = jnp.broadcast_to(jnp.sum(dn1 * tokens * inverse, axis=0, keepdims=True), gain_ref.shape)

    @pl.when(step == 0)
    def _():
        gain_ref[...] = gain_part

    @pl.when(step > 0)
    def _():
        gain_ref[...] += gain_part


def small_table(depth, sgrad_ref, grad_map_ref, gain_ref):
    kinds = grad_map_ref.shape[0]
    width = sgrad_ref.shape[1]
    row = iota((16, 1), 0)
    table = jnp.where(row == kinds + 6, gain_ref[0:1, :], sgrad_ref[...])
    chosen = jnp.where(iota((LANES, width), 1) % depth == iota((LANES, width), 0), 1.0, 0.0).astype(BF16)
    maps = nn(grad_map_ref[...].astype(BF16), chosen)
    table = jnp.concatenate([table, maps, jnp.zeros((LANES - 16 - kinds, width), F32)], axis=0)
    return jnp.transpose(table).astype(BF16)


def backward_kernel(
    x_ref,
    seg_ref,
    q_ref,
    k_ref,
    v_ref,
    dob_ref,
    lse_ref,
    dh_ref,
    small_ref,
    w_ref,
    cos_ref,
    sin_ref,
    gin_ref,
    grad_w_ref,
    gain_ref,
    bias_ref,
    lse_t_ref,
    dqkv_ref,
    acc_ref,
):
    step = pl.program_id(0)
    sequence_backward(
        step,
        x_ref,
        seg_ref[0],
        q_ref,
        k_ref,
        v_ref,
        dob_ref,
        lse_ref,
        dh_ref,
        small_ref,
        w_ref,
        cos_ref,
        sin_ref,
        gin_ref,
        gain_ref,
        bias_ref,
        lse_t_ref,
        dqkv_ref,
        acc_ref,
    )

    @pl.when(step == pl.num_programs(0) - 1)
    def _():
        grad_w_ref[...] = acc_ref[...].astype(BF16)


class ReducedChunk:
    def __init__(self, here, depth, begin, value_of, send_buffer, core_buffer, buffers, out_ref, sems):
        self.here, self.depth, self.begin, self.value_of = here, depth, begin, value_of
        self.send_buffer, self.acc, self.out_ref = send_buffer, core_buffer, out_ref
        y_first, x_first, x_second, y_second, self.z_buffer, self.done, self.other = buffers
        send, recv, z_send, z_recv = sems
        planes, x, y = here.planes, here.x, here.y
        near = planes // 2
        self.half = send_buffer.shape[3] // 2
        self.mine = pl.ds(pl.multiple_of(y * self.half, LANES), self.half)
        theirs = pl.ds(pl.multiple_of((1 - y) * self.half, LANES), self.half)
        self.received = (y_first, x_first, x_second, y_second)
        acc = core_buffer
        self.swap = remote(send_buffer, acc, send.at[0], recv.at[0], here.core_peer)
        self.y_first = remote(acc.at[0:near, :, :, theirs], y_first, send.at[1], recv.at[1], here.y_peer)
        self.x_first = remote(acc.at[near:planes, 1 - x], x_first, send.at[2], recv.at[2], here.x_peer)
        self.x_second = remote(acc.at[0:near, 1 - x, :, self.mine], x_second, send.at[3], recv.at[3], here.x_peer)
        self.y_second = remote(acc.at[near:planes, x, :, theirs], y_second, send.at[4], recv.at[4], here.y_peer)
        self.along = [
            remote(
                acc.at[(here.z + k) % planes, x, :, self.mine],
                self.z_buffer.at[k - 1],
                z_send.at[k - 1],
                z_recv.at[k - 1],
                here.z_peer(k),
            )
            for k in range(1, planes)
        ]
        self.back = remote(self.done, self.other, send.at[5], recv.at[5], here.y_peer)
        self.phases = (self.first, self.second, self.third, self.fourth, self.fifth)

    def rows_of(self, z, column, core):
        return pl.ds(pl.multiple_of(self.here.block(z, column, core) * self.depth, 16), self.depth)

    def lower(self):
        def body(z, carry):
            for column in range(2):
                rows = self.rows_of(z, column, 1 - self.here.core)
                self.send_buffer[z, column] = self.value_of(rows).astype(BF16)
            return carry

        lax.fori_loop(0, self.here.planes, body, 0)

    def add(self, target, source):
        target[...] = (target[...].astype(F32) + source[...].astype(F32)).astype(BF16)

    def first(self):
        self.swap.wait_recv()

        def body(z, carry):
            for column in range(2):
                own = self.value_of(self.rows_of(z, column, self.here.core)).astype(F32)
                self.acc[z, column] = (own + self.acc[z, column].astype(F32)).astype(BF16)
            return carry

        lax.fori_loop(0, self.here.planes, body, 0)
        self.y_first.start()
        self.x_first.start()

    def second(self):
        planes = self.here.planes
        self.y_first.wait_recv()
        for z in range(planes // 2):
            for column in range(2):
                self.add(self.acc.at[z, column, :, self.mine], self.received[0].at[z, column])
        self.x_second.start()
        self.x_first.wait_recv()
        for z in range(planes // 2, planes):
            self.add(self.acc.at[z, self.here.x], self.received[1].at[z - planes // 2])
        self.y_second.start()

    def third(self):
        planes = self.here.planes
        self.x_second.wait_recv()
        for z in range(planes // 2):
            self.add(self.acc.at[z, self.here.x, :, self.mine], self.received[2].at[z])
        self.y_second.wait_recv()
        for z in range(planes // 2, planes):
            self.add(self.acc.at[z, self.here.x, :, self.mine], self.received[3].at[z - planes // 2])
        for copy in self.along:
            copy.start()

    def fourth(self):
        total = self.acc[self.here.z, self.here.x, :, self.mine].astype(F32)
        for k, copy in enumerate(self.along):
            copy.wait_recv()
            total = total + self.z_buffer[k].astype(F32)
        self.done[...] = total.astype(BF16)
        self.back.start()

    def fifth(self):
        self.back.wait_recv()
        y = self.here.y
        spot = pl.ds(pl.multiple_of(self.begin + y * self.half, LANES), self.half)
        other = pl.ds(pl.multiple_of(self.begin + (1 - y) * self.half, LANES), self.half)
        self.out_ref[:, spot] = self.done[...].astype(F32)
        self.out_ref[:, other] = self.other[...].astype(F32)
        for copy in [self.swap, self.y_first, self.x_first, self.x_second, self.y_second, self.back] + self.along:
            copy.wait_send()


def attention_columns(acc_ref, acc_wo_ref, table_ref, begin, columns, rows):
    pieces = []
    width = acc_wo_ref.shape[1]
    for start, size, ref in (
        (0, 3 * width, acc_ref),
        (3 * width, width, acc_wo_ref),
        (4 * width, LANES, table_ref),
        (4 * width + LANES, LANES, None),
    ):
        low, high = max(begin, start) - start, min(begin + columns, start + size) - start
        if low < high:
            if ref is None:
                pieces.append(jnp.zeros((rows.size, high - low), F32))
            else:
                pieces.append(ref[rows, low:high].astype(F32))
    return pieces[0] if len(pieces) == 1 else jnp.concatenate(pieces, axis=1)


def reduce_attention(chunks, free_sem):
    chunks[0].lower()
    pl.semaphore_wait(free_sem, 1)
    chunks[0].swap.start()
    for chunk in chunks[1:]:
        chunk.lower()
        chunk.swap.start()
    phases = len(chunks[0].phases)
    for step in range(len(chunks) + phases - 1):
        for number, chunk in enumerate(chunks):
            if 0 <= step - number < phases:
                chunk.phases[step - number]()


def fused_backward_kernel(
    group,
    depth,
    pos_ref,
    aux_ref,
    prev_ref,
    h_ref,
    g_ref,
    o_ref,
    x_ref,
    seg_ref,
    q_ref,
    k_ref,
    v_ref,
    lse_ref,
    small_ref,
    w_ref,
    wo_ref,
    cos_ref,
    sin_ref,
    d_ref,
    val_ref,
    gate_ref,
    up_ref,
    down_ref,
    gin_ref,
    sums_ref,
    d_in_ref,
    val_in_ref,
    gate_out_ref,
    up_out_ref,
    down_out_ref,
    acc_ref,
    acc_wo_ref,
    table_ref,
    send_buffers,
    chunk_buffers,
    cols_ref,
    dh_ref,
    dob_ref,
    sgrad_ref,
    grad_map_ref,
    gain_ref,
    bias_ref,
    lse_t_ref,
    dqkv_ref,
    rows_ref,
    gate_own,
    up_own,
    down_own,
    gate_swap,
    up_swap,
    down_swap,
    gate_near,
    up_near,
    down_near,
    gate_far,
    up_far,
    down_far,
    row_local,
    row_send,
    row_recv,
    ffn_local,
    ffn_send,
    ffn_recv,
    free_sem,
    reduce_send,
    reduce_recv,
    reduce_z_send,
    reduce_z_recv,
):
    step = pl.program_id(0)
    last = pl.num_programs(0) - 1
    here = Place(group)
    planes = here.planes
    batches = d_ref.shape[1]
    width = x_ref.shape[2]
    grads = (gate_ref, up_ref, down_ref)
    owns = (gate_own, up_own, down_own)
    swaps = (gate_swap, up_swap, down_swap)
    nears = (gate_near, up_near, down_near)
    fars = (gate_far, up_far, down_far)
    outs = (gate_out_ref, up_out_ref, down_out_ref)
    side = (here.z_peer(1), here.z_peer(planes - 1))

    def z_at(k):
        return (here.z + k) % planes

    def row_copy(kind, member, number):
        source, target = ((d_ref, d_in_ref), (val_ref, val_in_ref))[kind]
        src, dst = source.at[number, member], target.at[number, member]
        if number == 0:
            return pltpu.make_async_copy(src, dst, row_local.at[batches * 4 + member])
        return remote(
            src, dst, row_send.at[kind, member, number], row_recv.at[kind, member, number], here.plane_peers[number]
        )

    def load_rows(member, number):
        source = d_ref if number == 0 else d_in_ref
        return pltpu.make_async_copy(
            source.at[number, member], rows_ref.at[number, 0], row_local.at[member * 4 + number]
        )

    def own_copy(j):
        return pltpu.make_async_copy(grads[j].at[:, :, here.core], owns[j], ffn_local.at[j, 0])

    def swap_copy(j):
        return remote(
            grads[j].at[:, :, 1 - here.core], swaps[j], ffn_send.at[j, 0], ffn_recv.at[j, 0], here.core_peer
        )

    def near_copy(j, k):
        return remote(
            owns[j].at[z_at(2), k], nears[j].at[k], ffn_send.at[j, 1 + k], ffn_recv.at[j, 1 + k], side[k]
        )

    def far_copy(j, k):
        return remote(
            owns[j].at[z_at(1 if k == 0 else planes - 1)],
            fars[j].at[k],
            ffn_send.at[j, 3 + k],
            ffn_recv.at[j, 3 + k],
            side[k],
        )

    def plane_copy(j, number):
        x = here.x if number % 2 == 0 else 1 - here.x
        src, dst = owns[j].at[here.z, x], outs[j].at[here.expert(0)]
        if number == 0:
            return pltpu.make_async_copy(src, dst, ffn_local.at[j, 1])
        return remote(
            src, dst, ffn_send.at[j, 4 + number], ffn_recv.at[j, 4 + number], here.plane_peers[number]
        )

    def plane_arrival(j, number):
        dst = outs[j].at[here.expert(number)]
        return remote(
            dst, dst, ffn_send.at[j, 4 + number], ffn_recv.at[j, 4 + number], here.plane_peers[number]
        )

    def add(target, *sources):
        value = target[...].astype(F32)
        for source in sources:
            value = value + source[...].astype(F32)
        target[...] = value.astype(BF16)

    @pl.when(step == 0)
    def _():
        for j in range(3):
            own_copy(j).start()
        here.barrier(
            [here.core_peer, here.x_peer, here.y_peer, here.xy_peer] + [here.z_peer(k) for k in range(1, planes)]
        )
        for number in range(1, 4):
            row_copy(0, 0, number).start()
        for j in range(3):
            swap_copy(j).start()
        for j in range(3):
            own_copy(j).wait()
            swap_copy(j).wait_recv()
            for x in range(2):

                def add_core(z, carry):
                    add(owns[j].at[z, x], swaps[j].at[z, x])
                    return carry

                lax.fori_loop(0, planes, add_core, 0)
            near_copy(j, 0).start()
            near_copy(j, 1).start()
        pl.semaphore_signal(free_sem, inc=1, device_id=here.core_peer, device_id_type=MESH)

    for member in range(batches):

        @pl.when(step == member)
        def _():
            for number in range(1, 4):
                row_copy(0, member, number).wait_recv()
            if member + 1 < batches:
                for number in range(1, 4):
                    row_copy(0, member + 1, number).start()
            for number in range(4):
                row_copy(1, member, number).start()
            for number in range(4):
                load_rows(member, number).start()
            for number in range(4):
                load_rows(member, number).wait()

    sequence_combine(
        step,
        rows_ref,
        pos_ref,
        aux_ref,
        prev_ref,
        h_ref,
        g_ref,
        o_ref,
        small_ref,
        wo_ref,
        dh_ref,
        dob_ref,
        sgrad_ref,
        grad_map_ref,
        acc_wo_ref,
        cols_ref,
        here.expert,
    )

    @pl.when(step == 0)
    def _():
        for j in range(3):
            for k in range(2):
                near_copy(j, k).wait_recv()
                add(owns[j].at[z_at(1 if k == 0 else planes - 1), k], nears[j].at[k])
                far_copy(j, k).start()

    sequence_backward(
        step,
        x_ref,
        seg_ref[pl.ds(step, 1), :],
        q_ref,
        k_ref,
        v_ref,
        dob_ref,
        lse_ref,
        dh_ref,
        small_ref,
        w_ref,
        cos_ref,
        sin_ref,
        gin_ref,
        gain_ref,
        bias_ref,
        lse_t_ref,
        dqkv_ref,
        acc_ref,
    )

    @pl.when(step == last)
    def _():
        table_ref[...] = small_table(depth, sgrad_ref, grad_map_ref, gain_ref)
        for j in range(3):
            for k in range(2):
                far_copy(j, k).wait_recv()
            for x in range(2):
                add(owns[j].at[here.z, x], fars[j].at[0, x], fars[j].at[1, x])
            for number in range(4):
                plane_copy(j, number).start()
        chunks = []
        begin = 0
        for number, (send_buffer, buffers) in enumerate(zip(send_buffers, chunk_buffers)):
            columns = send_buffer.shape[3]
            home, place = (gate_swap, begin) if begin < gate_swap.shape[3] else (up_swap, begin - gate_swap.shape[3])
            chunks.append(
                ReducedChunk(
                    here,
                    depth,
                    begin,
                    functools.partial(attention_columns, acc_ref, acc_wo_ref, table_ref, begin, columns),
                    send_buffer,
                    home.at[:, :, :, place : place + columns],
                    buffers,
                    sums_ref,
                    (
                        reduce_send.at[number],
                        reduce_recv.at[number],
                        reduce_z_send.at[number],
                        reduce_z_recv.at[number],
                    ),
                )
            )
            begin += columns
        reduce_attention(chunks, free_sem)
        for j in range(3):
            swap_copy(j).wait_send()
            for k in range(2):
                near_copy(j, k).wait_send()
                far_copy(j, k).wait_send()
            plane_copy(j, 0).wait()
            for number in range(1, 4):
                plane_copy(j, number).wait_send()
                plane_arrival(j, number).wait_recv()
        for member in range(batches):
            row_copy(1, member, 0).wait()
            for number in range(1, 4):
                row_copy(0, member, number).wait_send()
                row_copy(1, member, number).wait()


def params(limit_mib):
    return pltpu.CompilerParams(vmem_limit_bytes=limit_mib * 1024 * 1024, dimension_semantics=("arbitrary",))


def rotary(length):
    halfway = HEAD_DIM // 2
    frequency = 10000.0 ** (-jnp.arange(halfway).astype(F32) / halfway)
    angles = jnp.arange(length).astype(F32)[:, None] * frequency[None, :]
    cosine, sine = jnp.cos(angles), jnp.sin(angles)
    return (
        jnp.concatenate([cosine] * 4, axis=1),
        jnp.concatenate([-sine, sine, -sine, sine], axis=1),
    )


def rotary_parts(length):
    halfway = HEAD_DIM // 2
    frequency = 10000.0 ** (-np.arange(halfway) / halfway)
    step = 32
    sign = np.tile(np.repeat([-1.0, 1.0], halfway), LANES // HEAD_DIM)

    def table(positions):
        angles = np.tile(positions[:, None] * frequency[None, :], (1, LANES // halfway))
        return np.cos(angles), np.sin(angles)

    coarse = table(np.arange(0, length, step))
    fine = table(np.arange(step))
    signs = np.broadcast_to(sign, fine[0].shape)
    return jnp.asarray(np.stack(coarse), F32), jnp.asarray(np.stack(fine + (signs,)), F32)


def local(
    reps,
    group,
    block_input,
    prev_logits,
    routes,
    segments,
    grad_out,
    gain_attn,
    w_query,
    w_key,
    w_value,
    w_output,
    gain_mix,
    router,
    route_map,
    const_proj,
    const_vec,
    w_gate,
    w_up,
    w_down,
):
    batches, length = segments.shape
    width = block_input.shape[1]
    kinds = router.shape[1]
    ffn = w_gate.shape[1]
    hidden = w_gate.shape[2]
    rows_d = w_gate.shape[0]
    rows_f = w_down.shape[0]
    capacity = length // 2
    planes = group // 4
    assert reps == 2 and ffn == 4 and group % 4 == 0
    g = lax.axis_index("grp")
    y = lax.axis_index("rep")
    core = g % 2
    x = (g // 2) % 2
    z = g // 4
    own = (2 * y + x).astype(jnp.int32)
    own_arr = own.reshape(1)

    x_flip = [(i, i ^ 2) for i in range(group)]
    core_flip = [(i, i ^ 1) for i in range(group)]
    y_flip = [(0, 1), (1, 0)]
    xy_flip = [(r * group + i, (1 - r) * group + (i ^ 2)) for r in range(2) for i in range(group)]

    def z_shift(k):
        return [(i, (i + 4 * k) % group) for i in range(group)]

    def to_plane(parts):
        return [
            parts[0],
            lax.ppermute(parts[1], "grp", x_flip),
            lax.ppermute(parts[2], "rep", y_flip),
            lax.ppermute(parts[3], ("rep", "grp"), xy_flip),
        ]

    tokens = block_input.reshape(batches, length, width)
    grads = grad_out.reshape(batches, length, width)
    route_rows = routes.T
    prev_rows = prev_logits.T
    row_spec = pl.BlockSpec((2, length), lambda b, *_: (0, b))
    prev_spec = pl.BlockSpec((kinds, length), lambda b, *_: (0, b))

    def spec_w(j):
        return pl.BlockSpec((width, width), lambda b, *_: (0, j), pipeline_mode=pl.Buffered(1))

    row_shape = jax.ShapeDtypeStruct((batches, capacity, width), BF16)
    seq_bf16 = jax.ShapeDtypeStruct((batches, length, width), BF16)
    seq_f32 = jax.ShapeDtypeStruct((batches, length, width), F32)
    fused = planes == 4 and rows_d % 16 == 0 and rows_f % 16 == 0
    if fused:
        any_space = pl.BlockSpec(memory_space=pl.ANY)
        coarse, fine = rotary_parts(length)
        smalls = [router.T, const_proj.T, const_vec.T, gain_attn[None], gain_mix[None]]
        out_struct = jax.ShapeDtypeStruct
        (
            q, k, v, o, h1, lse, aux, pos, small, cos, sin, attn, attn_o, a_rows, grad_rows, gate_full, up_full, down_full,
        ) = pl.pallas_call(
            functools.partial(fused_forward_kernel, group),
            grid=(batches,),
            in_specs=[
                per_seq((length, width)),
                whole((batches, length)),
                whole((2, batches * length)),
                prev_spec,
                whole((kinds, kinds)),
                whole((batches, length, width)),
                whole(coarse.shape),
                whole(fine.shape),
                [whole((rows_d, width))] * 4,
                [whole(part.shape) for part in smalls],
            ]
            + [any_space] * 3,
            out_specs=[per_seq((length, width))] * 5
            + [
                per_seq((length, LANES)),
                per_seq((16, length)),
                whole((batches, kinds, length)),
                whole((kinds + 8, width)),
                whole((length, LANES)),
                whole((length, LANES)),
            ]
            + [any_space] * 7,
            scratch_shapes=[
                pltpu.VMEM((width, 3 * width + 2 * LANES), BF16),
                pltpu.VMEM((width, width), BF16),
                pltpu.VMEM((length, length), F32),
                pltpu.VMEM((length, width), F32),
                pltpu.VMEM((batches, 4, capacity + 16, width), BF16),
                pltpu.VMEM((batches, 4, capacity, width), BF16),
                pltpu.VMEM((LANES, LANES), F32),
                pltpu.VMEM((kinds, LANES), F32),
                pltpu.SemaphoreType.DMA((2, 4 + 4 * planes)),
                pltpu.SemaphoreType.DMA((2, 4 + 4 * planes)),
                pltpu.SemaphoreType.DMA((3,)),
                pltpu.SemaphoreType.DMA((3, 5 + planes)),
                pltpu.SemaphoreType.DMA((3, 5 + planes)),
                pltpu.SemaphoreType.DMA((2,)),
                pltpu.SemaphoreType.DMA((2, batches)),
                pltpu.SemaphoreType.DMA((2, batches, 4)),
                pltpu.SemaphoreType.DMA((2, batches, 4)),
            ],
            out_shape=[seq_bf16] * 4
            + [
                seq_f32,
                out_struct((batches, length, LANES), F32),
                out_struct((batches, 16, length), F32),
                out_struct((batches, kinds, length), F32),
                out_struct((kinds + 8, width), F32),
                out_struct((length, LANES), F32),
                out_struct((length, LANES), F32),
                out_struct((width, 3 * width + 2 * LANES), BF16),
                out_struct((width, width), BF16),
                out_struct((4, batches, capacity + 16, width), BF16),
                out_struct((4, batches, capacity, width), BF16),
                out_struct((planes, 2, 2, rows_d, hidden), BF16),
                out_struct((planes, 2, 2, rows_d, hidden), BF16),
                out_struct((planes, 2, 2, rows_f, width), BF16),
            ],
            compiler_params=pltpu.CompilerParams(
                vmem_limit_bytes=58 * 1024 * 1024,
                dimension_semantics=("arbitrary",),
                collective_id=1,
                has_side_effects=True,
            ),
            cost_estimate=pl.CostEstimate(flops=40 * 10**9, bytes_accessed=60 * 10**6, transcendentals=10**7),
            name="fused_forward",
        )(
            tokens, segments, route_rows, prev_rows, route_map, grads, coarse, fine,
            [w_query, w_key, w_value, w_output], smalls,
            w_gate.astype(BF16).transpose(1, 0, 2),
            w_up.astype(BF16).transpose(1, 0, 2),
            w_down.astype(BF16).transpose(1, 0, 2),
        )
        gate_full = gate_full.reshape(width, hidden)
        up_full = up_full.reshape(width, hidden)
        down_full = down_full.reshape(hidden, width)
    else:
        cos, sin = rotary(length)
        small_shard = jnp.concatenate(
            [router, const_proj, const_vec, gain_attn[:, None], gain_mix[:, None]], axis=1
        ).astype(BF16)
        small_shard = jnp.pad(small_shard, ((0, 0), (0, 2 * LANES - small_shard.shape[1])))
        shard = jnp.concatenate([w.astype(BF16) for w in (w_query, w_key, w_value)] + [small_shard], axis=1)
        shard_o = w_output.astype(BF16)
        attn = lax.all_gather(shard, "grp", axis=0, tiled=True)
        attn_o = lax.all_gather(shard_o, "grp", axis=0, tiled=True)
        small = attn[:, 3 * width : 3 * width + kinds + 8].astype(F32).T

        def pick(array, expert):
            return lax.dynamic_index_in_dim(array, expert, axis=1, keepdims=False)

        def gather_expert(mine, other):
            crossed = lax.ppermute(other, "grp", x_flip)
            both = jnp.where(x == 0, jnp.stack([mine, crossed]), jnp.stack([crossed, mine]))
            pieces = [both] + [lax.ppermute(both, "grp", z_shift(k)) for k in range(1, planes)]
            stacked = jnp.stack(pieces)
            half = jnp.take(stacked, (z - jnp.arange(planes)) % planes, axis=0)
            swapped = lax.ppermute(half, "grp", core_flip)
            return jnp.where(core == 0, jnp.stack([half, swapped], axis=2), jnp.stack([swapped, half], axis=2))

        gate_up = gather_expert(
            jnp.stack([pick(w_gate, own), pick(w_up, own)]).astype(BF16),
            jnp.stack([pick(w_gate, own ^ 1), pick(w_up, own ^ 1)]).astype(BF16),
        )
        down = gather_expert(pick(w_down, own).astype(BF16), pick(w_down, own ^ 1).astype(BF16))
        gate_full = gate_up[:, :, :, 0].reshape(width, hidden)
        up_full = gate_up[:, :, :, 1].reshape(width, hidden)
        down_full = down.reshape(hidden, width)

        *grad_rows, pos = pl.pallas_call(
            grad_rows_kernel,
            grid_spec=pltpu.PrefetchScalarGridSpec(
                num_scalar_prefetch=1,
                grid=(batches,),
                in_specs=[row_spec, per_seq((length, width))],
                out_specs=[per_seq((capacity, width))] * 4 + [per_seq((kinds, length))],
            ),
            out_shape=[row_shape] * 4 + [jax.ShapeDtypeStruct((batches, kinds, length), F32)],
            compiler_params=params(32),
            cost_estimate=pl.CostEstimate(flops=4 * 10**9, bytes_accessed=8 * 10**6, transcendentals=0),
            name="grad_rows",
        )(own_arr, route_rows, grads)
        grad_rows = to_plane(grad_rows)

        q, k, v, o, h1, lse, aux, a_rows = pl.pallas_call(
            forward_kernel,
            grid_spec=pltpu.PrefetchScalarGridSpec(
                num_scalar_prefetch=1,
                grid=(batches,),
                in_specs=[
                    per_seq((length, width)),
                    per_seq((1, length)),
                    row_spec,
                    prev_spec,
                    whole((kinds, kinds)),
                    whole((kinds + 8, width)),
                    spec_w(0),
                    spec_w(1),
                    spec_w(2),
                    spec_w(0),
                    whole((length, LANES)),
                    whole((length, LANES)),
                    per_seq((kinds, length)),
                ],
                out_specs=[per_seq((length, width))] * 5
                + [per_seq((length, LANES)), per_seq((16, length))]
                + [pl.BlockSpec((4, 1, capacity + 16, width), lambda b, *_: (0, b, 0, 0))],
                scratch_shapes=[pltpu.VMEM((length, length), F32), pltpu.VMEM((length, width), F32)],
            ),
            out_shape=[seq_bf16] * 4
            + [
                seq_f32,
                jax.ShapeDtypeStruct((batches, length, LANES), F32),
                jax.ShapeDtypeStruct((batches, 16, length), F32),
            ]
            + [jax.ShapeDtypeStruct((4, batches, capacity + 16, width), BF16)],
            compiler_params=params(56),
            cost_estimate=pl.CostEstimate(flops=20 * 10**9, bytes_accessed=20 * 10**6, transcendentals=10**7),
            name="forward",
        )(own_arr, tokens, segments[:, None], route_rows, prev_rows, route_map.T, small, attn, attn, attn, attn_o, cos, sin, pos)
        a_rows = to_plane([a_rows[i] for i in range(4)])

        a_rows = jnp.stack(a_rows)
        grad_rows = jnp.stack(grad_rows)

    tile = hidden // 4
    total = 4 * batches * capacity
    any_spec = pl.BlockSpec(memory_space=pl.ANY)
    values, input_rows, grad_gate_full, grad_up_full, grad_down_full = pl.pallas_call(
        expert_kernel,
        grid=(hidden // tile,),
        in_specs=[any_spec] * 2
        + [
            pl.BlockSpec((width, tile), lambda f: (0, f)),
            pl.BlockSpec((width, tile), lambda f: (0, f)),
            pl.BlockSpec((tile, width), lambda f: (f, 0)),
        ],
        out_specs=[any_spec] * 2
        + [
            pl.BlockSpec((width, tile), lambda f: (0, f)),
            pl.BlockSpec((width, tile), lambda f: (0, f)),
            pl.BlockSpec((tile, width), lambda f: (f, 0)),
        ],
        scratch_shapes=[
            pltpu.VMEM((total + capacity, width), BF16),
            pltpu.VMEM((total + capacity, width), BF16),
            pltpu.VMEM((4 * batches, 16, capacity), BF16),
            pltpu.VMEM((width, total), BF16),
            pltpu.VMEM((width, total), BF16),
            pltpu.SMEM((4 * batches + 1,), jnp.int32),
            pltpu.VMEM((total, width), F32),
            pltpu.VMEM((total, width), F32),
            pltpu.VMEM((width, tile), F32),
            pltpu.VMEM((width, tile), F32),
            pltpu.VMEM((width, tile), F32),
            pltpu.VMEM((total + capacity, LANES), F32),
            pltpu.SemaphoreType.DMA((12 * batches,)),
        ],
        out_shape=[
            jax.ShapeDtypeStruct((4, batches, capacity, width), BF16),
            jax.ShapeDtypeStruct((4, batches, capacity + 16, width), BF16),
        ]
        + [
            jax.ShapeDtypeStruct((width, hidden), BF16),
            jax.ShapeDtypeStruct((width, hidden), BF16),
            jax.ShapeDtypeStruct((hidden, width), BF16),
        ],
        compiler_params=params(60),
        cost_estimate=pl.CostEstimate(flops=58 * 10**9, bytes_accessed=40 * 10**6, transcendentals=10**7),
        name="expert",
    )(a_rows, grad_rows, gate_full, up_full, down_full)
    if fused:
        columns = 4 * width + 2 * LANES
        once = lambda shape: pl.BlockSpec(
            (1,) + shape, lambda b, *_: (b, 0, 0), pipeline_mode=pl.Buffered(1)
        )
        wide = ((rows_d, hidden), (rows_d, hidden), (rows_f, width))
        near = planes // 2
        parts = (hidden // 2, hidden // 2, width, columns - hidden - width)
        gin, sums, _, values_in, grad_gate, grad_up, grad_down = pl.pallas_call(
            functools.partial(fused_backward_kernel, group, rows_d),
            grid=(batches,),
            in_specs=[
                per_seq((kinds, length)),
                per_seq((16, length)),
                prev_spec,
                once((length, width)),
                once((length, width)),
                once((length, width)),
                once((length, width)),
                whole((batches, length)),
                once((length, width)),
                once((length, width)),
                once((length, width)),
                once((length, LANES)),
                whole((kinds + 8, width), 1),
                pl.BlockSpec((width, 3 * width), lambda b, *_: (0, 0), pipeline_mode=pl.Buffered(1)),
                spec_w(0),
                whole((length, LANES), 1),
                whole((length, LANES), 1),
            ]
            + [any_spec] * 5,
            out_specs=[once((length, width)), whole((rows_d, columns), 1)] + [any_spec] * 5,
            out_shape=[
                seq_f32,
                jax.ShapeDtypeStruct((rows_d, columns), F32),
                jax.ShapeDtypeStruct((4, batches, capacity + 16, width), BF16),
                jax.ShapeDtypeStruct((4, batches, capacity, width), BF16),
            ]
            + [jax.ShapeDtypeStruct((4,) + shape, BF16) for shape in wide],
            scratch_shapes=[
                pltpu.VMEM((width, 3 * width), F32),
                pltpu.VMEM((width, width), F32),
                pltpu.VMEM((width, LANES), BF16),
            ]
            + [[pltpu.VMEM((planes, 2, rows_d, part), BF16) for part in parts]]
            + [
                [[
                    pltpu.VMEM((near, 2, rows_d, part // 2), BF16),
                    pltpu.VMEM((near, rows_d, part), BF16),
                    pltpu.VMEM((near, rows_d, part // 2), BF16),
                    pltpu.VMEM((near, rows_d, part // 2), BF16),
                    pltpu.VMEM((planes - 1, rows_d, part // 2), BF16),
                    pltpu.VMEM((rows_d, part // 2), BF16),
                    pltpu.VMEM((rows_d, part // 2), BF16),
                ] for part in parts]
            ]
            + [
                pltpu.VMEM((LANES, length), F32),
                pltpu.VMEM((1, length, width), F32),
                pltpu.VMEM((1, length, width), BF16),
                pltpu.VMEM((16, width), F32),
                pltpu.VMEM((kinds, LANES), F32),
                pltpu.VMEM((8, width), F32),
                pltpu.VMEM((length, length), F32),
                pltpu.VMEM((LANES, length), F32),
                pltpu.VMEM((length, 3 * width), BF16),
                pltpu.VMEM((4, 1, capacity + 16, width), BF16),
            ]
            + [pltpu.VMEM((planes, 2) + shape, BF16) for shape in wide]
            + [pltpu.VMEM((planes, 2) + shape, BF16) for shape in wide]
            + [pltpu.VMEM((2,) + shape, BF16) for shape in wide]
            + [pltpu.VMEM((2, 2) + shape, BF16) for shape in wide]
            + [
                pltpu.SemaphoreType.DMA((5 * batches,)),
                pltpu.SemaphoreType.DMA((2, batches, 4)),
                pltpu.SemaphoreType.DMA((2, batches, 4)),
                pltpu.SemaphoreType.DMA((3, 2)),
                pltpu.SemaphoreType.DMA((3, 8)),
                pltpu.SemaphoreType.DMA((3, 8)),
                pltpu.SemaphoreType.REGULAR,
                pltpu.SemaphoreType.DMA((len(parts), 6)),
                pltpu.SemaphoreType.DMA((len(parts), 6)),
                pltpu.SemaphoreType.DMA((len(parts), planes - 1)),
                pltpu.SemaphoreType.DMA((len(parts), planes - 1)),
            ],
            compiler_params=pltpu.CompilerParams(
                vmem_limit_bytes=63 * 1024 * 1024,
                dimension_semantics=("arbitrary",),
                collective_id=3,
                has_side_effects=True,
            ),
            cost_estimate=pl.CostEstimate(flops=60 * 10**9, bytes_accessed=60 * 10**6, transcendentals=10**7),
            name="fused_backward",
        )(
            pos, aux, prev_rows, h1, grads, o, tokens, segments, q, k, v, lse, small,
            attn, attn_o, cos, sin, input_rows, values,
            grad_gate_full.reshape(planes, 2, 2, rows_d, hidden),
            grad_up_full.reshape(planes, 2, 2, rows_d, hidden),
            grad_down_full.reshape(planes, 2, 2, rows_f, width),
        )
        grad_gate = grad_gate.transpose(1, 0, 2).astype(F32)
        grad_up = grad_up.transpose(1, 0, 2).astype(F32)
        grad_down = grad_down.transpose(1, 0, 2).astype(F32)
    else:
        values_in = jnp.stack(to_plane([values[i] for i in range(4)]))
        def scatter_expert(full):
            keep = lax.dynamic_index_in_dim(full, core, axis=2, keepdims=False)
            send = lax.dynamic_index_in_dim(full, 1 - core, axis=2, keepdims=False)
            half = (keep.astype(F32) + lax.ppermute(send, "grp", core_flip).astype(F32)).astype(BF16)
            summed = lax.dynamic_index_in_dim(half, z, axis=0, keepdims=False).astype(F32)
            for k in range(1, planes):
                part = lax.dynamic_index_in_dim(half, (z + k) % planes, axis=0, keepdims=False)
                summed = summed + lax.ppermute(part, "grp", z_shift(k)).astype(F32)
            summed = summed.astype(BF16)
            mine = lax.dynamic_index_in_dim(summed, x, axis=0, keepdims=False)
            other = lax.dynamic_index_in_dim(summed, 1 - x, axis=0, keepdims=False)
            arrived = to_plane([mine, other, mine, other])

            def order(first):
                return lambda: tuple(arrived[first ^ e] for e in range(4))

            return lax.switch(own, [order(i) for i in range(4)])

        grad_gate_up = scatter_expert(
            jnp.stack(
                [
                    grad_gate_full.reshape(planes, 2, 2, rows_d, hidden),
                    grad_up_full.reshape(planes, 2, 2, rows_d, hidden),
                ],
                axis=3,
            )
        )
        grad_down = scatter_expert(grad_down_full.reshape(planes, 2, 2, rows_f, width))
        grad_gate = jnp.stack([part[0] for part in grad_gate_up], axis=1).astype(F32)
        grad_up = jnp.stack([part[1] for part in grad_gate_up], axis=1).astype(F32)
        grad_down = jnp.stack(grad_down, axis=1).astype(F32)

        dh1, dob, grad_wo, sgrad, grad_map = pl.pallas_call(
            combine_kernel,
            grid_spec=pltpu.PrefetchScalarGridSpec(
                num_scalar_prefetch=1,
                grid=(batches,),
                in_specs=[pl.BlockSpec((4, 1, capacity + 16, width), lambda b, *_: (0, b, 0, 0))]
                + [
                    per_seq((kinds, length)),
                    per_seq((16, length)),
                    prev_spec,
                    per_seq((length, width)),
                    per_seq((length, width)),
                    per_seq((length, width)),
                    whole((kinds + 8, width)),
                    spec_w(0),
                ],
                out_specs=[per_seq((length, width))] * 2
                + [whole((width, width)), whole((16, width)), whole((kinds, LANES))],
                scratch_shapes=[pltpu.VMEM((width, width), F32), pltpu.VMEM((LANES, length), F32)],
            ),
            out_shape=[
                seq_f32,
                seq_bf16,
                jax.ShapeDtypeStruct((width, width), BF16),
                jax.ShapeDtypeStruct((16, width), F32),
                jax.ShapeDtypeStruct((kinds, LANES), F32),
            ],
            compiler_params=params(56),
            cost_estimate=pl.CostEstimate(flops=12 * 10**9, bytes_accessed=20 * 10**6, transcendentals=10**5),
            name="combine",
        )(own_arr, jnp.stack(to_plane([input_rows[i] for i in range(4)])), pos, aux, prev_rows, h1, grads, o, small, attn_o)

        gin, grad_attn, gain_one = pl.pallas_call(
            backward_kernel,
            grid=(batches,),
            in_specs=[
                per_seq((length, width)),
                per_seq((1, length)),
                per_seq((length, width)),
                per_seq((length, width)),
                per_seq((length, width)),
                per_seq((length, width)),
                per_seq((length, LANES)),
                per_seq((length, width)),
                whole((kinds + 8, width)),
                pl.BlockSpec((width, 3 * width), lambda b, *_: (0, 0), pipeline_mode=pl.Buffered(1)),
                whole((length, LANES)),
                whole((length, LANES)),
            ],
            out_specs=[per_seq((length, width)), whole((width, 3 * width)), whole((8, width))],
            scratch_shapes=[
                pltpu.VMEM((length, length), F32),
                pltpu.VMEM((LANES, length), F32),
                pltpu.VMEM((length, 3 * width), BF16),
                pltpu.VMEM((width, 3 * width), F32),
            ],
            out_shape=[
                seq_f32,
                jax.ShapeDtypeStruct((width, 3 * width), BF16),
                jax.ShapeDtypeStruct((8, width), F32),
            ],
            compiler_params=params(56),
            cost_estimate=pl.CostEstimate(flops=30 * 10**9, bytes_accessed=20 * 10**6, transcendentals=10**7),
            name="backward",
        )(tokens, segments[:, None], q, k, v, dob, lse, dh1, small, attn, cos, sin)

    finish_specs = dict(
        num_scalar_prefetch=1,
        grid=(batches,),
    )
    finish_in = [
        pl.BlockSpec((4, 1, capacity, width), lambda b, *_: (0, b, 0, 0)),
        per_seq((kinds, length)),
        per_seq((16, length)),
        per_seq((length, width)),
        whole((kinds + 8, width)),
    ]
    finish_cost = pl.CostEstimate(flops=4 * 10**9, bytes_accessed=12 * 10**6, transcendentals=0)
    if fused:
        small_shapes = [(rows_d, width)] * 4 + [
            (kinds, rows_d), (4, rows_d), (2, rows_d), (1, rows_d), (1, rows_d), (kinds, kinds)
        ]
        result, gq, gk, gv, go, *small_sums = pl.pallas_call(
            finish_kernel,
            grid_spec=pltpu.PrefetchScalarGridSpec(
                in_specs=finish_in + [whole((rows_d, columns))],
                out_specs=[per_seq((length, width))] + [whole(shape) for shape in small_shapes],
                scratch_shapes=[pltpu.VMEM((LANES, length), F32), pltpu.VMEM((LANES, LANES), F32)],
                **finish_specs,
            ),
            out_shape=[seq_f32] + [jax.ShapeDtypeStruct(shape, F32) for shape in small_shapes],
            compiler_params=params(60),
            cost_estimate=finish_cost,
            name="finish",
        )(own_arr, values_in, pos, aux, h1, small, sums)
        grad_router, grad_proj, grad_vec, grad_one, grad_two, map_total = small_sums
        return (
            result.reshape(batches * length, width),
            gin.reshape(batches * length, width),
            grad_one[0],
            gq,
            gk,
            gv,
            go,
            grad_two[0],
            grad_router.T,
            map_total,
            grad_proj.T,
            grad_vec.T,
            grad_gate,
            grad_up,
            grad_down,
        )

    result = pl.pallas_call(
        result_kernel,
        grid_spec=pltpu.PrefetchScalarGridSpec(
            in_specs=finish_in,
            out_specs=per_seq((length, width)),
            scratch_shapes=[pltpu.VMEM((LANES, length), F32)],
            **finish_specs,
        ),
        out_shape=seq_f32,
        compiler_params=params(40),
        cost_estimate=finish_cost,
        name="result",
    )(own_arr, values_in, pos, aux, h1, small)

    part = lax.psum_scatter(jnp.concatenate([grad_attn, grad_wo], axis=1), "grp", scatter_dimension=0, tiled=True)
    attn_total = lax.psum(part, "rep").astype(F32)
    sgrad = jnp.where(iota((16, 1), 0) == kinds + 6, gain_one[0:1], sgrad)
    packed = jnp.concatenate([sgrad, jnp.pad(grad_map, ((0, 0), (0, width - LANES)))], axis=0)
    packed = lax.psum(packed, ("rep", "grp"))
    sums = lax.dynamic_slice_in_dim(packed[0:16], g * rows_d, rows_d, axis=1).T
    map_total = packed[16:, 0:kinds].T
    return (
        result.reshape(batches * length, width),
        gin.reshape(batches * length, width),
        sums[:, kinds + 6],
        attn_total[:, 0:width],
        attn_total[:, width : 2 * width],
        attn_total[:, 2 * width : 3 * width],
        attn_total[:, 3 * width :],
        sums[:, kinds + 7],
        sums[:, 0:kinds],
        map_total,
        sums[:, kinds : kinds + 4],
        sums[:, kinds + 4 : kinds + 6],
        grad_gate,
        grad_up,
        grad_down,
    )


def solution(mesh):
    rows = P(("rep", "grp"), None)
    in_specs = (
        (rows,) * 5
        + (P("grp"),)
        + (P("grp", None),) * 4
        + (P("grp"), P("grp", None), P(), P("grp", None), P("grp", None))
        + (P("grp", None, None),) * 3
    )
    out_specs = (
        (rows,) * 2
        + (P("grp"),)
        + (P("grp", None),) * 4
        + (P("grp"), P("grp", None), P(), P("grp", None), P("grp", None))
        + (P("grp", None, None),) * 3
    )
    body = functools.partial(local, mesh.shape["rep"], mesh.shape["grp"])
    return jax.shard_map(body, mesh=mesh, in_specs=in_specs, out_specs=out_specs, check_vma=False)
```

```python
import functools

import jax
import jax.numpy as jnp
import numpy as np
from jax import lax
from jax.experimental import pallas as pl
from jax.experimental.pallas import tpu as pltpu
from jax.sharding import PartitionSpec as P

HEAD_DIM = 64
BLOCK = 256
EPS = 1e-05
NEG = -1000000000.0
F32 = jnp.float32
BF16 = jnp.bfloat16
LANES = 128


def nn(a, b):
    return lax.dot_general(a, b, (((1,), (0,)), ((), ())), preferred_element_type=F32)


def nt(a, b):
    return lax.dot_general(a, b, (((1,), (1,)), ((), ())), preferred_element_type=F32)


def tn(a, b):
    return lax.dot_general(a, b, (((0,), (0,)), ((), ())), preferred_element_type=F32)


def iota(shape, dim):
    return lax.broadcasted_iota(jnp.int32, shape, dim)


def split2(values):
    high = values.astype(BF16)
    low = (values - high.astype(F32)).astype(BF16)
    return high, low


def whole(shape, buffers=None):
    zeros = (0,) * len(shape)
    if buffers:
        return pl.BlockSpec(shape, lambda *_: zeros, pipeline_mode=pl.Buffered(buffers))
    return pl.BlockSpec(shape, lambda *_: zeros)


def per_seq(shape):
    tail = (0,) * len(shape)
    return pl.BlockSpec((1,) + shape, lambda b, *_: (b,) + tail)


def same_document(segments):
    hot = jnp.where(segments == iota((16, segments.shape[1]), 0), 1.0, 0.0).astype(BF16)
    return tn(hot, hot) > 0.5


def rms_scale(values):
    return lax.rsqrt(jnp.mean(values * values, axis=-1, keepdims=True) + EPS)


def slot_mask(position_row, capacity):
    places = iota((capacity, position_row.shape[1]), 0).astype(F32)
    return jnp.where(places == position_row, 1.0, 0.0).astype(BF16)


def grad_rows_kernel(own_ref, routes_ref, grad_ref, r0, r1, r2, r3, pos_ref):
    own = own_ref[0]
    kinds, length = pos_ref.shape[1:]
    capacity = r0.shape[1]
    ids = iota((kinds, length), 0)
    first = routes_ref[0:1, :] == ids
    second = routes_ref[1:2, :] == ids
    hits = jnp.where(first | second, 1.0, 0.0)
    before = jnp.where(iota((length, length), 0) < iota((length, length), 1), 1.0, 0.0)
    slots = nn(hits.astype(BF16), before.astype(BF16))
    pos_ref[0] = jnp.where(hits > 0.0, slots, -1.0)
    for number, rows in enumerate((r0, r1, r2, r3)):
        line = pos_ref[0, pl.ds(own ^ number, 1), :]
        rows[0] = nn(slot_mask(line, capacity), grad_ref[0]).astype(BF16)


def swap_halves(values, low_half):
    return jnp.where(low_half, pltpu.roll(values, 96, 1), pltpu.roll(values, 32, 1))


def sequence_forward(
    x_ref,
    segments,
    routes,
    prev_ref,
    map_ref,
    small_ref,
    wq_ref,
    wk_ref,
    wv_ref,
    wo_ref,
    cos_ref,
    sin_ref,
    pos_ref,
    q_ref,
    k_ref,
    v_ref,
    o_ref,
    h_ref,
    lse_ref,
    aux_ref,
    rows_at,
    bias_ref,
    proj_ref,
    expert_of,
    between=None,
):
    length, width = x_ref.shape[1:]
    kinds = pos_ref.shape[1]
    capacity = length // 2
    tokens = x_ref[0].astype(F32)
    gain_one = small_ref[kinds + 6 : kinds + 7, :]
    gain_two = small_ref[kinds + 7 : kinds + 8, :]
    a1 = (tokens * rms_scale(tokens) * gain_one).astype(BF16)
    lane = iota((1, LANES), 1)
    low_half = (lane % HEAD_DIM) < (HEAD_DIM // 2)
    first_head = lane < HEAD_DIM
    mask_a = jnp.where(first_head, 1.0, 0.0).astype(BF16)
    mask_b = jnp.where(first_head, 0.0, 1.0).astype(BF16)
    pairs = width // LANES

    for weights, target, scale in ((wq_ref, q_ref, 0.125), (wk_ref, k_ref, 1.0)):
        proj_ref[...] = nn(a1, weights[...])

        def turn(h, carry):
            cols = pl.ds(pl.multiple_of(h * LANES, LANES), LANES)
            part = proj_ref[:, cols]
            turned = part * cos_ref[...] + swap_halves(part, low_half) * sin_ref[...]
            target[0, :, cols] = turned.astype(BF16) * jnp.asarray(scale, BF16)
            return carry

        lax.fori_loop(0, pairs, turn, 0)
    v_ref[0] = nn(a1, wv_ref[...]).astype(BF16)

    allowed = same_document(segments) & (
        iota((length, length), 1) // BLOCK <= iota((length, length), 0) // BLOCK
    )
    bias_ref[...] = jnp.where(allowed, 0.0, NEG)
    lse_ref[...] = jnp.zeros_like(lse_ref)
    if between is not None:
        between()

    def pair(h, carry):
        cols = pl.ds(pl.multiple_of(h * LANES, LANES), LANES)
        for begin in range(0, length, BLOCK):
            end = begin + BLOCK
            queries = q_ref[0, begin:end, cols]
            keys = k_ref[0, 0:end, cols]
            values = v_ref[0, 0:end, cols]
            bias = bias_ref[begin:end, 0:end]
            sums = lse_ref[0, begin:end, :]
            outs = []
            for half, mask in enumerate((mask_a, mask_b)):
                scores = nt(queries * mask, keys) + bias
                top = jnp.max(scores, axis=-1, keepdims=True)
                grown = jnp.exp(scores - top)
                total = jnp.sum(grown, axis=-1, keepdims=True)
                chances = (grown * (1.0 / total)).astype(BF16)
                outs.append(nn(chances, values))
                sums = jnp.where(lane == 2 * h + half, top + jnp.log(total), sums)
            lse_ref[0, begin:end, :] = sums
            o_ref[0, begin:end, cols] = jnp.where(first_head, outs[0], outs[1]).astype(BF16)
        return carry

    lax.fori_loop(0, pairs, pair, 0, unroll=2)

    hidden = tokens + nn(o_ref[0], wo_ref[...])
    h_ref[0] = hidden
    a2 = (hidden * rms_scale(hidden) * gain_two).astype(BF16)
    logits = nt(small_ref[...].astype(BF16), a2)[0:kinds, :]
    for j in range(kinds):
        logits = logits + map_ref[:, j : j + 1] * prev_ref[j : j + 1, :]
    ids = iota((kinds, length), 0)
    first = jnp.where(routes[0:1, :] == ids, 1.0, 0.0)
    second = jnp.where(routes[1:2, :] == ids, 1.0, 0.0)
    one = jnp.sum(logits * first, axis=0, keepdims=True)
    two = jnp.sum(logits * second, axis=0, keepdims=True)
    top = jnp.maximum(one, two)
    grown_one, grown_two = jnp.exp(one - top), jnp.exp(two - top)
    gate_one = grown_one / (grown_one + grown_two)
    gate_two = grown_two / (grown_one + grown_two)
    aux_ref[0, 0:kinds, :] = gate_one * first + gate_two * second
    aux_ref[0, kinds : kinds + 1, :] = gate_one
    aux_ref[0, kinds + 1 : kinds + 2, :] = gate_two
    aux_ref[0, kinds + 2 : kinds + 4, :] = routes.astype(F32)
    aux_ref[0, kinds + 4 :, :] = jnp.zeros((aux_ref.shape[1] - kinds - 4, length), F32)

    place = iota((16, length), 0)

    def send_rows(number, carry):
        rows = rows_at(number)
        mask = slot_mask(pos_ref[0, pl.ds(expert_of(number), 1), :], capacity)
        rows[0, 0:capacity, :] = nn(mask, a2).astype(BF16)
        line = aux_ref[0, pl.ds(expert_of(number), 1), :]
        high = line.astype(BF16).astype(F32)
        mid = (line - high).astype(BF16).astype(F32)
        low = line - high - mid
        parts = jnp.where(place == 0, high, jnp.where(place == 1, mid, jnp.where(place == 2, low, 0.0)))
        spread = nt(parts.astype(BF16), mask)
        filled = jnp.max(pos_ref[0, pl.ds(expert_of(number), 1), :], axis=1, keepdims=True) + 1.0
        spread = jnp.where(iota((16, 1), 0) == 3, filled, spread)
        rows[0, capacity:, 0:capacity] = spread.astype(BF16)
        rows[0, capacity:, capacity:] = jnp.zeros((16, width - capacity), BF16)
        return carry

    lax.fori_loop(0, 4, send_rows, 0)


def forward_kernel(
    own_ref,
    x_ref,
    seg_ref,
    routes_ref,
    prev_ref,
    map_ref,
    small_ref,
    wq_ref,
    wk_ref,
    wv_ref,
    wo_ref,
    cos_ref,
    sin_ref,
    pos_ref,
    q_ref,
    k_ref,
    v_ref,
    o_ref,
    h_ref,
    lse_ref,
    aux_ref,
    rows_ref,
    bias_ref,
    proj_ref,
):
    own = own_ref[0]
    sequence_forward(
        x_ref,
        seg_ref[0],
        routes_ref[...],
        prev_ref,
        map_ref,
        small_ref,
        wq_ref,
        wk_ref,
        wv_ref,
        wo_ref,
        cos_ref,
        sin_ref,
        pos_ref,
        q_ref,
        k_ref,
        v_ref,
        o_ref,
        h_ref,
        lse_ref,
        aux_ref,
        lambda number: rows_ref.at[number],
        bias_ref,
        proj_ref,
        lambda number: own ^ number,
    )


MESH = pl.DeviceIdType.MESH


class Place:
    def __init__(self, group):
        self.group = group
        self.planes = group // 4
        self.g = lax.axis_index("grp")
        self.y = lax.axis_index("rep")
        self.core = self.g % 2
        self.x = (self.g // 2) % 2
        self.z = self.g // 4
        self.core_peer = (self.y, self.g + 1 - 2 * self.core)
        self.x_peer = (self.y, self.g + 2 - 4 * self.x)
        self.y_peer = (1 - self.y, self.g)
        self.xy_peer = (1 - self.y, self.g + 2 - 4 * self.x)
        self.plane_peers = (None, self.x_peer, self.y_peer, self.xy_peer)

    def z_peer(self, k):
        return (self.y, (self.g + 4 * k) % self.group)

    def block(self, z, x, core):
        return (z * 2 + x) * 2 + core

    def expert(self, number):
        return 2 * ((self.y + number // 2) % 2) + (self.x + number % 2) % 2

    def barrier(self, peers):
        semaphore = pltpu.get_barrier_semaphore()
        for peer in peers:
            pl.semaphore_signal(semaphore, inc=1, device_id=peer, device_id_type=MESH)
        pl.semaphore_wait(semaphore, len(peers))


def remote(src, dst, send, recv, peer):
    return pltpu.make_async_remote_copy(
        src_ref=src, dst_ref=dst, send_sem=send, recv_sem=recv, device_id=peer, device_id_type=MESH
    )


def fused_forward_kernel(
    group,
    x_ref,
    seg_ref,
    routes_ref,
    prev_ref,
    map_ref,
    grad_ref,
    coarse_ref,
    fine_ref,
    shard_refs,
    small_refs,
    gate4_ref,
    up4_ref,
    down4_ref,
    q_ref,
    k_ref,
    v_ref,
    o_ref,
    h_ref,
    lse_ref,
    aux_ref,
    pos_ref,
    small_ref,
    cos_ref,
    sin_ref,
    attn_out_ref,
    attn_o_out_ref,
    rows_in_ref,
    grads_in_ref,
    gate_full_ref,
    up_full_ref,
    down_full_ref,
    attn_ref,
    attn_o_ref,
    bias_ref,
    proj_ref,
    rows_ref,
    grows_ref,
    tile_ref,
    map_t_ref,
    attn_send,
    attn_recv,
    ffn_local,
    ffn_send,
    ffn_recv,
    out_sem,
    row_local,
    row_send,
    row_recv,
):
    step = pl.program_id(0)
    last = pl.num_programs(0) - 1
    here = Place(group)
    planes = here.planes
    batches, kinds, length = pos_ref.shape
    width = x_ref.shape[2]
    capacity = length // 2
    shards = (attn_ref, attn_o_ref)
    experts = ((gate4_ref, gate_full_ref), (up4_ref, up_full_ref), (down4_ref, down_full_ref))
    depth = shard_refs[0].shape[0]
    mine = here.block(here.z, here.x, here.core)

    def rows_of(block):
        return pl.ds(pl.multiple_of(block * depth, 16), depth)

    def attn_part(t, block, part):
        full = shards[t]
        half = full.shape[1] // 2
        if part is None:
            return full.at[rows_of(block), :]
        return full.at[rows_of(block), pl.ds(pl.multiple_of(part * half, LANES), half)]

    def attn_copy(t, slot, z, x, part, peer):
        ref = attn_part(t, here.block(z, x, here.core), part)
        return remote(ref, ref, attn_send.at[t, slot], attn_recv.at[t, slot], peer)

    def to_z(t, k):
        return attn_copy(t, k, here.z, here.x, None, here.z_peer(1 if k == 0 else planes - 1))

    def from_z(t, k):
        return attn_copy(t, k, z_at(planes - 1 if k == 0 else 1), here.x, None, here.x_peer)

    def pass_z(t, k):
        z = z_at(planes - 1 if k == 0 else 1)
        return attn_copy(t, 2 + k, z, here.x, k, here.z_peer(1 if k == 0 else planes - 1))

    def passed_z(t, k):
        return attn_copy(t, 2 + k, z_at(2), here.x, k, here.x_peer)

    def to_x(t, step_z):
        return attn_copy(t, 4 + step_z, z_at(step_z), here.x, here.y, here.x_peer)

    def from_x(t, step_z):
        return attn_copy(t, 4 + step_z, z_at(step_z), 1 - here.x, here.y, here.x_peer)

    def to_y(t, step_z):
        return attn_copy(t, 4 + planes + step_z, z_at(step_z), 1 - here.x, here.y, here.y_peer)

    def from_y(t, step_z):
        return attn_copy(t, 4 + planes + step_z, z_at(step_z), 1 - here.x, 1 - here.y, here.y_peer)

    def to_core(t, step_z, x):
        return attn_copy(t, 4 + 2 * planes + 2 * step_z + x, z_at(step_z), here.x if x == 0 else 1 - here.x, None, here.core_peer)

    def from_core(t, step_z, x):
        ref = attn_part(t, here.block(z_at(step_z), here.x if x == 0 else 1 - here.x, 1 - here.core), None)
        slot = 4 + 2 * planes + 2 * step_z + x
        return remote(ref, ref, attn_send.at[t, slot], attn_recv.at[t, slot], here.core_peer)

    def z_at(k):
        return (here.z + k) % planes

    def ffn_to_x(j):
        source, full = experts[j]
        return remote(
            source.at[here.expert(1)],
            full.at[here.z, here.x, here.core],
            ffn_send.at[j, 0],
            ffn_recv.at[j, 0],
            here.x_peer,
        )

    def ffn_from_x(j):
        source, full = experts[j]
        return remote(
            source.at[here.expert(1)],
            full.at[here.z, 1 - here.x, here.core],
            ffn_send.at[j, 0],
            ffn_recv.at[j, 0],
            here.x_peer,
        )

    def ffn_mine(j):
        source, full = experts[j]
        return pltpu.make_async_copy(source.at[here.expert(0)], full.at[here.z, here.x, here.core], ffn_local.at[j])

    def ffn_copy(j, slot, z, x, core, peer):
        full = experts[j][1]
        part = full.at[z, :, core] if x is None else full.at[z, x, core]
        return remote(part, part, ffn_send.at[j, slot], ffn_recv.at[j, slot], peer)

    def ffn_to_z(j, k):
        return ffn_copy(j, 1 + k, here.z, None, here.core, here.z_peer(1 if k == 0 else planes - 1))

    def ffn_from_z(j, k):
        return ffn_copy(j, 1 + k, z_at(planes - 1 if k == 0 else 1), None, here.core, here.x_peer)

    def ffn_pass_z(j, k):
        z = z_at(planes - 1 if k == 0 else 1)
        return ffn_copy(j, 3 + k, z, k, here.core, here.z_peer(1 if k == 0 else planes - 1))

    def ffn_passed_z(j, k):
        return ffn_copy(j, 3 + k, z_at(2), k, here.core, here.x_peer)

    def ffn_to_core(j, step_z):
        return ffn_copy(j, 5 + step_z, z_at(step_z), None, here.core, here.core_peer)

    def ffn_from_core(j, step_z):
        return ffn_copy(j, 5 + step_z, z_at(step_z), None, 1 - here.core, here.core_peer)

    def row_copy(kind, member, number):
        source, target = ((grows_ref, grads_in_ref), (rows_ref, rows_in_ref))[kind]
        src, dst = source.at[member, number], target.at[number, member]
        if number == 0:
            return pltpu.make_async_copy(src, dst, row_local.at[kind, member])
        return remote(
            src,
            dst,
            row_send.at[kind, member, number],
            row_recv.at[kind, member, number],
            here.plane_peers[number],
        )

    def outs(t):
        full, target = ((attn_ref, attn_out_ref), (attn_o_ref, attn_o_out_ref))[t]
        return pltpu.make_async_copy(full, target, out_sem.at[t])

    @pl.when(step == 0)
    def _():
        for j in range(3):
            ffn_mine(j).start()
        for part in range(3):
            attn_ref[rows_of(mine), part * width : (part + 1) * width] = shard_refs[part][...].astype(BF16)
        attn_o_ref[rows_of(mine), :] = shard_refs[3][...].astype(BF16)
        tile_ref[...] = jnp.zeros_like(tile_ref)
        at = 0
        for part in small_refs:
            tile_ref[at : at + part.shape[0], 0:depth] = part[...]
            at += part.shape[0]
        tile_ref[at : at + kinds, 0:kinds] = map_ref[...]
        turned = jnp.transpose(tile_ref[...])
        map_t_ref[...] = pltpu.roll(turned[0:kinds, :], LANES - kinds - 8, 1)
        attn_ref[rows_of(mine), 3 * width : 3 * width + LANES] = turned[0:depth, :].astype(BF16)
        attn_ref[rows_of(mine), 3 * width + LANES :] = jnp.zeros((depth, LANES), BF16)
        here.barrier(
            [here.core_peer, here.x_peer, here.y_peer, here.xy_peer, here.z_peer(1), here.z_peer(planes - 1)]
        )
        for t in range(2):
            to_z(t, 0).start()
            to_z(t, 1).start()
            to_x(t, 0).start()
            to_core(t, 0, 0).start()
        for j in range(3):
            ffn_to_x(j).start()

        ids = iota((kinds, length), 0)
        before = jnp.where(iota((length, length), 0) < iota((length, length), 1), 1.0, 0.0).astype(BF16)
        for member in range(batches):
            first = routes_ref[0:1, member * length : (member + 1) * length] == ids
            second = routes_ref[1:2, member * length : (member + 1) * length] == ids
            hits = jnp.where(first | second, 1.0, 0.0)
            pos_ref[member] = jnp.where(hits > 0.0, nn(hits.astype(BF16), before), -1.0)

        def grad_rows(index, carry):
            member, number = index // 4, index % 4
            line = pos_ref[member, pl.ds(here.expert(number), 1), :]
            grows_ref[member, number] = nn(slot_mask(line, capacity), grad_ref[member]).astype(BF16)
            return carry

        lax.fori_loop(0, 4 * batches, grad_rows, 0)
        for member in range(batches):
            row_copy(0, member, 0).start()
            row_copy(0, member, 2).start()

        for high in range(coarse_ref.shape[1]):
            rows = slice(high * fine_ref.shape[1], (high + 1) * fine_ref.shape[1])
            cos_high, sin_high = coarse_ref[0, high : high + 1, :], coarse_ref[1, high : high + 1, :]
            cos_ref[rows, :] = cos_high * fine_ref[0] - sin_high * fine_ref[1]
            sin_ref[rows, :] = (sin_high * fine_ref[0] + cos_high * fine_ref[1]) * fine_ref[2]

        for t in range(2):
            for k, step_z in enumerate((planes - 1, 1)):
                from_z(t, k).wait_recv()
                pass_z(t, k).start()
                to_x(t, step_z).start()
                to_core(t, step_z, 0).start()
        for t in range(2):
            from_x(t, 0).wait_recv()
            to_y(t, 0).start()
        for j in range(3):
            ffn_mine(j).wait()
            ffn_from_x(j).wait_recv()
            ffn_to_z(j, 0).start()
            ffn_to_z(j, 1).start()
            ffn_to_core(j, 0).start()
        for t in range(2):
            passed_z(t, 0).wait_recv()
            passed_z(t, 1).wait_recv()
            to_x(t, 2).start()
            to_core(t, 2, 0).start()
        for member in range(batches):
            row_copy(0, member, 1).start()
            row_copy(0, member, 3).start()
        for t in range(2):
            for step_z in (planes - 1, 1, 2):
                from_x(t, step_z).wait_recv()
                to_y(t, step_z).start()
        for t in range(2):
            for step_z in (0, planes - 1, 1, 2):
                from_y(t, step_z).wait_recv()
                to_core(t, step_z, 1).start()
        for t in range(2):
            for step_z in range(planes):
                for x in range(2):
                    from_core(t, step_z, x).wait_recv()
        for t in range(2):
            outs(t).start()
        small_ref[...] = jnp.transpose(attn_ref[:, 3 * width : 3 * width + LANES].astype(F32))[0 : kinds + 8, :]

    def between():
        @pl.when(step == last)
        def _():
            for j in range(3):
                for k, step_z in enumerate((planes - 1, 1)):
                    ffn_from_z(j, k).wait_recv()
                    ffn_pass_z(j, k).start()
                    ffn_to_core(j, step_z).start()

    sequence_forward(
        x_ref,
        seg_ref[pl.ds(step, 1), :],
        routes_ref[:, pl.ds(pl.multiple_of(step * length, LANES), length)],
        prev_ref,
        map_t_ref,
        small_ref,
        attn_ref.at[:, 0:width],
        attn_ref.at[:, width : 2 * width],
        attn_ref.at[:, 2 * width : 3 * width],
        attn_o_ref,
        cos_ref,
        sin_ref,
        pos_ref.at[pl.ds(step, 1)],
        q_ref,
        k_ref,
        v_ref,
        o_ref,
        h_ref,
        lse_ref,
        aux_ref,
        lambda number: rows_ref.at[pl.ds(step, 1), number],
        bias_ref,
        proj_ref,
        here.expert,
        between,
    )
    for member in range(batches):

        @pl.when(step == member)
        def _():
            for number in range(4):
                row_copy(1, member, number).start()

    @pl.when(step == last)
    def _():
        for j in range(3):
            for k in range(2):
                ffn_passed_z(j, k).wait_recv()
            ffn_to_core(j, 2).start()
        for t in range(2):
            outs(t).wait()
            for k in range(2):
                to_z(t, k).wait_send()
                pass_z(t, k).wait_send()
            for step_z in range(planes):
                to_x(t, step_z).wait_send()
                to_y(t, step_z).wait_send()
                for x in range(2):
                    to_core(t, step_z, x).wait_send()
        for j in range(3):
            ffn_to_x(j).wait_send()
            for k in range(2):
                ffn_to_z(j, k).wait_send()
                ffn_pass_z(j, k).wait_send()
            for step_z in range(planes):
                ffn_to_core(j, step_z).wait_send()
                ffn_from_core(j, step_z).wait_recv()
        for kind in range(2):
            for member in range(batches):
                for number in range(4):
                    copy = row_copy(kind, member, number)
                    copy.wait()


def expert_kernel(
    a_ref,
    g_ref,
    gate_ref,
    up_ref,
    down_ref,
    v_ref,
    d_ref,
    grad_gate_ref,
    grad_up_ref,
    grad_down_ref,
    rows_ref,
    grads_ref,
    gates_ref,
    rows_t_ref,
    grads_t_ref,
    places_ref,
    acc_value_ref,
    acc_input_ref,
    acc_gate_ref,
    acc_up_ref,
    acc_down_ref,
    share_ref,
    sems,
):
    step = pl.program_id(0)
    last = pl.num_programs(0) - 1
    batches, capacity, width = g_ref.shape[1:]
    blocks = 4 * batches

    @pl.when(step == 0)
    def _():
        copies = []
        for number in range(4):
            rows, grads = a_ref.at[number], g_ref.at[number]
            for member in range(batches):
                block = number * batches + member
                span = pl.ds(block * capacity, capacity)
                copies.append(
                    pltpu.make_async_copy(
                        rows.at[member, pl.ds(capacity, 16), pl.ds(0, capacity)],
                        gates_ref.at[block],
                        sems.at[3 * block],
                    )
                )
                copies.append(
                    pltpu.make_async_copy(
                        rows.at[member, pl.ds(0, capacity), :], rows_ref.at[span, :], sems.at[3 * block + 1]
                    )
                )
                copies.append(
                    pltpu.make_async_copy(grads.at[member], grads_ref.at[span, :], sems.at[3 * block + 2])
                )
        for copy in copies:
            copy.start()
        for copy in copies:
            copy.wait()
        same = iota((capacity, capacity), 0) == iota((capacity, capacity), 1)
        spare = jnp.zeros((capacity, width), BF16)
        rows_ref[blocks * capacity :, :] = spare
        grads_ref[blocks * capacity :, :] = spare
        share_ref[...] = jnp.zeros_like(share_ref)

        def pack(block, place):
            span = pl.ds(pl.multiple_of(block * capacity, capacity), capacity)
            target = pl.ds(pl.multiple_of(place, 16), capacity)
            parts = gates_ref[block].astype(F32)
            count = jnp.max(parts[3:4, :]).astype(jnp.int32)
            line = jnp.sum(parts[0:3, :], axis=0, keepdims=True)
            column = jnp.sum(jnp.where(same, line, 0.0), axis=1, keepdims=True)
            rows = rows_ref[span, :]
            grads = (grads_ref[span, :].astype(F32) * column).astype(BF16)
            rows_ref[target, :] = rows
            grads_ref[target, :] = grads
            places_ref[block] = place
            return place + (count + 15) // 16 * 16

        total = lax.fori_loop(0, blocks, pack, 0)
        target = pl.ds(pl.multiple_of(total, 16), capacity)
        rows_ref[target, :] = spare
        grads_ref[target, :] = spare
        places_ref[blocks] = (total + capacity - 1) // capacity

        def turn(block, carry):
            span = pl.ds(pl.multiple_of(block * capacity, capacity), capacity)
            grads_t_ref[:, span] = jnp.transpose(grads_ref[span, :])
            rows_t_ref[:, span] = jnp.transpose(rows_ref[span, :])
            return carry

        lax.fori_loop(0, places_ref[blocks], turn, 0)

    acc_gate_ref[...] = jnp.zeros_like(acc_gate_ref)
    acc_up_ref[...] = jnp.zeros_like(acc_up_ref)
    acc_down_ref[...] = jnp.zeros_like(acc_down_ref)

    def work(block, carry):
        span = pl.ds(pl.multiple_of(block * capacity, capacity), capacity)
        rows = rows_ref[span, :]
        grads = grads_ref[span, :]
        gate = nn(rows, gate_ref[...])
        up = nn(rows, up_ref[...])
        back = nt(grads, down_ref[...])
        sig = 1.0 / (1.0 + jnp.exp(-gate))
        silu = gate * sig
        act = (silu * up).astype(BF16)
        grad_gate = (back * up * (sig * (1.0 + gate * (1.0 - sig)))).astype(BF16)
        grad_up = (back * silu).astype(BF16)
        value = nn(act, down_ref[...])
        grad_rows = nt(grad_gate, gate_ref[...]) + nt(grad_up, up_ref[...])
        rows_t = rows_t_ref[:, span]
        acc_gate_ref[...] += nn(rows_t, grad_gate)
        acc_up_ref[...] += nn(rows_t, grad_up)
        acc_down_ref[...] += nn(grads_t_ref[:, span], act)
        share = jnp.broadcast_to(
            jnp.sum(act.astype(F32) * back, axis=1, keepdims=True), (capacity, LANES)
        )

        @pl.when(step == 0)
        def _():
            share_ref[span, :] = share
            acc_value_ref[span, :] = value
            acc_input_ref[span, :] = grad_rows

        @pl.when(step > 0)
        def _():
            share_ref[span, :] += share

        @pl.when((step > 0) & (step < last))
        def _():
            acc_value_ref[span, :] += value
            acc_input_ref[span, :] += grad_rows

        @pl.when(step == last)
        def _():
            rows_ref[span, :] = (acc_value_ref[span, :] + value).astype(BF16)
            grads_ref[span, :] = (acc_input_ref[span, :] + grad_rows).astype(BF16)

        return carry

    lax.fori_loop(0, places_ref[blocks], work, 0)
    grad_gate_ref[...] = acc_gate_ref[...].astype(BF16)
    grad_up_ref[...] = acc_up_ref[...].astype(BF16)
    grad_down_ref[...] = jnp.transpose(acc_down_ref[...].astype(BF16))

    @pl.when(step == last)
    def _():
        same = iota((capacity, capacity), 0) == iota((capacity, capacity), 1)
        place = iota((16, capacity), 0)

        def shares(block, carry):
            column = share_ref[pl.ds(pl.multiple_of(places_ref[block], 16), capacity), 0:1]
            line = jnp.sum(jnp.where(same, column, 0.0), axis=0, keepdims=True)
            high = line.astype(BF16).astype(F32)
            mid = (line - high).astype(BF16).astype(F32)
            low = line - high - mid
            parts = jnp.where(place == 0, high, jnp.where(place == 1, mid, jnp.where(place == 2, low, 0.0)))
            gates_ref[block] = parts.astype(BF16)
            return carry

        lax.fori_loop(0, blocks, shares, 0)
        copies = []
        for number in range(4):
            values, grads = v_ref.at[number], d_ref.at[number]
            for member in range(batches):
                block = number * batches + member
                span = pl.ds(pl.multiple_of(places_ref[block], 16), capacity)
                copies.append(pltpu.make_async_copy(rows_ref.at[span, :], values.at[member], sems.at[3 * block]))
                copies.append(
                    pltpu.make_async_copy(
                        grads_ref.at[span, :], grads.at[member, pl.ds(0, capacity), :], sems.at[3 * block + 1]
                    )
                )
                copies.append(
                    pltpu.make_async_copy(
                        gates_ref.at[block],
                        grads.at[member, pl.ds(capacity, 16), pl.ds(0, capacity)],
                        sems.at[3 * block + 2],
                    )
                )
        for copy in copies:
            copy.start()
        for copy in copies:
            copy.wait()


def constant_mix(zs, index):
    za, zb = zs[:, index : index + 1], zs[:, index + 1 : index + 2]
    top = jnp.maximum(za, zb)
    ea, eb = jnp.exp(za - top), jnp.exp(zb - top)
    return ea / (ea + eb), eb / (ea + eb)


def token_columns(pos_ref, aux_ref, cols_ref):
    kinds, length = pos_ref.shape[1:]
    cols_ref[0:kinds, :] = pos_ref[0]
    cols_ref[kinds : kinds + 16, :] = aux_ref[0]
    cols_ref[kinds + 16 :, :] = jnp.zeros((LANES - kinds - 16, length), F32)
    return jnp.transpose(cols_ref[...])


def column(source, index):
    return jnp.sum(jnp.where(iota((1, LANES), 1) == index, source, 0.0), axis=1, keepdims=True)


def result_kernel(own_ref, v_ref, pos_ref, aux_ref, h_ref, small_ref, out_ref, cols_ref):
    block_output(own_ref, v_ref, pos_ref, aux_ref, h_ref, small_ref, out_ref, cols_ref)


def finish_kernel(
    own_ref,
    v_ref,
    pos_ref,
    aux_ref,
    h_ref,
    small_ref,
    sums_ref,
    out_ref,
    gq_ref,
    gk_ref,
    gv_ref,
    go_ref,
    router_ref,
    proj_ref,
    vec_ref,
    gain_one_ref,
    gain_two_ref,
    map_ref,
    cols_ref,
    tile_ref,
):
    @pl.when(pl.program_id(0) == 0)
    def _():
        depth, width = gq_ref.shape
        kinds = pos_ref.shape[1]
        for part, ref in enumerate((gq_ref, gk_ref, gv_ref, go_ref)):
            ref[...] = sums_ref[:, part * width : (part + 1) * width]
        small = sums_ref[:, 4 * width : 4 * width + LANES]
        tile_ref[...] = jnp.zeros_like(tile_ref)
        tile_ref[0:depth, :] = small
        turned = jnp.transpose(tile_ref[...])
        at = 0
        for ref in (router_ref, proj_ref, vec_ref, gain_one_ref, gain_two_ref):
            ref[...] = turned[at : at + ref.shape[0], 0:depth]
            at += ref.shape[0]
        map_ref[...] = pltpu.roll(small[0:kinds, :], LANES - kinds - 8, 1)[:, 0:kinds]

    block_output(own_ref, v_ref, pos_ref, aux_ref, h_ref, small_ref, out_ref, cols_ref)


def block_output(own_ref, v_ref, pos_ref, aux_ref, h_ref, small_ref, out_ref, cols_ref):
    own = own_ref[0]
    length, width = h_ref.shape[1:]
    kinds = pos_ref.shape[1]
    ffn = kinds - 4
    capacity = v_ref.shape[2]
    hidden = h_ref[0]
    n2 = hidden * rms_scale(hidden) * small_ref[kinds + 7 : kinds + 8, :]
    n2_high, n2_low = split2(n2)
    small = small_ref[...].astype(BF16)
    cols = token_columns(pos_ref, aux_ref, cols_ref)
    out_ref[0] = hidden
    slot_lane = iota((1, capacity), 1).astype(F32)

    def take(number, carry):
        expert = own ^ number
        mask = jnp.where(column(cols, expert) == slot_lane, 1.0, 0.0).astype(BF16)
        out_ref[0] += column(cols, kinds + expert) * nn(mask, v_ref[number, 0])
        return carry

    lax.fori_loop(0, 4, take, 0)
    result = out_ref[0]
    mixes = nt(n2_high, small) + nt(n2_low, small)
    share = column(cols, kinds + ffn + 1)
    for constant in range(2):
        weight = column(cols, kinds + ffn + 2 + constant)
        alpha_a, alpha_b = constant_mix(mixes, kinds + 2 * constant)
        result = result + (weight * alpha_b) * small_ref[kinds + 4 + constant : kinds + 5 + constant, :]
        share = share + weight * alpha_a
    out_ref[0] = result + share * n2


def sequence_combine(
    step,
    d_ref,
    pos_ref,
    aux_ref,
    prev_ref,
    h_ref,
    g_ref,
    o_ref,
    small_ref,
    wo_ref,
    dh_ref,
    dob_ref,
    sgrad_ref,
    grad_map_ref,
    acc_ref,
    cols_ref,
    expert_of,
    arrived=lambda: None,
):
    length, width = h_ref.shape[1:]
    kinds = pos_ref.shape[1]
    ffn = kinds - 4
    capacity = d_ref.shape[2] - 16
    hidden = h_ref[0]
    inverse = rms_scale(hidden)
    gain = small_ref[kinds + 7 : kinds + 8, :]
    n2 = hidden * inverse * gain
    n2_high, n2_low = split2(n2)
    grad_low = g_ref[0]
    grad = grad_low.astype(F32)
    small = small_ref[...].astype(BF16)
    cols = token_columns(pos_ref, aux_ref, cols_ref)
    lane = iota((1, LANES), 1)
    gate_one = column(cols, 2 * kinds)
    gate_two = column(cols, 2 * kinds + 1)
    ids = lane.astype(F32)
    hot_one = jnp.where(column(cols, 2 * kinds + 2) == ids, 1.0, 0.0)
    hot_two = jnp.where(column(cols, 2 * kinds + 3) == ids, 1.0, 0.0)

    shares = jnp.zeros((length, LANES), F32)
    mixes = nt(n2_high, small) + nt(n2_low, small)
    inner = nt(grad_low, small)
    with_n2 = jnp.sum(grad * n2, axis=1, keepdims=True)
    weight_copy = column(cols, kinds + ffn + 1)
    shares = jnp.where(lane == ffn + 1, weight_copy * with_n2, shares)
    share = weight_copy
    coefs = jnp.zeros((length, LANES), F32)
    for constant in range(2):
        weight = column(cols, kinds + ffn + 2 + constant)
        alpha_a, alpha_b = constant_mix(mixes, kinds + 2 * constant)
        with_vec = inner[:, kinds + 4 + constant : kinds + 5 + constant]
        share = share + weight * alpha_a
        da = weight * with_n2
        db = weight * with_vec
        mean = alpha_a * da + alpha_b * db
        shares = jnp.where(lane == ffn + 2 + constant, mean, shares)
        coefs = jnp.where(lane == kinds + 2 * constant, alpha_a * (da - mean), coefs)
        coefs = jnp.where(lane == kinds + 2 * constant + 1, alpha_b * (db - mean), coefs)
        coefs = jnp.where(lane == kinds + 4 + constant, weight * alpha_b, coefs)

    arrived()
    dh_ref[0] = jnp.zeros((length, width), F32)
    slot_lane = iota((1, capacity), 1).astype(F32)

    def take(number, shares):
        expert = expert_of(number)
        mask = jnp.where(column(cols, expert) == slot_lane, 1.0, 0.0).astype(BF16)
        dh_ref[0] += nn(mask, d_ref[number, 0, 0:capacity, :])
        parts = nt(mask, d_ref[number, 0, capacity:, 0:capacity])
        return jnp.where(lane == expert, jnp.sum(parts, axis=1, keepdims=True), shares)

    shares = lax.fori_loop(0, 4, take, shares)
    grad_n2 = dh_ref[0]

    share_one = jnp.sum(shares * hot_one, axis=1, keepdims=True)
    share_two = jnp.sum(shares * hot_two, axis=1, keepdims=True)
    both = share_one + share_two
    dlogits = (share_one - gate_one * both) * hot_one + (share_two - gate_two * both) * hot_two
    coefs = jnp.where(lane < kinds, dlogits, coefs)
    back = jnp.where(lane < kinds + 4, coefs, 0.0)[:, 0:16]
    back_high, back_low = split2(back)
    grad_n2 = grad_n2 + nn(back_high, small) + nn(back_low, small) + share * grad

    coefs_t = jnp.transpose(coefs)[0:16, :]
    high, low = split2(coefs_t)
    by_n2 = nn(high, n2_high) + nn(low, n2_high)
    by_low = nn(high, n2_low)
    by_grad = nn(high, grad_low) + nn(low, grad_low)
    row = iota((16, 1), 0)
    parts = jnp.where(row < kinds, by_n2, jnp.where(row < kinds + 4, by_n2 + by_low, by_grad))
    gain_part = jnp.sum(grad_n2 * hidden * inverse, axis=0, keepdims=True)
    parts = jnp.where(row == kinds + 7, gain_part, jnp.where(row == kinds + 6, 0.0, parts))
    dlog_t = coefs_t[0:kinds, :]
    map_lane = iota((kinds, LANES), 1)
    map_part = jnp.zeros((kinds, LANES), F32)
    for j in range(kinds):
        map_part = jnp.where(
            map_lane == j, jnp.sum(dlog_t * prev_ref[j : j + 1, :], axis=1, keepdims=True), map_part
        )

    scaled = gain * grad_n2
    inner_mean = jnp.mean(scaled * hidden, axis=-1, keepdims=True)
    dh = grad + inverse * scaled - hidden * (inverse * inverse * inverse) * inner_mean
    dh_ref[0] = dh
    db = dh.astype(BF16)
    dob_ref[0] = nt(db, wo_ref[...]).astype(BF16)
    wo_part = nn(jnp.transpose(o_ref[0]), db)

    @pl.when(step == 0)
    def _():
        acc_ref[...] = wo_part
        sgrad_ref[...] = parts
        grad_map_ref[...] = map_part

    @pl.when(step > 0)
    def _():
        acc_ref[...] += wo_part
        sgrad_ref[...] += parts
        grad_map_ref[...] += map_part


def combine_kernel(
    own_ref,
    d_ref,
    pos_ref,
    aux_ref,
    prev_ref,
    h_ref,
    g_ref,
    o_ref,
    small_ref,
    wo_ref,
    dh_ref,
    dob_ref,
    grad_wo_ref,
    sgrad_ref,
    grad_map_ref,
    acc_ref,
    cols_ref,
):
    own = own_ref[0]
    step = pl.program_id(0)
    sequence_combine(
        step,
        d_ref,
        pos_ref,
        aux_ref,
        prev_ref,
        h_ref,
        g_ref,
        o_ref,
        small_ref,
        wo_ref,
        dh_ref,
        dob_ref,
        sgrad_ref,
        grad_map_ref,
        acc_ref,
        cols_ref,
        lambda number: own ^ number,
    )

    @pl.when(step == pl.num_programs(0) - 1)
    def _():
        grad_wo_ref[...] = acc_ref[...].astype(BF16)


def backward_tables(segments, lse_ref, bias_ref, lse_t_ref):
    length = lse_ref.shape[1]
    allowed = same_document(segments) & (
        iota((length, length), 0) // BLOCK <= iota((length, length), 1) // BLOCK
    )
    bias_ref[...] = jnp.where(allowed, 0.0, NEG)
    lse_t_ref[...] = jnp.transpose(lse_ref[0])


def sequence_backward(
    step,
    x_ref,
    q_ref,
    k_ref,
    v_ref,
    dob_ref,
    dh_ref,
    small_ref,
    w_ref,
    cos_ref,
    sin_ref,
    gin_ref,
    gain_ref,
    bias_ref,
    lse_t_ref,
    dqkv_ref,
    acc_ref,
    between=lambda: None,
):
    length, width = x_ref.shape[1:]
    kinds = small_ref.shape[0] - 8
    pairs = width // LANES
    lane = iota((1, LANES), 1)
    low_half = (lane % HEAD_DIM) < (HEAD_DIM // 2)
    first_head = lane < HEAD_DIM
    mask_a = jnp.where(first_head, 1.0, 0.0).astype(BF16)
    mask_b = jnp.where(first_head, 0.0, 1.0).astype(BF16)

    def pair(h, carry):
        cols = pl.ds(pl.multiple_of(h * LANES, LANES), LANES)
        keys_t = jnp.transpose(k_ref[0, :, cols])
        grad_keys = None
        grad_values = None
        grad_queries = []
        for begin in range(0, length, BLOCK):
            end = begin + BLOCK
            queries = q_ref[0, begin:end, cols]
            outs = dob_ref[0, begin:end, cols]
            keys = k_ref[0, 0:end, cols]
            values = v_ref[0, 0:end, cols]
            queries = jnp.concatenate([queries * mask_a, queries * mask_b], axis=0)
            outs = jnp.concatenate([outs * mask_a, outs * mask_b], axis=0)
            bias = bias_ref[0:end, begin:end]
            bias = jnp.concatenate([bias, bias], axis=1)
            line = jnp.concatenate(
                [lse_t_ref[pl.ds(2 * h, 1), begin:end], lse_t_ref[pl.ds(2 * h + 1, 1), begin:end]], axis=1
            )
            chances = jnp.exp(nt(keys, queries) + bias - line)
            grad_chances = nt(values, outs)
            delta = jnp.sum(chances * grad_chances, axis=0, keepdims=True)
            grad_scores = (chances * (grad_chances - delta)).astype(BF16)
            dv = nn(chances.astype(BF16), outs)
            dk = nn(grad_scores, queries)
            dq = jnp.transpose(nn(keys_t[:, 0:end], grad_scores))
            grad_queries.append(jnp.where(first_head, dq[0:BLOCK], dq[BLOCK:]))
            if grad_keys is None:
                grad_keys, grad_values = dk, dv
            else:
                grad_keys = jnp.concatenate([grad_keys + dk[0:begin], dk[begin:]], axis=0)
                grad_values = jnp.concatenate([grad_values + dv[0:begin], dv[begin:]], axis=0)
        dq = jnp.concatenate(grad_queries, axis=0) * 0.125
        dq = dq * cos_ref[...] - swap_halves(dq, low_half) * sin_ref[...]
        dk = grad_keys * cos_ref[...] - swap_halves(grad_keys, low_half) * sin_ref[...]
        dqkv_ref[:, cols] = dq.astype(BF16)
        dqkv_ref[:, pl.ds(pl.multiple_of(width + h * LANES, LANES), LANES)] = dk.astype(BF16)
        dqkv_ref[:, pl.ds(pl.multiple_of(2 * width + h * LANES, LANES), LANES)] = grad_values.astype(BF16)
        return carry

    lax.fori_loop(0, pairs, pair, 0, unroll=2)
    between()

    tokens = x_ref[0].astype(F32)
    inverse = rms_scale(tokens)
    gain = small_ref[kinds + 6 : kinds + 7, :]
    a1_t = jnp.transpose((tokens * inverse * gain).astype(BF16))

    @pl.when(step == 0)
    def _():
        acc_ref[...] = jnp.zeros_like(acc_ref)

    gin_ref[0] = jnp.zeros((length, width), F32)

    def project(part, carry):
        span = pl.ds(pl.multiple_of(part * width, LANES), width)
        gin_ref[0] += nt(dqkv_ref[:, span], w_ref[:, span])
        acc_ref[:, span] += nn(a1_t, dqkv_ref[:, span])
        return carry

    lax.fori_loop(0, 3, project, 0)
    dn1 = gin_ref[0]
    scaled = gain * dn1
    inner_mean = jnp.mean(scaled * tokens, axis=-1, keepdims=True)
    gin_ref[0] = dh_ref[0] + inverse * scaled - tokens * (inverse * inverse * inverse) * inner_mean
    gain_part = jnp.broadcast_to(jnp.sum(dn1 * tokens * inverse, axis=0, keepdims=True), gain_ref.shape)

    @pl.when(step == 0)
    def _():
        gain_ref[...] = gain_part

    @pl.when(step > 0)
    def _():
        gain_ref[...] += gain_part


def small_table(depth, sgrad_ref, grad_map_ref, gain_ref):
    kinds = grad_map_ref.shape[0]
    width = sgrad_ref.shape[1]
    row = iota((16, 1), 0)
    table = jnp.where(row == kinds + 6, gain_ref[0:1, :], sgrad_ref[...])
    chosen = jnp.where(iota((LANES, width), 1) % depth == iota((LANES, width), 0), 1.0, 0.0).astype(BF16)
    maps = nn(grad_map_ref[...].astype(BF16), chosen)
    table = jnp.concatenate([table, maps, jnp.zeros((LANES - 16 - kinds, width), F32)], axis=0)
    return jnp.transpose(table).astype(BF16)


def backward_kernel(
    x_ref,
    seg_ref,
    q_ref,
    k_ref,
    v_ref,
    dob_ref,
    lse_ref,
    dh_ref,
    small_ref,
    w_ref,
    cos_ref,
    sin_ref,
    gin_ref,
    grad_w_ref,
    gain_ref,
    bias_ref,
    lse_t_ref,
    dqkv_ref,
    acc_ref,
):
    step = pl.program_id(0)
    backward_tables(seg_ref[0], lse_ref, bias_ref, lse_t_ref)
    sequence_backward(
        step,
        x_ref,
        q_ref,
        k_ref,
        v_ref,
        dob_ref,
        dh_ref,
        small_ref,
        w_ref,
        cos_ref,
        sin_ref,
        gin_ref,
        gain_ref,
        bias_ref,
        lse_t_ref,
        dqkv_ref,
        acc_ref,
    )

    @pl.when(step == pl.num_programs(0) - 1)
    def _():
        grad_w_ref[...] = acc_ref[...].astype(BF16)


class ReducedChunk:
    def __init__(self, here, depth, begin, value_of, send_buffer, core_buffer, buffers, out_ref, sems):
        self.here, self.depth, self.begin, self.value_of = here, depth, begin, value_of
        self.send_buffer, self.acc, self.out_ref = send_buffer, core_buffer, out_ref
        y_first, x_first, x_second, y_second, self.z_buffer, self.done, self.other = buffers
        send, recv, z_send, z_recv = sems
        planes, x, y = here.planes, here.x, here.y
        near = planes // 2
        self.half = send_buffer.shape[3] // 2
        self.mine = pl.ds(pl.multiple_of(y * self.half, LANES), self.half)
        theirs = pl.ds(pl.multiple_of((1 - y) * self.half, LANES), self.half)
        self.received = (y_first, x_first, x_second, y_second)
        acc = core_buffer
        self.swap = remote(send_buffer, acc, send.at[0], recv.at[0], here.core_peer)
        self.y_first = remote(acc.at[0:near, :, :, theirs], y_first, send.at[1], recv.at[1], here.y_peer)
        self.x_first = remote(acc.at[near:planes, 1 - x], x_first, send.at[2], recv.at[2], here.x_peer)
        self.x_second = remote(acc.at[0:near, 1 - x, :, self.mine], x_second, send.at[3], recv.at[3], here.x_peer)
        self.y_second = remote(acc.at[near:planes, x, :, theirs], y_second, send.at[4], recv.at[4], here.y_peer)
        self.along = [
            remote(
                acc.at[(here.z + k) % planes, x, :, self.mine],
                self.z_buffer.at[k - 1],
                z_send.at[k - 1],
                z_recv.at[k - 1],
                here.z_peer(k),
            )
            for k in range(1, planes)
        ]
        self.back = remote(self.done, self.other, send.at[5], recv.at[5], here.y_peer)
        self.phases = (self.first, self.second, self.third, self.fourth, self.fifth)

    def rows_of(self, z, column, core):
        return pl.ds(pl.multiple_of(self.here.block(z, column, core) * self.depth, 16), self.depth)

    def lower(self):
        def body(z, carry):
            for column in range(2):
                rows = self.rows_of(z, column, 1 - self.here.core)
                self.send_buffer[z, column] = self.value_of(rows).astype(BF16)
            return carry

        lax.fori_loop(0, self.here.planes, body, 0)

    def add(self, target, source):
        target[...] = (target[...].astype(F32) + source[...].astype(F32)).astype(BF16)

    def first(self):
        self.swap.wait_recv()

        def body(z, carry):
            for column in range(2):
                own = self.value_of(self.rows_of(z, column, self.here.core)).astype(F32)
                self.acc[z, column] = (own + self.acc[z, column].astype(F32)).astype(BF16)
            return carry

        lax.fori_loop(0, self.here.planes, body, 0)
        self.y_first.start()
        self.x_first.start()

    def second(self):
        planes = self.here.planes
        self.y_first.wait_recv()
        for z in range(planes // 2):
            for column in range(2):
                self.add(self.acc.at[z, column, :, self.mine], self.received[0].at[z, column])
        self.x_second.start()
        self.x_first.wait_recv()
        for z in range(planes // 2, planes):
            self.add(self.acc.at[z, self.here.x], self.received[1].at[z - planes // 2])
        self.y_second.start()

    def third(self):
        planes = self.here.planes
        self.x_second.wait_recv()
        for z in range(planes // 2):
            self.add(self.acc.at[z, self.here.x, :, self.mine], self.received[2].at[z])
        self.y_second.wait_recv()
        for z in range(planes // 2, planes):
            self.add(self.acc.at[z, self.here.x, :, self.mine], self.received[3].at[z - planes // 2])
        for copy in self.along:
            copy.start()

    def fourth(self):
        total = self.acc[self.here.z, self.here.x, :, self.mine].astype(F32)
        for k, copy in enumerate(self.along):
            copy.wait_recv()
            total = total + self.z_buffer[k].astype(F32)
        self.done[...] = total.astype(BF16)
        self.back.start()

    def fifth(self):
        self.back.wait_recv()
        y = self.here.y
        spot = pl.ds(pl.multiple_of(self.begin + y * self.half, LANES), self.half)
        other = pl.ds(pl.multiple_of(self.begin + (1 - y) * self.half, LANES), self.half)
        self.out_ref[:, spot] = self.done[...].astype(F32)
        self.out_ref[:, other] = self.other[...].astype(F32)
        for copy in [self.swap, self.y_first, self.x_first, self.x_second, self.y_second, self.back] + self.along:
            copy.wait_send()


def attention_columns(acc_ref, acc_wo_ref, table_ref, begin, columns, rows):
    pieces = []
    width = acc_wo_ref.shape[1]
    for start, size, ref in (
        (0, 3 * width, acc_ref),
        (3 * width, width, acc_wo_ref),
        (4 * width, LANES, table_ref),
        (4 * width + LANES, LANES, None),
    ):
        low, high = max(begin, start) - start, min(begin + columns, start + size) - start
        if low < high:
            if ref is None:
                pieces.append(jnp.zeros((rows.size, high - low), F32))
            else:
                pieces.append(ref[rows, low:high].astype(F32))
    return pieces[0] if len(pieces) == 1 else jnp.concatenate(pieces, axis=1)


def reduce_attention(chunks, free_sem, beside):
    chunks[0].lower()
    pl.semaphore_wait(free_sem, 1)
    chunks[0].swap.start()
    for chunk in chunks[1:]:
        chunk.lower()
        chunk.swap.start()
    phases = len(chunks[0].phases)
    for step in range(len(chunks) + phases - 1):
        for number, chunk in enumerate(chunks):
            if 0 <= step - number < phases:
                chunk.phases[step - number]()
        if step in beside:
            beside[step]()


def fused_backward_kernel(
    group,
    depth,
    pos_ref,
    aux_ref,
    prev_ref,
    h_ref,
    g_ref,
    o_ref,
    x_ref,
    seg_ref,
    q_ref,
    k_ref,
    v_ref,
    lse_ref,
    small_ref,
    w_ref,
    wo_ref,
    cos_ref,
    sin_ref,
    d_ref,
    val_ref,
    gate_ref,
    up_ref,
    down_ref,
    gin_ref,
    sums_ref,
    d_in_ref,
    val_in_ref,
    gate_out_ref,
    up_out_ref,
    down_out_ref,
    acc_ref,
    acc_wo_ref,
    table_ref,
    send_buffers,
    chunk_buffers,
    cols_ref,
    dh_ref,
    dob_ref,
    sgrad_ref,
    grad_map_ref,
    gain_ref,
    bias_ref,
    lse_t_ref,
    dqkv_ref,
    rows_ref,
    gate_own,
    up_own,
    down_own,
    gate_swap,
    up_swap,
    down_swap,
    gate_near,
    up_near,
    down_near,
    gate_far,
    up_far,
    down_far,
    row_local,
    row_send,
    row_recv,
    ffn_local,
    ffn_send,
    ffn_recv,
    free_sem,
    reduce_send,
    reduce_recv,
    reduce_z_send,
    reduce_z_recv,
):
    step = pl.program_id(0)
    last = pl.num_programs(0) - 1
    here = Place(group)
    planes = here.planes
    batches = d_ref.shape[1]
    width = x_ref.shape[2]
    grads = (gate_ref, up_ref, down_ref)
    owns = (gate_own, up_own, down_own)
    swaps = (gate_swap, up_swap, down_swap)
    nears = (gate_near, up_near, down_near)
    fars = (gate_far, up_far, down_far)
    outs = (gate_out_ref, up_out_ref, down_out_ref)
    side = (here.z_peer(1), here.z_peer(planes - 1))

    def z_at(k):
        return (here.z + k) % planes

    def row_copy(kind, member, number):
        source, target = ((d_ref, d_in_ref), (val_ref, val_in_ref))[kind]
        src, dst = source.at[number, member], target.at[number, member]
        if number == 0:
            return pltpu.make_async_copy(src, dst, row_local.at[batches * 4 + member])
        return remote(
            src, dst, row_send.at[kind, member, number], row_recv.at[kind, member, number], here.plane_peers[number]
        )

    def load_rows(member, number):
        source = d_ref if number == 0 else d_in_ref
        return pltpu.make_async_copy(
            source.at[number, member], rows_ref.at[number, 0], row_local.at[member * 4 + number]
        )

    def own_copy(j):
        return pltpu.make_async_copy(grads[j].at[:, :, here.core], owns[j], ffn_local.at[j, 0])

    def swap_copy(j):
        return remote(
            grads[j].at[:, :, 1 - here.core], swaps[j], ffn_send.at[j, 0], ffn_recv.at[j, 0], here.core_peer
        )

    def near_copy(j, k):
        return remote(
            owns[j].at[z_at(2), k], nears[j].at[k], ffn_send.at[j, 1 + k], ffn_recv.at[j, 1 + k], side[k]
        )

    def far_copy(j, k):
        return remote(
            owns[j].at[z_at(1 if k == 0 else planes - 1)],
            fars[j].at[k],
            ffn_send.at[j, 3 + k],
            ffn_recv.at[j, 3 + k],
            side[k],
        )

    def plane_copy(j, number):
        x = here.x if number % 2 == 0 else 1 - here.x
        src, dst = owns[j].at[here.z, x], outs[j].at[here.expert(0)]
        if number == 0:
            return pltpu.make_async_copy(src, dst, ffn_local.at[j, 1])
        return remote(
            src, dst, ffn_send.at[j, 4 + number], ffn_recv.at[j, 4 + number], here.plane_peers[number]
        )

    def plane_arrival(j, number):
        dst = outs[j].at[here.expert(number)]
        return remote(
            dst, dst, ffn_send.at[j, 4 + number], ffn_recv.at[j, 4 + number], here.plane_peers[number]
        )

    def add(target, *sources):
        value = target[...].astype(F32)
        for source in sources:
            value = value + source[...].astype(F32)
        target[...] = value.astype(BF16)

    @pl.when(step == 0)
    def _():
        for j in range(3):
            own_copy(j).start()
        here.barrier(
            [here.core_peer, here.x_peer, here.y_peer, here.xy_peer] + [here.z_peer(k) for k in range(1, planes)]
        )
        for number in range(1, 4):
            row_copy(0, 0, number).start()
        for j in range(3):
            swap_copy(j).start()
        for j in range(3):
            own_copy(j).wait()
            swap_copy(j).wait_recv()
            for x in range(2):

                def add_core(z, carry):
                    add(owns[j].at[z, x], swaps[j].at[z, x])
                    return carry

                lax.fori_loop(0, planes, add_core, 0)
            near_copy(j, 0).start()
            near_copy(j, 1).start()
        pl.semaphore_signal(free_sem, inc=1, device_id=here.core_peer, device_id_type=MESH)

    def arrived():
        for member in range(batches):

            @pl.when(step == member)
            def _():
                for number in range(1, 4):
                    row_copy(0, member, number).wait_recv()
                if member + 1 < batches:
                    for number in range(1, 4):
                        row_copy(0, member + 1, number).start()
                for number in range(4):
                    row_copy(1, member, number).start()
                for number in range(4):
                    load_rows(member, number).start()
                for number in range(4):
                    load_rows(member, number).wait()

    backward_tables(seg_ref[pl.ds(step, 1), :], lse_ref, bias_ref, lse_t_ref)
    sequence_combine(
        step,
        rows_ref,
        pos_ref,
        aux_ref,
        prev_ref,
        h_ref,
        g_ref,
        o_ref,
        small_ref,
        wo_ref,
        dh_ref,
        dob_ref,
        sgrad_ref,
        grad_map_ref,
        acc_wo_ref,
        cols_ref,
        here.expert,
        arrived,
    )

    def start_far(j):
        far_copy(j, 0).start()
        far_copy(j, 1).start()

    def finish_far(j):
        for k in range(2):
            far_copy(j, k).wait_recv()
        for x in range(2):
            add(owns[j].at[here.z, x], fars[j].at[0, x], fars[j].at[1, x])
        for number in range(4):
            plane_copy(j, number).start()

    def between():
        @pl.when(step == 0)
        def _():
            for j in range(3):
                for k in range(2):
                    near_copy(j, k).wait_recv()
                    add(owns[j].at[z_at(1 if k == 0 else planes - 1), k], nears[j].at[k])
            start_far(0)

        @pl.when(step == last)
        def _():
            finish_far(0)
            start_far(2)

    sequence_backward(
        step,
        x_ref,
        q_ref,
        k_ref,
        v_ref,
        dob_ref,
        dh_ref,
        small_ref,
        w_ref,
        cos_ref,
        sin_ref,
        gin_ref,
        gain_ref,
        bias_ref,
        lse_t_ref,
        dqkv_ref,
        acc_ref,
        between,
    )

    @pl.when(step == 0)
    def _():
        start_far(1)

    @pl.when(step == last)
    def _():
        table_ref[...] = small_table(depth, sgrad_ref, grad_map_ref, gain_ref)
        chunks = []
        begin = 0
        for number, (send_buffer, buffers) in enumerate(zip(send_buffers, chunk_buffers)):
            columns = send_buffer.shape[3]
            home, place = (gate_swap, begin) if begin < gate_swap.shape[3] else (up_swap, begin - gate_swap.shape[3])
            chunks.append(
                ReducedChunk(
                    here,
                    depth,
                    begin,
                    functools.partial(attention_columns, acc_ref, acc_wo_ref, table_ref, begin, columns),
                    send_buffer,
                    home.at[:, :, :, place : place + columns],
                    buffers,
                    sums_ref,
                    (
                        reduce_send.at[number],
                        reduce_recv.at[number],
                        reduce_z_send.at[number],
                        reduce_z_recv.at[number],
                    ),
                )
            )
            begin += columns
        reduce_attention(chunks, free_sem, {0: lambda: finish_far(1), len(chunks): lambda: finish_far(2)})
        for j in range(3):
            swap_copy(j).wait_send()
            for k in range(2):
                near_copy(j, k).wait_send()
                far_copy(j, k).wait_send()
            plane_copy(j, 0).wait()
            for number in range(1, 4):
                plane_copy(j, number).wait_send()
                plane_arrival(j, number).wait_recv()
        for member in range(batches):
            row_copy(1, member, 0).wait()
            for number in range(1, 4):
                row_copy(0, member, number).wait_send()
                row_copy(1, member, number).wait()


def params(limit_mib):
    return pltpu.CompilerParams(vmem_limit_bytes=limit_mib * 1024 * 1024, dimension_semantics=("arbitrary",))


def rotary(length):
    halfway = HEAD_DIM // 2
    frequency = 10000.0 ** (-jnp.arange(halfway).astype(F32) / halfway)
    angles = jnp.arange(length).astype(F32)[:, None] * frequency[None, :]
    cosine, sine = jnp.cos(angles), jnp.sin(angles)
    return (
        jnp.concatenate([cosine] * 4, axis=1),
        jnp.concatenate([-sine, sine, -sine, sine], axis=1),
    )


def rotary_parts(length):
    halfway = HEAD_DIM // 2
    frequency = 10000.0 ** (-np.arange(halfway) / halfway)
    step = 32
    sign = np.tile(np.repeat([-1.0, 1.0], halfway), LANES // HEAD_DIM)

    def table(positions):
        angles = np.tile(positions[:, None] * frequency[None, :], (1, LANES // halfway))
        return np.cos(angles), np.sin(angles)

    coarse = table(np.arange(0, length, step))
    fine = table(np.arange(step))
    signs = np.broadcast_to(sign, fine[0].shape)
    return jnp.asarray(np.stack(coarse), F32), jnp.asarray(np.stack(fine + (signs,)), F32)


def local(
    reps,
    group,
    block_input,
    prev_logits,
    routes,
    segments,
    grad_out,
    gain_attn,
    w_query,
    w_key,
    w_value,
    w_output,
    gain_mix,
    router,
    route_map,
    const_proj,
    const_vec,
    w_gate,
    w_up,
    w_down,
):
    batches, length = segments.shape
    width = block_input.shape[1]
    kinds = router.shape[1]
    ffn = w_gate.shape[1]
    hidden = w_gate.shape[2]
    rows_d = w_gate.shape[0]
    rows_f = w_down.shape[0]
    capacity = length // 2
    planes = group // 4
    assert reps == 2 and ffn == 4 and group % 4 == 0
    g = lax.axis_index("grp")
    y = lax.axis_index("rep")
    core = g % 2
    x = (g // 2) % 2
    z = g // 4
    own = (2 * y + x).astype(jnp.int32)
    own_arr = own.reshape(1)

    x_flip = [(i, i ^ 2) for i in range(group)]
    core_flip = [(i, i ^ 1) for i in range(group)]
    y_flip = [(0, 1), (1, 0)]
    xy_flip = [(r * group + i, (1 - r) * group + (i ^ 2)) for r in range(2) for i in range(group)]

    def z_shift(k):
        return [(i, (i + 4 * k) % group) for i in range(group)]

    def to_plane(parts):
        return [
            parts[0],
            lax.ppermute(parts[1], "grp", x_flip),
            lax.ppermute(parts[2], "rep", y_flip),
            lax.ppermute(parts[3], ("rep", "grp"), xy_flip),
        ]

    tokens = block_input.reshape(batches, length, width)
    grads = grad_out.reshape(batches, length, width)
    route_rows = routes.T
    prev_rows = prev_logits.T
    row_spec = pl.BlockSpec((2, length), lambda b, *_: (0, b))
    prev_spec = pl.BlockSpec((kinds, length), lambda b, *_: (0, b))

    def spec_w(j):
        return pl.BlockSpec((width, width), lambda b, *_: (0, j), pipeline_mode=pl.Buffered(1))

    row_shape = jax.ShapeDtypeStruct((batches, capacity, width), BF16)
    seq_bf16 = jax.ShapeDtypeStruct((batches, length, width), BF16)
    seq_f32 = jax.ShapeDtypeStruct((batches, length, width), F32)
    fused = planes == 4 and rows_d % 16 == 0 and rows_f % 16 == 0
    if fused:
        any_space = pl.BlockSpec(memory_space=pl.ANY)
        coarse, fine = rotary_parts(length)
        smalls = [router.T, const_proj.T, const_vec.T, gain_attn[None], gain_mix[None]]
        out_struct = jax.ShapeDtypeStruct
        (
            q, k, v, o, h1, lse, aux, pos, small, cos, sin, attn, attn_o, a_rows, grad_rows, gate_full, up_full, down_full,
        ) = pl.pallas_call(
            functools.partial(fused_forward_kernel, group),
            grid=(batches,),
            in_specs=[
                per_seq((length, width)),
                whole((batches, length)),
                whole((2, batches * length)),
                prev_spec,
                whole((kinds, kinds)),
                whole((batches, length, width)),
                whole(coarse.shape),
                whole(fine.shape),
                [whole((rows_d, width))] * 4,
                [whole(part.shape) for part in smalls],
            ]
            + [any_space] * 3,
            out_specs=[per_seq((length, width))] * 5
            + [
                per_seq((length, LANES)),
                per_seq((16, length)),
                whole((batches, kinds, length)),
                whole((kinds + 8, width)),
                whole((length, LANES)),
                whole((length, LANES)),
            ]
            + [any_space] * 7,
            scratch_shapes=[
                pltpu.VMEM((width, 3 * width + 2 * LANES), BF16),
                pltpu.VMEM((width, width), BF16),
                pltpu.VMEM((length, length), F32),
                pltpu.VMEM((length, width), F32),
                pltpu.VMEM((batches, 4, capacity + 16, width), BF16),
                pltpu.VMEM((batches, 4, capacity, width), BF16),
                pltpu.VMEM((LANES, LANES), F32),
                pltpu.VMEM((kinds, LANES), F32),
                pltpu.SemaphoreType.DMA((2, 4 + 4 * planes)),
                pltpu.SemaphoreType.DMA((2, 4 + 4 * planes)),
                pltpu.SemaphoreType.DMA((3,)),
                pltpu.SemaphoreType.DMA((3, 5 + planes)),
                pltpu.SemaphoreType.DMA((3, 5 + planes)),
                pltpu.SemaphoreType.DMA((2,)),
                pltpu.SemaphoreType.DMA((2, batches)),
                pltpu.SemaphoreType.DMA((2, batches, 4)),
                pltpu.SemaphoreType.DMA((2, batches, 4)),
            ],
            out_shape=[seq_bf16] * 4
            + [
                seq_f32,
                out_struct((batches, length, LANES), F32),
                out_struct((batches, 16, length), F32),
                out_struct((batches, kinds, length), F32),
                out_struct((kinds + 8, width), F32),
                out_struct((length, LANES), F32),
                out_struct((length, LANES), F32),
                out_struct((width, 3 * width + 2 * LANES), BF16),
                out_struct((width, width), BF16),
                out_struct((4, batches, capacity + 16, width), BF16),
                out_struct((4, batches, capacity, width), BF16),
                out_struct((planes, 2, 2, rows_d, hidden), BF16),
                out_struct((planes, 2, 2, rows_d, hidden), BF16),
                out_struct((planes, 2, 2, rows_f, width), BF16),
            ],
            compiler_params=pltpu.CompilerParams(
                vmem_limit_bytes=58 * 1024 * 1024,
                dimension_semantics=("arbitrary",),
                collective_id=1,
                has_side_effects=True,
            ),
            cost_estimate=pl.CostEstimate(flops=40 * 10**9, bytes_accessed=60 * 10**6, transcendentals=10**7),
            name="fused_forward",
        )(
            tokens, segments, route_rows, prev_rows, route_map, grads, coarse, fine,
            [w_query, w_key, w_value, w_output], smalls,
            w_gate.astype(BF16).transpose(1, 0, 2),
            w_up.astype(BF16).transpose(1, 0, 2),
            w_down.astype(BF16).transpose(1, 0, 2),
        )
        gate_full = gate_full.reshape(width, hidden)
        up_full = up_full.reshape(width, hidden)
        down_full = down_full.reshape(hidden, width)
    else:
        cos, sin = rotary(length)
        small_shard = jnp.concatenate(
            [router, const_proj, const_vec, gain_attn[:, None], gain_mix[:, None]], axis=1
        ).astype(BF16)
        small_shard = jnp.pad(small_shard, ((0, 0), (0, 2 * LANES - small_shard.shape[1])))
        shard = jnp.concatenate([w.astype(BF16) for w in (w_query, w_key, w_value)] + [small_shard], axis=1)
        shard_o = w_output.astype(BF16)
        attn = lax.all_gather(shard, "grp", axis=0, tiled=True)
        attn_o = lax.all_gather(shard_o, "grp", axis=0, tiled=True)
        small = attn[:, 3 * width : 3 * width + kinds + 8].astype(F32).T

        def pick(array, expert):
            return lax.dynamic_index_in_dim(array, expert, axis=1, keepdims=False)

        def gather_expert(mine, other):
            crossed = lax.ppermute(other, "grp", x_flip)
            both = jnp.where(x == 0, jnp.stack([mine, crossed]), jnp.stack([crossed, mine]))
            pieces = [both] + [lax.ppermute(both, "grp", z_shift(k)) for k in range(1, planes)]
            stacked = jnp.stack(pieces)
            half = jnp.take(stacked, (z - jnp.arange(planes)) % planes, axis=0)
            swapped = lax.ppermute(half, "grp", core_flip)
            return jnp.where(core == 0, jnp.stack([half, swapped], axis=2), jnp.stack([swapped, half], axis=2))

        gate_up = gather_expert(
            jnp.stack([pick(w_gate, own), pick(w_up, own)]).astype(BF16),
            jnp.stack([pick(w_gate, own ^ 1), pick(w_up, own ^ 1)]).astype(BF16),
        )
        down = gather_expert(pick(w_down, own).astype(BF16), pick(w_down, own ^ 1).astype(BF16))
        gate_full = gate_up[:, :, :, 0].reshape(width, hidden)
        up_full = gate_up[:, :, :, 1].reshape(width, hidden)
        down_full = down.reshape(hidden, width)

        *grad_rows, pos = pl.pallas_call(
            grad_rows_kernel,
            grid_spec=pltpu.PrefetchScalarGridSpec(
                num_scalar_prefetch=1,
                grid=(batches,),
                in_specs=[row_spec, per_seq((length, width))],
                out_specs=[per_seq((capacity, width))] * 4 + [per_seq((kinds, length))],
            ),
            out_shape=[row_shape] * 4 + [jax.ShapeDtypeStruct((batches, kinds, length), F32)],
            compiler_params=params(32),
            cost_estimate=pl.CostEstimate(flops=4 * 10**9, bytes_accessed=8 * 10**6, transcendentals=0),
            name="grad_rows",
        )(own_arr, route_rows, grads)
        grad_rows = to_plane(grad_rows)

        q, k, v, o, h1, lse, aux, a_rows = pl.pallas_call(
            forward_kernel,
            grid_spec=pltpu.PrefetchScalarGridSpec(
                num_scalar_prefetch=1,
                grid=(batches,),
                in_specs=[
                    per_seq((length, width)),
                    per_seq((1, length)),
                    row_spec,
                    prev_spec,
                    whole((kinds, kinds)),
                    whole((kinds + 8, width)),
                    spec_w(0),
                    spec_w(1),
                    spec_w(2),
                    spec_w(0),
                    whole((length, LANES)),
                    whole((length, LANES)),
                    per_seq((kinds, length)),
                ],
                out_specs=[per_seq((length, width))] * 5
                + [per_seq((length, LANES)), per_seq((16, length))]
                + [pl.BlockSpec((4, 1, capacity + 16, width), lambda b, *_: (0, b, 0, 0))],
                scratch_shapes=[pltpu.VMEM((length, length), F32), pltpu.VMEM((length, width), F32)],
            ),
            out_shape=[seq_bf16] * 4
            + [
                seq_f32,
                jax.ShapeDtypeStruct((batches, length, LANES), F32),
                jax.ShapeDtypeStruct((batches, 16, length), F32),
            ]
            + [jax.ShapeDtypeStruct((4, batches, capacity + 16, width), BF16)],
            compiler_params=params(56),
            cost_estimate=pl.CostEstimate(flops=20 * 10**9, bytes_accessed=20 * 10**6, transcendentals=10**7),
            name="forward",
        )(own_arr, tokens, segments[:, None], route_rows, prev_rows, route_map.T, small, attn, attn, attn, attn_o, cos, sin, pos)
        a_rows = to_plane([a_rows[i] for i in range(4)])

        a_rows = jnp.stack(a_rows)
        grad_rows = jnp.stack(grad_rows)

    tile = hidden // 4
    total = 4 * batches * capacity
    any_spec = pl.BlockSpec(memory_space=pl.ANY)
    values, input_rows, grad_gate_full, grad_up_full, grad_down_full = pl.pallas_call(
        expert_kernel,
        grid=(hidden // tile,),
        in_specs=[any_spec] * 2
        + [
            pl.BlockSpec((width, tile), lambda f: (0, f)),
            pl.BlockSpec((width, tile), lambda f: (0, f)),
            pl.BlockSpec((tile, width), lambda f: (f, 0)),
        ],
        out_specs=[any_spec] * 2
        + [
            pl.BlockSpec((width, tile), lambda f: (0, f)),
            pl.BlockSpec((width, tile), lambda f: (0, f)),
            pl.BlockSpec((tile, width), lambda f: (f, 0)),
        ],
        scratch_shapes=[
            pltpu.VMEM((total + capacity, width), BF16),
            pltpu.VMEM((total + capacity, width), BF16),
            pltpu.VMEM((4 * batches, 16, capacity), BF16),
            pltpu.VMEM((width, total), BF16),
            pltpu.VMEM((width, total), BF16),
            pltpu.SMEM((4 * batches + 1,), jnp.int32),
            pltpu.VMEM((total, width), F32),
            pltpu.VMEM((total, width), F32),
            pltpu.VMEM((width, tile), F32),
            pltpu.VMEM((width, tile), F32),
            pltpu.VMEM((width, tile), F32),
            pltpu.VMEM((total + capacity, LANES), F32),
            pltpu.SemaphoreType.DMA((12 * batches,)),
        ],
        out_shape=[
            jax.ShapeDtypeStruct((4, batches, capacity, width), BF16),
            jax.ShapeDtypeStruct((4, batches, capacity + 16, width), BF16),
        ]
        + [
            jax.ShapeDtypeStruct((width, hidden), BF16),
            jax.ShapeDtypeStruct((width, hidden), BF16),
            jax.ShapeDtypeStruct((hidden, width), BF16),
        ],
        compiler_params=params(60),
        cost_estimate=pl.CostEstimate(flops=58 * 10**9, bytes_accessed=40 * 10**6, transcendentals=10**7),
        name="expert",
    )(a_rows, grad_rows, gate_full, up_full, down_full)
    if fused:
        columns = 4 * width + 2 * LANES
        once = lambda shape: pl.BlockSpec(
            (1,) + shape, lambda b, *_: (b, 0, 0), pipeline_mode=pl.Buffered(1)
        )
        wide = ((rows_d, hidden), (rows_d, hidden), (rows_f, width))
        near = planes // 2
        parts = (hidden // 2, hidden // 2, width, columns - hidden - width)
        gin, sums, _, values_in, grad_gate, grad_up, grad_down = pl.pallas_call(
            functools.partial(fused_backward_kernel, group, rows_d),
            grid=(batches,),
            in_specs=[
                per_seq((kinds, length)),
                per_seq((16, length)),
                prev_spec,
                once((length, width)),
                once((length, width)),
                once((length, width)),
                once((length, width)),
                whole((batches, length)),
                once((length, width)),
                once((length, width)),
                once((length, width)),
                once((length, LANES)),
                whole((kinds + 8, width), 1),
                pl.BlockSpec((width, 3 * width), lambda b, *_: (0, 0), pipeline_mode=pl.Buffered(1)),
                spec_w(0),
                whole((length, LANES), 1),
                whole((length, LANES), 1),
            ]
            + [any_spec] * 5,
            out_specs=[once((length, width)), whole((rows_d, columns), 1)] + [any_spec] * 5,
            out_shape=[
                seq_f32,
                jax.ShapeDtypeStruct((rows_d, columns), F32),
                jax.ShapeDtypeStruct((4, batches, capacity + 16, width), BF16),
                jax.ShapeDtypeStruct((4, batches, capacity, width), BF16),
            ]
            + [jax.ShapeDtypeStruct((4,) + shape, BF16) for shape in wide],
            scratch_shapes=[
                pltpu.VMEM((width, 3 * width), F32),
                pltpu.VMEM((width, width), F32),
                pltpu.VMEM((width, LANES), BF16),
            ]
            + [[pltpu.VMEM((planes, 2, rows_d, part), BF16) for part in parts]]
            + [
                [[
                    pltpu.VMEM((near, 2, rows_d, part // 2), BF16),
                    pltpu.VMEM((near, rows_d, part), BF16),
                    pltpu.VMEM((near, rows_d, part // 2), BF16),
                    pltpu.VMEM((near, rows_d, part // 2), BF16),
                    pltpu.VMEM((planes - 1, rows_d, part // 2), BF16),
                    pltpu.VMEM((rows_d, part // 2), BF16),
                    pltpu.VMEM((rows_d, part // 2), BF16),
                ] for part in parts]
            ]
            + [
                pltpu.VMEM((LANES, length), F32),
                pltpu.VMEM((1, length, width), F32),
                pltpu.VMEM((1, length, width), BF16),
                pltpu.VMEM((16, width), F32),
                pltpu.VMEM((kinds, LANES), F32),
                pltpu.VMEM((8, width), F32),
                pltpu.VMEM((length, length), F32),
                pltpu.VMEM((LANES, length), F32),
                pltpu.VMEM((length, 3 * width), BF16),
                pltpu.VMEM((4, 1, capacity + 16, width), BF16),
            ]
            + [pltpu.VMEM((planes, 2) + shape, BF16) for shape in wide]
            + [pltpu.VMEM((planes, 2) + shape, BF16) for shape in wide]
            + [pltpu.VMEM((2,) + shape, BF16) for shape in wide]
            + [pltpu.VMEM((2, 2) + shape, BF16) for shape in wide]
            + [
                pltpu.SemaphoreType.DMA((5 * batches,)),
                pltpu.SemaphoreType.DMA((2, batches, 4)),
                pltpu.SemaphoreType.DMA((2, batches, 4)),
                pltpu.SemaphoreType.DMA((3, 2)),
                pltpu.SemaphoreType.DMA((3, 8)),
                pltpu.SemaphoreType.DMA((3, 8)),
                pltpu.SemaphoreType.REGULAR,
                pltpu.SemaphoreType.DMA((len(parts), 6)),
                pltpu.SemaphoreType.DMA((len(parts), 6)),
                pltpu.SemaphoreType.DMA((len(parts), planes - 1)),
                pltpu.SemaphoreType.DMA((len(parts), planes - 1)),
            ],
            compiler_params=pltpu.CompilerParams(
                vmem_limit_bytes=63 * 1024 * 1024,
                dimension_semantics=("arbitrary",),
                collective_id=3,
                has_side_effects=True,
            ),
            cost_estimate=pl.CostEstimate(flops=60 * 10**9, bytes_accessed=60 * 10**6, transcendentals=10**7),
            name="fused_backward",
        )(
            pos, aux, prev_rows, h1, grads, o, tokens, segments, q, k, v, lse, small,
            attn, attn_o, cos, sin, input_rows, values,
            grad_gate_full.reshape(planes, 2, 2, rows_d, hidden),
            grad_up_full.reshape(planes, 2, 2, rows_d, hidden),
            grad_down_full.reshape(planes, 2, 2, rows_f, width),
        )
        grad_gate = grad_gate.transpose(1, 0, 2).astype(F32)
        grad_up = grad_up.transpose(1, 0, 2).astype(F32)
        grad_down = grad_down.transpose(1, 0, 2).astype(F32)
    else:
        values_in = jnp.stack(to_plane([values[i] for i in range(4)]))
        def scatter_expert(full):
            keep = lax.dynamic_index_in_dim(full, core, axis=2, keepdims=False)
            send = lax.dynamic_index_in_dim(full, 1 - core, axis=2, keepdims=False)
            half = (keep.astype(F32) + lax.ppermute(send, "grp", core_flip).astype(F32)).astype(BF16)
            summed = lax.dynamic_index_in_dim(half, z, axis=0, keepdims=False).astype(F32)
            for k in range(1, planes):
                part = lax.dynamic_index_in_dim(half, (z + k) % planes, axis=0, keepdims=False)
                summed = summed + lax.ppermute(part, "grp", z_shift(k)).astype(F32)
            summed = summed.astype(BF16)
            mine = lax.dynamic_index_in_dim(summed, x, axis=0, keepdims=False)
            other = lax.dynamic_index_in_dim(summed, 1 - x, axis=0, keepdims=False)
            arrived = to_plane([mine, other, mine, other])

            def order(first):
                return lambda: tuple(arrived[first ^ e] for e in range(4))

            return lax.switch(own, [order(i) for i in range(4)])

        grad_gate_up = scatter_expert(
            jnp.stack(
                [
                    grad_gate_full.reshape(planes, 2, 2, rows_d, hidden),
                    grad_up_full.reshape(planes, 2, 2, rows_d, hidden),
                ],
                axis=3,
            )
        )
        grad_down = scatter_expert(grad_down_full.reshape(planes, 2, 2, rows_f, width))
        grad_gate = jnp.stack([part[0] for part in grad_gate_up], axis=1).astype(F32)
        grad_up = jnp.stack([part[1] for part in grad_gate_up], axis=1).astype(F32)
        grad_down = jnp.stack(grad_down, axis=1).astype(F32)

        dh1, dob, grad_wo, sgrad, grad_map = pl.pallas_call(
            combine_kernel,
            grid_spec=pltpu.PrefetchScalarGridSpec(
                num_scalar_prefetch=1,
                grid=(batches,),
                in_specs=[pl.BlockSpec((4, 1, capacity + 16, width), lambda b, *_: (0, b, 0, 0))]
                + [
                    per_seq((kinds, length)),
                    per_seq((16, length)),
                    prev_spec,
                    per_seq((length, width)),
                    per_seq((length, width)),
                    per_seq((length, width)),
                    whole((kinds + 8, width)),
                    spec_w(0),
                ],
                out_specs=[per_seq((length, width))] * 2
                + [whole((width, width)), whole((16, width)), whole((kinds, LANES))],
                scratch_shapes=[pltpu.VMEM((width, width), F32), pltpu.VMEM((LANES, length), F32)],
            ),
            out_shape=[
                seq_f32,
                seq_bf16,
                jax.ShapeDtypeStruct((width, width), BF16),
                jax.ShapeDtypeStruct((16, width), F32),
                jax.ShapeDtypeStruct((kinds, LANES), F32),
            ],
            compiler_params=params(56),
            cost_estimate=pl.CostEstimate(flops=12 * 10**9, bytes_accessed=20 * 10**6, transcendentals=10**5),
            name="combine",
        )(own_arr, jnp.stack(to_plane([input_rows[i] for i in range(4)])), pos, aux, prev_rows, h1, grads, o, small, attn_o)

        gin, grad_attn, gain_one = pl.pallas_call(
            backward_kernel,
            grid=(batches,),
            in_specs=[
                per_seq((length, width)),
                per_seq((1, length)),
                per_seq((length, width)),
                per_seq((length, width)),
                per_seq((length, width)),
                per_seq((length, width)),
                per_seq((length, LANES)),
                per_seq((length, width)),
                whole((kinds + 8, width)),
                pl.BlockSpec((width, 3 * width), lambda b, *_: (0, 0), pipeline_mode=pl.Buffered(1)),
                whole((length, LANES)),
                whole((length, LANES)),
            ],
            out_specs=[per_seq((length, width)), whole((width, 3 * width)), whole((8, width))],
            scratch_shapes=[
                pltpu.VMEM((length, length), F32),
                pltpu.VMEM((LANES, length), F32),
                pltpu.VMEM((length, 3 * width), BF16),
                pltpu.VMEM((width, 3 * width), F32),
            ],
            out_shape=[
                seq_f32,
                jax.ShapeDtypeStruct((width, 3 * width), BF16),
                jax.ShapeDtypeStruct((8, width), F32),
            ],
            compiler_params=params(56),
            cost_estimate=pl.CostEstimate(flops=30 * 10**9, bytes_accessed=20 * 10**6, transcendentals=10**7),
            name="backward",
        )(tokens, segments[:, None], q, k, v, dob, lse, dh1, small, attn, cos, sin)

    finish_specs = dict(
        num_scalar_prefetch=1,
        grid=(batches,),
    )
    finish_in = [
        pl.BlockSpec((4, 1, capacity, width), lambda b, *_: (0, b, 0, 0)),
        per_seq((kinds, length)),
        per_seq((16, length)),
        per_seq((length, width)),
        whole((kinds + 8, width)),
    ]
    finish_cost = pl.CostEstimate(flops=4 * 10**9, bytes_accessed=12 * 10**6, transcendentals=0)
    if fused:
        small_shapes = [(rows_d, width)] * 4 + [
            (kinds, rows_d), (4, rows_d), (2, rows_d), (1, rows_d), (1, rows_d), (kinds, kinds)
        ]
        result, gq, gk, gv, go, *small_sums = pl.pallas_call(
            finish_kernel,
            grid_spec=pltpu.PrefetchScalarGridSpec(
                in_specs=finish_in + [whole((rows_d, columns))],
                out_specs=[per_seq((length, width))] + [whole(shape) for shape in small_shapes],
                scratch_shapes=[pltpu.VMEM((LANES, length), F32), pltpu.VMEM((LANES, LANES), F32)],
                **finish_specs,
            ),
            out_shape=[seq_f32] + [jax.ShapeDtypeStruct(shape, F32) for shape in small_shapes],
            compiler_params=params(60),
            cost_estimate=finish_cost,
            name="finish",
        )(own_arr, values_in, pos, aux, h1, small, sums)
        grad_router, grad_proj, grad_vec, grad_one, grad_two, map_total = small_sums
        return (
            result.reshape(batches * length, width),
            gin.reshape(batches * length, width),
            grad_one[0],
            gq,
            gk,
            gv,
            go,
            grad_two[0],
            grad_router.T,
            map_total,
            grad_proj.T,
            grad_vec.T,
            grad_gate,
            grad_up,
            grad_down,
        )

    result = pl.pallas_call(
        result_kernel,
        grid_spec=pltpu.PrefetchScalarGridSpec(
            in_specs=finish_in,
            out_specs=per_seq((length, width)),
            scratch_shapes=[pltpu.VMEM((LANES, length), F32)],
            **finish_specs,
        ),
        out_shape=seq_f32,
        compiler_params=params(40),
        cost_estimate=finish_cost,
        name="result",
    )(own_arr, values_in, pos, aux, h1, small)

    part = lax.psum_scatter(jnp.concatenate([grad_attn, grad_wo], axis=1), "grp", scatter_dimension=0, tiled=True)
    attn_total = lax.psum(part, "rep").astype(F32)
    sgrad = jnp.where(iota((16, 1), 0) == kinds + 6, gain_one[0:1], sgrad)
    packed = jnp.concatenate([sgrad, jnp.pad(grad_map, ((0, 0), (0, width - LANES)))], axis=0)
    packed = lax.psum(packed, ("rep", "grp"))
    sums = lax.dynamic_slice_in_dim(packed[0:16], g * rows_d, rows_d, axis=1).T
    map_total = packed[16:, 0:kinds].T
    return (
        result.reshape(batches * length, width),
        gin.reshape(batches * length, width),
        sums[:, kinds + 6],
        attn_total[:, 0:width],
        attn_total[:, width : 2 * width],
        attn_total[:, 2 * width : 3 * width],
        attn_total[:, 3 * width :],
        sums[:, kinds + 7],
        sums[:, 0:kinds],
        map_total,
        sums[:, kinds : kinds + 4],
        sums[:, kinds + 4 : kinds + 6],
        grad_gate,
        grad_up,
        grad_down,
    )


def solution(mesh):
    rows = P(("rep", "grp"), None)
    in_specs = (
        (rows,) * 5
        + (P("grp"),)
        + (P("grp", None),) * 4
        + (P("grp"), P("grp", None), P(), P("grp", None), P("grp", None))
        + (P("grp", None, None),) * 3
    )
    out_specs = (
        (rows,) * 2
        + (P("grp"),)
        + (P("grp", None),) * 4
        + (P("grp"), P("grp", None), P(), P("grp", None), P("grp", None))
        + (P("grp", None, None),) * 3
    )
    body = functools.partial(local, mesh.shape["rep"], mesh.shape["grp"])
    return jax.shard_map(body, mesh=mesh, in_specs=in_specs, out_specs=out_specs, check_vma=False)
```

```python
import functools

import jax
import jax.numpy as jnp
import numpy as np
from jax import lax
from jax.experimental import pallas as pl
from jax.experimental.pallas import tpu as pltpu
from jax.sharding import PartitionSpec as P

HEAD_DIM = 64
BLOCK = 256
EPS = 1e-05
NEG = -1000000000.0
F32 = jnp.float32
BF16 = jnp.bfloat16
LANES = 128


def nn(a, b):
    return lax.dot_general(a, b, (((1,), (0,)), ((), ())), preferred_element_type=F32)


def nt(a, b):
    return lax.dot_general(a, b, (((1,), (1,)), ((), ())), preferred_element_type=F32)


def tn(a, b):
    return lax.dot_general(a, b, (((0,), (0,)), ((), ())), preferred_element_type=F32)


def iota(shape, dim):
    return lax.broadcasted_iota(jnp.int32, shape, dim)


def split2(values):
    high = values.astype(BF16)
    low = (values - high.astype(F32)).astype(BF16)
    return high, low


def whole(shape, buffers=None):
    zeros = (0,) * len(shape)
    if buffers:
        return pl.BlockSpec(shape, lambda *_: zeros, pipeline_mode=pl.Buffered(buffers))
    return pl.BlockSpec(shape, lambda *_: zeros)


def per_seq(shape):
    tail = (0,) * len(shape)
    return pl.BlockSpec((1,) + shape, lambda b, *_: (b,) + tail)


def same_document(segments):
    hot = jnp.where(segments == iota((16, segments.shape[1]), 0), 1.0, 0.0).astype(BF16)
    return tn(hot, hot) > 0.5


def rms_scale(values):
    return lax.rsqrt(jnp.mean(values * values, axis=-1, keepdims=True) + EPS)


def slot_mask(position_row, capacity):
    places = iota((capacity, position_row.shape[1]), 0).astype(F32)
    return jnp.where(places == position_row, 1.0, 0.0).astype(BF16)


def grad_rows_kernel(own_ref, routes_ref, grad_ref, r0, r1, r2, r3, pos_ref):
    own = own_ref[0]
    kinds, length = pos_ref.shape[1:]
    capacity = r0.shape[1]
    ids = iota((kinds, length), 0)
    first = routes_ref[0:1, :] == ids
    second = routes_ref[1:2, :] == ids
    hits = jnp.where(first | second, 1.0, 0.0)
    before = jnp.where(iota((length, length), 0) < iota((length, length), 1), 1.0, 0.0)
    slots = nn(hits.astype(BF16), before.astype(BF16))
    pos_ref[0] = jnp.where(hits > 0.0, slots, -1.0)
    for number, rows in enumerate((r0, r1, r2, r3)):
        line = pos_ref[0, pl.ds(own ^ number, 1), :]
        rows[0] = nn(slot_mask(line, capacity), grad_ref[0]).astype(BF16)


def swap_halves(values, low_half):
    return jnp.where(low_half, pltpu.roll(values, 96, 1), pltpu.roll(values, 32, 1))


def sequence_forward(
    x_ref,
    segments,
    routes,
    prev_ref,
    map_ref,
    small_ref,
    wq_ref,
    wk_ref,
    wv_ref,
    wo_ref,
    cos_ref,
    sin_ref,
    pos_ref,
    q_ref,
    k_ref,
    v_ref,
    o_ref,
    h_ref,
    lse_ref,
    aux_ref,
    rows_at,
    bias_ref,
    proj_ref,
    expert_of,
    between=None,
):
    length, width = x_ref.shape[1:]
    kinds = pos_ref.shape[1]
    capacity = length // 2
    tokens = x_ref[0].astype(F32)
    gain_one = small_ref[kinds + 6 : kinds + 7, :]
    gain_two = small_ref[kinds + 7 : kinds + 8, :]
    a1 = (tokens * rms_scale(tokens) * gain_one).astype(BF16)
    lane = iota((1, LANES), 1)
    low_half = (lane % HEAD_DIM) < (HEAD_DIM // 2)
    first_head = lane < HEAD_DIM
    mask_a = jnp.where(first_head, 1.0, 0.0).astype(BF16)
    mask_b = jnp.where(first_head, 0.0, 1.0).astype(BF16)
    pairs = width // LANES

    for weights, target, scale in ((wq_ref, q_ref, 0.125), (wk_ref, k_ref, 1.0)):
        proj_ref[...] = nn(a1, weights[...])

        def turn(h, carry):
            cols = pl.ds(pl.multiple_of(h * LANES, LANES), LANES)
            part = proj_ref[:, cols]
            turned = part * cos_ref[...] + swap_halves(part, low_half) * sin_ref[...]
            target[0, :, cols] = turned.astype(BF16) * jnp.asarray(scale, BF16)
            return carry

        lax.fori_loop(0, pairs, turn, 0)
    v_ref[0] = nn(a1, wv_ref[...]).astype(BF16)

    allowed = same_document(segments) & (
        iota((length, length), 1) // BLOCK <= iota((length, length), 0) // BLOCK
    )
    bias_ref[...] = jnp.where(allowed, 0.0, NEG)
    lse_ref[...] = jnp.zeros_like(lse_ref)
    if between is not None:
        between()

    def pair(h, carry):
        cols = pl.ds(pl.multiple_of(h * LANES, LANES), LANES)
        for begin in range(0, length, BLOCK):
            end = begin + BLOCK
            queries = q_ref[0, begin:end, cols]
            keys = k_ref[0, 0:end, cols]
            values = v_ref[0, 0:end, cols]
            bias = bias_ref[begin:end, 0:end]
            sums = lse_ref[0, begin:end, :]
            outs = []
            for half, mask in enumerate((mask_a, mask_b)):
                scores = nt(queries * mask, keys) + bias
                top = jnp.max(scores, axis=-1, keepdims=True)
                grown = jnp.exp(scores - top)
                total = jnp.sum(grown, axis=-1, keepdims=True)
                chances = (grown * (1.0 / total)).astype(BF16)
                outs.append(nn(chances, values))
                sums = jnp.where(lane == 2 * h + half, top + jnp.log(total), sums)
            lse_ref[0, begin:end, :] = sums
            o_ref[0, begin:end, cols] = jnp.where(first_head, outs[0], outs[1]).astype(BF16)
        return carry

    lax.fori_loop(0, pairs, pair, 0, unroll=2)

    hidden = tokens + nn(o_ref[0], wo_ref[...])
    h_ref[0] = hidden
    a2 = (hidden * rms_scale(hidden) * gain_two).astype(BF16)
    logits = nt(small_ref[...].astype(BF16), a2)[0:kinds, :]
    for j in range(kinds):
        logits = logits + map_ref[:, j : j + 1] * prev_ref[j : j + 1, :]
    ids = iota((kinds, length), 0)
    first = jnp.where(routes[0:1, :] == ids, 1.0, 0.0)
    second = jnp.where(routes[1:2, :] == ids, 1.0, 0.0)
    one = jnp.sum(logits * first, axis=0, keepdims=True)
    two = jnp.sum(logits * second, axis=0, keepdims=True)
    top = jnp.maximum(one, two)
    grown_one, grown_two = jnp.exp(one - top), jnp.exp(two - top)
    gate_one = grown_one / (grown_one + grown_two)
    gate_two = grown_two / (grown_one + grown_two)
    aux_ref[0, 0:kinds, :] = gate_one * first + gate_two * second
    aux_ref[0, kinds : kinds + 1, :] = gate_one
    aux_ref[0, kinds + 1 : kinds + 2, :] = gate_two
    aux_ref[0, kinds + 2 : kinds + 4, :] = routes.astype(F32)
    aux_ref[0, kinds + 4 :, :] = jnp.zeros((aux_ref.shape[1] - kinds - 4, length), F32)

    place = iota((16, length), 0)

    def send_rows(number, carry):
        rows = rows_at(number)
        mask = slot_mask(pos_ref[0, pl.ds(expert_of(number), 1), :], capacity)
        rows[0, 0:capacity, :] = nn(mask, a2).astype(BF16)
        line = aux_ref[0, pl.ds(expert_of(number), 1), :]
        high = line.astype(BF16).astype(F32)
        mid = (line - high).astype(BF16).astype(F32)
        low = line - high - mid
        parts = jnp.where(place == 0, high, jnp.where(place == 1, mid, jnp.where(place == 2, low, 0.0)))
        spread = nt(parts.astype(BF16), mask)
        filled = jnp.max(pos_ref[0, pl.ds(expert_of(number), 1), :], axis=1, keepdims=True) + 1.0
        spread = jnp.where(iota((16, 1), 0) == 3, filled, spread)
        rows[0, capacity:, 0:capacity] = spread.astype(BF16)
        rows[0, capacity:, capacity:] = jnp.zeros((16, width - capacity), BF16)
        return carry

    lax.fori_loop(0, 4, send_rows, 0)


def forward_kernel(
    own_ref,
    x_ref,
    seg_ref,
    routes_ref,
    prev_ref,
    map_ref,
    small_ref,
    wq_ref,
    wk_ref,
    wv_ref,
    wo_ref,
    cos_ref,
    sin_ref,
    pos_ref,
    q_ref,
    k_ref,
    v_ref,
    o_ref,
    h_ref,
    lse_ref,
    aux_ref,
    rows_ref,
    bias_ref,
    proj_ref,
):
    own = own_ref[0]
    sequence_forward(
        x_ref,
        seg_ref[0],
        routes_ref[...],
        prev_ref,
        map_ref,
        small_ref,
        wq_ref,
        wk_ref,
        wv_ref,
        wo_ref,
        cos_ref,
        sin_ref,
        pos_ref,
        q_ref,
        k_ref,
        v_ref,
        o_ref,
        h_ref,
        lse_ref,
        aux_ref,
        lambda number: rows_ref.at[number],
        bias_ref,
        proj_ref,
        lambda number: own ^ number,
    )


MESH = pl.DeviceIdType.MESH


class Place:
    def __init__(self, group):
        self.group = group
        self.planes = group // 4
        self.g = lax.axis_index("grp")
        self.y = lax.axis_index("rep")
        self.core = self.g % 2
        self.x = (self.g // 2) % 2
        self.z = self.g // 4
        self.core_peer = (self.y, self.g + 1 - 2 * self.core)
        self.x_peer = (self.y, self.g + 2 - 4 * self.x)
        self.y_peer = (1 - self.y, self.g)
        self.xy_peer = (1 - self.y, self.g + 2 - 4 * self.x)
        self.plane_peers = (None, self.x_peer, self.y_peer, self.xy_peer)

    def z_peer(self, k):
        return (self.y, (self.g + 4 * k) % self.group)

    def block(self, z, x, core):
        return (z * 2 + x) * 2 + core

    def expert(self, number):
        return 2 * ((self.y + number // 2) % 2) + (self.x + number % 2) % 2

    def barrier(self, peers):
        semaphore = pltpu.get_barrier_semaphore()
        for peer in peers:
            pl.semaphore_signal(semaphore, inc=1, device_id=peer, device_id_type=MESH)
        pl.semaphore_wait(semaphore, len(peers))


def remote(src, dst, send, recv, peer):
    return pltpu.make_async_remote_copy(
        src_ref=src, dst_ref=dst, send_sem=send, recv_sem=recv, device_id=peer, device_id_type=MESH
    )


def fused_forward_kernel(
    group,
    x_ref,
    seg_ref,
    routes_ref,
    prev_ref,
    map_ref,
    grad_ref,
    coarse_ref,
    fine_ref,
    shard_refs,
    small_refs,
    gate4_ref,
    up4_ref,
    down4_ref,
    q_ref,
    k_ref,
    v_ref,
    o_ref,
    h_ref,
    lse_ref,
    aux_ref,
    pos_ref,
    small_ref,
    cos_ref,
    sin_ref,
    attn_out_ref,
    attn_o_out_ref,
    rows_in_ref,
    grads_in_ref,
    gate_full_ref,
    up_full_ref,
    down_full_ref,
    attn_ref,
    attn_o_ref,
    bias_ref,
    proj_ref,
    rows_ref,
    grows_ref,
    tile_ref,
    map_t_ref,
    attn_send,
    attn_recv,
    ffn_local,
    ffn_send,
    ffn_recv,
    out_sem,
    row_local,
    row_send,
    row_recv,
):
    step = pl.program_id(0)
    last = pl.num_programs(0) - 1
    here = Place(group)
    planes = here.planes
    batches, kinds, length = pos_ref.shape
    width = x_ref.shape[2]
    capacity = length // 2
    shards = (attn_ref, attn_o_ref)
    experts = ((gate4_ref, gate_full_ref), (up4_ref, up_full_ref), (down4_ref, down_full_ref))
    depth = shard_refs[0].shape[0]
    mine = here.block(here.z, here.x, here.core)

    def rows_of(block):
        return pl.ds(pl.multiple_of(block * depth, 16), depth)

    def attn_part(t, block, part):
        full = shards[t]
        half = full.shape[1] // 2
        if part is None:
            return full.at[rows_of(block), :]
        return full.at[rows_of(block), pl.ds(pl.multiple_of(part * half, LANES), half)]

    def attn_copy(t, slot, z, x, part, peer):
        ref = attn_part(t, here.block(z, x, here.core), part)
        return remote(ref, ref, attn_send.at[t, slot], attn_recv.at[t, slot], peer)

    def to_z(t, k):
        return attn_copy(t, k, here.z, here.x, None, here.z_peer(1 if k == 0 else planes - 1))

    def from_z(t, k):
        return attn_copy(t, k, z_at(planes - 1 if k == 0 else 1), here.x, None, here.x_peer)

    def pass_z(t, k):
        z = z_at(planes - 1 if k == 0 else 1)
        return attn_copy(t, 2 + k, z, here.x, k, here.z_peer(1 if k == 0 else planes - 1))

    def passed_z(t, k):
        return attn_copy(t, 2 + k, z_at(2), here.x, k, here.x_peer)

    def to_x(t, step_z):
        return attn_copy(t, 4 + step_z, z_at(step_z), here.x, here.y, here.x_peer)

    def from_x(t, step_z):
        return attn_copy(t, 4 + step_z, z_at(step_z), 1 - here.x, here.y, here.x_peer)

    def to_y(t, step_z):
        return attn_copy(t, 4 + planes + step_z, z_at(step_z), 1 - here.x, here.y, here.y_peer)

    def from_y(t, step_z):
        return attn_copy(t, 4 + planes + step_z, z_at(step_z), 1 - here.x, 1 - here.y, here.y_peer)

    def to_core(t, step_z, x):
        return attn_copy(t, 4 + 2 * planes + 2 * step_z + x, z_at(step_z), here.x if x == 0 else 1 - here.x, None, here.core_peer)

    def from_core(t, step_z, x):
        ref = attn_part(t, here.block(z_at(step_z), here.x if x == 0 else 1 - here.x, 1 - here.core), None)
        slot = 4 + 2 * planes + 2 * step_z + x
        return remote(ref, ref, attn_send.at[t, slot], attn_recv.at[t, slot], here.core_peer)

    def z_at(k):
        return (here.z + k) % planes

    def ffn_to_x(j):
        source, full = experts[j]
        return remote(
            source.at[here.expert(1)],
            full.at[here.z, here.x, here.core],
            ffn_send.at[j, 0],
            ffn_recv.at[j, 0],
            here.x_peer,
        )

    def ffn_from_x(j):
        source, full = experts[j]
        return remote(
            source.at[here.expert(1)],
            full.at[here.z, 1 - here.x, here.core],
            ffn_send.at[j, 0],
            ffn_recv.at[j, 0],
            here.x_peer,
        )

    def ffn_mine(j):
        source, full = experts[j]
        return pltpu.make_async_copy(source.at[here.expert(0)], full.at[here.z, here.x, here.core], ffn_local.at[j])

    def ffn_copy(j, slot, z, x, core, peer):
        full = experts[j][1]
        part = full.at[z, :, core] if x is None else full.at[z, x, core]
        return remote(part, part, ffn_send.at[j, slot], ffn_recv.at[j, slot], peer)

    def ffn_to_z(j, k):
        return ffn_copy(j, 1 + k, here.z, None, here.core, here.z_peer(1 if k == 0 else planes - 1))

    def ffn_from_z(j, k):
        return ffn_copy(j, 1 + k, z_at(planes - 1 if k == 0 else 1), None, here.core, here.x_peer)

    def ffn_pass_z(j, k):
        z = z_at(planes - 1 if k == 0 else 1)
        return ffn_copy(j, 3 + k, z, k, here.core, here.z_peer(1 if k == 0 else planes - 1))

    def ffn_passed_z(j, k):
        return ffn_copy(j, 3 + k, z_at(2), k, here.core, here.x_peer)

    def ffn_to_core(j, step_z):
        return ffn_copy(j, 5 + step_z, z_at(step_z), None, here.core, here.core_peer)

    def ffn_from_core(j, step_z):
        return ffn_copy(j, 5 + step_z, z_at(step_z), None, 1 - here.core, here.core_peer)

    def row_copy(kind, member, number):
        source, target = ((grows_ref, grads_in_ref), (rows_ref, rows_in_ref))[kind]
        src, dst = source.at[member, number], target.at[number, member]
        if number == 0:
            return pltpu.make_async_copy(src, dst, row_local.at[kind, member])
        return remote(
            src,
            dst,
            row_send.at[kind, member, number],
            row_recv.at[kind, member, number],
            here.plane_peers[number],
        )

    def outs(t):
        full, target = ((attn_ref, attn_out_ref), (attn_o_ref, attn_o_out_ref))[t]
        return pltpu.make_async_copy(full, target, out_sem.at[t])

    @pl.when(step == 0)
    def _():
        for j in range(3):
            ffn_mine(j).start()
        for part in range(3):
            attn_ref[rows_of(mine), part * width : (part + 1) * width] = shard_refs[part][...].astype(BF16)
        attn_o_ref[rows_of(mine), :] = shard_refs[3][...].astype(BF16)
        tile_ref[...] = jnp.zeros_like(tile_ref)
        at = 0
        for part in small_refs:
            tile_ref[at : at + part.shape[0], 0:depth] = part[...]
            at += part.shape[0]
        tile_ref[at : at + kinds, 0:kinds] = map_ref[...]
        turned = jnp.transpose(tile_ref[...])
        map_t_ref[...] = pltpu.roll(turned[0:kinds, :], LANES - kinds - 8, 1)
        attn_ref[rows_of(mine), 3 * width : 3 * width + LANES] = turned[0:depth, :].astype(BF16)
        attn_ref[rows_of(mine), 3 * width + LANES :] = jnp.zeros((depth, LANES), BF16)
        here.barrier(
            [here.core_peer, here.x_peer, here.y_peer, here.xy_peer, here.z_peer(1), here.z_peer(planes - 1)]
        )
        for t in range(2):
            to_z(t, 0).start()
            to_z(t, 1).start()
            to_x(t, 0).start()
            to_core(t, 0, 0).start()
        for j in range(3):
            ffn_to_x(j).start()

        ids = iota((kinds, length), 0)
        before = jnp.where(iota((length, length), 0) < iota((length, length), 1), 1.0, 0.0).astype(BF16)
        for member in range(batches):
            first = routes_ref[0:1, member * length : (member + 1) * length] == ids
            second = routes_ref[1:2, member * length : (member + 1) * length] == ids
            hits = jnp.where(first | second, 1.0, 0.0)
            pos_ref[member] = jnp.where(hits > 0.0, nn(hits.astype(BF16), before), -1.0)

        def grad_rows(index, carry):
            member, number = index // 4, index % 4
            line = pos_ref[member, pl.ds(here.expert(number), 1), :]
            grows_ref[member, number] = nn(slot_mask(line, capacity), grad_ref[member]).astype(BF16)
            return carry

        lax.fori_loop(0, 4 * batches, grad_rows, 0)
        for member in range(batches):
            row_copy(0, member, 0).start()
            row_copy(0, member, 2).start()

        for high in range(coarse_ref.shape[1]):
            rows = slice(high * fine_ref.shape[1], (high + 1) * fine_ref.shape[1])
            cos_high, sin_high = coarse_ref[0, high : high + 1, :], coarse_ref[1, high : high + 1, :]
            cos_ref[rows, :] = cos_high * fine_ref[0] - sin_high * fine_ref[1]
            sin_ref[rows, :] = (sin_high * fine_ref[0] + cos_high * fine_ref[1]) * fine_ref[2]

        for t in range(2):
            for k, step_z in enumerate((planes - 1, 1)):
                from_z(t, k).wait_recv()
                pass_z(t, k).start()
                to_x(t, step_z).start()
                to_core(t, step_z, 0).start()
        for t in range(2):
            from_x(t, 0).wait_recv()
            to_y(t, 0).start()
        for j in range(3):
            ffn_mine(j).wait()
            ffn_from_x(j).wait_recv()
            ffn_to_z(j, 0).start()
            ffn_to_z(j, 1).start()
            ffn_to_core(j, 0).start()
        for t in range(2):
            passed_z(t, 0).wait_recv()
            passed_z(t, 1).wait_recv()
            to_x(t, 2).start()
            to_core(t, 2, 0).start()
        for member in range(batches):
            row_copy(0, member, 1).start()
            row_copy(0, member, 3).start()
        for t in range(2):
            for step_z in (planes - 1, 1, 2):
                from_x(t, step_z).wait_recv()
                to_y(t, step_z).start()
        for t in range(2):
            for step_z in (0, planes - 1, 1, 2):
                from_y(t, step_z).wait_recv()
                to_core(t, step_z, 1).start()
        for t in range(2):
            for step_z in range(planes):
                for x in range(2):
                    from_core(t, step_z, x).wait_recv()
        for t in range(2):
            outs(t).start()
        small_ref[...] = jnp.transpose(attn_ref[:, 3 * width : 3 * width + LANES].astype(F32))[0 : kinds + 8, :]

    def between():
        @pl.when(step == last)
        def _():
            for j in range(3):
                for k, step_z in enumerate((planes - 1, 1)):
                    ffn_from_z(j, k).wait_recv()
                    ffn_pass_z(j, k).start()
                    ffn_to_core(j, step_z).start()

    sequence_forward(
        x_ref,
        seg_ref[pl.ds(step, 1), :],
        routes_ref[:, pl.ds(pl.multiple_of(step * length, LANES), length)],
        prev_ref,
        map_t_ref,
        small_ref,
        attn_ref.at[:, 0:width],
        attn_ref.at[:, width : 2 * width],
        attn_ref.at[:, 2 * width : 3 * width],
        attn_o_ref,
        cos_ref,
        sin_ref,
        pos_ref.at[pl.ds(step, 1)],
        q_ref,
        k_ref,
        v_ref,
        o_ref,
        h_ref,
        lse_ref,
        aux_ref,
        lambda number: rows_ref.at[pl.ds(step, 1), number],
        bias_ref,
        proj_ref,
        here.expert,
        between,
    )
    for member in range(batches):

        @pl.when(step == member)
        def _():
            for number in range(4):
                row_copy(1, member, number).start()

    @pl.when(step == last)
    def _():
        for j in range(3):
            for k in range(2):
                ffn_passed_z(j, k).wait_recv()
            ffn_to_core(j, 2).start()
        for t in range(2):
            outs(t).wait()
            for k in range(2):
                to_z(t, k).wait_send()
                pass_z(t, k).wait_send()
            for step_z in range(planes):
                to_x(t, step_z).wait_send()
                to_y(t, step_z).wait_send()
                for x in range(2):
                    to_core(t, step_z, x).wait_send()
        for j in range(3):
            ffn_to_x(j).wait_send()
            for k in range(2):
                ffn_to_z(j, k).wait_send()
                ffn_pass_z(j, k).wait_send()
            for step_z in range(planes):
                ffn_to_core(j, step_z).wait_send()
                ffn_from_core(j, step_z).wait_recv()
        for kind in range(2):
            for member in range(batches):
                for number in range(4):
                    copy = row_copy(kind, member, number)
                    copy.wait()


def expert_kernel(
    a_ref,
    g_ref,
    gate_ref,
    up_ref,
    down_ref,
    v_ref,
    d_ref,
    grad_gate_ref,
    grad_up_ref,
    grad_down_ref,
    rows_ref,
    grads_ref,
    gates_ref,
    rows_t_ref,
    grads_t_ref,
    places_ref,
    acc_value_ref,
    acc_input_ref,
    acc_gate_ref,
    acc_up_ref,
    acc_down_ref,
    share_ref,
    sems,
):
    step = pl.program_id(0)
    last = pl.num_programs(0) - 1
    batches, capacity, width = g_ref.shape[1:]
    blocks = 4 * batches

    @pl.when(step == 0)
    def _():
        copies = []
        for number in range(4):
            rows, grads = a_ref.at[number], g_ref.at[number]
            for member in range(batches):
                block = number * batches + member
                span = pl.ds(block * capacity, capacity)
                copies.append(
                    pltpu.make_async_copy(
                        rows.at[member, pl.ds(capacity, 16), pl.ds(0, capacity)],
                        gates_ref.at[block],
                        sems.at[3 * block],
                    )
                )
                copies.append(
                    pltpu.make_async_copy(
                        rows.at[member, pl.ds(0, capacity), :], rows_ref.at[span, :], sems.at[3 * block + 1]
                    )
                )
                copies.append(
                    pltpu.make_async_copy(grads.at[member], grads_ref.at[span, :], sems.at[3 * block + 2])
                )
        for copy in copies:
            copy.start()
        for copy in copies:
            copy.wait()
        same = iota((capacity, capacity), 0) == iota((capacity, capacity), 1)
        spare = jnp.zeros((capacity, width), BF16)
        rows_ref[blocks * capacity :, :] = spare
        grads_ref[blocks * capacity :, :] = spare
        share_ref[...] = jnp.zeros_like(share_ref)

        def pack(block, place):
            span = pl.ds(pl.multiple_of(block * capacity, capacity), capacity)
            target = pl.ds(pl.multiple_of(place, 16), capacity)
            parts = gates_ref[block].astype(F32)
            count = jnp.max(parts[3:4, :]).astype(jnp.int32)
            line = jnp.sum(parts[0:3, :], axis=0, keepdims=True)
            column = jnp.sum(jnp.where(same, line, 0.0), axis=1, keepdims=True)
            rows = rows_ref[span, :]
            grads = (grads_ref[span, :].astype(F32) * column).astype(BF16)
            rows_ref[target, :] = rows
            grads_ref[target, :] = grads
            places_ref[block] = place
            return place + (count + 15) // 16 * 16

        total = lax.fori_loop(0, blocks, pack, 0)
        target = pl.ds(pl.multiple_of(total, 16), capacity)
        rows_ref[target, :] = spare
        grads_ref[target, :] = spare
        places_ref[blocks] = (total + capacity - 1) // capacity

        def turn(block, carry):
            span = pl.ds(pl.multiple_of(block * capacity, capacity), capacity)
            grads_t_ref[:, span] = jnp.transpose(grads_ref[span, :])
            rows_t_ref[:, span] = jnp.transpose(rows_ref[span, :])
            return carry

        lax.fori_loop(0, places_ref[blocks], turn, 0)

    acc_gate_ref[...] = jnp.zeros_like(acc_gate_ref)
    acc_up_ref[...] = jnp.zeros_like(acc_up_ref)
    acc_down_ref[...] = jnp.zeros_like(acc_down_ref)

    def work(block, carry):
        span = pl.ds(pl.multiple_of(block * capacity, capacity), capacity)
        rows = rows_ref[span, :]
        grads = grads_ref[span, :]
        gate = nn(rows, gate_ref[...])
        up = nn(rows, up_ref[...])
        back = nt(grads, down_ref[...])
        sig = 1.0 / (1.0 + jnp.exp(-gate))
        silu = gate * sig
        act = (silu * up).astype(BF16)
        grad_gate = (back * up * (sig * (1.0 + gate * (1.0 - sig)))).astype(BF16)
        grad_up = (back * silu).astype(BF16)
        value = nn(act, down_ref[...])
        grad_rows = nt(grad_gate, gate_ref[...]) + nt(grad_up, up_ref[...])
        rows_t = rows_t_ref[:, span]
        acc_gate_ref[...] += nn(rows_t, grad_gate)
        acc_up_ref[...] += nn(rows_t, grad_up)
        acc_down_ref[...] += nn(grads_t_ref[:, span], act)
        share = jnp.broadcast_to(
            jnp.sum(act.astype(F32) * back, axis=1, keepdims=True), (capacity, LANES)
        )

        @pl.when(step == 0)
        def _():
            share_ref[span, :] = share
            acc_value_ref[span, :] = value
            acc_input_ref[span, :] = grad_rows

        @pl.when(step > 0)
        def _():
            share_ref[span, :] += share

        @pl.when((step > 0) & (step < last))
        def _():
            acc_value_ref[span, :] += value
            acc_input_ref[span, :] += grad_rows

        @pl.when(step == last)
        def _():
            rows_ref[span, :] = (acc_value_ref[span, :] + value).astype(BF16)
            grads_ref[span, :] = (acc_input_ref[span, :] + grad_rows).astype(BF16)

        return carry

    lax.fori_loop(0, places_ref[blocks], work, 0)
    grad_gate_ref[...] = acc_gate_ref[...].astype(BF16)
    grad_up_ref[...] = acc_up_ref[...].astype(BF16)
    grad_down_ref[...] = jnp.transpose(acc_down_ref[...].astype(BF16))

    @pl.when(step == last)
    def _():
        same = iota((capacity, capacity), 0) == iota((capacity, capacity), 1)
        place = iota((16, capacity), 0)

        def shares(block, carry):
            column = share_ref[pl.ds(pl.multiple_of(places_ref[block], 16), capacity), 0:1]
            line = jnp.sum(jnp.where(same, column, 0.0), axis=0, keepdims=True)
            high = line.astype(BF16).astype(F32)
            mid = (line - high).astype(BF16).astype(F32)
            low = line - high - mid
            parts = jnp.where(place == 0, high, jnp.where(place == 1, mid, jnp.where(place == 2, low, 0.0)))
            gates_ref[block] = parts.astype(BF16)
            return carry

        lax.fori_loop(0, blocks, shares, 0)
        copies = []
        for number in range(4):
            values, grads = v_ref.at[number], d_ref.at[number]
            for member in range(batches):
                block = number * batches + member
                span = pl.ds(pl.multiple_of(places_ref[block], 16), capacity)
                copies.append(pltpu.make_async_copy(rows_ref.at[span, :], values.at[member], sems.at[3 * block]))
                copies.append(
                    pltpu.make_async_copy(
                        grads_ref.at[span, :], grads.at[member, pl.ds(0, capacity), :], sems.at[3 * block + 1]
                    )
                )
                copies.append(
                    pltpu.make_async_copy(
                        gates_ref.at[block],
                        grads.at[member, pl.ds(capacity, 16), pl.ds(0, capacity)],
                        sems.at[3 * block + 2],
                    )
                )
        for copy in copies:
            copy.start()
        for copy in copies:
            copy.wait()


def constant_mix(zs, index):
    za, zb = zs[:, index : index + 1], zs[:, index + 1 : index + 2]
    top = jnp.maximum(za, zb)
    ea, eb = jnp.exp(za - top), jnp.exp(zb - top)
    return ea / (ea + eb), eb / (ea + eb)


def token_columns(pos_ref, aux_ref, cols_ref):
    kinds, length = pos_ref.shape[1:]
    cols_ref[0:kinds, :] = pos_ref[0]
    cols_ref[kinds : kinds + 16, :] = aux_ref[0]
    cols_ref[kinds + 16 :, :] = jnp.zeros((LANES - kinds - 16, length), F32)
    return jnp.transpose(cols_ref[...])


def column(source, index):
    return jnp.sum(jnp.where(iota((1, LANES), 1) == index, source, 0.0), axis=1, keepdims=True)


def result_kernel(own_ref, v_ref, pos_ref, aux_ref, h_ref, small_ref, out_ref, cols_ref):
    block_output(own_ref, v_ref, pos_ref, aux_ref, h_ref, small_ref, out_ref, cols_ref)


def finish_kernel(
    own_ref,
    v_ref,
    pos_ref,
    aux_ref,
    h_ref,
    small_ref,
    sums_ref,
    out_ref,
    gq_ref,
    gk_ref,
    gv_ref,
    go_ref,
    router_ref,
    proj_ref,
    vec_ref,
    gain_one_ref,
    gain_two_ref,
    map_ref,
    cols_ref,
    tile_ref,
):
    @pl.when(pl.program_id(0) == 0)
    def _():
        depth, width = gq_ref.shape
        kinds = pos_ref.shape[1]
        for part, ref in enumerate((gq_ref, gk_ref, gv_ref, go_ref)):
            ref[...] = sums_ref[:, part * width : (part + 1) * width]
        small = sums_ref[:, 4 * width : 4 * width + LANES]
        tile_ref[...] = jnp.zeros_like(tile_ref)
        tile_ref[0:depth, :] = small
        turned = jnp.transpose(tile_ref[...])
        at = 0
        for ref in (router_ref, proj_ref, vec_ref, gain_one_ref, gain_two_ref):
            ref[...] = turned[at : at + ref.shape[0], 0:depth]
            at += ref.shape[0]
        map_ref[...] = pltpu.roll(small[0:kinds, :], LANES - kinds - 8, 1)[:, 0:kinds]

    block_output(own_ref, v_ref, pos_ref, aux_ref, h_ref, small_ref, out_ref, cols_ref)


def block_output(own_ref, v_ref, pos_ref, aux_ref, h_ref, small_ref, out_ref, cols_ref):
    own = own_ref[0]
    length, width = h_ref.shape[1:]
    kinds = pos_ref.shape[1]
    ffn = kinds - 4
    capacity = v_ref.shape[2]
    hidden = h_ref[0]
    n2 = hidden * rms_scale(hidden) * small_ref[kinds + 7 : kinds + 8, :]
    n2_high, n2_low = split2(n2)
    small = small_ref[...].astype(BF16)
    cols = token_columns(pos_ref, aux_ref, cols_ref)
    out_ref[0] = hidden
    slot_lane = iota((1, capacity), 1).astype(F32)

    def take(number, carry):
        expert = own ^ number
        mask = jnp.where(column(cols, expert) == slot_lane, 1.0, 0.0).astype(BF16)
        out_ref[0] += column(cols, kinds + expert) * nn(mask, v_ref[number, 0])
        return carry

    lax.fori_loop(0, 4, take, 0, unroll=2)
    result = out_ref[0]
    mixes = nt(n2_high, small) + nt(n2_low, small)
    share = column(cols, kinds + ffn + 1)
    for constant in range(2):
        weight = column(cols, kinds + ffn + 2 + constant)
        alpha_a, alpha_b = constant_mix(mixes, kinds + 2 * constant)
        result = result + (weight * alpha_b) * small_ref[kinds + 4 + constant : kinds + 5 + constant, :]
        share = share + weight * alpha_a
    out_ref[0] = result + share * n2


def sequence_combine(
    step,
    d_ref,
    pos_ref,
    aux_ref,
    prev_ref,
    h_ref,
    g_ref,
    o_ref,
    small_ref,
    wo_ref,
    dh_ref,
    dob_ref,
    sgrad_ref,
    grad_map_ref,
    acc_ref,
    cols_ref,
    expert_of,
    arrived=lambda: None,
):
    length, width = h_ref.shape[1:]
    kinds = pos_ref.shape[1]
    ffn = kinds - 4
    capacity = d_ref.shape[2] - 16
    hidden = h_ref[0]
    inverse = rms_scale(hidden)
    gain = small_ref[kinds + 7 : kinds + 8, :]
    n2 = hidden * inverse * gain
    n2_high, n2_low = split2(n2)
    grad_low = g_ref[0]
    grad = grad_low.astype(F32)
    small = small_ref[...].astype(BF16)
    cols = token_columns(pos_ref, aux_ref, cols_ref)
    lane = iota((1, LANES), 1)
    gate_one = column(cols, 2 * kinds)
    gate_two = column(cols, 2 * kinds + 1)
    ids = lane.astype(F32)
    hot_one = jnp.where(column(cols, 2 * kinds + 2) == ids, 1.0, 0.0)
    hot_two = jnp.where(column(cols, 2 * kinds + 3) == ids, 1.0, 0.0)

    shares = jnp.zeros((length, LANES), F32)
    mixes = nt(n2_high, small) + nt(n2_low, small)
    inner = nt(grad_low, small)
    with_n2 = jnp.sum(grad * n2, axis=1, keepdims=True)
    weight_copy = column(cols, kinds + ffn + 1)
    shares = jnp.where(lane == ffn + 1, weight_copy * with_n2, shares)
    share = weight_copy
    coefs = jnp.zeros((length, LANES), F32)
    for constant in range(2):
        weight = column(cols, kinds + ffn + 2 + constant)
        alpha_a, alpha_b = constant_mix(mixes, kinds + 2 * constant)
        with_vec = inner[:, kinds + 4 + constant : kinds + 5 + constant]
        share = share + weight * alpha_a
        da = weight * with_n2
        db = weight * with_vec
        mean = alpha_a * da + alpha_b * db
        shares = jnp.where(lane == ffn + 2 + constant, mean, shares)
        coefs = jnp.where(lane == kinds + 2 * constant, alpha_a * (da - mean), coefs)
        coefs = jnp.where(lane == kinds + 2 * constant + 1, alpha_b * (db - mean), coefs)
        coefs = jnp.where(lane == kinds + 4 + constant, weight * alpha_b, coefs)

    arrived()
    dh_ref[0] = jnp.zeros((length, width), F32)
    slot_lane = iota((1, capacity), 1).astype(F32)

    def take(number, shares):
        expert = expert_of(number)
        mask = jnp.where(column(cols, expert) == slot_lane, 1.0, 0.0).astype(BF16)
        dh_ref[0] += nn(mask, d_ref[number, 0, 0:capacity, :])
        parts = nt(mask, d_ref[number, 0, capacity:, 0:capacity])
        return jnp.where(lane == expert, jnp.sum(parts, axis=1, keepdims=True), shares)

    shares = lax.fori_loop(0, 4, take, shares)
    grad_n2 = dh_ref[0]

    share_one = jnp.sum(shares * hot_one, axis=1, keepdims=True)
    share_two = jnp.sum(shares * hot_two, axis=1, keepdims=True)
    both = share_one + share_two
    dlogits = (share_one - gate_one * both) * hot_one + (share_two - gate_two * both) * hot_two
    coefs = jnp.where(lane < kinds, dlogits, coefs)
    back = jnp.where(lane < kinds + 4, coefs, 0.0)[:, 0:16]
    back_high, back_low = split2(back)
    grad_n2 = grad_n2 + nn(back_high, small) + nn(back_low, small) + share * grad

    coefs_t = jnp.transpose(coefs)[0:16, :]
    high, low = split2(coefs_t)
    by_n2 = nn(high, n2_high) + nn(low, n2_high)
    by_low = nn(high, n2_low)
    by_grad = nn(high, grad_low) + nn(low, grad_low)
    row = iota((16, 1), 0)
    parts = jnp.where(row < kinds, by_n2, jnp.where(row < kinds + 4, by_n2 + by_low, by_grad))
    gain_part = jnp.sum(grad_n2 * hidden * inverse, axis=0, keepdims=True)
    parts = jnp.where(row == kinds + 7, gain_part, jnp.where(row == kinds + 6, 0.0, parts))
    dlog_t = coefs_t[0:kinds, :]
    map_lane = iota((kinds, LANES), 1)
    map_part = jnp.zeros((kinds, LANES), F32)
    for j in range(kinds):
        map_part = jnp.where(
            map_lane == j, jnp.sum(dlog_t * prev_ref[j : j + 1, :], axis=1, keepdims=True), map_part
        )

    scaled = gain * grad_n2
    inner_mean = jnp.mean(scaled * hidden, axis=-1, keepdims=True)
    dh = grad + inverse * scaled - hidden * (inverse * inverse * inverse) * inner_mean
    dh_ref[0] = dh
    db = dh.astype(BF16)
    dob_ref[0] = nt(db, wo_ref[...]).astype(BF16)
    wo_part = nn(jnp.transpose(o_ref[0]), db)

    @pl.when(step == 0)
    def _():
        acc_ref[...] = wo_part
        sgrad_ref[...] = parts
        grad_map_ref[...] = map_part

    @pl.when(step > 0)
    def _():
        acc_ref[...] += wo_part
        sgrad_ref[...] += parts
        grad_map_ref[...] += map_part


def combine_kernel(
    own_ref,
    d_ref,
    pos_ref,
    aux_ref,
    prev_ref,
    h_ref,
    g_ref,
    o_ref,
    small_ref,
    wo_ref,
    dh_ref,
    dob_ref,
    grad_wo_ref,
    sgrad_ref,
    grad_map_ref,
    acc_ref,
    cols_ref,
):
    own = own_ref[0]
    step = pl.program_id(0)
    sequence_combine(
        step,
        d_ref,
        pos_ref,
        aux_ref,
        prev_ref,
        h_ref,
        g_ref,
        o_ref,
        small_ref,
        wo_ref,
        dh_ref,
        dob_ref,
        sgrad_ref,
        grad_map_ref,
        acc_ref,
        cols_ref,
        lambda number: own ^ number,
    )

    @pl.when(step == pl.num_programs(0) - 1)
    def _():
        grad_wo_ref[...] = acc_ref[...].astype(BF16)


def backward_tables(segments, lse_ref, bias_ref, lse_t_ref):
    length = lse_ref.shape[1]
    allowed = same_document(segments) & (
        iota((length, length), 0) // BLOCK <= iota((length, length), 1) // BLOCK
    )
    bias_ref[...] = jnp.where(allowed, 0.0, NEG)
    lse_t_ref[...] = jnp.transpose(lse_ref[0])


def sequence_backward(
    step,
    x_ref,
    q_ref,
    k_ref,
    v_ref,
    dob_ref,
    dh_ref,
    small_ref,
    w_ref,
    cos_ref,
    sin_ref,
    gin_ref,
    gain_ref,
    bias_ref,
    lse_t_ref,
    dqkv_ref,
    acc_ref,
    between=lambda: None,
):
    length, width = x_ref.shape[1:]
    kinds = small_ref.shape[0] - 8
    pairs = width // LANES
    lane = iota((1, LANES), 1)
    low_half = (lane % HEAD_DIM) < (HEAD_DIM // 2)
    first_head = lane < HEAD_DIM
    mask_a = jnp.where(first_head, 1.0, 0.0).astype(BF16)
    mask_b = jnp.where(first_head, 0.0, 1.0).astype(BF16)

    def pair(h, carry):
        cols = pl.ds(pl.multiple_of(h * LANES, LANES), LANES)
        keys_t = jnp.transpose(k_ref[0, :, cols])
        grad_keys = None
        grad_values = None
        grad_queries = []
        for begin in range(0, length, BLOCK):
            end = begin + BLOCK
            queries = q_ref[0, begin:end, cols]
            outs = dob_ref[0, begin:end, cols]
            keys = k_ref[0, 0:end, cols]
            values = v_ref[0, 0:end, cols]
            queries = jnp.concatenate([queries * mask_a, queries * mask_b], axis=0)
            outs = jnp.concatenate([outs * mask_a, outs * mask_b], axis=0)
            bias = bias_ref[0:end, begin:end]
            bias = jnp.concatenate([bias, bias], axis=1)
            line = jnp.concatenate(
                [lse_t_ref[pl.ds(2 * h, 1), begin:end], lse_t_ref[pl.ds(2 * h + 1, 1), begin:end]], axis=1
            )
            chances = jnp.exp(nt(keys, queries) + bias - line)
            grad_chances = nt(values, outs)
            delta = jnp.sum(chances * grad_chances, axis=0, keepdims=True)
            grad_scores = (chances * (grad_chances - delta)).astype(BF16)
            dv = nn(chances.astype(BF16), outs)
            dk = nn(grad_scores, queries)
            dq = jnp.transpose(nn(keys_t[:, 0:end], grad_scores))
            grad_queries.append(jnp.where(first_head, dq[0:BLOCK], dq[BLOCK:]))
            if grad_keys is None:
                grad_keys, grad_values = dk, dv
            else:
                grad_keys = jnp.concatenate([grad_keys + dk[0:begin], dk[begin:]], axis=0)
                grad_values = jnp.concatenate([grad_values + dv[0:begin], dv[begin:]], axis=0)
        dq = jnp.concatenate(grad_queries, axis=0) * 0.125
        dq = dq * cos_ref[...] - swap_halves(dq, low_half) * sin_ref[...]
        dk = grad_keys * cos_ref[...] - swap_halves(grad_keys, low_half) * sin_ref[...]
        dqkv_ref[:, cols] = dq.astype(BF16)
        dqkv_ref[:, pl.ds(pl.multiple_of(width + h * LANES, LANES), LANES)] = dk.astype(BF16)
        dqkv_ref[:, pl.ds(pl.multiple_of(2 * width + h * LANES, LANES), LANES)] = grad_values.astype(BF16)
        return carry

    lax.fori_loop(0, pairs, pair, 0, unroll=2)
    between()

    tokens = x_ref[0].astype(F32)
    inverse = rms_scale(tokens)
    gain = small_ref[kinds + 6 : kinds + 7, :]
    a1_t = jnp.transpose((tokens * inverse * gain).astype(BF16))

    @pl.when(step == 0)
    def _():
        acc_ref[...] = jnp.zeros_like(acc_ref)

    gin_ref[0] = jnp.zeros((length, width), F32)

    def project(part, carry):
        span = pl.ds(pl.multiple_of(part * width, LANES), width)
        gin_ref[0] += nt(dqkv_ref[:, span], w_ref[:, span])
        acc_ref[:, span] += nn(a1_t, dqkv_ref[:, span])
        return carry

    lax.fori_loop(0, 3, project, 0)
    dn1 = gin_ref[0]
    scaled = gain * dn1
    inner_mean = jnp.mean(scaled * tokens, axis=-1, keepdims=True)
    gin_ref[0] = dh_ref[0] + inverse * scaled - tokens * (inverse * inverse * inverse) * inner_mean
    gain_part = jnp.broadcast_to(jnp.sum(dn1 * tokens * inverse, axis=0, keepdims=True), gain_ref.shape)

    @pl.when(step == 0)
    def _():
        gain_ref[...] = gain_part

    @pl.when(step > 0)
    def _():
        gain_ref[...] += gain_part


def small_table(depth, sgrad_ref, grad_map_ref, gain_ref):
    kinds = grad_map_ref.shape[0]
    width = sgrad_ref.shape[1]
    row = iota((16, 1), 0)
    table = jnp.where(row == kinds + 6, gain_ref[0:1, :], sgrad_ref[...])
    chosen = jnp.where(iota((LANES, width), 1) % depth == iota((LANES, width), 0), 1.0, 0.0).astype(BF16)
    maps = nn(grad_map_ref[...].astype(BF16), chosen)
    table = jnp.concatenate([table, maps, jnp.zeros((LANES - 16 - kinds, width), F32)], axis=0)
    return jnp.transpose(table).astype(BF16)


def backward_kernel(
    x_ref,
    seg_ref,
    q_ref,
    k_ref,
    v_ref,
    dob_ref,
    lse_ref,
    dh_ref,
    small_ref,
    w_ref,
    cos_ref,
    sin_ref,
    gin_ref,
    grad_w_ref,
    gain_ref,
    bias_ref,
    lse_t_ref,
    dqkv_ref,
    acc_ref,
):
    step = pl.program_id(0)
    backward_tables(seg_ref[0], lse_ref, bias_ref, lse_t_ref)
    sequence_backward(
        step,
        x_ref,
        q_ref,
        k_ref,
        v_ref,
        dob_ref,
        dh_ref,
        small_ref,
        w_ref,
        cos_ref,
        sin_ref,
        gin_ref,
        gain_ref,
        bias_ref,
        lse_t_ref,
        dqkv_ref,
        acc_ref,
    )

    @pl.when(step == pl.num_programs(0) - 1)
    def _():
        grad_w_ref[...] = acc_ref[...].astype(BF16)


class ReducedChunk:
    def __init__(self, here, depth, begin, value_of, send_buffer, core_buffer, buffers, out_ref, sems):
        self.here, self.depth, self.begin, self.value_of = here, depth, begin, value_of
        self.send_buffer, self.acc, self.out_ref = send_buffer, core_buffer, out_ref
        y_first, x_first, x_second, y_second, self.z_buffer, self.done, self.other = buffers
        send, recv, z_send, z_recv = sems
        planes, x, y = here.planes, here.x, here.y
        near = planes // 2
        self.half = send_buffer.shape[3] // 2
        self.mine = pl.ds(pl.multiple_of(y * self.half, LANES), self.half)
        theirs = pl.ds(pl.multiple_of((1 - y) * self.half, LANES), self.half)
        self.received = (y_first, x_first, x_second, y_second)
        acc = core_buffer
        self.swap = remote(send_buffer, acc, send.at[0], recv.at[0], here.core_peer)
        self.y_first = remote(acc.at[0:near, :, :, theirs], y_first, send.at[1], recv.at[1], here.y_peer)
        self.x_first = remote(acc.at[near:planes, 1 - x], x_first, send.at[2], recv.at[2], here.x_peer)
        self.x_second = remote(acc.at[0:near, 1 - x, :, self.mine], x_second, send.at[3], recv.at[3], here.x_peer)
        self.y_second = remote(acc.at[near:planes, x, :, theirs], y_second, send.at[4], recv.at[4], here.y_peer)
        self.along = [
            remote(
                acc.at[(here.z + k) % planes, x, :, self.mine],
                self.z_buffer.at[k - 1],
                z_send.at[k - 1],
                z_recv.at[k - 1],
                here.z_peer(k),
            )
            for k in range(1, planes)
        ]
        self.back = remote(self.done, self.other, send.at[5], recv.at[5], here.y_peer)
        self.phases = (self.first, self.second, self.third, self.fourth, self.fifth)

    def rows_of(self, z, column, core):
        return pl.ds(pl.multiple_of(self.here.block(z, column, core) * self.depth, 16), self.depth)

    def lower(self):
        def body(z, carry):
            for column in range(2):
                rows = self.rows_of(z, column, 1 - self.here.core)
                self.send_buffer[z, column] = self.value_of(rows).astype(BF16)
            return carry

        lax.fori_loop(0, self.here.planes, body, 0)

    def add(self, target, source):
        target[...] = (target[...].astype(F32) + source[...].astype(F32)).astype(BF16)

    def first(self):
        self.swap.wait_recv()

        def body(z, carry):
            for column in range(2):
                own = self.value_of(self.rows_of(z, column, self.here.core)).astype(F32)
                self.acc[z, column] = (own + self.acc[z, column].astype(F32)).astype(BF16)
            return carry

        lax.fori_loop(0, self.here.planes, body, 0)
        self.y_first.start()
        self.x_first.start()

    def second(self):
        planes = self.here.planes
        self.y_first.wait_recv()
        for z in range(planes // 2):
            for column in range(2):
                self.add(self.acc.at[z, column, :, self.mine], self.received[0].at[z, column])
        self.x_second.start()
        self.x_first.wait_recv()
        for z in range(planes // 2, planes):
            self.add(self.acc.at[z, self.here.x], self.received[1].at[z - planes // 2])
        self.y_second.start()

    def third(self):
        planes = self.here.planes
        self.x_second.wait_recv()
        for z in range(planes // 2):
            self.add(self.acc.at[z, self.here.x, :, self.mine], self.received[2].at[z])
        self.y_second.wait_recv()
        for z in range(planes // 2, planes):
            self.add(self.acc.at[z, self.here.x, :, self.mine], self.received[3].at[z - planes // 2])
        for copy in self.along:
            copy.start()

    def fourth(self):
        total = self.acc[self.here.z, self.here.x, :, self.mine].astype(F32)
        for k, copy in enumerate(self.along):
            copy.wait_recv()
            total = total + self.z_buffer[k].astype(F32)
        self.done[...] = total.astype(BF16)
        self.back.start()

    def fifth(self):
        self.back.wait_recv()
        y = self.here.y
        spot = pl.ds(pl.multiple_of(self.begin + y * self.half, LANES), self.half)
        other = pl.ds(pl.multiple_of(self.begin + (1 - y) * self.half, LANES), self.half)
        self.out_ref[:, spot] = self.done[...].astype(F32)
        self.out_ref[:, other] = self.other[...].astype(F32)
        for copy in [self.swap, self.y_first, self.x_first, self.x_second, self.y_second, self.back] + self.along:
            copy.wait_send()


def attention_columns(acc_ref, acc_wo_ref, table_ref, begin, columns, rows):
    pieces = []
    width = acc_wo_ref.shape[1]
    for start, size, ref in (
        (0, 3 * width, acc_ref),
        (3 * width, width, acc_wo_ref),
        (4 * width, LANES, table_ref),
        (4 * width + LANES, LANES, None),
    ):
        low, high = max(begin, start) - start, min(begin + columns, start + size) - start
        if low < high:
            if ref is None:
                pieces.append(jnp.zeros((rows.size, high - low), F32))
            else:
                pieces.append(ref[rows, low:high].astype(F32))
    return pieces[0] if len(pieces) == 1 else jnp.concatenate(pieces, axis=1)


def reduce_attention(chunks, free_sem, beside):
    chunks[0].lower()
    pl.semaphore_wait(free_sem, 1)
    chunks[0].swap.start()
    for chunk in chunks[1:]:
        chunk.lower()
        chunk.swap.start()
    phases = len(chunks[0].phases)
    for step in range(len(chunks) + phases - 1):
        for number, chunk in enumerate(chunks):
            if 0 <= step - number < phases:
                chunk.phases[step - number]()
        if step in beside:
            beside[step]()


def fused_backward_kernel(
    group,
    depth,
    pos_ref,
    aux_ref,
    prev_ref,
    h_ref,
    g_ref,
    o_ref,
    x_ref,
    seg_ref,
    q_ref,
    k_ref,
    v_ref,
    lse_ref,
    small_ref,
    w_ref,
    wo_ref,
    cos_ref,
    sin_ref,
    d_ref,
    val_ref,
    gate_ref,
    up_ref,
    down_ref,
    gin_ref,
    sums_ref,
    d_in_ref,
    val_in_ref,
    gate_out_ref,
    up_out_ref,
    down_out_ref,
    acc_ref,
    acc_wo_ref,
    table_ref,
    send_buffers,
    chunk_buffers,
    cols_ref,
    dh_ref,
    dob_ref,
    sgrad_ref,
    grad_map_ref,
    gain_ref,
    bias_ref,
    lse_t_ref,
    dqkv_ref,
    rows_ref,
    gate_own,
    up_own,
    down_own,
    gate_swap,
    up_swap,
    down_swap,
    gate_near,
    up_near,
    down_near,
    gate_far,
    up_far,
    down_far,
    row_local,
    row_send,
    row_recv,
    ffn_local,
    ffn_send,
    ffn_recv,
    free_sem,
    reduce_send,
    reduce_recv,
    reduce_z_send,
    reduce_z_recv,
):
    step = pl.program_id(0)
    last = pl.num_programs(0) - 1
    here = Place(group)
    planes = here.planes
    batches = d_ref.shape[1]
    width = x_ref.shape[2]
    grads = (gate_ref, up_ref, down_ref)
    owns = (gate_own, up_own, down_own)
    swaps = (gate_swap, up_swap, down_swap)
    nears = (gate_near, up_near, down_near)
    fars = (gate_far, up_far, down_far)
    outs = (gate_out_ref, up_out_ref, down_out_ref)
    side = (here.z_peer(1), here.z_peer(planes - 1))

    def z_at(k):
        return (here.z + k) % planes

    def row_copy(kind, member, number):
        source, target = ((d_ref, d_in_ref), (val_ref, val_in_ref))[kind]
        src, dst = source.at[number, member], target.at[number, member]
        if number == 0:
            return pltpu.make_async_copy(src, dst, row_local.at[batches * 4 + member])
        return remote(
            src, dst, row_send.at[kind, member, number], row_recv.at[kind, member, number], here.plane_peers[number]
        )

    def load_rows(member, number):
        source = d_ref if number == 0 else d_in_ref
        return pltpu.make_async_copy(
            source.at[number, member], rows_ref.at[number, 0], row_local.at[member * 4 + number]
        )

    def own_copy(j):
        return pltpu.make_async_copy(grads[j].at[:, :, here.core], owns[j], ffn_local.at[j, 0])

    def swap_copy(j):
        return remote(
            grads[j].at[:, :, 1 - here.core], swaps[j], ffn_send.at[j, 0], ffn_recv.at[j, 0], here.core_peer
        )

    def near_copy(j, k):
        return remote(
            owns[j].at[z_at(2), k], nears[j].at[k], ffn_send.at[j, 1 + k], ffn_recv.at[j, 1 + k], side[k]
        )

    def far_copy(j, k):
        return remote(
            owns[j].at[z_at(1 if k == 0 else planes - 1)],
            fars[j].at[k],
            ffn_send.at[j, 3 + k],
            ffn_recv.at[j, 3 + k],
            side[k],
        )

    def plane_copy(j, number):
        x = here.x if number % 2 == 0 else 1 - here.x
        src, dst = owns[j].at[here.z, x], outs[j].at[here.expert(0)]
        if number == 0:
            return pltpu.make_async_copy(src, dst, ffn_local.at[j, 1])
        return remote(
            src, dst, ffn_send.at[j, 4 + number], ffn_recv.at[j, 4 + number], here.plane_peers[number]
        )

    def plane_arrival(j, number):
        dst = outs[j].at[here.expert(number)]
        return remote(
            dst, dst, ffn_send.at[j, 4 + number], ffn_recv.at[j, 4 + number], here.plane_peers[number]
        )

    def add(target, *sources):
        value = target[...].astype(F32)
        for source in sources:
            value = value + source[...].astype(F32)
        target[...] = value.astype(BF16)

    @pl.when(step == 0)
    def _():
        for j in range(3):
            own_copy(j).start()
        here.barrier(
            [here.core_peer, here.x_peer, here.y_peer, here.xy_peer] + [here.z_peer(k) for k in range(1, planes)]
        )
        for number in range(1, 4):
            row_copy(0, 0, number).start()
        for j in range(3):
            swap_copy(j).start()
        for j in range(3):
            own_copy(j).wait()
            swap_copy(j).wait_recv()
            for x in range(2):

                def add_core(z, carry):
                    add(owns[j].at[z, x], swaps[j].at[z, x])
                    return carry

                lax.fori_loop(0, planes, add_core, 0)
            near_copy(j, 0).start()
            near_copy(j, 1).start()
        pl.semaphore_signal(free_sem, inc=1, device_id=here.core_peer, device_id_type=MESH)

    def arrived():
        for member in range(batches):

            @pl.when(step == member)
            def _():
                for number in range(1, 4):
                    row_copy(0, member, number).wait_recv()
                if member + 1 < batches:
                    for number in range(1, 4):
                        row_copy(0, member + 1, number).start()
                for number in range(4):
                    row_copy(1, member, number).start()
                for number in range(4):
                    load_rows(member, number).start()
                for number in range(4):
                    load_rows(member, number).wait()

    backward_tables(seg_ref[pl.ds(step, 1), :], lse_ref, bias_ref, lse_t_ref)
    sequence_combine(
        step,
        rows_ref,
        pos_ref,
        aux_ref,
        prev_ref,
        h_ref,
        g_ref,
        o_ref,
        small_ref,
        wo_ref,
        dh_ref,
        dob_ref,
        sgrad_ref,
        grad_map_ref,
        acc_wo_ref,
        cols_ref,
        here.expert,
        arrived,
    )

    def start_far(j):
        far_copy(j, 0).start()
        far_copy(j, 1).start()

    def finish_far(j):
        for k in range(2):
            far_copy(j, k).wait_recv()
        for x in range(2):
            add(owns[j].at[here.z, x], fars[j].at[0, x], fars[j].at[1, x])
        for number in range(4):
            plane_copy(j, number).start()

    def between():
        @pl.when(step == 0)
        def _():
            for j in range(3):
                for k in range(2):
                    near_copy(j, k).wait_recv()
                    add(owns[j].at[z_at(1 if k == 0 else planes - 1), k], nears[j].at[k])
            start_far(0)

        @pl.when(step == last)
        def _():
            finish_far(0)
            start_far(2)

    sequence_backward(
        step,
        x_ref,
        q_ref,
        k_ref,
        v_ref,
        dob_ref,
        dh_ref,
        small_ref,
        w_ref,
        cos_ref,
        sin_ref,
        gin_ref,
        gain_ref,
        bias_ref,
        lse_t_ref,
        dqkv_ref,
        acc_ref,
        between,
    )

    @pl.when(step == 0)
    def _():
        start_far(1)

    @pl.when(step == last)
    def _():
        table_ref[...] = small_table(depth, sgrad_ref, grad_map_ref, gain_ref)
        chunks = []
        begin = 0
        for number, (send_buffer, buffers) in enumerate(zip(send_buffers, chunk_buffers)):
            columns = send_buffer.shape[3]
            home, place = (gate_swap, begin) if begin < gate_swap.shape[3] else (up_swap, begin - gate_swap.shape[3])
            chunks.append(
                ReducedChunk(
                    here,
                    depth,
                    begin,
                    functools.partial(attention_columns, acc_ref, acc_wo_ref, table_ref, begin, columns),
                    send_buffer,
                    home.at[:, :, :, place : place + columns],
                    buffers,
                    sums_ref,
                    (
                        reduce_send.at[number],
                        reduce_recv.at[number],
                        reduce_z_send.at[number],
                        reduce_z_recv.at[number],
                    ),
                )
            )
            begin += columns
        reduce_attention(chunks, free_sem, {2: lambda: finish_far(1), len(chunks) + 1: lambda: finish_far(2)})
        for j in range(3):
            swap_copy(j).wait_send()
            for k in range(2):
                near_copy(j, k).wait_send()
                far_copy(j, k).wait_send()
            plane_copy(j, 0).wait()
            for number in range(1, 4):
                plane_copy(j, number).wait_send()
                plane_arrival(j, number).wait_recv()
        for member in range(batches):
            row_copy(1, member, 0).wait()
            for number in range(1, 4):
                row_copy(0, member, number).wait_send()
                row_copy(1, member, number).wait()


def params(limit_mib):
    return pltpu.CompilerParams(vmem_limit_bytes=limit_mib * 1024 * 1024, dimension_semantics=("arbitrary",))


def rotary(length):
    halfway = HEAD_DIM // 2
    frequency = 10000.0 ** (-jnp.arange(halfway).astype(F32) / halfway)
    angles = jnp.arange(length).astype(F32)[:, None] * frequency[None, :]
    cosine, sine = jnp.cos(angles), jnp.sin(angles)
    return (
        jnp.concatenate([cosine] * 4, axis=1),
        jnp.concatenate([-sine, sine, -sine, sine], axis=1),
    )


def rotary_parts(length):
    halfway = HEAD_DIM // 2
    frequency = 10000.0 ** (-np.arange(halfway) / halfway)
    step = 32
    sign = np.tile(np.repeat([-1.0, 1.0], halfway), LANES // HEAD_DIM)

    def table(positions):
        angles = np.tile(positions[:, None] * frequency[None, :], (1, LANES // halfway))
        return np.cos(angles), np.sin(angles)

    coarse = table(np.arange(0, length, step))
    fine = table(np.arange(step))
    signs = np.broadcast_to(sign, fine[0].shape)
    return jnp.asarray(np.stack(coarse), F32), jnp.asarray(np.stack(fine + (signs,)), F32)


def local(
    reps,
    group,
    block_input,
    prev_logits,
    routes,
    segments,
    grad_out,
    gain_attn,
    w_query,
    w_key,
    w_value,
    w_output,
    gain_mix,
    router,
    route_map,
    const_proj,
    const_vec,
    w_gate,
    w_up,
    w_down,
):
    batches, length = segments.shape
    width = block_input.shape[1]
    kinds = router.shape[1]
    ffn = w_gate.shape[1]
    hidden = w_gate.shape[2]
    rows_d = w_gate.shape[0]
    rows_f = w_down.shape[0]
    capacity = length // 2
    planes = group // 4
    assert reps == 2 and ffn == 4 and group % 4 == 0
    g = lax.axis_index("grp")
    y = lax.axis_index("rep")
    core = g % 2
    x = (g // 2) % 2
    z = g // 4
    own = (2 * y + x).astype(jnp.int32)
    own_arr = own.reshape(1)

    x_flip = [(i, i ^ 2) for i in range(group)]
    core_flip = [(i, i ^ 1) for i in range(group)]
    y_flip = [(0, 1), (1, 0)]
    xy_flip = [(r * group + i, (1 - r) * group + (i ^ 2)) for r in range(2) for i in range(group)]

    def z_shift(k):
        return [(i, (i + 4 * k) % group) for i in range(group)]

    def to_plane(parts):
        return [
            parts[0],
            lax.ppermute(parts[1], "grp", x_flip),
            lax.ppermute(parts[2], "rep", y_flip),
            lax.ppermute(parts[3], ("rep", "grp"), xy_flip),
        ]

    tokens = block_input.reshape(batches, length, width)
    grads = grad_out.reshape(batches, length, width)
    route_rows = routes.T
    prev_rows = prev_logits.T
    row_spec = pl.BlockSpec((2, length), lambda b, *_: (0, b))
    prev_spec = pl.BlockSpec((kinds, length), lambda b, *_: (0, b))

    def spec_w(j):
        return pl.BlockSpec((width, width), lambda b, *_: (0, j), pipeline_mode=pl.Buffered(1))

    row_shape = jax.ShapeDtypeStruct((batches, capacity, width), BF16)
    seq_bf16 = jax.ShapeDtypeStruct((batches, length, width), BF16)
    seq_f32 = jax.ShapeDtypeStruct((batches, length, width), F32)
    fused = planes == 4 and rows_d % 16 == 0 and rows_f % 16 == 0
    if fused:
        any_space = pl.BlockSpec(memory_space=pl.ANY)
        coarse, fine = rotary_parts(length)
        smalls = [router.T, const_proj.T, const_vec.T, gain_attn[None], gain_mix[None]]
        out_struct = jax.ShapeDtypeStruct
        (
            q, k, v, o, h1, lse, aux, pos, small, cos, sin, attn, attn_o, a_rows, grad_rows, gate_full, up_full, down_full,
        ) = pl.pallas_call(
            functools.partial(fused_forward_kernel, group),
            grid=(batches,),
            in_specs=[
                per_seq((length, width)),
                whole((batches, length)),
                whole((2, batches * length)),
                prev_spec,
                whole((kinds, kinds)),
                whole((batches, length, width)),
                whole(coarse.shape),
                whole(fine.shape),
                [whole((rows_d, width))] * 4,
                [whole(part.shape) for part in smalls],
            ]
            + [any_space] * 3,
            out_specs=[per_seq((length, width))] * 5
            + [
                per_seq((length, LANES)),
                per_seq((16, length)),
                whole((batches, kinds, length)),
                whole((kinds + 8, width)),
                whole((length, LANES)),
                whole((length, LANES)),
            ]
            + [any_space] * 7,
            scratch_shapes=[
                pltpu.VMEM((width, 3 * width + 2 * LANES), BF16),
                pltpu.VMEM((width, width), BF16),
                pltpu.VMEM((length, length), F32),
                pltpu.VMEM((length, width), F32),
                pltpu.VMEM((batches, 4, capacity + 16, width), BF16),
                pltpu.VMEM((batches, 4, capacity, width), BF16),
                pltpu.VMEM((LANES, LANES), F32),
                pltpu.VMEM((kinds, LANES), F32),
                pltpu.SemaphoreType.DMA((2, 4 + 4 * planes)),
                pltpu.SemaphoreType.DMA((2, 4 + 4 * planes)),
                pltpu.SemaphoreType.DMA((3,)),
                pltpu.SemaphoreType.DMA((3, 5 + planes)),
                pltpu.SemaphoreType.DMA((3, 5 + planes)),
                pltpu.SemaphoreType.DMA((2,)),
                pltpu.SemaphoreType.DMA((2, batches)),
                pltpu.SemaphoreType.DMA((2, batches, 4)),
                pltpu.SemaphoreType.DMA((2, batches, 4)),
            ],
            out_shape=[seq_bf16] * 4
            + [
                seq_f32,
                out_struct((batches, length, LANES), F32),
                out_struct((batches, 16, length), F32),
                out_struct((batches, kinds, length), F32),
                out_struct((kinds + 8, width), F32),
                out_struct((length, LANES), F32),
                out_struct((length, LANES), F32),
                out_struct((width, 3 * width + 2 * LANES), BF16),
                out_struct((width, width), BF16),
                out_struct((4, batches, capacity + 16, width), BF16),
                out_struct((4, batches, capacity, width), BF16),
                out_struct((planes, 2, 2, rows_d, hidden), BF16),
                out_struct((planes, 2, 2, rows_d, hidden), BF16),
                out_struct((planes, 2, 2, rows_f, width), BF16),
            ],
            compiler_params=pltpu.CompilerParams(
                vmem_limit_bytes=58 * 1024 * 1024,
                dimension_semantics=("arbitrary",),
                collective_id=1,
                has_side_effects=True,
            ),
            cost_estimate=pl.CostEstimate(flops=40 * 10**9, bytes_accessed=60 * 10**6, transcendentals=10**7),
            name="fused_forward",
        )(
            tokens, segments, route_rows, prev_rows, route_map, grads, coarse, fine,
            [w_query, w_key, w_value, w_output], smalls,
            w_gate.astype(BF16).transpose(1, 0, 2),
            w_up.astype(BF16).transpose(1, 0, 2),
            w_down.astype(BF16).transpose(1, 0, 2),
        )
        gate_full = gate_full.reshape(width, hidden)
        up_full = up_full.reshape(width, hidden)
        down_full = down_full.reshape(hidden, width)
    else:
        cos, sin = rotary(length)
        small_shard = jnp.concatenate(
            [router, const_proj, const_vec, gain_attn[:, None], gain_mix[:, None]], axis=1
        ).astype(BF16)
        small_shard = jnp.pad(small_shard, ((0, 0), (0, 2 * LANES - small_shard.shape[1])))
        shard = jnp.concatenate([w.astype(BF16) for w in (w_query, w_key, w_value)] + [small_shard], axis=1)
        shard_o = w_output.astype(BF16)
        attn = lax.all_gather(shard, "grp", axis=0, tiled=True)
        attn_o = lax.all_gather(shard_o, "grp", axis=0, tiled=True)
        small = attn[:, 3 * width : 3 * width + kinds + 8].astype(F32).T

        def pick(array, expert):
            return lax.dynamic_index_in_dim(array, expert, axis=1, keepdims=False)

        def gather_expert(mine, other):
            crossed = lax.ppermute(other, "grp", x_flip)
            both = jnp.where(x == 0, jnp.stack([mine, crossed]), jnp.stack([crossed, mine]))
            pieces = [both] + [lax.ppermute(both, "grp", z_shift(k)) for k in range(1, planes)]
            stacked = jnp.stack(pieces)
            half = jnp.take(stacked, (z - jnp.arange(planes)) % planes, axis=0)
            swapped = lax.ppermute(half, "grp", core_flip)
            return jnp.where(core == 0, jnp.stack([half, swapped], axis=2), jnp.stack([swapped, half], axis=2))

        gate_up = gather_expert(
            jnp.stack([pick(w_gate, own), pick(w_up, own)]).astype(BF16),
            jnp.stack([pick(w_gate, own ^ 1), pick(w_up, own ^ 1)]).astype(BF16),
        )
        down = gather_expert(pick(w_down, own).astype(BF16), pick(w_down, own ^ 1).astype(BF16))
        gate_full = gate_up[:, :, :, 0].reshape(width, hidden)
        up_full = gate_up[:, :, :, 1].reshape(width, hidden)
        down_full = down.reshape(hidden, width)

        *grad_rows, pos = pl.pallas_call(
            grad_rows_kernel,
            grid_spec=pltpu.PrefetchScalarGridSpec(
                num_scalar_prefetch=1,
                grid=(batches,),
                in_specs=[row_spec, per_seq((length, width))],
                out_specs=[per_seq((capacity, width))] * 4 + [per_seq((kinds, length))],
            ),
            out_shape=[row_shape] * 4 + [jax.ShapeDtypeStruct((batches, kinds, length), F32)],
            compiler_params=params(32),
            cost_estimate=pl.CostEstimate(flops=4 * 10**9, bytes_accessed=8 * 10**6, transcendentals=0),
            name="grad_rows",
        )(own_arr, route_rows, grads)
        grad_rows = to_plane(grad_rows)

        q, k, v, o, h1, lse, aux, a_rows = pl.pallas_call(
            forward_kernel,
            grid_spec=pltpu.PrefetchScalarGridSpec(
                num_scalar_prefetch=1,
                grid=(batches,),
                in_specs=[
                    per_seq((length, width)),
                    per_seq((1, length)),
                    row_spec,
                    prev_spec,
                    whole((kinds, kinds)),
                    whole((kinds + 8, width)),
                    spec_w(0),
                    spec_w(1),
                    spec_w(2),
                    spec_w(0),
                    whole((length, LANES)),
                    whole((length, LANES)),
                    per_seq((kinds, length)),
                ],
                out_specs=[per_seq((length, width))] * 5
                + [per_seq((length, LANES)), per_seq((16, length))]
                + [pl.BlockSpec((4, 1, capacity + 16, width), lambda b, *_: (0, b, 0, 0))],
                scratch_shapes=[pltpu.VMEM((length, length), F32), pltpu.VMEM((length, width), F32)],
            ),
            out_shape=[seq_bf16] * 4
            + [
                seq_f32,
                jax.ShapeDtypeStruct((batches, length, LANES), F32),
                jax.ShapeDtypeStruct((batches, 16, length), F32),
            ]
            + [jax.ShapeDtypeStruct((4, batches, capacity + 16, width), BF16)],
            compiler_params=params(56),
            cost_estimate=pl.CostEstimate(flops=20 * 10**9, bytes_accessed=20 * 10**6, transcendentals=10**7),
            name="forward",
        )(own_arr, tokens, segments[:, None], route_rows, prev_rows, route_map.T, small, attn, attn, attn, attn_o, cos, sin, pos)
        a_rows = to_plane([a_rows[i] for i in range(4)])

        a_rows = jnp.stack(a_rows)
        grad_rows = jnp.stack(grad_rows)

    tile = hidden // 4
    total = 4 * batches * capacity
    any_spec = pl.BlockSpec(memory_space=pl.ANY)
    values, input_rows, grad_gate_full, grad_up_full, grad_down_full = pl.pallas_call(
        expert_kernel,
        grid=(hidden // tile,),
        in_specs=[any_spec] * 2
        + [
            pl.BlockSpec((width, tile), lambda f: (0, f)),
            pl.BlockSpec((width, tile), lambda f: (0, f)),
            pl.BlockSpec((tile, width), lambda f: (f, 0)),
        ],
        out_specs=[any_spec] * 2
        + [
            pl.BlockSpec((width, tile), lambda f: (0, f)),
            pl.BlockSpec((width, tile), lambda f: (0, f)),
            pl.BlockSpec((tile, width), lambda f: (f, 0)),
        ],
        scratch_shapes=[
            pltpu.VMEM((total + capacity, width), BF16),
            pltpu.VMEM((total + capacity, width), BF16),
            pltpu.VMEM((4 * batches, 16, capacity), BF16),
            pltpu.VMEM((width, total), BF16),
            pltpu.VMEM((width, total), BF16),
            pltpu.SMEM((4 * batches + 1,), jnp.int32),
            pltpu.VMEM((total, width), F32),
            pltpu.VMEM((total, width), F32),
            pltpu.VMEM((width, tile), F32),
            pltpu.VMEM((width, tile), F32),
            pltpu.VMEM((width, tile), F32),
            pltpu.VMEM((total + capacity, LANES), F32),
            pltpu.SemaphoreType.DMA((12 * batches,)),
        ],
        out_shape=[
            jax.ShapeDtypeStruct((4, batches, capacity, width), BF16),
            jax.ShapeDtypeStruct((4, batches, capacity + 16, width), BF16),
        ]
        + [
            jax.ShapeDtypeStruct((width, hidden), BF16),
            jax.ShapeDtypeStruct((width, hidden), BF16),
            jax.ShapeDtypeStruct((hidden, width), BF16),
        ],
        compiler_params=params(60),
        cost_estimate=pl.CostEstimate(flops=58 * 10**9, bytes_accessed=40 * 10**6, transcendentals=10**7),
        name="expert",
    )(a_rows, grad_rows, gate_full, up_full, down_full)
    if fused:
        columns = 4 * width + 2 * LANES
        once = lambda shape: pl.BlockSpec(
            (1,) + shape, lambda b, *_: (b, 0, 0), pipeline_mode=pl.Buffered(1)
        )
        wide = ((rows_d, hidden), (rows_d, hidden), (rows_f, width))
        near = planes // 2
        parts = (hidden // 2, hidden // 2, width, columns - hidden - width)
        gin, sums, _, values_in, grad_gate, grad_up, grad_down = pl.pallas_call(
            functools.partial(fused_backward_kernel, group, rows_d),
            grid=(batches,),
            in_specs=[
                per_seq((kinds, length)),
                per_seq((16, length)),
                prev_spec,
                once((length, width)),
                once((length, width)),
                once((length, width)),
                once((length, width)),
                whole((batches, length)),
                once((length, width)),
                once((length, width)),
                once((length, width)),
                once((length, LANES)),
                whole((kinds + 8, width), 1),
                pl.BlockSpec((width, 3 * width), lambda b, *_: (0, 0), pipeline_mode=pl.Buffered(1)),
                spec_w(0),
                whole((length, LANES), 1),
                whole((length, LANES), 1),
            ]
            + [any_spec] * 5,
            out_specs=[once((length, width)), whole((rows_d, columns), 1)] + [any_spec] * 5,
            out_shape=[
                seq_f32,
                jax.ShapeDtypeStruct((rows_d, columns), F32),
                jax.ShapeDtypeStruct((4, batches, capacity + 16, width), BF16),
                jax.ShapeDtypeStruct((4, batches, capacity, width), BF16),
            ]
            + [jax.ShapeDtypeStruct((4,) + shape, BF16) for shape in wide],
            scratch_shapes=[
                pltpu.VMEM((width, 3 * width), F32),
                pltpu.VMEM((width, width), F32),
                pltpu.VMEM((width, LANES), BF16),
            ]
            + [[pltpu.VMEM((planes, 2, rows_d, part), BF16) for part in parts]]
            + [
                [[
                    pltpu.VMEM((near, 2, rows_d, part // 2), BF16),
                    pltpu.VMEM((near, rows_d, part), BF16),
                    pltpu.VMEM((near, rows_d, part // 2), BF16),
                    pltpu.VMEM((near, rows_d, part // 2), BF16),
                    pltpu.VMEM((planes - 1, rows_d, part // 2), BF16),
                    pltpu.VMEM((rows_d, part // 2), BF16),
                    pltpu.VMEM((rows_d, part // 2), BF16),
                ] for part in parts]
            ]
            + [
                pltpu.VMEM((LANES, length), F32),
                pltpu.VMEM((1, length, width), F32),
                pltpu.VMEM((1, length, width), BF16),
                pltpu.VMEM((16, width), F32),
                pltpu.VMEM((kinds, LANES), F32),
                pltpu.VMEM((8, width), F32),
                pltpu.VMEM((length, length), F32),
                pltpu.VMEM((LANES, length), F32),
                pltpu.VMEM((length, 3 * width), BF16),
                pltpu.VMEM((4, 1, capacity + 16, width), BF16),
            ]
            + [pltpu.VMEM((planes, 2) + shape, BF16) for shape in wide]
            + [pltpu.VMEM((planes, 2) + shape, BF16) for shape in wide]
            + [pltpu.VMEM((2,) + shape, BF16) for shape in wide]
            + [pltpu.VMEM((2, 2) + shape, BF16) for shape in wide]
            + [
                pltpu.SemaphoreType.DMA((5 * batches,)),
                pltpu.SemaphoreType.DMA((2, batches, 4)),
                pltpu.SemaphoreType.DMA((2, batches, 4)),
                pltpu.SemaphoreType.DMA((3, 2)),
                pltpu.SemaphoreType.DMA((3, 8)),
                pltpu.SemaphoreType.DMA((3, 8)),
                pltpu.SemaphoreType.REGULAR,
                pltpu.SemaphoreType.DMA((len(parts), 6)),
                pltpu.SemaphoreType.DMA((len(parts), 6)),
                pltpu.SemaphoreType.DMA((len(parts), planes - 1)),
                pltpu.SemaphoreType.DMA((len(parts), planes - 1)),
            ],
            compiler_params=pltpu.CompilerParams(
                vmem_limit_bytes=63 * 1024 * 1024,
                dimension_semantics=("arbitrary",),
                collective_id=3,
                has_side_effects=True,
            ),
            cost_estimate=pl.CostEstimate(flops=60 * 10**9, bytes_accessed=60 * 10**6, transcendentals=10**7),
            name="fused_backward",
        )(
            pos, aux, prev_rows, h1, grads, o, tokens, segments, q, k, v, lse, small,
            attn, attn_o, cos, sin, input_rows, values,
            grad_gate_full.reshape(planes, 2, 2, rows_d, hidden),
            grad_up_full.reshape(planes, 2, 2, rows_d, hidden),
            grad_down_full.reshape(planes, 2, 2, rows_f, width),
        )
        grad_gate = grad_gate.transpose(1, 0, 2).astype(F32)
        grad_up = grad_up.transpose(1, 0, 2).astype(F32)
        grad_down = grad_down.transpose(1, 0, 2).astype(F32)
    else:
        values_in = jnp.stack(to_plane([values[i] for i in range(4)]))
        def scatter_expert(full):
            keep = lax.dynamic_index_in_dim(full, core, axis=2, keepdims=False)
            send = lax.dynamic_index_in_dim(full, 1 - core, axis=2, keepdims=False)
            half = (keep.astype(F32) + lax.ppermute(send, "grp", core_flip).astype(F32)).astype(BF16)
            summed = lax.dynamic_index_in_dim(half, z, axis=0, keepdims=False).astype(F32)
            for k in range(1, planes):
                part = lax.dynamic_index_in_dim(half, (z + k) % planes, axis=0, keepdims=False)
                summed = summed + lax.ppermute(part, "grp", z_shift(k)).astype(F32)
            summed = summed.astype(BF16)
            mine = lax.dynamic_index_in_dim(summed, x, axis=0, keepdims=False)
            other = lax.dynamic_index_in_dim(summed, 1 - x, axis=0, keepdims=False)
            arrived = to_plane([mine, other, mine, other])

            def order(first):
                return lambda: tuple(arrived[first ^ e] for e in range(4))

            return lax.switch(own, [order(i) for i in range(4)])

        grad_gate_up = scatter_expert(
            jnp.stack(
                [
                    grad_gate_full.reshape(planes, 2, 2, rows_d, hidden),
                    grad_up_full.reshape(planes, 2, 2, rows_d, hidden),
                ],
                axis=3,
            )
        )
        grad_down = scatter_expert(grad_down_full.reshape(planes, 2, 2, rows_f, width))
        grad_gate = jnp.stack([part[0] for part in grad_gate_up], axis=1).astype(F32)
        grad_up = jnp.stack([part[1] for part in grad_gate_up], axis=1).astype(F32)
        grad_down = jnp.stack(grad_down, axis=1).astype(F32)

        dh1, dob, grad_wo, sgrad, grad_map = pl.pallas_call(
            combine_kernel,
            grid_spec=pltpu.PrefetchScalarGridSpec(
                num_scalar_prefetch=1,
                grid=(batches,),
                in_specs=[pl.BlockSpec((4, 1, capacity + 16, width), lambda b, *_: (0, b, 0, 0))]
                + [
                    per_seq((kinds, length)),
                    per_seq((16, length)),
                    prev_spec,
                    per_seq((length, width)),
                    per_seq((length, width)),
                    per_seq((length, width)),
                    whole((kinds + 8, width)),
                    spec_w(0),
                ],
                out_specs=[per_seq((length, width))] * 2
                + [whole((width, width)), whole((16, width)), whole((kinds, LANES))],
                scratch_shapes=[pltpu.VMEM((width, width), F32), pltpu.VMEM((LANES, length), F32)],
            ),
            out_shape=[
                seq_f32,
                seq_bf16,
                jax.ShapeDtypeStruct((width, width), BF16),
                jax.ShapeDtypeStruct((16, width), F32),
                jax.ShapeDtypeStruct((kinds, LANES), F32),
            ],
            compiler_params=params(56),
            cost_estimate=pl.CostEstimate(flops=12 * 10**9, bytes_accessed=20 * 10**6, transcendentals=10**5),
            name="combine",
        )(own_arr, jnp.stack(to_plane([input_rows[i] for i in range(4)])), pos, aux, prev_rows, h1, grads, o, small, attn_o)

        gin, grad_attn, gain_one = pl.pallas_call(
            backward_kernel,
            grid=(batches,),
            in_specs=[
                per_seq((length, width)),
                per_seq((1, length)),
                per_seq((length, width)),
                per_seq((length, width)),
                per_seq((length, width)),
                per_seq((length, width)),
                per_seq((length, LANES)),
                per_seq((length, width)),
                whole((kinds + 8, width)),
                pl.BlockSpec((width, 3 * width), lambda b, *_: (0, 0), pipeline_mode=pl.Buffered(1)),
                whole((length, LANES)),
                whole((length, LANES)),
            ],
            out_specs=[per_seq((length, width)), whole((width, 3 * width)), whole((8, width))],
            scratch_shapes=[
                pltpu.VMEM((length, length), F32),
                pltpu.VMEM((LANES, length), F32),
                pltpu.VMEM((length, 3 * width), BF16),
                pltpu.VMEM((width, 3 * width), F32),
            ],
            out_shape=[
                seq_f32,
                jax.ShapeDtypeStruct((width, 3 * width), BF16),
                jax.ShapeDtypeStruct((8, width), F32),
            ],
            compiler_params=params(56),
            cost_estimate=pl.CostEstimate(flops=30 * 10**9, bytes_accessed=20 * 10**6, transcendentals=10**7),
            name="backward",
        )(tokens, segments[:, None], q, k, v, dob, lse, dh1, small, attn, cos, sin)

    finish_specs = dict(
        num_scalar_prefetch=1,
        grid=(batches,),
    )
    finish_in = [
        pl.BlockSpec((4, 1, capacity, width), lambda b, *_: (0, b, 0, 0)),
        per_seq((kinds, length)),
        per_seq((16, length)),
        per_seq((length, width)),
        whole((kinds + 8, width)),
    ]
    finish_cost = pl.CostEstimate(flops=4 * 10**9, bytes_accessed=12 * 10**6, transcendentals=0)
    if fused:
        small_shapes = [(rows_d, width)] * 4 + [
            (kinds, rows_d), (4, rows_d), (2, rows_d), (1, rows_d), (1, rows_d), (kinds, kinds)
        ]
        result, gq, gk, gv, go, *small_sums = pl.pallas_call(
            finish_kernel,
            grid_spec=pltpu.PrefetchScalarGridSpec(
                in_specs=finish_in + [whole((rows_d, columns))],
                out_specs=[per_seq((length, width))] + [whole(shape) for shape in small_shapes],
                scratch_shapes=[pltpu.VMEM((LANES, length), F32), pltpu.VMEM((LANES, LANES), F32)],
                **finish_specs,
            ),
            out_shape=[seq_f32] + [jax.ShapeDtypeStruct(shape, F32) for shape in small_shapes],
            compiler_params=params(60),
            cost_estimate=finish_cost,
            name="finish",
        )(own_arr, values_in, pos, aux, h1, small, sums)
        grad_router, grad_proj, grad_vec, grad_one, grad_two, map_total = small_sums
        return (
            result.reshape(batches * length, width),
            gin.reshape(batches * length, width),
            grad_one[0],
            gq,
            gk,
            gv,
            go,
            grad_two[0],
            grad_router.T,
            map_total,
            grad_proj.T,
            grad_vec.T,
            grad_gate,
            grad_up,
            grad_down,
        )

    result = pl.pallas_call(
        result_kernel,
        grid_spec=pltpu.PrefetchScalarGridSpec(
            in_specs=finish_in,
            out_specs=per_seq((length, width)),
            scratch_shapes=[pltpu.VMEM((LANES, length), F32)],
            **finish_specs,
        ),
        out_shape=seq_f32,
        compiler_params=params(40),
        cost_estimate=finish_cost,
        name="result",
    )(own_arr, values_in, pos, aux, h1, small)

    part = lax.psum_scatter(jnp.concatenate([grad_attn, grad_wo], axis=1), "grp", scatter_dimension=0, tiled=True)
    attn_total = lax.psum(part, "rep").astype(F32)
    sgrad = jnp.where(iota((16, 1), 0) == kinds + 6, gain_one[0:1], sgrad)
    packed = jnp.concatenate([sgrad, jnp.pad(grad_map, ((0, 0), (0, width - LANES)))], axis=0)
    packed = lax.psum(packed, ("rep", "grp"))
    sums = lax.dynamic_slice_in_dim(packed[0:16], g * rows_d, rows_d, axis=1).T
    map_total = packed[16:, 0:kinds].T
    return (
        result.reshape(batches * length, width),
        gin.reshape(batches * length, width),
        sums[:, kinds + 6],
        attn_total[:, 0:width],
        attn_total[:, width : 2 * width],
        attn_total[:, 2 * width : 3 * width],
        attn_total[:, 3 * width :],
        sums[:, kinds + 7],
        sums[:, 0:kinds],
        map_total,
        sums[:, kinds : kinds + 4],
        sums[:, kinds + 4 : kinds + 6],
        grad_gate,
        grad_up,
        grad_down,
    )


def solution(mesh):
    rows = P(("rep", "grp"), None)
    in_specs = (
        (rows,) * 5
        + (P("grp"),)
        + (P("grp", None),) * 4
        + (P("grp"), P("grp", None), P(), P("grp", None), P("grp", None))
        + (P("grp", None, None),) * 3
    )
    out_specs = (
        (rows,) * 2
        + (P("grp"),)
        + (P("grp", None),) * 4
        + (P("grp"), P("grp", None), P(), P("grp", None), P("grp", None))
        + (P("grp", None, None),) * 3
    )
    body = functools.partial(local, mesh.shape["rep"], mesh.shape["grp"])
    return jax.shard_map(body, mesh=mesh, in_specs=in_specs, out_specs=out_specs, check_vma=False)
```
